32 devices in a mesh: rows: 4 (over z), keys: 8 (over y, x, core).
Axes of the slice: x: 2, y: 2, z: 4, core: 2. Of those that a mesh axis runs over, the one named last changes fastest.
Arguments:
- tokens: bfloat16 [2, 4, 2048, 768], P(None, 'rows', 'keys'), may hold values from -6 to 6
- prev_logits: bfloat16 [2, 4, 12, 2048, 2048], P(None, 'rows', None, 'keys'), may hold values from -6 to 6
- segments: int32 [2, 4, 2048], P(None, 'rows'), may hold values from 0 to 63, as said below
- out_cot: bfloat16 [2, 4, 2048, 768], P(None, 'rows', 'keys'), may hold values from -6 to 6
- master_mat: float32 [8, 768, 1152], P('rows', None, 'keys'), may hold values from -6 to 6
- mom1_mat: float32 [8, 768, 1152], P('rows', None, 'keys'), may hold values from -38.4 to 38.4
- mom2_mat: float32 [8, 768, 1152], P('rows', None, 'keys'), as said below
- eigen_bases: float32 [8, 768, 768], P('rows'), may hold values from -1 to 1
- master_small: float32 [8, 1152], P('rows', 'keys'), may hold values from -2 to 2
- mom1_small: float32 [8, 1152], P('rows', 'keys'), may hold values from -38.4 to 38.4
- mom2_small: float32 [8, 1152], P('rows', 'keys'), as said below
- owners: int32 [8], replicated, may hold values from 0 to 7, as said below
- step_count: int32 [1], replicated, may hold values from 2 to 20
Outputs:
- out_hidden: bfloat16 [2, 4, 2048, 768], P(None, 'rows', 'keys')
- logits: bfloat16 [2, 4, 12, 2048, 2048], P(None, 'rows', None, 'keys')
- grad_tokens: bfloat16 [2, 4, 2048, 768], P(None, 'rows', 'keys')
- grad_prev: bfloat16 [2, 4, 12, 2048, 2048], P(None, 'rows', None, 'keys')
- grad_mat: float32 [8, 768, 1152], P('rows', None, 'keys')
- new_mom1_mat: float32 [8, 768, 1152], P('rows', None, 'keys')
- new_mom2_mat: float32 [8, 768, 1152], P('rows', None, 'keys')
- new_master_mat: float32 [8, 768, 1152], P('rows', None, 'keys')
- copy_mat: bfloat16 [8, 768, 1152], P('rows', None, 'keys')
- grad_small: float32 [8, 1152], P('rows', 'keys')
- new_mom1_small: float32 [8, 1152], P('rows', 'keys')
- new_mom2_small: float32 [8, 1152], P('rows', 'keys')
- new_master_small: float32 [8, 1152], P('rows', 'keys')
- copy_small: bfloat16 [8, 1152], P('rows', 'keys')
The draws below stay inside these ranges and needn't reach their ends.
Inputs may be any that keep to these rules, and one draw needn't show every extreme that they name: `segments`: in every packed row the ids start at 0 and rise by one at the first slot of each document; documents start only at multiples of 32 slots; a quarter of a row is wholly inside one document with probability g / 3 for rows index g, and two such quarters side by side belong to the same document; every other quarter starts a new document at its first slot and is cut at each further multiple of 32 with probability one half; the first row of the first micro-batch holds 64 documents. `owners`: A permutation. `mom2_mat`: Positive. `mom2_small`: Positive.
All inputs are finite; a program needn't handle non-finite values.
Results may differ from the reference program's by a relative error of at most 0.025.
Values may be sent and summed in bfloat16 or wider, within the bound.
A program may use at most 448 MiB of HBM per device.

```python
import jax
import jax.numpy as jnp
from jax import lax

MODEL_WIDTH = 768
H = 12
HD = 64
FF = 3072
SLOTS = 2048
MB = 2
RPG = 1
SLOT_BLOCKS = 8
ROWS_MB = 4
BLOCK_COLUMNS = 1152
GAIN_ROW_WIDTH = 1152


def slot_owners(key):
    return jax.random.permutation(jax.random.fold_in(key, 17), SLOT_BLOCKS).astype(jnp.int32)


def slot_columns(key):
    owners = slot_owners(key)
    slot_index_list = jnp.arange(SLOT_BLOCKS, dtype=jnp.int32)
    matches = (owners[None, :] == slot_index_list[:, None]).astype(jnp.int32)
    weight_blocks = jnp.sum(matches * slot_index_list[None, :], axis=1)
    return weight_blocks[:, None] * BLOCK_COLUMNS + jnp.arange(BLOCK_COLUMNS, dtype=jnp.int32)[None, :]


def weight_spread(columns):
    inner = MODEL_WIDTH ** (-0.5)
    return jnp.where(columns < 3 * MODEL_WIDTH, inner, jnp.where(columns < 4 * MODEL_WIDTH, 4.0 * inner, jnp.where(columns < 4 * MODEL_WIDTH + FF, inner, FF ** (-0.5))))


def grad_spread(columns):
    root_tok = (MB * ROWS_MB * SLOTS) ** 0.5
    scale_factor = jnp.where(columns < 2 * MODEL_WIDTH, 0.5, jnp.where(columns < 3 * MODEL_WIDTH, 0.6, jnp.where(columns < 4 * MODEL_WIDTH, 0.15, jnp.where(columns < 4 * MODEL_WIDTH + FF, 0.25, 0.5))))
    return root_tok * scale_factor


def noise_spread(key, shape):
    return jax.random.normal(key, shape, jnp.float32)


def small_index():
    return jnp.arange(SLOT_BLOCKS, dtype=jnp.int32)[:, None] * GAIN_ROW_WIDTH + jnp.arange(GAIN_ROW_WIDTH, dtype=jnp.int32)[None, :]


def gain_entries(index):
    return (index >= 3 * MODEL_WIDTH) & (index < 4 * MODEL_WIDTH) | (index >= 6 * MODEL_WIDTH + FF) & (index < 7 * MODEL_WIDTH + FF)


def small_grad_spread(index):
    root_tok = (MB * ROWS_MB * SLOTS) ** 0.5
    scale_factor = jnp.where(index < MODEL_WIDTH, 0.5, jnp.where(index < 2 * MODEL_WIDTH, 0.6, jnp.where(index < 5 * MODEL_WIDTH, 0.7, jnp.where(index < 5 * MODEL_WIDTH + FF, 0.25, jnp.where(index < 6 * MODEL_WIDTH + FF, 0.5, 0.8)))))
    return root_tok * scale_factor


def draw_owners(key, part):
    return slot_owners(key)


def draw_master_mat(key, part):
    spread_width = weight_spread(slot_columns(key))
    return noise_spread(jax.random.fold_in(key, 3), (SLOT_BLOCKS, MODEL_WIDTH, BLOCK_COLUMNS)) * spread_width[:, None, :]


def draw_mom1_mat(key, part):
    column_scale = 0.05 / 0.95 * grad_spread(slot_columns(key))
    return noise_spread(jax.random.fold_in(key, 4), (SLOT_BLOCKS, MODEL_WIDTH, BLOCK_COLUMNS)) * column_scale[:, None, :]


def draw_mom2_mat(key, part):
    spread_width = grad_spread(slot_columns(key))
    scale_factor = jnp.exp(jax.random.uniform(jax.random.fold_in(key, 5), (SLOT_BLOCKS, MODEL_WIDTH, BLOCK_COLUMNS), jnp.float32, jnp.log(0.5), jnp.log(8.0)))
    return scale_factor * (0.05 / 0.95 * spread_width * spread_width)[:, None, :]


def draw_eigen_bases(key, part):
    slot_random_keys = jax.random.split(jax.random.fold_in(key, 6), SLOT_BLOCKS)
    orders = jax.vmap(lambda one_key: jax.random.permutation(one_key, MODEL_WIDTH))(slot_random_keys).astype(jnp.int32)
    sign_values = (2 * jax.random.randint(jax.random.fold_in(key, 7), (SLOT_BLOCKS, 1, MODEL_WIDTH), 0, 2) - 1).astype(jnp.float32)
    positions = jnp.arange(MODEL_WIDTH, dtype=jnp.int32)[None, None, :]
    phase = (2 * positions + 1) * orders[:, :, None] % (4 * MODEL_WIDTH)
    angle = jnp.pi * phase.astype(jnp.float32) / (2.0 * MODEL_WIDTH)
    norms = jnp.where(orders[:, :, None] == 0, (1.0 / MODEL_WIDTH) ** 0.5, (2.0 / MODEL_WIDTH) ** 0.5)
    return norms * jnp.cos(angle) * sign_values


def draw_master_small(key, part):
    index = small_index()
    gain_table = jnp.exp(jax.random.uniform(jax.random.fold_in(key, 8), (SLOT_BLOCKS, GAIN_ROW_WIDTH), jnp.float32, -0.3, 0.3))
    bias_table = 0.2 * noise_spread(jax.random.fold_in(key, 9), (SLOT_BLOCKS, GAIN_ROW_WIDTH))
    return jnp.where(gain_entries(index), gain_table, bias_table)


def draw_mom1_small(key, part):
    scale_amount = 0.05 / 0.95 * small_grad_spread(small_index())
    return noise_spread(jax.random.fold_in(key, 10), (SLOT_BLOCKS, GAIN_ROW_WIDTH)) * scale_amount


def draw_mom2_small(key, part):
    spread_width = small_grad_spread(small_index())
    scale_factor = jnp.exp(jax.random.uniform(jax.random.fold_in(key, 11), (SLOT_BLOCKS, GAIN_ROW_WIDTH), jnp.float32, jnp.log(0.5), jnp.log(8.0)))
    return scale_factor * (0.05 / 0.95) * spread_width * spread_width


def draw_segments(key, part):
    grain = SLOTS // 64
    groups = ROWS_MB // RPG
    group_ids = jnp.arange(ROWS_MB, dtype=jnp.int32) // RPG
    longs = jax.random.randint(jax.random.fold_in(key, 1), (MB, ROWS_MB, 4), 0, groups - 1) < group_ids[None, :, None]
    before = jnp.concatenate([jnp.zeros((MB, ROWS_MB, 1), dtype=bool), longs[:, :, :3]], axis=-1)
    start_flag = jnp.where(longs & before, 0, 1)
    cuts = jax.random.randint(jax.random.fold_in(key, 2), (MB, ROWS_MB, 4, 16), 0, 2)
    first_grain = (jnp.arange(16, dtype=jnp.int32) == 0)[None, None, None, :]
    flags = jnp.where(first_grain, start_flag[..., None], jnp.where(longs[..., None], 0, cuts))
    forced = ((jnp.arange(MB) == 0)[:, None] & (jnp.arange(ROWS_MB) == 0)[None, :])[:, :, None, None]
    flags = jnp.where(forced, 1, flags).reshape(MB, ROWS_MB, 64)
    doc_ids = jnp.cumsum(flags, axis=-1) - 1
    return jnp.repeat(doc_ids, grain, axis=-1).astype(jnp.int32)


def shard_levels(stream_key, dims, cuts, least, largest):
    loudness = 1.0
    for dim, blocks in cuts:
        steps = jax.random.uniform(jax.random.fold_in(jax.random.fold_in(stream_key, 6), dim), (blocks,), jnp.float32, least / len(cuts), largest / len(cuts))
        loudness = loudness * jnp.repeat(jnp.exp(steps), dims[dim] // blocks).reshape((-1,) + (1,) * (len(dims) - 1 - dim))
    return loudness


def normal_values(key, dims, deviation, reach, pieces=(), held_as=jnp.bfloat16):
    drawn = jax.random.normal(key, dims, jnp.float32) * deviation
    if len(pieces) > 0:
        drawn = shard_levels(key, dims, pieces, -0.22, 0.18) * drawn
    return jnp.clip(drawn, min=-reach, max=reach).astype(held_as)


def setup_inputs(seed: int = 0) -> dict:
    arg_keys = jax.random.split(jax.random.key(seed), 14)
    tokens = normal_values(arg_keys[0], (MB, ROWS_MB, SLOTS, MODEL_WIDTH), 1.0, 6.0, ((1, 4), (2, 8)))
    prev_logits = normal_values(arg_keys[1], (MB, ROWS_MB, H, SLOTS, SLOTS), 1.0, 6.0, ((1, 4), (3, 8)))
    segments = draw_segments(jax.random.fold_in(arg_keys[13], 71), 0)
    out_cot = normal_values(arg_keys[3], (MB, ROWS_MB, SLOTS, MODEL_WIDTH), 1.0, 6.0, ((1, 4), (2, 8)))
    master_mat = draw_master_mat(jax.random.fold_in(arg_keys[13], 71), 0)
    mom1_mat = draw_mom1_mat(jax.random.fold_in(arg_keys[13], 71), 0)
    mom2_mat = draw_mom2_mat(jax.random.fold_in(arg_keys[13], 71), 0)
    eigen_bases = draw_eigen_bases(jax.random.fold_in(arg_keys[13], 71), 0)
    master_small = draw_master_small(jax.random.fold_in(arg_keys[13], 71), 0)
    mom1_small = draw_mom1_small(jax.random.fold_in(arg_keys[13], 71), 0)
    mom2_small = draw_mom2_small(jax.random.fold_in(arg_keys[13], 71), 0)
    owners = draw_owners(jax.random.fold_in(arg_keys[13], 71), 0)
    step_count = jax.random.randint(arg_keys[12], (1,), 2, 21).astype(jnp.int32)
    return {"tokens": tokens, "prev_logits": prev_logits, "segments": segments, "out_cot": out_cot, "master_mat": master_mat, "mom1_mat": mom1_mat, "mom2_mat": mom2_mat, "eigen_bases": eigen_bases, "master_small": master_small, "mom1_small": mom1_small, "mom2_small": mom2_small, "owners": owners, "step_count": step_count}


EPS_NORM = 1e-06
BETA_ONE = 0.95
BETA_TWO = 0.95
EPS_ADAM = 1e-08
DECAY = 0.01
RATE_SMALL = 0.3
NEG_BIG = -1e+30
HIGHEST_PREC = lax.Precision.HIGHEST

@jax.custom_vjp
def low(v):
    return lax.optimization_barrier(v.astype(jnp.bfloat16)).astype(jnp.float32)

@jax.custom_vjp
def low_back(v):
    return v

def low_keep(v):
    return (low(v), None)

def low_pass(kept, grad):
    return (grad,)

def back_keep(v):
    return (v, None)

def back_low(kept, grad):
    return (low(grad),)
low.defvjp(low_keep, low_pass)
low_back.defvjp(back_keep, back_low)

def rounded(value):
    return low_back(low(value))

def matmul(left, right):
    return jnp.dot(left, right, precision=HIGHEST_PREC, preferred_element_type=jnp.float32)

def layer_norm(value, gain, shift):
    mean_val = lax.optimization_barrier(jnp.mean(value, axis=-1, keepdims=True))
    centered = value - mean_val
    return centered * lax.rsqrt(lax.optimization_barrier(jnp.mean(centered * centered, axis=-1, keepdims=True)) + EPS_NORM) * gain + shift

def inverse_order(owners):
    slot_index_list = jnp.arange(owners.shape[0], dtype=jnp.int32)
    matches = (owners[None, :] == slot_index_list[:, None]).astype(jnp.int32)
    return lax.optimization_barrier(jnp.sum(matches * slot_index_list[None, :], axis=1)).astype(jnp.int32)

def column_rates(columns):
    inner = MODEL_WIDTH ** (-0.5)
    return jnp.where(columns < 3 * MODEL_WIDTH, inner, jnp.where(columns < 4 * MODEL_WIDTH, 4.0 * inner, jnp.where(columns < 4 * MODEL_WIDTH + FF, inner, FF ** (-0.5))))

def row_forward(master, small_vec, x_row, prev_row, seg_row, owners):
    weights = low(master)
    weight_blocks = jnp.take(weights, owners, axis=0)
    packed_weights = jnp.transpose(weight_blocks, (1, 0, 2)).reshape(MODEL_WIDTH, SLOT_BLOCKS * BLOCK_COLUMNS)
    params = low(small_vec).reshape(-1)
    bias_q = params[:MODEL_WIDTH]
    bias_v = params[MODEL_WIDTH:2 * MODEL_WIDTH]
    bias_o = params[2 * MODEL_WIDTH:3 * MODEL_WIDTH]
    gain_one = params[3 * MODEL_WIDTH:4 * MODEL_WIDTH]
    shift_one = params[4 * MODEL_WIDTH:5 * MODEL_WIDTH]
    bias_up = params[5 * MODEL_WIDTH:5 * MODEL_WIDTH + FF]
    bias_down = params[5 * MODEL_WIDTH + FF:6 * MODEL_WIDTH + FF]
    gain_two = params[6 * MODEL_WIDTH + FF:7 * MODEL_WIDTH + FF]
    shift_two = params[7 * MODEL_WIDTH + FF:]
    projected = matmul(x_row, packed_weights[:, :3 * MODEL_WIDTH])
    queries = rounded(projected[:, :MODEL_WIDTH] + bias_q).reshape(SLOTS, H, HD)
    keyed = rounded(projected[:, MODEL_WIDTH:2 * MODEL_WIDTH]).reshape(SLOTS, H, HD)
    valued = rounded(projected[:, 2 * MODEL_WIDTH:3 * MODEL_WIDTH] + bias_v).reshape(SLOTS, H, HD)
    raw_scores = low_back(jnp.einsum('jhd,ihd->hji', keyed, queries, precision=HIGHEST_PREC) * HD ** (-0.5) + prev_row)
    allowed = (seg_row[:, None] == seg_row[None, :])[None]
    row_top = lax.optimization_barrier(jnp.max(jnp.where(allowed, raw_scores, NEG_BIG), axis=1, keepdims=True))
    expo = jnp.where(allowed, jnp.exp(raw_scores - row_top), 0.0)
    soft_low = low(expo / lax.optimization_barrier(jnp.sum(expo, axis=1, keepdims=True)))
    attended = rounded(jnp.einsum('hji,jhd->ihd', soft_low, valued, precision=HIGHEST_PREC).reshape(SLOTS, MODEL_WIDTH))
    branch = low_back(matmul(attended, packed_weights[:, 3 * MODEL_WIDTH:4 * MODEL_WIDTH]) + bias_o)
    mid_act = layer_norm(x_row + branch, gain_one, shift_one)
    pre_act = low_back(matmul(low(mid_act), packed_weights[:, 4 * MODEL_WIDTH:4 * MODEL_WIDTH + FF]) + bias_up)
    hidden = low(jax.nn.gelu(pre_act, approximate=False))
    ffn_out = low_back(matmul(hidden, packed_weights[:, 4 * MODEL_WIDTH + FF:].T) + bias_down)
    out_row = layer_norm(mid_act + ffn_out, gain_two, shift_two)
    return (out_row, raw_scores)

def reference(tokens, prev_logits, segments, out_cot, master_mat, mom1_mat, mom2_mat, eigen_bases, master_small, mom1_small, mom2_small, owners, step_count):
    row_total = MB * ROWS_MB
    rows_in = (tokens.reshape(row_total, SLOTS, MODEL_WIDTH), prev_logits.reshape(row_total, H, SLOTS, SLOTS), segments.reshape(row_total, SLOTS), out_cot.reshape(row_total, SLOTS, MODEL_WIDTH))

    def scan_step(carry, row_data):
        x_row, prev_row, seg_row, cot_row = row_data

        def closed(master, small_vec, x_val, prev_val):
            return row_forward(master, small_vec, x_val, prev_val, seg_row, owners)
        out_row, back_fn, logit_row = jax.vjp(closed, master_mat, master_small, x_row.astype(jnp.float32), prev_row.astype(jnp.float32), has_aux=True)
        g_mat, g_small, g_x, g_prev = back_fn(cot_row.astype(jnp.float32))
        return ((carry[0] + g_mat, carry[1] + g_small), (out_row.astype(jnp.bfloat16), logit_row.astype(jnp.bfloat16), g_x.astype(jnp.bfloat16), g_prev.astype(jnp.bfloat16)))
    start = (jnp.zeros(master_mat.shape, jnp.float32), jnp.zeros(master_small.shape, jnp.float32))
    (grad_mat, grad_small), (out_rows, logit_rows, grad_x, grad_prev) = lax.scan(scan_step, start, rows_in)
    steps_done = step_count[0].astype(jnp.float32)
    fix_one = 1.0 - jnp.power(jnp.asarray(BETA_ONE, jnp.float32), steps_done)
    fix_two = 1.0 - jnp.power(jnp.asarray(BETA_TWO, jnp.float32), steps_done)
    rotated = jnp.einsum('sed,sec->sdc', eigen_bases, grad_mat, precision=HIGHEST_PREC)
    new_one = BETA_ONE * mom1_mat + (1.0 - BETA_ONE) * rotated
    new_two = BETA_TWO * mom2_mat + (1.0 - BETA_TWO) * rotated * rotated
    direction = new_one / fix_one / (jnp.sqrt(new_two / fix_two) + EPS_ADAM)
    back_rot = jnp.einsum('sdk,skc->sdc', eigen_bases, direction, precision=HIGHEST_PREC)
    inverse = inverse_order(owners)
    columns = inverse[:, None] * BLOCK_COLUMNS + jnp.arange(BLOCK_COLUMNS, dtype=jnp.int32)[None, :]
    rates = column_rates(columns)[:, None, :]
    new_master = master_mat - rates * (back_rot + DECAY * master_mat)
    small_one = BETA_ONE * mom1_small + (1.0 - BETA_ONE) * grad_small
    small_two = BETA_TWO * mom2_small + (1.0 - BETA_TWO) * grad_small * grad_small
    new_small = master_small - RATE_SMALL * (small_one / fix_one) / (jnp.sqrt(small_two / fix_two) + EPS_ADAM)
    return (out_rows.reshape(MB, ROWS_MB, SLOTS, MODEL_WIDTH), logit_rows.reshape(MB, ROWS_MB, H, SLOTS, SLOTS), grad_x.reshape(MB, ROWS_MB, SLOTS, MODEL_WIDTH), grad_prev.reshape(MB, ROWS_MB, H, SLOTS, SLOTS), grad_mat, new_one, new_two, new_master, new_master.astype(jnp.bfloat16), grad_small, small_one, small_two, new_small, new_small.astype(jnp.bfloat16))
```

```python
import functools
import math

import jax
import jax.numpy as jnp
from jax import lax
from jax.experimental import pallas as pl
from jax.experimental.pallas import tpu as pltpu
from jax.sharding import PartitionSpec as P

MODEL_WIDTH = 768
H = 12
HD = 64
FF = 3072
BLOCK_COLUMNS = 1152
GAIN_ROW_WIDTH = 1152

EPS_NORM = 1e-06
BETA_ONE = 0.95
BETA_TWO = 0.95
EPS_ADAM = 1e-08
DECAY = 0.01
RATE_SMALL = 0.3
NEG_BIG = -1e30
NEG_FLOOR = -1e29
HIGHEST_PREC = lax.Precision.HIGHEST
MESH = pl.DeviceIdType.MESH
F32 = jnp.float32
BF16 = jnp.bfloat16
ANY = pl.BlockSpec(memory_space=pl.ANY)
VMEM_SPEC = pl.BlockSpec(memory_space=pltpu.VMEM)
EXT = 16


def layer_norm(value):
    mean_val = jnp.mean(value, axis=-1, keepdims=True)
    centered = value - mean_val
    inv_dev = lax.rsqrt(jnp.mean(centered * centered, axis=-1, keepdims=True) + EPS_NORM)
    return (centered * inv_dev, inv_dev)


def norm_back(grad_in, normed, inv_dev, gain):
    scaled = grad_in * gain
    return inv_dev * (
        scaled
        - jnp.mean(scaled, axis=-1, keepdims=True)
        - normed * jnp.mean(scaled * normed, axis=-1, keepdims=True)
    )


def inverse_order(owners):
    slot_index_list = jnp.arange(owners.shape[0], dtype=jnp.int32)
    matches = (owners[None, :] == slot_index_list[:, None]).astype(jnp.int32)
    return jnp.sum(matches * slot_index_list[None, :], axis=1)


def column_rates(columns):
    inner = MODEL_WIDTH ** (-0.5)
    return jnp.where(
        columns < 3 * MODEL_WIDTH,
        inner,
        jnp.where(
            columns < 4 * MODEL_WIDTH,
            4.0 * inner,
            jnp.where(columns < 4 * MODEL_WIDTH + FF, inner, FF ** (-0.5)),
        ),
    )


def dot_f32(left, right, contract):
    return lax.dot_general(left, right, (contract, ((), ())), preferred_element_type=F32)


class Place:
    def __init__(self, side_y, side_x, rows):
        self.Y, self.X, self.R = side_y, side_x, rows
        key = lax.axis_index("keys")
        self.key = key
        self.r = lax.axis_index("rows")
        self.c = lax.rem(key, 2)
        self.x = lax.rem(key // 2, side_x)
        self.y = key // (2 * side_x)

    def keyof(self, y, x, c):
        return (y * self.X + x) * 2 + c

    def xo(self, d):
        return lax.rem(self.x + d, self.X)

    def yo(self, d):
        return lax.rem(self.y + d, self.Y)

    def ro(self, d):
        return lax.rem(self.r + d, self.R)

    def x_peer(self, d):
        return {"keys": self.keyof(self.y, self.xo(d), self.c)}

    def y_peer(self, d):
        return {"keys": self.keyof(self.yo(d), self.x, self.c)}

    def core_peer(self):
        return {"keys": self.keyof(self.y, self.x, 1 - self.c)}

    def z_peer(self, d):
        return {"rows": self.ro(d)}

    def barrier(self, with_z):
        sem = pltpu.get_barrier_semaphore()
        peers = [self.core_peer()]
        peers += [self.x_peer(d) for d in range(1, self.X)]
        peers += [self.y_peer(d) for d in range(1, self.Y)]
        if with_z:
            peers += [self.z_peer(d) for d in range(1, self.R)]
        for peer in peers:
            pl.semaphore_signal(sem, inc=1, device_id=peer, device_id_type=MESH)
        pl.semaphore_wait(sem, len(peers))


def remote(src, dst, send_sem, recv_sem, peer):
    return pltpu.make_async_remote_copy(
        src_ref=src,
        dst_ref=dst,
        send_sem=send_sem,
        recv_sem=recv_sem,
        device_id=peer,
        device_id_type=MESH,
    )


def sems_per_item(Y, X):
    return (X - 1) + (Y - 1) + 1


class Gather:
    def __init__(self, place, own, buf, send, recv, base, x_first):
        p = place
        self.sent = []
        n = sems_per_item(p.Y, p.X)
        idx = iter(range(base, base + n))
        first = [(p.x_peer(d)) for d in range(1, p.X)] if x_first else [p.y_peer(d) for d in range(1, p.Y)]
        second = [p.y_peer(d) for d in range(1, p.Y)] if x_first else [p.x_peer(d) for d in range(1, p.X)]
        line = buf.at[p.y, :, p.c] if x_first else buf.at[:, p.x, p.c]
        plane = buf.at[:, :, p.c]
        mine = buf.at[p.y, p.x, p.c]
        self.one = []
        for peer in first:
            i = next(idx)
            self.one.append(remote(own, mine, send.at[i], recv.at[i], peer))
        self.two = []
        for peer in second:
            i = next(idx)
            self.two.append(remote(line, line, send.at[i], recv.at[i], peer))
        i = next(idx)
        self.three = [remote(plane, plane, send.at[i], recv.at[i], p.core_peer())]

    def start1(self):
        for copy in self.one:
            copy.start()

    def start2(self):
        for copy in self.one:
            copy.wait_recv()
        for copy in self.two:
            copy.start()

    def start3(self):
        for copy in self.two:
            copy.wait_recv()
        for copy in self.three:
            copy.start()

    def finish(self):
        for copy in self.three:
            copy.wait_recv()
        for copy in self.one + self.two + self.three:
            copy.wait_send()


def gather_weights_kernel(
    Y, X, R, owners, w_ref, ext_ref, x_ref, wt_out, ext_out, xg_out,
    zbuf, zext, stage, sext, zsend, zrecv, send, recv, loc,
):
    p = Place(Y, X, R)
    slots_here = w_ref.shape[0]
    blocks = zbuf.shape[0]
    micro = x_ref.shape[0]
    n = sems_per_item(Y, X)
    p.barrier(True)
    zcopies = []
    here = pl.ds(p.r * slots_here, slots_here)
    for d in range(1, R):
        a = remote(w_ref, zbuf.at[here], zsend.at[d, 0], zrecv.at[d, 0], p.z_peer(d))
        a.start()
        b = remote(ext_ref, zext.at[p.r], zsend.at[d, 1], zrecv.at[d, 1], p.z_peer(d))
        b.start()
        zcopies += [a, b]
    xitems = []
    xlocal = []
    for m in range(micro):
        item = Gather(p, x_ref.at[m], xg_out.at[m], send, recv, m * n, m % 2 == 0)
        item.start1()
        xitems.append(item)
        copy = pltpu.make_async_copy(x_ref.at[m], xg_out.at[m, p.y, p.x, p.c], loc.at[m])
        copy.start()
        xlocal.append(copy)
    wl = pltpu.make_async_copy(w_ref, zbuf.at[here], loc.at[micro])
    wl.start()
    el = pltpu.make_async_copy(ext_ref, zext.at[p.r], loc.at[micro + 1])
    el.start()
    for m in range(micro):
        xlocal[m].wait()
        xitems[m].start2()
    wl.wait()
    el.wait()
    for copy in zcopies:
        copy.wait_recv()
    sext[...] = jnp.sum(zext[...].astype(F32), axis=0).astype(BF16)

    def reorder(b, carry):
        stage[b] = zbuf[owners[b]]
        return carry

    lax.fori_loop(0, blocks, reorder, 0)
    base = micro * n
    eitem = Gather(p, sext, ext_out, send, recv, base, True)
    base += n
    eitem.start1()
    lcopies = []
    ecopy = pltpu.make_async_copy(sext, ext_out.at[p.y, p.x, p.c], loc.at[micro + 2])
    ecopy.start()
    items = []
    for b in range(blocks):
        item = Gather(p, stage.at[b], wt_out.at[b], send, recv, base, b % 2 == 0)
        base += n
        item.start1()
        items.append(item)
        copy = pltpu.make_async_copy(stage.at[b], wt_out.at[b, p.y, p.x, p.c], loc.at[micro + 3 + b])
        copy.start()
        lcopies.append(copy)
    for m in range(micro):
        xitems[m].start3()
    ecopy.wait()
    eitem.start2()
    for b in range(blocks):
        lcopies[b].wait()
        items[b].start2()
    eitem.start3()
    for b in range(blocks):
        items[b].start3()
    for item in xitems + [eitem] + items:
        item.finish()
    for copy in zcopies:
        copy.wait_send()


def gather_weights(mesh_dims, owners, w_own, ext, x_own):
    Y, X, R = mesh_dims
    slots_here, n, width = w_own.shape
    micro, tok = x_own.shape[:2]
    blocks = slots_here * R
    total = sems_per_item(Y, X) * (micro + 1 + blocks)
    return pl.pallas_call(
        functools.partial(gather_weights_kernel, Y, X, R),
        out_shape=(
            jax.ShapeDtypeStruct((blocks, Y, X, 2, n, width), BF16),
            jax.ShapeDtypeStruct((Y, X, 2, EXT, width), BF16),
            jax.ShapeDtypeStruct((micro, Y, X, 2, tok, width), BF16),
        ),
        in_specs=[pl.BlockSpec(memory_space=pltpu.SMEM), ANY, ANY, ANY],
        out_specs=(ANY, ANY, ANY),
        scratch_shapes=[
            pltpu.VMEM((blocks, n, width), BF16),
            pltpu.VMEM((R, EXT, width), BF16),
            pltpu.VMEM((blocks, n, width), BF16),
            pltpu.VMEM((EXT, width), BF16),
            pltpu.SemaphoreType.DMA((R, 2)),
            pltpu.SemaphoreType.DMA((R, 2)),
            pltpu.SemaphoreType.DMA((total,)),
            pltpu.SemaphoreType.DMA((total,)),
            pltpu.SemaphoreType.DMA((micro + 3 + blocks,)),
        ],
        compiler_params=pltpu.CompilerParams(
            collective_id=1, has_side_effects=True, vmem_limit_bytes=40 << 20
        ),
        name="gather_weights",
    )(owners, w_own, ext, x_own)


class Scatter:
    def __init__(self, place, parts, accs, r1s, r2s, r3s, send, recv, loc, base, lbase, y_first, merge):
        p = place
        self.p, self.y_first, self.merge = p, y_first, merge
        self.accs, self.r1s, self.r2s, self.r3s = accs, r1s, r2s, r3s
        self.count = len(parts)
        n = sems_per_item(p.Y, p.X) * len(parts)
        idx = iter(range(base, base + n))
        self.zero, self.one, self.two, self.three = [], [], [], []
        for t, part in enumerate(parts):
            i = next(idx)
            self.zero.append(pltpu.make_async_copy(part.at[:, :, p.c], accs[t], loc.at[lbase + t]))
            self.one.append(remote(part.at[:, :, 1 - p.c], r1s[t], send.at[i], recv.at[i], p.core_peer()))
            if y_first:
                for d in range(1, p.Y):
                    i = next(idx)
                    self.two.append(
                        remote(accs[t].at[p.yo(d)], r2s[t].at[d - 1], send.at[i], recv.at[i], p.y_peer(d))
                    )
                for d in range(1, p.X):
                    i = next(idx)
                    self.three.append(
                        remote(accs[t].at[p.y, p.xo(d)], r3s[t].at[d - 1], send.at[i], recv.at[i], p.x_peer(d))
                    )
            else:
                for d in range(1, p.X):
                    i = next(idx)
                    self.two.append(
                        remote(accs[t].at[:, p.xo(d)], r2s[t].at[d - 1], send.at[i], recv.at[i], p.x_peer(d))
                    )
                for d in range(1, p.Y):
                    i = next(idx)
                    self.three.append(
                        remote(accs[t].at[p.yo(d), p.x], r3s[t].at[d - 1], send.at[i], recv.at[i], p.y_peer(d))
                    )

    def start1(self):
        for copy in self.zero + self.one:
            copy.start()

    def start2(self):
        p = self.p
        for copy in self.zero:
            copy.wait()
        for copy in self.one:
            copy.wait_recv()

        def body(i, carry):
            y, x = i // p.X, lax.rem(i, p.X)
            self.merge([a.at[y, x] for a in self.accs], [r.at[y, x] for r in self.r1s])
            return carry

        lax.fori_loop(0, p.Y * p.X, body, 0)
        for copy in self.two:
            copy.start()

    def start3(self):
        p = self.p
        for copy in self.two:
            copy.wait_recv()
        if self.y_first:
            for d in range(1, p.Y):
                for x in range(p.X):
                    self.merge([a.at[p.y, x] for a in self.accs], [r.at[d - 1, x] for r in self.r2s])
        else:
            for d in range(1, p.X):
                for y in range(p.Y):
                    self.merge([a.at[y, p.x] for a in self.accs], [r.at[d - 1, y] for r in self.r2s])
        for copy in self.three:
            copy.start()

    def finish(self):
        p = self.p
        for copy in self.three:
            copy.wait_recv()
        mine = [a.at[p.y, p.x] for a in self.accs]
        for d in range(1, p.X if self.y_first else p.Y):
            self.merge(mine, [r.at[d - 1] for r in self.r3s])
        return mine

    def drain(self):
        for copy in self.one + self.two + self.three:
            copy.wait_send()


def merge_sum(into, other):
    a, b = into[0], other[0]
    a[...] = (a[...].astype(F32) + b[...].astype(F32)).astype(BF16)


def merge_soft(into, other):
    (va, sa), (vb, sb) = into, other
    ta, tb = sa[...], sb[...]
    heads = ta.shape[0] // 2
    top_a, top_b = ta[:heads], tb[:heads]
    top = jnp.maximum(top_a, top_b)
    wa, wb = jnp.exp(top_a - top), jnp.exp(top_b - top)
    sa[...] = jnp.concatenate([top, wa * ta[heads:] + wb * tb[heads:]], axis=0)
    for h in range(heads):
        rows = slice(h * HD, (h + 1) * HD)
        va[rows, :] = (
            va[rows, :].astype(F32) * wa[h : h + 1] + vb[rows, :].astype(F32) * wb[h : h + 1]
        ).astype(BF16)


def scatter_scratch(Y, X, items, shape, dtype, y_first_of):
    most = max((Y - 1) * X, (X - 1) * Y)
    return [
        pltpu.VMEM((items, Y, X) + shape, dtype),
        pltpu.VMEM((items, Y, X) + shape, dtype),
        pltpu.VMEM((items, max(Y, X) - 1, max(Y, X)) + shape, dtype),
        pltpu.VMEM((items, max(Y, X) - 1) + shape, dtype),
    ]


GROUP = 4


def merge_attention_kernel(
    Y, X, R, o_ref, st_ref, att_out, st_out,
    oa, o1, o2, o3, sa, s1, s2, s3, send, recv, loc,
):
    p = Place(Y, X, R)
    micro = o_ref.shape[0]
    groups = st_ref.shape[1]
    rows = GROUP * HD
    n = sems_per_item(Y, X) * 2
    p.barrier(False)
    items = []
    for g in range(groups):
        for m in range(micro):
            i = m * groups + g
            item = Scatter(
                p,
                [o_ref.at[m, :, :, :, pl.ds(g * rows, rows)], st_ref.at[m, g]],
                [oa.at[i], sa.at[i]],
                [o1.at[i], s1.at[i]],
                [o2.at[i], s2.at[i]],
                [o3.at[i], s3.at[i]],
                send, recv, loc, i * n, i * 2, m % 2 == 0, merge_soft,
            )
            item.start1()
            items.append((m, g, item))
    for m, g, item in items:
        item.start2()
    for m, g, item in items:
        item.start3()
    for m, g, item in items:
        val, st = item.finish()
        tile = st[...]
        inv = 1.0 / tile[GROUP:]
        st_out[m, g] = jnp.concatenate([tile[:GROUP], inv], axis=0)
        for h in range(GROUP):
            att_out[m, g * rows + h * HD : g * rows + (h + 1) * HD, :] = (
                val[h * HD : (h + 1) * HD, :].astype(F32) * inv[h : h + 1]
            ).astype(BF16)
    for m, g, item in items:
        item.drain()


def merge_attention(mesh_dims, o_part, st_part):
    Y, X, R = mesh_dims
    micro, width, tok = o_part.shape[0], o_part.shape[4], o_part.shape[5]
    groups = st_part.shape[1]
    items = micro * groups
    total = sems_per_item(Y, X) * 2 * items
    return pl.pallas_call(
        functools.partial(merge_attention_kernel, Y, X, R),
        out_shape=(
            jax.ShapeDtypeStruct((micro, width, tok), BF16),
            jax.ShapeDtypeStruct((micro, groups, 2 * GROUP, tok), F32),
        ),
        in_specs=[ANY, ANY],
        out_specs=(VMEM_SPEC, VMEM_SPEC),
        scratch_shapes=scatter_scratch(Y, X, items, (GROUP * HD, tok), BF16, None)
        + scatter_scratch(Y, X, items, (2 * GROUP, tok), F32, None)
        + [
            pltpu.SemaphoreType.DMA((total,)),
            pltpu.SemaphoreType.DMA((total,)),
            pltpu.SemaphoreType.DMA((items * 2,)),
        ],
        compiler_params=pltpu.CompilerParams(
            collective_id=2, has_side_effects=True, vmem_limit_bytes=40 << 20
        ),
        name="merge_attention",
    )(o_part, st_part)


def gather_grads_kernel(Y, X, R, d_ref, st_ref, d_out, st_out, send, recv, loc):
    p = Place(Y, X, R)
    micro, groups = st_ref.shape[:2]
    rows = GROUP * HD
    n = sems_per_item(Y, X)
    p.barrier(False)
    items, local = [], []
    i = 0
    for g in range(groups):
        for m in range(micro):
            ds = pl.ds(g * rows, rows)
            for own, out in (
                (d_ref.at[m, ds], d_out.at[m, :, :, :, ds]),
                (st_ref.at[m, g], st_out.at[m, g]),
            ):
                item = Gather(p, own, out, send, recv, i * n, m % 2 == 0)
                item.start1()
                items.append(item)
                copy = pltpu.make_async_copy(own, out.at[p.y, p.x, p.c], loc.at[i])
                copy.start()
                local.append(copy)
                i += 1
    for item, copy in zip(items, local):
        copy.wait()
        item.start2()
    for item in items:
        item.start3()
    for item in items:
        item.finish()


def gather_grads(mesh_dims, datt, st):
    Y, X, R = mesh_dims
    micro, width, tok = datt.shape
    groups, strows = st.shape[1:3]
    items = micro * groups * 2
    total = sems_per_item(Y, X) * items
    return pl.pallas_call(
        functools.partial(gather_grads_kernel, Y, X, R),
        out_shape=(
            jax.ShapeDtypeStruct((micro, Y, X, 2, width, tok), BF16),
            jax.ShapeDtypeStruct((micro, groups, Y, X, 2, strows, tok), F32),
        ),
        in_specs=[ANY, ANY],
        out_specs=(ANY, ANY),
        scratch_shapes=[
            pltpu.SemaphoreType.DMA((total,)),
            pltpu.SemaphoreType.DMA((total,)),
            pltpu.SemaphoreType.DMA((items,)),
        ],
        compiler_params=pltpu.CompilerParams(collective_id=3, has_side_effects=True),
        name="gather_grads",
    )(datt, st)


def scatter_queries_kernel(Y, X, R, dq_ref, dq_out, a, r1, r2, r3, send, recv, loc):
    p = Place(Y, X, R)
    micro = dq_ref.shape[0]
    groups = a.shape[0] // micro
    rows = GROUP * HD
    n = sems_per_item(Y, X)
    p.barrier(False)
    items = []
    for g in range(groups):
        for m in range(micro):
            i = m * groups + g
            item = Scatter(
                p, [dq_ref.at[m, :, :, :, pl.ds(g * rows, rows)]],
                [a.at[i]], [r1.at[i]], [r2.at[i]], [r3.at[i]],
                send, recv, loc, i * n, i, m % 2 == 0, merge_sum,
            )
            item.start1()
            items.append((m, g, item))
    for m, g, item in items:
        item.start2()
    for m, g, item in items:
        item.start3()
    for m, g, item in items:
        (val,) = item.finish()
        dq_out[m, g * rows : (g + 1) * rows, :] = val[...]
    for m, g, item in items:
        item.drain()


def scatter_queries(mesh_dims, dq_part):
    Y, X, R = mesh_dims
    micro, width, tok = dq_part.shape[0], dq_part.shape[4], dq_part.shape[5]
    groups = width // (GROUP * HD)
    items = micro * groups
    total = sems_per_item(Y, X) * items
    return pl.pallas_call(
        functools.partial(scatter_queries_kernel, Y, X, R),
        out_shape=jax.ShapeDtypeStruct((micro, width, tok), BF16),
        in_specs=[ANY],
        out_specs=VMEM_SPEC,
        scratch_shapes=scatter_scratch(Y, X, items, (GROUP * HD, tok), BF16, None)
        + [
            pltpu.SemaphoreType.DMA((total,)),
            pltpu.SemaphoreType.DMA((total,)),
            pltpu.SemaphoreType.DMA((items,)),
        ],
        compiler_params=pltpu.CompilerParams(
            collective_id=4, has_side_effects=True, vmem_limit_bytes=40 << 20
        ),
        name="scatter_queries",
    )(dq_part)


def scatter_weights_kernel(
    Y, X, R, inverse, g_ref, e_ref, g_out, e_out,
    a, r1, r2, r3, ea, e1, e2, e3, stage, rz, ez, send, recv, loc, zsend, zrecv,
):
    p = Place(Y, X, R)
    blocks = g_ref.shape[0]
    slots_here = g_out.shape[0]
    n = sems_per_item(Y, X)
    p.barrier(True)
    items = []
    for b in range(blocks):
        item = Scatter(
            p, [g_ref.at[b]], [a.at[b]], [r1.at[b]], [r2.at[b]], [r3.at[b]],
            send, recv, loc, b * n, b, b % 2 == 0, merge_sum,
        )
        item.start1()
        items.append(item)
    eitem = Scatter(
        p, [e_ref], [ea.at[0]], [e1.at[0]], [e2.at[0]], [e3.at[0]],
        send, recv, loc, blocks * n, blocks, True, merge_sum,
    )
    eitem.start1()
    for item in items + [eitem]:
        item.start2()
    for item in items + [eitem]:
        item.start3()
    for item in items + [eitem]:
        item.finish()
    fin = a.at[:, p.y, p.x]

    def reorder(s, carry):
        stage[s] = fin[inverse[s]]
        return carry

    lax.fori_loop(0, blocks, reorder, 0)
    emine = ea.at[0, p.y, p.x]
    zcopies = []
    for d in range(1, R):
        there = pl.ds(p.ro(d) * slots_here, slots_here)
        copy = remote(stage.at[there], rz.at[d - 1], zsend.at[d, 0], zrecv.at[d, 0], p.z_peer(d))
        copy.start()
        zcopies.append(copy)
        copy = remote(emine, ez.at[d - 1], zsend.at[d, 1], zrecv.at[d, 1], p.z_peer(d))
        copy.start()
        zcopies.append(copy)
    for item in items + [eitem]:
        item.drain()
    for copy in zcopies:
        copy.wait_recv()
    e_out[...] = emine[...].astype(F32) + jnp.sum(ez[...].astype(F32), axis=0)
    for s in range(slots_here):
        total = stage[p.r * slots_here + s].astype(F32)
        for d in range(1, R):
            total = total + rz[d - 1, s].astype(F32)
        g_out[s] = total
    for copy in zcopies:
        copy.wait_send()


def scatter_weights(mesh_dims, inverse, grads, ext):
    Y, X, R = mesh_dims
    blocks, n, width = grads.shape[0], grads.shape[4], grads.shape[5]
    slots_here = blocks // R
    per = sems_per_item(Y, X)
    return pl.pallas_call(
        functools.partial(scatter_weights_kernel, Y, X, R),
        out_shape=(
            jax.ShapeDtypeStruct((slots_here, n, width), F32),
            jax.ShapeDtypeStruct((EXT, width), F32),
        ),
        in_specs=[pl.BlockSpec(memory_space=pltpu.SMEM), ANY, ANY],
        out_specs=(VMEM_SPEC, VMEM_SPEC),
        scratch_shapes=scatter_scratch(Y, X, blocks, (n, width), BF16, None)
        + scatter_scratch(Y, X, 1, (EXT, width), BF16, None)
        + [
            pltpu.VMEM((blocks, n, width), BF16),
            pltpu.VMEM((R - 1, slots_here, n, width), BF16),
            pltpu.VMEM((R - 1, EXT, width), BF16),
            pltpu.SemaphoreType.DMA((per * (blocks + 1),)),
            pltpu.SemaphoreType.DMA((per * (blocks + 1),)),
            pltpu.SemaphoreType.DMA((blocks + 1,)),
            pltpu.SemaphoreType.DMA((R, 2)),
            pltpu.SemaphoreType.DMA((R, 2)),
        ],
        compiler_params=pltpu.CompilerParams(
            collective_id=5, has_side_effects=True, vmem_limit_bytes=48 << 20
        ),
        name="scatter_weights",
    )(inverse, grads, ext)


def attention_forward_kernel(
    q_ref, k_ref, v_ref, prev_ref, segk_ref, segq_ref,
    logit_ref, e_ref, o_ref, st_ref, top_ref, mask_ref,
):
    h = pl.program_id(1)
    chunks, wide = o_ref.shape[1], o_ref.shape[3]

    @pl.when(h == 0)
    def _():
        mask_ref[...] = jnp.where(segk_ref[0] == segq_ref[0], 0.0, NEG_BIG)

    hg = lax.rem(h, GROUP)
    k_low, v_low = k_ref[...], v_ref[...]
    for t in range(chunks):
        cols = slice(t * wide, (t + 1) * wide)
        score = dot_f32(k_low, q_ref[:, cols], ((0,), (0,)))
        raw = score + prev_ref[0, 0, 0, :, cols].astype(F32)
        logit_ref[0, 0, 0, :, cols] = raw.astype(BF16)
        masked = raw + mask_ref[:, cols]
        top = jnp.maximum(jnp.max(masked, axis=0, keepdims=True), NEG_FLOOR)
        expo = jnp.exp(masked - top)
        total = jnp.sum(expo, axis=0, keepdims=True)
        low = expo.astype(BF16)
        e_ref[0, 0, :, cols] = low
        o_ref[0, t] = dot_f32(v_low, low, ((1,), (0,))).astype(BF16)
        st_ref[0, 0, t, pl.ds(hg, 1), :] = top
        st_ref[0, 0, t, pl.ds(GROUP + hg, 1), :] = total
        top_ref[0, 0, t, pl.ds(hg, 1), :] = top


def attention_forward(q_all, k_all, v_all, prev, segk, segq, chunks, wide):
    micro, _, heads, own, slots = prev.shape
    groups = heads // GROUP
    flops = micro * heads * 2 * 2 * own * slots * HD
    head = lambda m, h: (h, m)
    return pl.pallas_call(
        attention_forward_kernel,
        grid=(micro, heads),
        out_shape=(
            jax.ShapeDtypeStruct(prev.shape, BF16),
            jax.ShapeDtypeStruct((micro, heads, own, slots), BF16),
            jax.ShapeDtypeStruct((micro, chunks, heads * HD, wide), BF16),
            jax.ShapeDtypeStruct((micro, groups, chunks, 2 * GROUP, wide), F32),
            jax.ShapeDtypeStruct((micro, groups, chunks, 2 * GROUP, wide), F32),
        ),
        in_specs=[
            pl.BlockSpec((HD, slots), head),
            pl.BlockSpec((None, HD, own), lambda m, h: (m, h, 0)),
            pl.BlockSpec((None, HD, own), lambda m, h: (m, h, 0)),
            pl.BlockSpec((1, 1, 1, own, slots), lambda m, h: (m, 0, h, 0, 0)),
            pl.BlockSpec((1, own, 1), lambda m, h: (m, 0, 0)),
            pl.BlockSpec((1, 1, slots), lambda m, h: (m, 0, 0)),
        ],
        out_specs=(
            pl.BlockSpec((1, 1, 1, own, slots), lambda m, h: (m, 0, h, 0, 0)),
            pl.BlockSpec((1, 1, own, slots), lambda m, h: (m, h, 0, 0)),
            pl.BlockSpec((1, chunks, HD, wide), lambda m, h: (m, 0, h, 0)),
            pl.BlockSpec((1, 1, chunks, 2 * GROUP, wide), lambda m, h: (m, h // GROUP, 0, 0, 0)),
            pl.BlockSpec((1, 1, chunks, 2 * GROUP, wide), lambda m, h: (m, h // GROUP, 0, 0, 0)),
        ),
        scratch_shapes=[pltpu.VMEM((own, slots), F32)],
        compiler_params=pltpu.CompilerParams(vmem_limit_bytes=32 << 20),
        cost_estimate=pl.CostEstimate(
            flops=flops, bytes_accessed=micro * heads * own * slots * 6, transcendentals=micro * heads * own * slots
        ),
        name="attention_forward",
    )(q_all, k_all, v_all, prev, segk, segq)


def attention_backward_kernel(
    scale, e_ref, d_ref, st_ref, top_ref, q_ref, k_ref, v_ref, g_ref, dq_ref, dk_ref, dv_ref
):
    h = pl.program_id(1)
    chunks, wide = d_ref.shape[1], d_ref.shape[3]
    hg = lax.rem(h, GROUP)
    k_low, v_low = k_ref[...], v_ref[...]
    dk = jnp.zeros(dk_ref.shape[1:], F32)
    dv = jnp.zeros(dv_ref.shape[1:], F32)
    for t in range(chunks):
        cols = slice(t * wide, (t + 1) * wide)
        top = st_ref[0, 0, t, pl.ds(hg, 1), :]
        inv = st_ref[0, 0, t, pl.ds(GROUP + hg, 1), :]
        dots = st_ref[0, 0, t, pl.ds(2 * GROUP + hg, 1), :]
        weight = jnp.exp(top_ref[0, 0, t, pl.ds(hg, 1), :] - top) * inv
        low = e_ref[0, 0, :, cols]
        grad_in = (d_ref[0, t].astype(F32) * weight).astype(BF16)
        soft = dot_f32(v_low, grad_in, ((0,), (0,))) - dots * weight
        grad = (low.astype(F32) * soft).astype(BF16)
        g_ref[0, 0, 0, :, cols] = grad
        dq_ref[0, t] = (dot_f32(k_low, grad, ((1,), (0,))) * scale).astype(BF16)
        dv = dv + dot_f32(grad_in, low, ((1,), (1,)))
        dk = dk + dot_f32(q_ref[:, cols], grad, ((1,), (1,)))
    dk_ref[0] = dk.astype(BF16)
    dv_ref[0] = dv.astype(BF16)


def attention_backward(expo, datt, st, tops, q_all, k_all, v_all, scale):
    micro, heads, own, slots = expo.shape
    chunks, wide = datt.shape[1], datt.shape[3]
    flops = micro * heads * 2 * 4 * own * slots * HD
    sts = st.shape[3]
    return pl.pallas_call(
        functools.partial(attention_backward_kernel, scale),
        grid=(micro, heads),
        out_shape=(
            jax.ShapeDtypeStruct((micro, 1, heads, own, slots), BF16),
            jax.ShapeDtypeStruct((micro, chunks, heads * HD, wide), BF16),
            jax.ShapeDtypeStruct((micro, heads * HD, own), BF16),
            jax.ShapeDtypeStruct((micro, heads * HD, own), BF16),
        ),
        in_specs=[
            pl.BlockSpec((1, 1, own, slots), lambda m, h: (m, h, 0, 0)),
            pl.BlockSpec((1, chunks, HD, wide), lambda m, h: (m, 0, h, 0)),
            pl.BlockSpec((1, 1, chunks, sts, wide), lambda m, h: (m, h // GROUP, 0, 0, 0)),
            pl.BlockSpec((1, 1, chunks, 2 * GROUP, wide), lambda m, h: (m, h // GROUP, 0, 0, 0)),
            pl.BlockSpec((HD, slots), lambda m, h: (h, m)),
            pl.BlockSpec((None, HD, own), lambda m, h: (m, h, 0)),
            pl.BlockSpec((None, HD, own), lambda m, h: (m, h, 0)),
        ],
        out_specs=(
            pl.BlockSpec((1, 1, 1, own, slots), lambda m, h: (m, 0, h, 0, 0)),
            pl.BlockSpec((1, chunks, HD, wide), lambda m, h: (m, 0, h, 0)),
            pl.BlockSpec((1, HD, own), lambda m, h: (m, h, 0)),
            pl.BlockSpec((1, HD, own), lambda m, h: (m, h, 0)),
        ),
        compiler_params=pltpu.CompilerParams(vmem_limit_bytes=32 << 20),
        cost_estimate=pl.CostEstimate(
            flops=flops, bytes_accessed=micro * heads * own * slots * 4, transcendentals=0
        ),
        name="attention_backward",
    )(expo, datt, st, tops, q_all, k_all, v_all)


def to_chunks(arr, chunks):
    pieces, rows, own = arr.shape[-3:]
    lead = arr.shape[:-3]
    if pieces == chunks:
        return arr
    per = pieces // chunks
    arr = arr.reshape(lead + (chunks, per, rows, own))
    return jnp.moveaxis(arr, -3, -2).reshape(lead + (chunks, rows, per * own))


def from_chunks(arr, pieces):
    chunks, rows, wide = arr.shape[-3:]
    lead = arr.shape[:-3]
    if pieces == chunks:
        return arr
    per = pieces // chunks
    arr = arr.reshape(lead + (chunks, rows, per, wide // per))
    return jnp.moveaxis(arr, -2, -3).reshape(lead + (pieces, rows, wide // per))


def per_device(
    mesh_dims,
    tokens,
    prev_logits,
    segments,
    out_cot,
    master_mat,
    mom1_mat,
    mom2_mat,
    eigen_bases,
    master_small,
    mom1_small,
    mom2_small,
    owners,
    step_count,
):
    Y, X, R = mesh_dims
    keys = Y * X * 2
    micro, row_count, key_len, width = tokens.shape
    slot_count = prev_logits.shape[4]
    slots_here, _, cols_here = master_mat.shape
    blocks = slots_here * R
    token_count = micro * key_len
    scale = HD ** (-0.5)
    key_index = lax.axis_index("keys")
    row_index = lax.axis_index("rows")
    wide = max(key_len, min(256, slot_count))
    chunks = slot_count // wide
    groups = H // GROUP

    x_own = tokens.reshape(micro, key_len, width)
    w_own = jnp.swapaxes(master_mat, 1, 2).astype(BF16)
    small_low = master_small.astype(BF16).reshape(1, slots_here * cols_here)
    ext = lax.dynamic_update_slice(
        jnp.zeros((EXT, width), BF16), small_low, (row_index, jnp.int32(0))
    )
    wt, ext_all, xg = gather_weights(mesh_dims, owners, w_own, ext, x_own)
    w_t = wt.reshape(blocks * BLOCK_COLUMNS, width)
    small_all = ext_all.reshape(keys, EXT, width)[:, :R, : slots_here * cols_here]
    params = (
        jnp.transpose(small_all.reshape(keys, R, slots_here, cols_here), (1, 2, 0, 3))
        .reshape(blocks * GAIN_ROW_WIDTH)
        .astype(F32)
    )
    wq_t = w_t[:width]
    wkv_t = w_t[width : 3 * width]
    wqkv_t = w_t[: 3 * width]
    wo_t = w_t[3 * width : 4 * width]
    wu_t = w_t[4 * width : 4 * width + FF]
    wd_t = w_t[4 * width + FF :]
    bias_q = params[:width]
    bias_v = params[width : 2 * width]
    bias_o = params[2 * width : 3 * width]
    gain_one = params[3 * width : 4 * width]
    shift_one = params[4 * width : 5 * width]
    bias_up = params[5 * width : 5 * width + FF]
    bias_down = params[5 * width + FF : 6 * width + FF]
    gain_two = params[6 * width + FF : 7 * width + FF]
    shift_two = params[7 * width + FF :]

    q_all = (
        (dot_f32(wq_t, xg.reshape(micro * slot_count, width), ((1,), (1,))) + bias_q[:, None])
        .astype(BF16) * jnp.asarray(scale, BF16)
    )
    x_rows = x_own.reshape(token_count, width)
    kv = dot_f32(wkv_t, x_rows, ((1,), (1,))) + jnp.concatenate([jnp.zeros_like(bias_v), bias_v])[:, None]
    kv = jnp.swapaxes(kv.astype(BF16).reshape(2 * width, micro, key_len), 0, 1)
    k_all, v_all = kv[:, :width], kv[:, width:]

    seg_rows = segments.reshape(micro, slot_count)
    seg_keys = lax.dynamic_slice_in_dim(seg_rows, key_index * key_len, key_len, 1)
    logits, expo, o_part, st_part, tops = attention_forward(
        q_all, k_all, v_all, prev_logits, seg_keys[:, :, None], seg_rows[:, None, :], chunks, wide
    )
    o_part = from_chunks(o_part, keys).reshape(micro, Y, X, 2, width, key_len)
    st_part = from_chunks(st_part, keys).reshape(micro, groups, Y, X, 2, 2 * GROUP, key_len)
    att, st = merge_attention(mesh_dims, o_part, st_part)

    att_t = jnp.swapaxes(att, 0, 1).reshape(width, token_count)
    branch = dot_f32(att_t, wo_t, ((0,), (1,))) + bias_o
    normed_one, inv_one = layer_norm(x_rows.astype(F32) + branch)
    mid_act = normed_one * gain_one + shift_one
    mid_low = mid_act.astype(BF16)
    pre_act = dot_f32(mid_low, wu_t, ((1,), (1,))) + bias_up
    hidden = jax.nn.gelu(pre_act, approximate=False).astype(BF16)
    ffn_out = dot_f32(hidden, wd_t, ((1,), (0,))) + bias_down
    normed_two, inv_two = layer_norm(mid_act + ffn_out)
    out_hidden = (normed_two * gain_two + shift_two).astype(BF16).reshape(tokens.shape)
    grad_out = out_cot.reshape(token_count, width).astype(F32)
    grad_sum_two = norm_back(grad_out, normed_two, inv_two, gain_two)
    d_gain_two = jnp.sum(grad_out * normed_two, axis=0)
    d_shift_two = jnp.sum(grad_out, axis=0)
    grad_ffn = grad_sum_two.astype(BF16)
    d_bias_down = jnp.sum(grad_ffn.astype(F32), axis=0)
    d_down = dot_f32(hidden, grad_ffn, ((0,), (0,)))
    grad_hidden = dot_f32(grad_ffn, wd_t, ((1,), (1,)))
    _, gelu_back = jax.vjp(lambda value: jax.nn.gelu(value, approximate=False), pre_act)
    grad_pre = gelu_back(grad_hidden)[0].astype(BF16)
    d_bias_up = jnp.sum(grad_pre.astype(F32), axis=0)
    d_up = dot_f32(grad_pre, mid_low, ((0,), (0,)))
    grad_mid = grad_sum_two + dot_f32(grad_pre, wu_t, ((1,), (0,)))
    grad_one = norm_back(grad_mid, normed_one, inv_one, gain_one)
    d_gain_one = jnp.sum(grad_mid * normed_one, axis=0)
    d_shift_one = jnp.sum(grad_mid, axis=0)
    grad_branch = grad_one.astype(BF16)
    d_bias_o = jnp.sum(grad_branch.astype(F32), axis=0)
    d_out = dot_f32(grad_branch, att_t, ((0,), (1,)))
    datt = dot_f32(wo_t, grad_branch, ((0,), (1,))).astype(BF16)
    datt = jnp.swapaxes(datt.reshape(width, micro, key_len), 0, 1)
    dots = jnp.sum(
        (datt.astype(F32) * att.astype(F32)).reshape(micro, groups, GROUP, HD, key_len), axis=3
    )
    st_own = jnp.concatenate([st, dots, jnp.zeros_like(dots)], axis=2)
    datt_all, st_all = gather_grads(mesh_dims, datt, st_own)
    datt_all = to_chunks(datt_all.reshape(micro, keys, width, key_len), chunks)
    st_all = to_chunks(st_all.reshape(micro, groups, keys, 4 * GROUP, key_len), chunks)
    grad_prev, dq_part, dk, dv = attention_backward(
        expo, datt_all, st_all, tops, q_all, k_all, v_all, scale
    )
    dq_part = from_chunks(dq_part, keys).reshape(micro, Y, X, 2, width, key_len)
    dq = scatter_queries(mesh_dims, dq_part)

    grad_proj = jnp.swapaxes(jnp.concatenate([dq, dk, dv], axis=1), 0, 1).reshape(
        3 * width, token_count
    )
    d_qkv = dot_f32(grad_proj, x_rows, ((1,), (0,)))
    d_bias_q = jnp.sum(grad_proj[:width].astype(F32), axis=1)
    d_bias_v = jnp.sum(grad_proj[2 * width :].astype(F32), axis=1)
    grad_x = grad_one + dot_f32(grad_proj, wqkv_t, ((0,), (0,)))
    grad_tokens = grad_x.astype(BF16).reshape(tokens.shape)

    grads = jnp.concatenate(
        [d_qkv.astype(BF16), d_out.astype(BF16), d_up.astype(BF16), d_down.astype(BF16)], axis=0
    ).reshape(blocks, Y, X, 2, cols_here, width)
    small = jnp.concatenate(
        [d_bias_q, d_bias_v, d_bias_o, d_gain_one, d_shift_one, d_bias_up, d_bias_down, d_gain_two, d_shift_two]
    ).astype(BF16)
    small = jnp.transpose(
        small.reshape(R, slots_here, keys, cols_here), (2, 0, 1, 3)
    ).reshape(keys, R, slots_here * cols_here)
    small = jnp.pad(small, ((0, 0), (0, EXT - R), (0, width - slots_here * cols_here)))
    inverse = inverse_order(owners)
    mine_t, small_sum = scatter_weights(
        mesh_dims, inverse, grads, small.reshape(Y, X, 2, EXT, width)
    )
    mine_mat = jnp.swapaxes(mine_t, 1, 2)
    mine_small = lax.dynamic_slice_in_dim(small_sum, row_index, 1, 0)[
        :, : slots_here * cols_here
    ].reshape(master_small.shape)

    steps_done = step_count[0].astype(F32)
    fix_one = 1.0 - jnp.power(jnp.asarray(BETA_ONE, F32), steps_done)
    fix_two = 1.0 - jnp.power(jnp.asarray(BETA_TWO, F32), steps_done)
    rotated = jnp.einsum("sed,sec->sdc", eigen_bases, mine_mat, precision=HIGHEST_PREC)
    new_one = BETA_ONE * mom1_mat + (1.0 - BETA_ONE) * rotated
    new_two = BETA_TWO * mom2_mat + (1.0 - BETA_TWO) * rotated * rotated
    direction = new_one / fix_one / (jnp.sqrt(new_two / fix_two) + EPS_ADAM)
    back_rot = jnp.einsum("sdk,skc->sdc", eigen_bases, direction, precision=HIGHEST_PREC)
    slot_index_list = row_index * slots_here + jnp.arange(slots_here, dtype=jnp.int32)
    block_ids = jnp.take(inverse, slot_index_list)
    columns = (
        block_ids[:, None] * (cols_here * keys)
        + key_index * cols_here
        + jnp.arange(cols_here, dtype=jnp.int32)[None, :]
    )
    rates = column_rates(columns)[:, None, :]
    new_master = master_mat - rates * (back_rot + DECAY * master_mat)
    small_one = BETA_ONE * mom1_small + (1.0 - BETA_ONE) * mine_small
    small_two = BETA_TWO * mom2_small + (1.0 - BETA_TWO) * mine_small * mine_small
    new_small = master_small - RATE_SMALL * (small_one / fix_one) / (
        jnp.sqrt(small_two / fix_two) + EPS_ADAM
    )
    return (
        out_hidden,
        logits,
        grad_tokens,
        grad_prev,
        mine_mat,
        new_one,
        new_two,
        new_master,
        new_master.astype(BF16),
        mine_small,
        small_one,
        small_two,
        new_small,
        new_small.astype(BF16),
    )


def solution(mesh):
    chips = mesh.shape["keys"] // 2
    side = math.isqrt(chips)
    dims = (side, side, mesh.shape["rows"]) if side * side == chips else (1, chips, mesh.shape["rows"])
    acts = P(None, "rows", "keys", None)
    scores = P(None, "rows", None, "keys", None)
    mats = P("rows", None, "keys")
    smalls = P("rows", "keys")
    return jax.shard_map(
        functools.partial(per_device, dims),
        mesh=mesh,
        in_specs=(
            acts, scores, P(None, "rows", None), acts, mats, mats, mats,
            P("rows", None, None), smalls, smalls, smalls, P(), P(),
        ),
        out_specs=(acts, scores, acts, scores) + (mats,) * 5 + (smalls,) * 5,
        check_vma=False,
    )
```

```python
import functools
import math

import jax
import jax.numpy as jnp
from jax import lax
from jax.experimental import pallas as pl
from jax.experimental.pallas import tpu as pltpu
from jax.sharding import PartitionSpec as P

MODEL_WIDTH = 768
H = 12
HD = 64
FF = 3072
BLOCK_COLUMNS = 1152
GAIN_ROW_WIDTH = 1152

EPS_NORM = 1e-06
BETA_ONE = 0.95
BETA_TWO = 0.95
EPS_ADAM = 1e-08
DECAY = 0.01
RATE_SMALL = 0.3
NEG_BIG = -1e30
NEG_FLOOR = -1e29
HIGHEST_PREC = lax.Precision.HIGHEST
MESH = pl.DeviceIdType.MESH
F32 = jnp.float32
BF16 = jnp.bfloat16
ANY = pl.BlockSpec(memory_space=pl.ANY)
VMEM_SPEC = pl.BlockSpec(memory_space=pltpu.VMEM)
EXT = 16


def layer_norm(value):
    mean_val = jnp.mean(value, axis=-1, keepdims=True)
    centered = value - mean_val
    inv_dev = lax.rsqrt(jnp.mean(centered * centered, axis=-1, keepdims=True) + EPS_NORM)
    return (centered * inv_dev, inv_dev)


def norm_back(grad_in, normed, inv_dev, gain):
    scaled = grad_in * gain
    return inv_dev * (
        scaled
        - jnp.mean(scaled, axis=-1, keepdims=True)
        - normed * jnp.mean(scaled * normed, axis=-1, keepdims=True)
    )


def inverse_order(owners):
    slot_index_list = jnp.arange(owners.shape[0], dtype=jnp.int32)
    matches = (owners[None, :] == slot_index_list[:, None]).astype(jnp.int32)
    return jnp.sum(matches * slot_index_list[None, :], axis=1)


def column_rates(columns):
    inner = MODEL_WIDTH ** (-0.5)
    return jnp.where(
        columns < 3 * MODEL_WIDTH,
        inner,
        jnp.where(
            columns < 4 * MODEL_WIDTH,
            4.0 * inner,
            jnp.where(columns < 4 * MODEL_WIDTH + FF, inner, FF ** (-0.5)),
        ),
    )


def dot_f32(left, right, contract):
    return lax.dot_general(left, right, (contract, ((), ())), preferred_element_type=F32)


class Place:
    def __init__(self, side_y, side_x, rows):
        self.Y, self.X, self.R = side_y, side_x, rows
        key = lax.axis_index("keys")
        self.key = key
        self.r = lax.axis_index("rows")
        self.c = lax.rem(key, 2)
        self.x = lax.rem(key // 2, side_x)
        self.y = key // (2 * side_x)

    def keyof(self, y, x, c):
        return (y * self.X + x) * 2 + c

    def xo(self, d):
        return lax.rem(self.x + d, self.X)

    def yo(self, d):
        return lax.rem(self.y + d, self.Y)

    def ro(self, d):
        return lax.rem(self.r + d, self.R)

    def x_peer(self, d):
        return {"keys": self.keyof(self.y, self.xo(d), self.c)}

    def y_peer(self, d):
        return {"keys": self.keyof(self.yo(d), self.x, self.c)}

    def core_peer(self):
        return {"keys": self.keyof(self.y, self.x, 1 - self.c)}

    def z_peer(self, d):
        return {"rows": self.ro(d)}

    def barrier(self, with_z):
        sem = pltpu.get_barrier_semaphore()
        peers = [self.core_peer()]
        peers += [self.x_peer(d) for d in range(1, self.X)]
        peers += [self.y_peer(d) for d in range(1, self.Y)]
        if with_z:
            peers += [self.z_peer(d) for d in range(1, self.R)]
        for peer in peers:
            pl.semaphore_signal(sem, inc=1, device_id=peer, device_id_type=MESH)
        pl.semaphore_wait(sem, len(peers))


def remote(src, dst, send_sem, recv_sem, peer):
    return pltpu.make_async_remote_copy(
        src_ref=src,
        dst_ref=dst,
        send_sem=send_sem,
        recv_sem=recv_sem,
        device_id=peer,
        device_id_type=MESH,
    )


def sems_per_item(Y, X):
    return (X - 1) + (Y - 1) + 1


class Gather:
    def __init__(self, place, own, buf, send, recv, base, x_first):
        p = place
        self.sent = []
        n = sems_per_item(p.Y, p.X)
        idx = iter(range(base, base + n))
        first = [(p.x_peer(d)) for d in range(1, p.X)] if x_first else [p.y_peer(d) for d in range(1, p.Y)]
        second = [p.y_peer(d) for d in range(1, p.Y)] if x_first else [p.x_peer(d) for d in range(1, p.X)]
        line = buf.at[p.y, :, p.c] if x_first else buf.at[:, p.x, p.c]
        plane = buf.at[:, :, p.c]
        mine = buf.at[p.y, p.x, p.c]
        self.one = []
        for peer in first:
            i = next(idx)
            self.one.append(remote(own, mine, send.at[i], recv.at[i], peer))
        self.two = []
        for peer in second:
            i = next(idx)
            self.two.append(remote(line, line, send.at[i], recv.at[i], peer))
        i = next(idx)
        self.three = [remote(plane, plane, send.at[i], recv.at[i], p.core_peer())]

    def start1(self):
        for copy in self.one:
            copy.start()

    def start2(self):
        for copy in self.one:
            copy.wait_recv()
        for copy in self.two:
            copy.start()

    def start3(self):
        for copy in self.two:
            copy.wait_recv()
        for copy in self.three:
            copy.start()

    def finish(self):
        for copy in self.three:
            copy.wait_recv()
        for copy in self.one + self.two + self.three:
            copy.wait_send()


def gather_weights_kernel(
    Y, X, R, owners, w_ref, ext_ref, x_ref, wt_out, ext_out, xg_out,
    zbuf, zext, stage, sext, zsend, zrecv, send, recv, loc,
):
    p = Place(Y, X, R)
    slots_here = w_ref.shape[0]
    blocks = zbuf.shape[0]
    micro = x_ref.shape[0]
    n = sems_per_item(Y, X)
    p.barrier(True)
    zcopies = []
    here = pl.ds(p.r * slots_here, slots_here)
    for d in range(1, R):
        a = remote(w_ref, zbuf.at[here], zsend.at[d, 0], zrecv.at[d, 0], p.z_peer(d))
        a.start()
        b = remote(ext_ref, zext.at[p.r], zsend.at[d, 1], zrecv.at[d, 1], p.z_peer(d))
        b.start()
        zcopies += [a, b]
    xitems = []
    xlocal = []
    for m in range(micro):
        item = Gather(p, x_ref.at[m], xg_out.at[m], send, recv, m * n, m % 2 == 0)
        item.start1()
        xitems.append(item)
        copy = pltpu.make_async_copy(x_ref.at[m], xg_out.at[m, p.y, p.x, p.c], loc.at[m])
        copy.start()
        xlocal.append(copy)
    wl = pltpu.make_async_copy(w_ref, zbuf.at[here], loc.at[micro])
    wl.start()
    el = pltpu.make_async_copy(ext_ref, zext.at[p.r], loc.at[micro + 1])
    el.start()
    for m in range(micro):
        xlocal[m].wait()
        xitems[m].start2()
    wl.wait()
    el.wait()
    for copy in zcopies:
        copy.wait_recv()
    sext[...] = jnp.sum(zext[...].astype(F32), axis=0).astype(BF16)

    def reorder(b, carry):
        stage[b] = zbuf[owners[b]]
        return carry

    lax.fori_loop(0, blocks, reorder, 0)
    base = micro * n
    eitem = Gather(p, sext, ext_out, send, recv, base, True)
    base += n
    eitem.start1()
    lcopies = []
    ecopy = pltpu.make_async_copy(sext, ext_out.at[p.y, p.x, p.c], loc.at[micro + 2])
    ecopy.start()
    items = []
    for b in range(blocks):
        item = Gather(p, stage.at[b], wt_out.at[b], send, recv, base, b % 2 == 0)
        base += n
        item.start1()
        items.append(item)
        copy = pltpu.make_async_copy(stage.at[b], wt_out.at[b, p.y, p.x, p.c], loc.at[micro + 3 + b])
        copy.start()
        lcopies.append(copy)
    for m in range(micro):
        xitems[m].start3()
    ecopy.wait()
    eitem.start2()
    for b in range(blocks):
        lcopies[b].wait()
        items[b].start2()
    eitem.start3()
    for b in range(blocks):
        items[b].start3()
    for item in xitems + [eitem] + items:
        item.finish()
    for copy in zcopies:
        copy.wait_send()


def gather_weights(mesh_dims, owners, w_own, ext, x_own):
    Y, X, R = mesh_dims
    slots_here, n, width = w_own.shape
    micro, tok = x_own.shape[:2]
    blocks = slots_here * R
    total = sems_per_item(Y, X) * (micro + 1 + blocks)
    return pl.pallas_call(
        functools.partial(gather_weights_kernel, Y, X, R),
        out_shape=(
            jax.ShapeDtypeStruct((blocks, Y, X, 2, n, width), BF16),
            jax.ShapeDtypeStruct((Y, X, 2, EXT, width), BF16),
            jax.ShapeDtypeStruct((micro, Y, X, 2, tok, width), BF16),
        ),
        in_specs=[pl.BlockSpec(memory_space=pltpu.SMEM), ANY, ANY, ANY],
        out_specs=(ANY, ANY, ANY),
        scratch_shapes=[
            pltpu.VMEM((blocks, n, width), BF16),
            pltpu.VMEM((R, EXT, width), BF16),
            pltpu.VMEM((blocks, n, width), BF16),
            pltpu.VMEM((EXT, width), BF16),
            pltpu.SemaphoreType.DMA((R, 2)),
            pltpu.SemaphoreType.DMA((R, 2)),
            pltpu.SemaphoreType.DMA((total,)),
            pltpu.SemaphoreType.DMA((total,)),
            pltpu.SemaphoreType.DMA((micro + 3 + blocks,)),
        ],
        compiler_params=pltpu.CompilerParams(
            collective_id=1, has_side_effects=True, vmem_limit_bytes=40 << 20
        ),
        name="gather_weights",
    )(owners, w_own, ext, x_own)


class Scatter:
    def __init__(self, place, parts, accs, r1s, r2s, r3s, send, recv, loc, base, lbase, y_first, merge):
        p = place
        self.p, self.y_first, self.merge = p, y_first, merge
        self.accs, self.r1s, self.r2s, self.r3s = accs, r1s, r2s, r3s
        self.count = len(parts)
        n = sems_per_item(p.Y, p.X) * len(parts)
        idx = iter(range(base, base + n))
        self.zero, self.one, self.two, self.three = [], [], [], []
        for t, part in enumerate(parts):
            i = next(idx)
            self.zero.append(pltpu.make_async_copy(part.at[:, :, p.c], accs[t], loc.at[lbase + t]))
            self.one.append(remote(part.at[:, :, 1 - p.c], r1s[t], send.at[i], recv.at[i], p.core_peer()))
            if y_first:
                for d in range(1, p.Y):
                    i = next(idx)
                    self.two.append(
                        remote(accs[t].at[p.yo(d)], r2s[t].at[d - 1], send.at[i], recv.at[i], p.y_peer(d))
                    )
                for d in range(1, p.X):
                    i = next(idx)
                    self.three.append(
                        remote(accs[t].at[p.y, p.xo(d)], r3s[t].at[d - 1], send.at[i], recv.at[i], p.x_peer(d))
                    )
            else:
                for d in range(1, p.X):
                    i = next(idx)
                    self.two.append(
                        remote(accs[t].at[:, p.xo(d)], r2s[t].at[d - 1], send.at[i], recv.at[i], p.x_peer(d))
                    )
                for d in range(1, p.Y):
                    i = next(idx)
                    self.three.append(
                        remote(accs[t].at[p.yo(d), p.x], r3s[t].at[d - 1], send.at[i], recv.at[i], p.y_peer(d))
                    )

    def start1(self):
        for copy in self.zero + self.one:
            copy.start()

    def start2(self):
        p = self.p
        for copy in self.zero:
            copy.wait()
        for copy in self.one:
            copy.wait_recv()

        def body(i, carry):
            y, x = i // p.X, lax.rem(i, p.X)
            self.merge([a.at[y, x] for a in self.accs], [r.at[y, x] for r in self.r1s])
            return carry

        lax.fori_loop(0, p.Y * p.X, body, 0)
        for copy in self.two:
            copy.start()

    def start3(self):
        p = self.p
        for copy in self.two:
            copy.wait_recv()
        if self.y_first:
            for d in range(1, p.Y):
                for x in range(p.X):
                    self.merge([a.at[p.y, x] for a in self.accs], [r.at[d - 1, x] for r in self.r2s])
        else:
            for d in range(1, p.X):
                for y in range(p.Y):
                    self.merge([a.at[y, p.x] for a in self.accs], [r.at[d - 1, y] for r in self.r2s])
        for copy in self.three:
            copy.start()

    def finish(self):
        p = self.p
        for copy in self.three:
            copy.wait_recv()
        mine = [a.at[p.y, p.x] for a in self.accs]
        for d in range(1, p.X if self.y_first else p.Y):
            self.merge(mine, [r.at[d - 1] for r in self.r3s])
        return mine

    def drain(self):
        for copy in self.one + self.two + self.three:
            copy.wait_send()


def merge_sum(into, other):
    a, b = into[0], other[0]
    a[...] = (a[...].astype(F32) + b[...].astype(F32)).astype(BF16)


def merge_soft(into, other):
    (va, sa), (vb, sb) = into, other
    ta, tb = sa[...], sb[...]
    heads = ta.shape[0] // 2
    top_a, top_b = ta[:heads], tb[:heads]
    top = jnp.maximum(top_a, top_b)
    wa, wb = jnp.exp(top_a - top), jnp.exp(top_b - top)
    sa[...] = jnp.concatenate([top, wa * ta[heads:] + wb * tb[heads:]], axis=0)
    for h in range(heads):
        rows = slice(h * HD, (h + 1) * HD)
        va[rows, :] = (
            va[rows, :].astype(F32) * wa[h : h + 1] + vb[rows, :].astype(F32) * wb[h : h + 1]
        ).astype(BF16)


def scatter_scratch(Y, X, items, shape, dtype, y_first_of):
    most = max((Y - 1) * X, (X - 1) * Y)
    return [
        pltpu.VMEM((items, Y, X) + shape, dtype),
        pltpu.VMEM((items, Y, X) + shape, dtype),
        pltpu.VMEM((items, max(Y, X) - 1, max(Y, X)) + shape, dtype),
        pltpu.VMEM((items, max(Y, X) - 1) + shape, dtype),
    ]


GROUP = 3


def middle_kernel(
    Y, X, R,
    o_ref, st_ref, x_ref, cot_ref, w_ref, vec_ref, bu_ref,
    out_ref, datt_out, stat_out, dz_ref, dw_out, dvec_ref, dbu_ref,
    oa, o1, o2, o3, sa, s1, s2, s3, send, recv, loc, gsend, grecv, gloc, wsem, dwsem,
    w, att, attk, low, hid, dpre, slope, df, da, n1, n2, datt, stat, dw,
):
    p = Place(Y, X, R)
    micro, tok, width = x_ref.shape
    groups = st_ref.shape[1]
    rows = GROUP * HD
    bo, g1, e1, bd, g2, e2 = (vec_ref[i : i + 1] for i in range(6))
    stat[...] = jnp.zeros_like(stat)
    parts = FF // width
    wcopy = pltpu.make_async_copy(w_ref.at[pl.ds(3 * width, w.shape[0])], w, wsem)
    wcopy.start()
    p.barrier(False)

    n = sems_per_item(Y, X) * 2
    merges = []
    for m in range(micro):
        for g in range(groups):
            i = m * groups + g
            item = Scatter(
                p,
                [o_ref.at[m, :, :, :, pl.ds(g * rows, rows)], st_ref.at[m, g]],
                [oa.at[i], sa.at[i]], [o1.at[i], s1.at[i]], [o2.at[i], s2.at[i]], [o3.at[i], s3.at[i]],
                send, recv, loc, i * n, i * 2, g % 2 == 0, merge_soft,
            )
            item.start1()
            merges.append(item)

    def merge_two(m):
        for g in range(groups):
            merges[m * groups + g].start2()

    def merge_three(m):
        for g in range(groups):
            merges[m * groups + g].start3()

    def merge_finish(m):
        for g in range(groups):
            val, st = merges[m * groups + g].finish()
            tile = st[...]
            inv = 1.0 / tile[GROUP:]
            stat[m, g, : 2 * GROUP] = jnp.concatenate([tile[:GROUP], inv], axis=0)
            for h in range(GROUP):
                att[m, g * rows + h * HD : g * rows + (h + 1) * HD, :] = (
                    val[h * HD : (h + 1) * HD, :].astype(F32) * inv[h : h + 1]
                ).astype(BF16)

    n = sems_per_item(Y, X)
    gathers = [[], []]

    def gather_one(m):
        local = []
        for g in range(groups):
            ds = pl.ds(g * rows, rows)
            for t, (own, out) in enumerate(
                ((datt.at[m, ds], datt_out.at[m, :, :, :, ds]), (stat.at[m, g], stat_out.at[m, g]))
            ):
                i = (m * groups + g) * 2 + t
                item = Gather(p, own, out, gsend, grecv, i * n, g % 2 == 0)
                item.start1()
                copy = pltpu.make_async_copy(own, out.at[p.y, p.x, p.c], gloc.at[i])
                copy.start()
                gathers[m].append((item, copy))

    def gather_two(m):
        for item, copy in gathers[m]:
            copy.wait()
            item.start2()

    def gather_three(m):
        for item, copy in gathers[m]:
            item.start3()

    def forward(m):
        at = att[m].T
        attk[m] = at
        wo = w[:width]
        z1 = x_ref[m].astype(F32) + (dot_f32(at, wo, ((1,), (1,))) + bo)
        norm, inv = layer_norm(z1)
        n1[...] = norm
        mid = norm * g1 + e1
        low[m] = mid.astype(BF16)
        inner = low[m]

        def body(i, acc):
            r = pl.multiple_of(i * width, width)
            pre = dot_f32(inner, w[pl.ds(width + r, width)], ((1,), (1,))) + bu_ref[:, pl.ds(r, width)]
            half = 0.5 + 0.5 * lax.erf(pre * math.sqrt(0.5))
            low_h = (pre * half).astype(BF16)
            hid[m, :, pl.ds(r, width)] = low_h
            slope[:, pl.ds(r, width)] = half + pre * (
                jnp.exp(-0.5 * pre * pre) * (1.0 / math.sqrt(2.0 * math.pi))
            )
            return acc + dot_f32(low_h, w[pl.ds(width + FF + r, width)], ((1,), (0,)))

        f = lax.fori_loop(0, parts, body, jnp.zeros((tok, width), F32)) + bd
        norm2, inv2 = layer_norm(mid + f)
        n2[...] = norm2
        out_ref[m] = (norm2 * g2 + e2).astype(BF16)
        return inv, inv2

    def backward(m, invs):
        inv, inv2 = invs
        cot = cot_ref[m].astype(F32)
        norm2 = n2[...]
        dz2 = norm_back(cot, norm2, inv2, g2)
        dg2 = jnp.sum(cot * norm2, axis=0, keepdims=True)
        de2 = jnp.sum(cot, axis=0, keepdims=True)
        df_low = dz2.astype(BF16)
        df[m] = df_low
        dbd = jnp.sum(df_low.astype(F32), axis=0, keepdims=True)

        def body(i, acc):
            r = pl.multiple_of(i * width, width)
            dh = dot_f32(df_low, w[pl.ds(width + FF + r, width)], ((1,), (1,)))
            dp = (dh * slope[:, pl.ds(r, width)]).astype(BF16)
            dpre[m, :, pl.ds(r, width)] = dp
            part = jnp.sum(dp.astype(F32), axis=0, keepdims=True)
            if m == 0:
                dbu_ref[:, pl.ds(r, width)] = part
            else:
                dbu_ref[:, pl.ds(r, width)] += part
            return acc + dot_f32(dp, w[pl.ds(width + r, width)], ((1,), (0,)))

        dx1 = lax.fori_loop(0, parts, body, dz2)
        norm = n1[...]
        dg1 = jnp.sum(dx1 * norm, axis=0, keepdims=True)
        de1 = jnp.sum(dx1, axis=0, keepdims=True)
        dz1 = norm_back(dx1, norm, inv, g1)
        dz_ref[m] = dz1
        da_low = dz1.astype(BF16)
        da[m] = da_low
        dbo = jnp.sum(da_low.astype(F32), axis=0, keepdims=True)
        sums = jnp.concatenate([dbo, dg1, de1, dbd, dg2, de2, dg2, dg2], axis=0)
        if m == 0:
            dvec_ref[...] = sums
        else:
            dvec_ref[...] += sums
        dt = dot_f32(da_low, w[:width], ((1,), (0,))).astype(BF16).T
        datt[m] = dt
        for g in range(groups):
            for h in range(GROUP):
                r = g * rows + h * HD
                stat[m, g, 2 * GROUP + h : 2 * GROUP + h + 1] = jnp.sum(
                    dt[r : r + HD].astype(F32) * att[m, r : r + HD, :].astype(F32), axis=0, keepdims=True
                )

    def weight_grad(i, left, right):
        total = dot_f32(left(0), right[0], ((0,), (0,)))
        for m in range(1, micro):
            total = total + dot_f32(left(m), right[m], ((0,), (0,)))
        dw[i % 2] = total.astype(BF16)
        return pltpu.make_async_copy(dw.at[i % 2], dw_out.at[pl.ds(i * width, width)], dwsem.at[i % 2])

    merge_two(0)
    merge_three(0)
    merge_two(1)
    merge_finish(0)
    wcopy.wait()
    invs = forward(0)
    merge_three(1)
    backward(0, invs)
    gather_one(0)
    merge_finish(1)
    invs = forward(1)
    gather_two(0)
    backward(1, invs)
    gather_one(1)
    gather_three(0)
    jobs = [(lambda m: da[m], attk)]
    for i in range(parts):
        jobs.append((lambda m, i=i: dpre[m, :, i * width : (i + 1) * width], low))
    for i in range(parts):
        jobs.append((lambda m, i=i: hid[m, :, i * width : (i + 1) * width], df))
    copies = []
    for i, (left, right) in enumerate(jobs):
        if i >= 2:
            copies[i - 2].wait()
        copies.append(weight_grad(i, left, right))
        copies[-1].start()
        if i == len(jobs) // 2:
            gather_two(1)
    for copy in copies[-2:]:
        copy.wait()
    gather_three(1)
    for item in merges:
        item.drain()
    for m in range(micro):
        for item, copy in gathers[m]:
            item.finish()


def middle(mesh_dims, o_part, st_part, x_own, cot, w_t, vec, bias_up):
    Y, X, R = mesh_dims
    micro, tok, width = x_own.shape
    groups = st_part.shape[1]
    items = micro * groups
    merge_sems = sems_per_item(Y, X) * 2 * items
    strows = 16
    ffw = 2 * FF + width
    return pl.pallas_call(
        functools.partial(middle_kernel, Y, X, R),
        out_shape=(
            jax.ShapeDtypeStruct((micro, tok, width), BF16),
            jax.ShapeDtypeStruct((micro, Y, X, 2, width, tok), BF16),
            jax.ShapeDtypeStruct((micro, groups, Y, X, 2, strows, tok), F32),
            jax.ShapeDtypeStruct((micro, tok, width), F32),
            jax.ShapeDtypeStruct((ffw, width), BF16),
            jax.ShapeDtypeStruct((8, width), F32),
            jax.ShapeDtypeStruct((1, FF), F32),
        ),
        in_specs=[ANY, ANY, VMEM_SPEC, VMEM_SPEC, ANY, VMEM_SPEC, VMEM_SPEC],
        out_specs=(VMEM_SPEC, ANY, ANY, VMEM_SPEC, ANY, VMEM_SPEC, VMEM_SPEC),
        scratch_shapes=scatter_scratch(Y, X, items, (GROUP * HD, tok), BF16, None)
        + scatter_scratch(Y, X, items, (2 * GROUP, tok), F32, None)
        + [
            pltpu.SemaphoreType.DMA((merge_sems,)),
            pltpu.SemaphoreType.DMA((merge_sems,)),
            pltpu.SemaphoreType.DMA((items * 2,)),
            pltpu.SemaphoreType.DMA((merge_sems,)),
            pltpu.SemaphoreType.DMA((merge_sems,)),
            pltpu.SemaphoreType.DMA((items * 2,)),
            pltpu.SemaphoreType.DMA,
            pltpu.SemaphoreType.DMA((2,)),
            pltpu.VMEM((ffw, width), BF16),
            pltpu.VMEM((micro, width, tok), BF16),
            pltpu.VMEM((micro, tok, width), BF16),
            pltpu.VMEM((micro, tok, width), BF16),
            pltpu.VMEM((micro, tok, FF), BF16),
            pltpu.VMEM((micro, tok, FF), BF16),
            pltpu.VMEM((tok, FF), F32),
            pltpu.VMEM((micro, tok, width), BF16),
            pltpu.VMEM((micro, tok, width), BF16),
            pltpu.VMEM((tok, width), F32),
            pltpu.VMEM((tok, width), F32),
            pltpu.VMEM((micro, width, tok), BF16),
            pltpu.VMEM((micro, groups, strows, tok), F32),
            pltpu.VMEM((2, width, width), BF16),
        ],
        compiler_params=pltpu.CompilerParams(
            collective_id=2, has_side_effects=True, vmem_limit_bytes=58 << 20
        ),
        name="middle",
    )(o_part, st_part, x_own, cot, w_t, vec, bias_up)


def scatter_queries_kernel(Y, X, R, dq_ref, dq_out, a, r1, r2, r3, send, recv, loc):
    p = Place(Y, X, R)
    micro = dq_ref.shape[0]
    groups = a.shape[0] // micro
    rows = GROUP * HD
    n = sems_per_item(Y, X)
    p.barrier(False)
    items = []
    for g in range(groups):
        for m in range(micro):
            i = m * groups + g
            item = Scatter(
                p, [dq_ref.at[m, :, :, :, pl.ds(g * rows, rows)]],
                [a.at[i]], [r1.at[i]], [r2.at[i]], [r3.at[i]],
                send, recv, loc, i * n, i, m % 2 == 0, merge_sum,
            )
            item.start1()
            items.append((m, g, item))
    for m, g, item in items:
        item.start2()
    for m, g, item in items:
        item.start3()
    for m, g, item in items:
        (val,) = item.finish()
        dq_out[m, g * rows : (g + 1) * rows, :] = val[...]
    for m, g, item in items:
        item.drain()


def scatter_queries(mesh_dims, dq_part):
    Y, X, R = mesh_dims
    micro, width, tok = dq_part.shape[0], dq_part.shape[4], dq_part.shape[5]
    groups = width // (GROUP * HD)
    items = micro * groups
    total = sems_per_item(Y, X) * items
    return pl.pallas_call(
        functools.partial(scatter_queries_kernel, Y, X, R),
        out_shape=jax.ShapeDtypeStruct((micro, width, tok), BF16),
        in_specs=[ANY],
        out_specs=VMEM_SPEC,
        scratch_shapes=scatter_scratch(Y, X, items, (GROUP * HD, tok), BF16, None)
        + [
            pltpu.SemaphoreType.DMA((total,)),
            pltpu.SemaphoreType.DMA((total,)),
            pltpu.SemaphoreType.DMA((items,)),
        ],
        compiler_params=pltpu.CompilerParams(
            collective_id=4, has_side_effects=True, vmem_limit_bytes=40 << 20
        ),
        name="scatter_queries",
    )(dq_part)


def scatter_weights_kernel(
    Y, X, R, inverse, g_ref, e_ref, g_out, e_out,
    a, r1, r2, r3, ea, e1, e2, e3, stage, rz, ez, send, recv, loc, zsend, zrecv,
):
    p = Place(Y, X, R)
    blocks = g_ref.shape[0]
    slots_here = g_out.shape[0]
    n = sems_per_item(Y, X)
    p.barrier(True)
    items = []
    for b in range(blocks):
        item = Scatter(
            p, [g_ref.at[b]], [a.at[b]], [r1.at[b]], [r2.at[b]], [r3.at[b]],
            send, recv, loc, b * n, b, b % 2 == 0, merge_sum,
        )
        item.start1()
        items.append(item)
    eitem = Scatter(
        p, [e_ref], [ea.at[0]], [e1.at[0]], [e2.at[0]], [e3.at[0]],
        send, recv, loc, blocks * n, blocks, True, merge_sum,
    )
    eitem.start1()
    for item in items + [eitem]:
        item.start2()
    for item in items + [eitem]:
        item.start3()
    for item in items + [eitem]:
        item.finish()
    fin = a.at[:, p.y, p.x]

    def reorder(s, carry):
        stage[s] = fin[inverse[s]]
        return carry

    lax.fori_loop(0, blocks, reorder, 0)
    emine = ea.at[0, p.y, p.x]
    zcopies = []
    for d in range(1, R):
        there = pl.ds(p.ro(d) * slots_here, slots_here)
        copy = remote(stage.at[there], rz.at[d - 1], zsend.at[d, 0], zrecv.at[d, 0], p.z_peer(d))
        copy.start()
        zcopies.append(copy)
        copy = remote(emine, ez.at[d - 1], zsend.at[d, 1], zrecv.at[d, 1], p.z_peer(d))
        copy.start()
        zcopies.append(copy)
    for item in items + [eitem]:
        item.drain()
    for copy in zcopies:
        copy.wait_recv()
    e_out[...] = emine[...].astype(F32) + jnp.sum(ez[...].astype(F32), axis=0)
    for s in range(slots_here):
        total = stage[p.r * slots_here + s].astype(F32)
        for d in range(1, R):
            total = total + rz[d - 1, s].astype(F32)
        g_out[s] = total
    for copy in zcopies:
        copy.wait_send()


def scatter_weights(mesh_dims, inverse, grads, ext):
    Y, X, R = mesh_dims
    blocks, n, width = grads.shape[0], grads.shape[4], grads.shape[5]
    slots_here = blocks // R
    per = sems_per_item(Y, X)
    return pl.pallas_call(
        functools.partial(scatter_weights_kernel, Y, X, R),
        out_shape=(
            jax.ShapeDtypeStruct((slots_here, n, width), F32),
            jax.ShapeDtypeStruct((EXT, width), F32),
        ),
        in_specs=[pl.BlockSpec(memory_space=pltpu.SMEM), ANY, ANY],
        out_specs=(VMEM_SPEC, VMEM_SPEC),
        scratch_shapes=scatter_scratch(Y, X, blocks, (n, width), BF16, None)
        + scatter_scratch(Y, X, 1, (EXT, width), BF16, None)
        + [
            pltpu.VMEM((blocks, n, width), BF16),
            pltpu.VMEM((R - 1, slots_here, n, width), BF16),
            pltpu.VMEM((R - 1, EXT, width), BF16),
            pltpu.SemaphoreType.DMA((per * (blocks + 1),)),
            pltpu.SemaphoreType.DMA((per * (blocks + 1),)),
            pltpu.SemaphoreType.DMA((blocks + 1,)),
            pltpu.SemaphoreType.DMA((R, 2)),
            pltpu.SemaphoreType.DMA((R, 2)),
        ],
        compiler_params=pltpu.CompilerParams(
            collective_id=5, has_side_effects=True, vmem_limit_bytes=48 << 20
        ),
        name="scatter_weights",
    )(inverse, grads, ext)


def attention_forward_kernel(
    q_ref, k_ref, v_ref, prev_ref, segk_ref, segq_ref,
    logit_ref, e_ref, o_ref, st_ref, top_ref, mask_ref,
):
    h = pl.program_id(1)
    chunks, wide = o_ref.shape[1], o_ref.shape[3]

    @pl.when(h == 0)
    def _():
        mask_ref[...] = jnp.where(segk_ref[0] == segq_ref[0], 0.0, NEG_BIG)

    hg = lax.rem(h, GROUP)
    score = dot_f32(k_ref[...], q_ref[...], ((0,), (0,)))
    raw = score + prev_ref[0, 0, 0].astype(F32)
    logit_ref[0, 0, 0] = raw.astype(BF16)
    masked = raw + mask_ref[...]
    top = jnp.maximum(jnp.max(masked, axis=0, keepdims=True), NEG_FLOOR)
    expo = jnp.exp(masked - top)
    total = jnp.sum(expo, axis=0, keepdims=True)
    low = expo.astype(BF16)
    e_ref[0, 0] = low
    out = dot_f32(v_ref[...], low, ((1,), (0,))).astype(BF16)
    for t in range(chunks):
        cols = slice(t * wide, (t + 1) * wide)
        o_ref[0, t] = out[:, cols]
        st_ref[0, 0, t, pl.ds(hg, 1), :] = top[:, cols]
        st_ref[0, 0, t, pl.ds(GROUP + hg, 1), :] = total[:, cols]
        top_ref[0, 0, t, pl.ds(hg, 1), :] = top[:, cols]


def attention_forward(q_all, k_all, v_all, prev, segk, segq, chunks, wide):
    micro, _, heads, own, slots = prev.shape
    groups = heads // GROUP
    flops = micro * heads * 2 * 2 * own * slots * HD
    head = lambda m, h: (h, m)
    return pl.pallas_call(
        attention_forward_kernel,
        grid=(micro, heads),
        out_shape=(
            jax.ShapeDtypeStruct(prev.shape, BF16),
            jax.ShapeDtypeStruct((micro, heads, own, slots), BF16),
            jax.ShapeDtypeStruct((micro, chunks, heads * HD, wide), BF16),
            jax.ShapeDtypeStruct((micro, groups, chunks, 2 * GROUP, wide), F32),
            jax.ShapeDtypeStruct((micro, groups, chunks, 2 * GROUP, wide), F32),
        ),
        in_specs=[
            pl.BlockSpec((HD, slots), head),
            pl.BlockSpec((None, HD, own), lambda m, h: (m, h, 0)),
            pl.BlockSpec((None, HD, own), lambda m, h: (m, h, 0)),
            pl.BlockSpec((1, 1, 1, own, slots), lambda m, h: (m, 0, h, 0, 0)),
            pl.BlockSpec((1, own, 1), lambda m, h: (m, 0, 0)),
            pl.BlockSpec((1, 1, slots), lambda m, h: (m, 0, 0)),
        ],
        out_specs=(
            pl.BlockSpec((1, 1, 1, own, slots), lambda m, h: (m, 0, h, 0, 0)),
            pl.BlockSpec((1, 1, own, slots), lambda m, h: (m, h, 0, 0)),
            pl.BlockSpec((1, chunks, HD, wide), lambda m, h: (m, 0, h, 0)),
            pl.BlockSpec((1, 1, chunks, 2 * GROUP, wide), lambda m, h: (m, h // GROUP, 0, 0, 0)),
            pl.BlockSpec((1, 1, chunks, 2 * GROUP, wide), lambda m, h: (m, h // GROUP, 0, 0, 0)),
        ),
        scratch_shapes=[pltpu.VMEM((own, slots), F32)],
        compiler_params=pltpu.CompilerParams(vmem_limit_bytes=32 << 20),
        cost_estimate=pl.CostEstimate(
            flops=flops, bytes_accessed=micro * heads * own * slots * 6, transcendentals=micro * heads * own * slots
        ),
        name="attention_forward",
    )(q_all, k_all, v_all, prev, segk, segq)


def attention_backward_kernel(
    scale, e_ref, d_ref, st_ref, top_ref, q_ref, k_ref, v_ref, g_ref, dq_ref, dk_ref, dv_ref
):
    h = pl.program_id(1)
    chunks, wide = d_ref.shape[1], d_ref.shape[3]
    hg = lax.rem(h, GROUP)

    def row(ref, first):
        return jnp.concatenate([ref[0, 0, t, pl.ds(first + hg, 1), :] for t in range(chunks)], axis=1)

    weight = jnp.exp(row(top_ref, 0) - row(st_ref, 0)) * row(st_ref, GROUP)
    dots = row(st_ref, 2 * GROUP) * weight
    low = e_ref[0, 0]
    datt = jnp.concatenate([d_ref[0, t] for t in range(chunks)], axis=1)
    grad_in = (datt.astype(F32) * weight).astype(BF16)
    soft = dot_f32(v_ref[...], grad_in, ((0,), (0,))) - dots
    grad = (low.astype(F32) * soft).astype(BF16)
    g_ref[0, 0, 0] = grad
    dq = (dot_f32(k_ref[...], grad, ((1,), (0,))) * scale).astype(BF16)
    for t in range(chunks):
        dq_ref[0, t] = dq[:, t * wide : (t + 1) * wide]
    dv_ref[0] = dot_f32(grad_in, low, ((1,), (1,))).astype(BF16)
    dk_ref[0] = dot_f32(q_ref[...], grad, ((1,), (1,))).astype(BF16)


def attention_backward(expo, datt, st, tops, q_all, k_all, v_all, scale):
    micro, heads, own, slots = expo.shape
    chunks, wide = datt.shape[1], datt.shape[3]
    flops = micro * heads * 2 * 4 * own * slots * HD
    sts = st.shape[3]
    return pl.pallas_call(
        functools.partial(attention_backward_kernel, scale),
        grid=(micro, heads),
        out_shape=(
            jax.ShapeDtypeStruct((micro, 1, heads, own, slots), BF16),
            jax.ShapeDtypeStruct((micro, chunks, heads * HD, wide), BF16),
            jax.ShapeDtypeStruct((micro, heads * HD, own), BF16),
            jax.ShapeDtypeStruct((micro, heads * HD, own), BF16),
        ),
        in_specs=[
            pl.BlockSpec((1, 1, own, slots), lambda m, h: (m, h, 0, 0)),
            pl.BlockSpec((1, chunks, HD, wide), lambda m, h: (m, 0, h, 0)),
            pl.BlockSpec((1, 1, chunks, sts, wide), lambda m, h: (m, h // GROUP, 0, 0, 0)),
            pl.BlockSpec((1, 1, chunks, 2 * GROUP, wide), lambda m, h: (m, h // GROUP, 0, 0, 0)),
            pl.BlockSpec((HD, slots), lambda m, h: (h, m)),
            pl.BlockSpec((None, HD, own), lambda m, h: (m, h, 0)),
            pl.BlockSpec((None, HD, own), lambda m, h: (m, h, 0)),
        ],
        out_specs=(
            pl.BlockSpec((1, 1, 1, own, slots), lambda m, h: (m, 0, h, 0, 0)),
            pl.BlockSpec((1, chunks, HD, wide), lambda m, h: (m, 0, h, 0)),
            pl.BlockSpec((1, HD, own), lambda m, h: (m, h, 0)),
            pl.BlockSpec((1, HD, own), lambda m, h: (m, h, 0)),
        ),
        compiler_params=pltpu.CompilerParams(vmem_limit_bytes=32 << 20),
        cost_estimate=pl.CostEstimate(
            flops=flops, bytes_accessed=micro * heads * own * slots * 4, transcendentals=0
        ),
        name="attention_backward",
    )(expo, datt, st, tops, q_all, k_all, v_all)


def to_chunks(arr, chunks):
    pieces, rows, own = arr.shape[-3:]
    lead = arr.shape[:-3]
    if pieces == chunks:
        return arr
    per = pieces // chunks
    arr = arr.reshape(lead + (chunks, per, rows, own))
    return jnp.moveaxis(arr, -3, -2).reshape(lead + (chunks, rows, per * own))


def from_chunks(arr, pieces):
    chunks, rows, wide = arr.shape[-3:]
    lead = arr.shape[:-3]
    if pieces == chunks:
        return arr
    per = pieces // chunks
    arr = arr.reshape(lead + (chunks, rows, per, wide // per))
    return jnp.moveaxis(arr, -2, -3).reshape(lead + (pieces, rows, wide // per))


def per_device(
    mesh_dims,
    tokens,
    prev_logits,
    segments,
    out_cot,
    master_mat,
    mom1_mat,
    mom2_mat,
    eigen_bases,
    master_small,
    mom1_small,
    mom2_small,
    owners,
    step_count,
):
    Y, X, R = mesh_dims
    keys = Y * X * 2
    micro, row_count, key_len, width = tokens.shape
    slot_count = prev_logits.shape[4]
    slots_here, _, cols_here = master_mat.shape
    blocks = slots_here * R
    token_count = micro * key_len
    scale = HD ** (-0.5)
    key_index = lax.axis_index("keys")
    row_index = lax.axis_index("rows")
    wide = max(key_len, min(256, slot_count))
    chunks = slot_count // wide
    groups = H // GROUP

    x_own = tokens.reshape(micro, key_len, width)
    w_own = jnp.swapaxes(master_mat, 1, 2).astype(BF16)
    small_low = master_small.astype(BF16).reshape(1, slots_here * cols_here)
    ext = lax.dynamic_update_slice(
        jnp.zeros((EXT, width), BF16), small_low, (row_index, jnp.int32(0))
    )
    wt, ext_all, xg = gather_weights(mesh_dims, owners, w_own, ext, x_own)
    w_t = wt.reshape(blocks * BLOCK_COLUMNS, width)
    small_all = ext_all.reshape(keys, EXT, width)[:, :R, : slots_here * cols_here]
    params = (
        jnp.transpose(small_all.reshape(keys, R, slots_here, cols_here), (1, 2, 0, 3))
        .reshape(blocks * GAIN_ROW_WIDTH)
        .astype(F32)
    )
    wq_t = w_t[:width]
    wkv_t = w_t[width : 3 * width]
    wqkv_t = w_t[: 3 * width]
    bias_q = params[:width]
    bias_v = params[width : 2 * width]
    bias_o = params[2 * width : 3 * width]
    gain_one = params[3 * width : 4 * width]
    shift_one = params[4 * width : 5 * width]
    bias_up = params[5 * width : 5 * width + FF]
    bias_down = params[5 * width + FF : 6 * width + FF]
    gain_two = params[6 * width + FF : 7 * width + FF]
    shift_two = params[7 * width + FF :]

    q_all = (
        (dot_f32(wq_t, xg.reshape(micro * slot_count, width), ((1,), (1,))) + bias_q[:, None])
        .astype(BF16) * jnp.asarray(scale, BF16)
    )
    x_rows = x_own.reshape(token_count, width)
    kv = dot_f32(wkv_t, x_rows, ((1,), (1,))) + jnp.concatenate([jnp.zeros_like(bias_v), bias_v])[:, None]
    kv = jnp.swapaxes(kv.astype(BF16).reshape(2 * width, micro, key_len), 0, 1)
    k_all, v_all = kv[:, :width], kv[:, width:]

    seg_rows = segments.reshape(micro, slot_count)
    seg_keys = lax.dynamic_slice_in_dim(seg_rows, key_index * key_len, key_len, 1)
    logits, expo, o_part, st_part, tops = attention_forward(
        q_all, k_all, v_all, prev_logits, seg_keys[:, :, None], seg_rows[:, None, :], chunks, wide
    )
    o_part = from_chunks(o_part, keys).reshape(micro, Y, X, 2, width, key_len)
    st_part = from_chunks(st_part, keys).reshape(micro, groups, Y, X, 2, 2 * GROUP, key_len)
    zero = jnp.zeros_like(bias_o)
    vec = jnp.stack([bias_o, gain_one, shift_one, bias_down, gain_two, shift_two, zero, zero])
    out_hidden, datt_all, st_all, grad_one, dw_rest, dvec, d_bias_up = middle(
        mesh_dims, o_part, st_part, x_own, out_cot.reshape(x_own.shape), w_t, vec, bias_up[None]
    )
    out_hidden = out_hidden.reshape(tokens.shape)
    d_bias_o, d_gain_one, d_shift_one, d_bias_down, d_gain_two, d_shift_two = (dvec[i] for i in range(6))
    d_bias_up = d_bias_up[0]
    grad_one = grad_one.reshape(token_count, width)
    datt_all = to_chunks(datt_all.reshape(micro, keys, width, key_len), chunks)
    st_all = to_chunks(st_all.reshape(micro, groups, keys, 16, key_len), chunks)
    grad_prev, dq_part, dk, dv = attention_backward(
        expo, datt_all, st_all, tops, q_all, k_all, v_all, scale
    )
    dq_part = from_chunks(dq_part, keys).reshape(micro, Y, X, 2, width, key_len)
    dq = scatter_queries(mesh_dims, dq_part)

    grad_proj = jnp.swapaxes(jnp.concatenate([dq, dk, dv], axis=1), 0, 1).reshape(
        3 * width, token_count
    )
    d_qkv = dot_f32(grad_proj, x_rows, ((1,), (0,)))
    d_bias_q = jnp.sum(grad_proj[:width].astype(F32), axis=1)
    d_bias_v = jnp.sum(grad_proj[2 * width :].astype(F32), axis=1)
    grad_x = grad_one + dot_f32(grad_proj, wqkv_t, ((0,), (0,)))
    grad_tokens = grad_x.astype(BF16).reshape(tokens.shape)

    grads = jnp.concatenate(
        [d_qkv.astype(BF16), dw_rest], axis=0
    ).reshape(blocks, Y, X, 2, cols_here, width)
    small = jnp.concatenate(
        [d_bias_q, d_bias_v, d_bias_o, d_gain_one, d_shift_one, d_bias_up, d_bias_down, d_gain_two, d_shift_two]
    ).astype(BF16)
    small = jnp.transpose(
        small.reshape(R, slots_here, keys, cols_here), (2, 0, 1, 3)
    ).reshape(keys, R, slots_here * cols_here)
    small = jnp.pad(small, ((0, 0), (0, EXT - R), (0, width - slots_here * cols_here)))
    inverse = inverse_order(owners)
    mine_t, small_sum = scatter_weights(
        mesh_dims, inverse, grads, small.reshape(Y, X, 2, EXT, width)
    )
    mine_mat = jnp.swapaxes(mine_t, 1, 2)
    mine_small = lax.dynamic_slice_in_dim(small_sum, row_index, 1, 0)[
        :, : slots_here * cols_here
    ].reshape(master_small.shape)

    steps_done = step_count[0].astype(F32)
    fix_one = 1.0 - jnp.power(jnp.asarray(BETA_ONE, F32), steps_done)
    fix_two = 1.0 - jnp.power(jnp.asarray(BETA_TWO, F32), steps_done)
    rotated = jnp.einsum("sed,sec->sdc", eigen_bases, mine_mat, precision=HIGHEST_PREC)
    new_one = BETA_ONE * mom1_mat + (1.0 - BETA_ONE) * rotated
    new_two = BETA_TWO * mom2_mat + (1.0 - BETA_TWO) * rotated * rotated
    direction = new_one / fix_one / (jnp.sqrt(new_two / fix_two) + EPS_ADAM)
    back_rot = jnp.einsum("sdk,skc->sdc", eigen_bases, direction, precision=HIGHEST_PREC)
    slot_index_list = row_index * slots_here + jnp.arange(slots_here, dtype=jnp.int32)
    block_ids = jnp.take(inverse, slot_index_list)
    columns = (
        block_ids[:, None] * (cols_here * keys)
        + key_index * cols_here
        + jnp.arange(cols_here, dtype=jnp.int32)[None, :]
    )
    rates = column_rates(columns)[:, None, :]
    new_master = master_mat - rates * (back_rot + DECAY * master_mat)
    small_one = BETA_ONE * mom1_small + (1.0 - BETA_ONE) * mine_small
    small_two = BETA_TWO * mom2_small + (1.0 - BETA_TWO) * mine_small * mine_small
    new_small = master_small - RATE_SMALL * (small_one / fix_one) / (
        jnp.sqrt(small_two / fix_two) + EPS_ADAM
    )
    return (
        out_hidden,
        logits,
        grad_tokens,
        grad_prev,
        mine_mat,
        new_one,
        new_two,
        new_master,
        new_master.astype(BF16),
        mine_small,
        small_one,
        small_two,
        new_small,
        new_small.astype(BF16),
    )


def solution(mesh):
    chips = mesh.shape["keys"] // 2
    side = math.isqrt(chips)
    dims = (side, side, mesh.shape["rows"]) if side * side == chips else (1, chips, mesh.shape["rows"])
    acts = P(None, "rows", "keys", None)
    scores = P(None, "rows", None, "keys", None)
    mats = P("rows", None, "keys")
    smalls = P("rows", "keys")
    return jax.shard_map(
        functools.partial(per_device, dims),
        mesh=mesh,
        in_specs=(
            acts, scores, P(None, "rows", None), acts, mats, mats, mats,
            P("rows", None, None), smalls, smalls, smalls, P(), P(),
        ),
        out_specs=(acts, scores, acts, scores) + (mats,) * 5 + (smalls,) * 5,
        check_vma=False,
    )
```

```python
import functools
import math

import jax
import jax.numpy as jnp
from jax import lax
from jax.experimental import pallas as pl
from jax.experimental.pallas import tpu as pltpu
from jax.sharding import PartitionSpec as P

MODEL_WIDTH = 768
H = 12
HD = 64
FF = 3072
BLOCK_COLUMNS = 1152
GAIN_ROW_WIDTH = 1152

EPS_NORM = 1e-06
BETA_ONE = 0.95
BETA_TWO = 0.95
EPS_ADAM = 1e-08
DECAY = 0.01
RATE_SMALL = 0.3
NEG_BIG = -1e30
NEG_FLOOR = -1e29
HIGHEST_PREC = lax.Precision.HIGHEST
MESH = pl.DeviceIdType.MESH
F32 = jnp.float32
BF16 = jnp.bfloat16
ANY = pl.BlockSpec(memory_space=pl.ANY)
VMEM_SPEC = pl.BlockSpec(memory_space=pltpu.VMEM)
EXT = 16
EARLY = 2
VMEM_LIMIT = 60 << 20


def layer_norm(value):
    mean_val = jnp.mean(value, axis=-1, keepdims=True)
    centered = value - mean_val
    inv_dev = lax.rsqrt(jnp.mean(centered * centered, axis=-1, keepdims=True) + EPS_NORM)
    return (centered * inv_dev, inv_dev)


def norm_back(grad_in, normed, inv_dev, gain):
    scaled = grad_in * gain
    return inv_dev * (
        scaled
        - jnp.mean(scaled, axis=-1, keepdims=True)
        - normed * jnp.mean(scaled * normed, axis=-1, keepdims=True)
    )


def inverse_order(owners):
    slot_index_list = jnp.arange(owners.shape[0], dtype=jnp.int32)
    matches = (owners[None, :] == slot_index_list[:, None]).astype(jnp.int32)
    return jnp.sum(matches * slot_index_list[None, :], axis=1)


def column_rates(columns):
    inner = MODEL_WIDTH ** (-0.5)
    return jnp.where(
        columns < 3 * MODEL_WIDTH,
        inner,
        jnp.where(
            columns < 4 * MODEL_WIDTH,
            4.0 * inner,
            jnp.where(columns < 4 * MODEL_WIDTH + FF, inner, FF ** (-0.5)),
        ),
    )


def dot_f32(left, right, contract):
    return lax.dot_general(left, right, (contract, ((), ())), preferred_element_type=F32)


class Place:
    def __init__(self, side_y, side_x, rows):
        self.Y, self.X, self.R = side_y, side_x, rows
        key = lax.axis_index("keys")
        self.key = key
        self.r = lax.axis_index("rows")
        self.c = lax.rem(key, 2)
        self.x = lax.rem(key // 2, side_x)
        self.y = key // (2 * side_x)

    def keyof(self, y, x, c):
        return (y * self.X + x) * 2 + c

    def xo(self, d):
        return lax.rem(self.x + d, self.X)

    def yo(self, d):
        return lax.rem(self.y + d, self.Y)

    def ro(self, d):
        return lax.rem(self.r + d, self.R)

    def x_peer(self, d):
        return {"keys": self.keyof(self.y, self.xo(d), self.c)}

    def y_peer(self, d):
        return {"keys": self.keyof(self.yo(d), self.x, self.c)}

    def core_peer(self):
        return {"keys": self.keyof(self.y, self.x, 1 - self.c)}

    def z_peer(self, d):
        return {"rows": self.ro(d)}

    def barrier(self, with_z):
        sem = pltpu.get_barrier_semaphore()
        peers = [self.core_peer()]
        peers += [self.x_peer(d) for d in range(1, self.X)]
        peers += [self.y_peer(d) for d in range(1, self.Y)]
        if with_z:
            peers += [self.z_peer(d) for d in range(1, self.R)]
        for peer in peers:
            pl.semaphore_signal(sem, inc=1, device_id=peer, device_id_type=MESH)
        pl.semaphore_wait(sem, len(peers))


def remote(src, dst, send_sem, recv_sem, peer):
    return pltpu.make_async_remote_copy(
        src_ref=src,
        dst_ref=dst,
        send_sem=send_sem,
        recv_sem=recv_sem,
        device_id=peer,
        device_id_type=MESH,
    )


def sems_per_item(Y, X):
    return (X - 1) + (Y - 1) + 1


class Gather:
    def __init__(self, place, own, buf, send, recv, base, x_first):
        p = place
        self.sent = []
        n = sems_per_item(p.Y, p.X)
        idx = iter(range(base, base + n))
        first = [(p.x_peer(d)) for d in range(1, p.X)] if x_first else [p.y_peer(d) for d in range(1, p.Y)]
        second = [p.y_peer(d) for d in range(1, p.Y)] if x_first else [p.x_peer(d) for d in range(1, p.X)]
        line = buf.at[p.y, :, p.c] if x_first else buf.at[:, p.x, p.c]
        plane = buf.at[:, :, p.c]
        mine = buf.at[p.y, p.x, p.c]
        self.one = []
        for peer in first:
            i = next(idx)
            self.one.append(remote(own, mine, send.at[i], recv.at[i], peer))
        self.two = []
        for peer in second:
            i = next(idx)
            self.two.append(remote(line, line, send.at[i], recv.at[i], peer))
        i = next(idx)
        self.three = [remote(plane, plane, send.at[i], recv.at[i], p.core_peer())]

    def start1(self):
        for copy in self.one:
            copy.start()

    def start2(self):
        for copy in self.one:
            copy.wait_recv()
        for copy in self.two:
            copy.start()

    def start3(self):
        for copy in self.two:
            copy.wait_recv()
        for copy in self.three:
            copy.start()

    def finish(self):
        for copy in self.three:
            copy.wait_recv()
        for copy in self.one + self.two + self.three:
            copy.wait_send()


def gather_weights_kernel(
    Y, X, R, owners, w_ref, ext_ref, x_ref, wt_out, own_out, ext_out, xg_out,
    zbuf, zext, stage, sext, zsend, zrecv, send, recv, loc,
):
    p = Place(Y, X, R)
    slots_here = w_ref.shape[0]
    blocks = zbuf.shape[0]
    early = wt_out.shape[0]
    micro = x_ref.shape[0]
    n = sems_per_item(Y, X)
    p.barrier(True)
    here = pl.ds(p.r * slots_here, slots_here)

    def hop(src, step, own):
        there = pl.ds(src * slots_here, slots_here)
        way = (step + 1) // 2
        peer = {"rows": p.r + step}
        return [
            remote(w_ref if own else zbuf.at[there], zbuf.at[there], zsend.at[way, src, 0], zrecv.at[src, 0], peer),
            remote(ext_ref if own else zext.at[src], zext.at[src], zsend.at[way, src, 1], zrecv.at[src, 1], peer),
        ]

    def can(step):
        return p.r < R - 1 if step > 0 else p.r > 0

    def pass_on(dist, act):
        for step in (1, -1):
            src = p.r - step * dist

            @pl.when((src >= 0) & (src < R) & can(step))
            def _():
                for copy in hop(src, step, dist == 0):
                    act(copy)

    def arrived(dist):
        for step in (1, -1):
            src = p.r - step * dist

            @pl.when((src >= 0) & (src < R))
            def _():
                for copy in hop(src, step, False):
                    copy.wait_recv()

    pass_on(0, lambda copy: copy.start())
    xitems = []
    xlocal = []
    for m in range(micro):
        item = Gather(p, x_ref.at[m], xg_out.at[m], send, recv, m * n, m % 2 == 0)
        item.start1()
        xitems.append(item)
        copy = pltpu.make_async_copy(x_ref.at[m], xg_out.at[m, p.y, p.x, p.c], loc.at[m])
        copy.start()
        xlocal.append(copy)
    wl = pltpu.make_async_copy(w_ref, zbuf.at[here], loc.at[micro])
    wl.start()
    el = pltpu.make_async_copy(ext_ref, zext.at[p.r], loc.at[micro + 1])
    el.start()
    for m in range(micro):
        xlocal[m].wait()
        xitems[m].start2()
    for dist in range(1, R):
        arrived(dist)
        pass_on(dist, lambda copy: copy.start())
    wl.wait()
    el.wait()
    sext[...] = jnp.sum(zext[...].astype(F32), axis=0).astype(BF16)

    def reorder(b, carry):
        stage[b] = zbuf[owners[b]]
        return carry

    lax.fori_loop(0, blocks, reorder, 0)
    base = micro * n
    eitem = Gather(p, sext, ext_out, send, recv, base, True)
    base += n
    lcopies = []
    items = []
    for b in range(early):
        item = Gather(p, stage.at[b], wt_out.at[b], send, recv, base, b % 2 == 0)
        base += n
        item.start1()
        items.append(item)
        copy = pltpu.make_async_copy(stage.at[b], wt_out.at[b, p.y, p.x, p.c], loc.at[micro + 3 + b])
        copy.start()
        lcopies.append(copy)
    eitem.start1()
    ecopy = pltpu.make_async_copy(sext, ext_out.at[p.y, p.x, p.c], loc.at[micro + 2])
    ecopy.start()
    rest = pltpu.make_async_copy(stage.at[pl.ds(early, blocks - early)], own_out, loc.at[micro + 3 + early])
    rest.start()
    for m in range(micro):
        xitems[m].start3()
    for b in range(early):
        lcopies[b].wait()
        items[b].start2()
    ecopy.wait()
    eitem.start2()
    for b in range(early):
        items[b].start3()
    eitem.start3()
    for item in xitems + [eitem] + items:
        item.finish()
    for dist in range(R):
        pass_on(dist, lambda copy: copy.wait_send())
    rest.wait()


def gather_weights(mesh_dims, owners, w_own, ext, x_own):
    Y, X, R = mesh_dims
    slots_here, n, width = w_own.shape
    micro, tok = x_own.shape[:2]
    blocks = slots_here * R
    total = sems_per_item(Y, X) * (micro + 1 + EARLY)
    return pl.pallas_call(
        functools.partial(gather_weights_kernel, Y, X, R),
        out_shape=(
            jax.ShapeDtypeStruct((EARLY, Y, X, 2, n, width), BF16),
            jax.ShapeDtypeStruct((blocks - EARLY, n, width), BF16),
            jax.ShapeDtypeStruct((Y, X, 2, EXT, width), BF16),
            jax.ShapeDtypeStruct((micro, Y, X, 2, tok, width), BF16),
        ),
        in_specs=[pl.BlockSpec(memory_space=pltpu.SMEM), VMEM_SPEC, VMEM_SPEC, VMEM_SPEC],
        out_specs=(ANY, ANY, ANY, ANY),
        scratch_shapes=[
            pltpu.VMEM((blocks, n, width), BF16),
            pltpu.VMEM((R, EXT, width), BF16),
            pltpu.VMEM((blocks, n, width), BF16),
            pltpu.VMEM((EXT, width), BF16),
            pltpu.SemaphoreType.DMA((2, R, 2)),
            pltpu.SemaphoreType.DMA((R, 2)),
            pltpu.SemaphoreType.DMA((total,)),
            pltpu.SemaphoreType.DMA((total,)),
            pltpu.SemaphoreType.DMA((micro + 4 + EARLY,)),
        ],
        compiler_params=pltpu.CompilerParams(
            collective_id=1, has_side_effects=True, vmem_limit_bytes=VMEM_LIMIT
        ),
        name="gather_weights",
    )(owners, w_own, ext, x_own)


class Scatter:
    def __init__(self, place, parts, accs, r1s, r2s, r3s, send, recv, loc, base, lbase, y_first, merge):
        p = place
        self.p, self.y_first, self.merge = p, y_first, merge
        self.accs, self.r1s, self.r2s, self.r3s = accs, r1s, r2s, r3s
        self.count = len(parts)
        n = sems_per_item(p.Y, p.X) * len(parts)
        idx = iter(range(base, base + n))
        self.zero, self.one, self.two, self.three = [], [], [], []
        for t, part in enumerate(parts):
            i = next(idx)
            self.zero.append(pltpu.make_async_copy(part.at[:, :, p.c], accs[t], loc.at[lbase + t]))
            self.one.append(remote(part.at[:, :, 1 - p.c], r1s[t], send.at[i], recv.at[i], p.core_peer()))
            if y_first:
                for d in range(1, p.Y):
                    i = next(idx)
                    self.two.append(
                        remote(accs[t].at[p.yo(d)], r2s[t].at[d - 1], send.at[i], recv.at[i], p.y_peer(d))
                    )
                for d in range(1, p.X):
                    i = next(idx)
                    self.three.append(
                        remote(accs[t].at[p.y, p.xo(d)], r3s[t].at[d - 1], send.at[i], recv.at[i], p.x_peer(d))
                    )
            else:
                for d in range(1, p.X):
                    i = next(idx)
                    self.two.append(
                        remote(accs[t].at[:, p.xo(d)], r2s[t].at[d - 1], send.at[i], recv.at[i], p.x_peer(d))
                    )
                for d in range(1, p.Y):
                    i = next(idx)
                    self.three.append(
                        remote(accs[t].at[p.yo(d), p.x], r3s[t].at[d - 1], send.at[i], recv.at[i], p.y_peer(d))
                    )

    def start1(self):
        for copy in self.zero + self.one:
            copy.start()

    def start2(self):
        p = self.p
        for copy in self.zero:
            copy.wait()
        for copy in self.one:
            copy.wait_recv()

        def body(i, carry):
            y, x = i // p.X, lax.rem(i, p.X)
            self.merge([a.at[y, x] for a in self.accs], [r.at[y, x] for r in self.r1s])
            return carry

        lax.fori_loop(0, p.Y * p.X, body, 0)
        for copy in self.two:
            copy.start()

    def start3(self):
        p = self.p
        for copy in self.two:
            copy.wait_recv()
        if self.y_first:
            for d in range(1, p.Y):
                for x in range(p.X):
                    self.merge([a.at[p.y, x] for a in self.accs], [r.at[d - 1, x] for r in self.r2s])
        else:
            for d in range(1, p.X):
                for y in range(p.Y):
                    self.merge([a.at[y, p.x] for a in self.accs], [r.at[d - 1, y] for r in self.r2s])
        for copy in self.three:
            copy.start()

    def finish(self):
        p = self.p
        for copy in self.three:
            copy.wait_recv()
        mine = [a.at[p.y, p.x] for a in self.accs]
        for d in range(1, p.X if self.y_first else p.Y):
            self.merge(mine, [r.at[d - 1] for r in self.r3s])
        return mine

    def drain(self):
        for copy in self.one + self.two + self.three:
            copy.wait_send()


def merge_sum(into, other):
    a, b = into[0], other[0]
    a[...] = (a[...].astype(F32) + b[...].astype(F32)).astype(BF16)


def merge_soft(into, other):
    (va, sa), (vb, sb) = into, other
    ta, tb = sa[...], sb[...]
    heads = ta.shape[0] // 2
    top_a, top_b = ta[:heads], tb[:heads]
    top = jnp.maximum(top_a, top_b)
    wa, wb = jnp.exp(top_a - top), jnp.exp(top_b - top)
    sa[...] = jnp.concatenate([top, wa * ta[heads:] + wb * tb[heads:]], axis=0)
    for h in range(heads):
        rows = slice(h * HD, (h + 1) * HD)
        va[rows, :] = (
            va[rows, :].astype(F32) * wa[h : h + 1] + vb[rows, :].astype(F32) * wb[h : h + 1]
        ).astype(BF16)


def scatter_scratch(Y, X, items, shape, dtype, y_first_of):
    most = max((Y - 1) * X, (X - 1) * Y)
    return [
        pltpu.VMEM((items, Y, X) + shape, dtype),
        pltpu.VMEM((items, Y, X) + shape, dtype),
        pltpu.VMEM((items, max(Y, X) - 1, max(Y, X)) + shape, dtype),
        pltpu.VMEM((items, max(Y, X) - 1) + shape, dtype),
    ]


GROUP = 3


def middle_kernel(Y, X, R, blocks, pieces, *refs):
    o_ref, st_ref, x_ref, cot_ref, vec_ref, bu_ref = refs[:6]
    refs = refs[6:]
    count = 2 * Y * X if pieces else 1
    w_refs, refs = refs[:count], refs[count:]
    out_ref, datt_out, stat_out, dz_ref, dvec_ref, dbu_ref = refs[:6]
    refs = refs[6:]
    if pieces:
        send_a, keep_a, send_b, keep_b = refs[:4]
        refs = refs[4:]
    else:
        (dw_out,) = refs[:1]
        refs = refs[1:]
    (
        oa, o1, o2, o3, sa, s1, s2, s3, send, recv, loc, gsend, grecv, gloc, wsem, wsend, wrecv, dwsem,
        w, att, attk, low, hid, dpre, slope, df, da, n1, n2, datt, stat, dw,
    ) = refs[:32]
    if pieces:
        core_acc, core_in, csend, crecv = refs[32:]
    p = Place(Y, X, R)
    micro, tok, width = x_ref.shape
    groups = st_ref.shape[1]
    rows = GROUP * HD
    bo, g1, e1, bd, g2, e2 = (vec_ref[i : i + 1] for i in range(6))
    stat[...] = jnp.zeros_like(stat)
    parts = FF // width
    wcopies, wremote = [], []
    if pieces:
        half, piece = w_refs[0].shape[:2]
        for t in range(2):
            for dy in range(Y):
                for dx in range(X):
                    src = w_refs[(t * Y + dy) * X + dx]
                    key = p.keyof(p.yo(Y - dy), p.xo(X - dx), p.c)
                    for b in range(half):
                        at = (t * half + b) * BLOCK_COLUMNS + key * piece
                        dst = w.at[pl.ds(pl.multiple_of(at, 16), piece)]
                        i = ((t * Y + dy) * X + dx) * half + b
                        wcopies.append(pltpu.make_async_copy(src.at[b], dst, wsem.at[i]))
                        wremote.append(remote(src.at[b], dst, wsend.at[i], wrecv.at[i], p.core_peer()))
    else:
        wcopies.append(pltpu.make_async_copy(w_refs[0], w, wsem.at[0]))
    for copy in wcopies:
        copy.start()
    p.barrier(False)

    n = sems_per_item(Y, X) * 2
    merges = []
    for m in range(micro):
        for g in range(groups):
            i = m * groups + g
            item = Scatter(
                p,
                [o_ref.at[m, :, :, :, pl.ds(g * rows, rows)], st_ref.at[m, g]],
                [oa.at[i], sa.at[i]], [o1.at[i], s1.at[i]], [o2.at[i], s2.at[i]], [o3.at[i], s3.at[i]],
                send, recv, loc, i * n, i * 2, g % 2 == 0, merge_soft,
            )
            item.start1()
            merges.append(item)

    def merge_two(m):
        for g in range(groups):
            merges[m * groups + g].start2()

    def merge_three(m):
        for g in range(groups):
            merges[m * groups + g].start3()

    def merge_finish(m):
        for g in range(groups):
            val, st = merges[m * groups + g].finish()
            tile = st[...]
            inv = 1.0 / tile[GROUP:]
            stat[m, g, : 2 * GROUP] = jnp.concatenate([tile[:GROUP], inv], axis=0)
            for h in range(GROUP):
                att[m, g * rows + h * HD : g * rows + (h + 1) * HD, :] = (
                    val[h * HD : (h + 1) * HD, :].astype(F32) * inv[h : h + 1]
                ).astype(BF16)

    n = sems_per_item(Y, X)
    gathers = [[], []]

    def gather_one(m):
        local = []
        for g in range(groups):
            ds = pl.ds(g * rows, rows)
            for t, (own, out) in enumerate(
                ((datt.at[m, ds], datt_out.at[m, :, :, :, ds]), (stat.at[m, g], stat_out.at[m, g]))
            ):
                i = (m * groups + g) * 2 + t
                item = Gather(p, own, out, gsend, grecv, i * n, g % 2 == 0)
                item.start1()
                copy = pltpu.make_async_copy(own, out.at[p.y, p.x, p.c], gloc.at[i])
                copy.start()
                gathers[m].append((item, copy))

    def gather_two(m):
        for item, copy in gathers[m]:
            copy.wait()
            item.start2()

    def gather_three(m):
        for item, copy in gathers[m]:
            item.start3()

    def forward(m):
        at = att[m].T
        attk[m] = at
        wo = w[:width]
        z1 = x_ref[m].astype(F32) + (dot_f32(at, wo, ((1,), (1,))) + bo)
        norm, inv = layer_norm(z1)
        n1[...] = norm
        mid = norm * g1 + e1
        low[m] = mid.astype(BF16)
        inner = low[m]

        def body(i, acc):
            r = pl.multiple_of(i * width, width)
            pre = dot_f32(inner, w[pl.ds(width + r, width)], ((1,), (1,))) + bu_ref[:, pl.ds(r, width)]
            half = 0.5 + 0.5 * lax.erf(pre * math.sqrt(0.5))
            low_h = (pre * half).astype(BF16)
            hid[m, :, pl.ds(r, width)] = low_h
            slope[:, pl.ds(r, width)] = half + pre * (
                jnp.exp(-0.5 * pre * pre) * (1.0 / math.sqrt(2.0 * math.pi))
            )
            return acc + dot_f32(low_h, w[pl.ds(width + FF + r, width)], ((1,), (0,)))

        f = lax.fori_loop(0, parts, body, jnp.zeros((tok, width), F32)) + bd
        norm2, inv2 = layer_norm(mid + f)
        n2[...] = norm2
        out_ref[m] = (norm2 * g2 + e2).astype(BF16)
        return inv, inv2

    def backward(m, invs):
        inv, inv2 = invs
        cot = cot_ref[m].astype(F32)
        norm2 = n2[...]
        dz2 = norm_back(cot, norm2, inv2, g2)
        dg2 = jnp.sum(cot * norm2, axis=0, keepdims=True)
        de2 = jnp.sum(cot, axis=0, keepdims=True)
        df_low = dz2.astype(BF16)
        df[m] = df_low
        dbd = jnp.sum(df_low.astype(F32), axis=0, keepdims=True)

        def body(i, acc):
            r = pl.multiple_of(i * width, width)
            dh = dot_f32(df_low, w[pl.ds(width + FF + r, width)], ((1,), (1,)))
            dp = (dh * slope[:, pl.ds(r, width)]).astype(BF16)
            dpre[m, :, pl.ds(r, width)] = dp
            part = jnp.sum(dp.astype(F32), axis=0, keepdims=True)
            if m == 0:
                dbu_ref[:, pl.ds(r, width)] = part
            else:
                dbu_ref[:, pl.ds(r, width)] += part
            return acc + dot_f32(dp, w[pl.ds(width + r, width)], ((1,), (0,)))

        dx1 = lax.fori_loop(0, parts, body, dz2)
        norm = n1[...]
        dg1 = jnp.sum(dx1 * norm, axis=0, keepdims=True)
        de1 = jnp.sum(dx1, axis=0, keepdims=True)
        dz1 = norm_back(dx1, norm, inv, g1)
        dz_ref[m] = dz1
        da_low = dz1.astype(BF16)
        da[m] = da_low
        dbo = jnp.sum(da_low.astype(F32), axis=0, keepdims=True)
        sums = jnp.concatenate([dbo, dg1, de1, dbd, dg2, de2, dg2, dg2], axis=0)
        if m == 0:
            dvec_ref[...] = sums
        else:
            dvec_ref[...] += sums
        dt = dot_f32(da_low, w[:width], ((1,), (0,))).astype(BF16).T
        datt[m] = dt
        for g in range(groups):
            for h in range(GROUP):
                r = g * rows + h * HD
                stat[m, g, 2 * GROUP + h : 2 * GROUP + h + 1] = jnp.sum(
                    dt[r : r + HD].astype(F32) * att[m, r : r + HD, :].astype(F32), axis=0, keepdims=True
                )

    step = width // 2

    def chunk_grad(slot, at, chunk):
        for left, right, lo, count in ((da, attk, 0, width), (dpre, low, width, FF), (hid, df, width + FF, FF)):

            @pl.when((chunk * step >= lo) & (chunk * step < lo + count))
            def _():
                cols = pl.ds(pl.multiple_of(chunk * step - lo, step), step)
                total = dot_f32(left[0, :, cols], right[0], ((0,), (0,)))
                for m in range(1, micro):
                    total = total + dot_f32(left[m, :, cols], right[m], ((0,), (0,)))
                dw[slot, pl.ds(pl.multiple_of(at, step), step)] = total.astype(BF16)

    def block_grad(b, slot):
        per = BLOCK_COLUMNS // step

        def body(t, carry):
            chunk_grad(slot, t * step, b * per + t)
            return carry

        lax.fori_loop(0, per, body, 0)

    merge_two(0)
    for copy in wremote:
        copy.start()
    merge_three(0)
    merge_two(1)
    merge_finish(0)
    for copy in wcopies:
        copy.wait()
    for copy in wremote:
        copy.wait_recv()
    invs = forward(0)
    merge_three(1)
    backward(0, invs)
    gather_one(0)
    merge_finish(1)
    invs = forward(1)
    gather_two(0)
    backward(1, invs)
    gather_one(1)
    gather_three(0)
    if pieces:
        half, piece = w_refs[0].shape[:2]
        keeps = []

        def cores(b):
            slot = lax.rem(b, 2)
            copies = []
            for y in range(Y):
                for x in range(X):
                    i = (b * Y + y) * X + x
                    there = pl.multiple_of(p.keyof(y, x, 1 - p.c) * piece, 16)
                    copies.append(
                        remote(
                            dw.at[slot, pl.ds(there, piece)], core_in.at[b, y, x],
                            csend.at[i], crecv.at[i], p.core_peer(),
                        )
                    )
            return copies

        def one_block(b, carry):
            slot = lax.rem(b, 2)

            @pl.when(b >= 2)
            def _():
                for copy in cores(b - 2):
                    copy.wait_send()

            block_grad(b, slot)
            for copy in cores(b):
                copy.start()
            for y in range(Y):
                for x in range(X):
                    here = pl.multiple_of(p.keyof(y, x, p.c) * piece, 16)
                    core_acc[b, y, x] = dw[slot, pl.ds(here, piece)]
            return carry

        lax.fori_loop(0, blocks // 2, one_block, 0)
        gather_two(1)
        lax.fori_loop(blocks // 2, blocks, one_block, 0)
        gather_three(1)

        def add(i, carry):
            b, y, x = i // (Y * X), lax.rem(i // X, Y), lax.rem(i, X)
            merge_sum([core_acc.at[b, y, x]], [core_in.at[b, y, x]])
            return carry

        def add_block(b, carry):
            for copy in cores(b):
                copy.wait_recv()
            lax.fori_loop(b * Y * X, (b + 1) * Y * X, add, 0)
            return carry

        lax.fori_loop(0, blocks, add_block, 0)
        first, last = pl.ds(0, half), pl.ds(half, half)
        for x in range(X):
            keeps.append((core_acc.at[first, p.y, x], keep_a.at[x]))
            for d in range(1, Y):
                keeps.append((core_acc.at[first, p.yo(d), x], send_a.at[d - 1, x]))
        for y in range(Y):
            keeps.append((core_acc.at[last, y, p.x], keep_b.at[y]))
            for d in range(1, X):
                keeps.append((core_acc.at[last, y, p.xo(d)], send_b.at[d - 1, y]))
        keeps = [pltpu.make_async_copy(src, dst, dwsem.at[i]) for i, (src, dst) in enumerate(keeps)]
        for copy in keeps:
            copy.start()
        for copy in keeps:
            copy.wait()
        for b in (blocks - 2, blocks - 1):
            for copy in cores(jnp.int32(b)):
                copy.wait_send()
    else:
        copies = []
        for b in range(blocks):
            slot = b % 2
            if b >= 2:
                copies[b - 2].wait()
            block_grad(b, slot)
            copies.append(
                pltpu.make_async_copy(
                    dw.at[slot], dw_out.at[pl.ds(b * BLOCK_COLUMNS, BLOCK_COLUMNS)], dwsem.at[slot]
                )
            )
            copies[-1].start()
            if b == blocks // 2:
                gather_two(1)
        for copy in copies[-2:]:
            copy.wait()
        gather_three(1)
    for item in merges:
        item.drain()
    for copy in wremote:
        copy.wait_send()
    for m in range(micro):
        for item, copy in gathers[m]:
            item.finish()


def middle(mesh_dims, o_part, st_part, x_own, cot, weights, vec, bias_up):
    Y, X, R = mesh_dims
    micro, tok, width = x_own.shape
    groups = st_part.shape[1]
    items = micro * groups
    merge_sems = sems_per_item(Y, X) * 2 * items
    strows = 16
    ffw = 2 * FF + width
    blocks = ffw // BLOCK_COLUMNS
    pieces = len(weights) > 1
    outs = [
        (jax.ShapeDtypeStruct((micro, tok, width), BF16), VMEM_SPEC),
        (jax.ShapeDtypeStruct((micro, Y, X, 2, width, tok), BF16), ANY),
        (jax.ShapeDtypeStruct((micro, groups, Y, X, 2, strows, tok), F32), ANY),
        (jax.ShapeDtypeStruct((micro, tok, width), F32), VMEM_SPEC),
        (jax.ShapeDtypeStruct((8, width), F32), VMEM_SPEC),
        (jax.ShapeDtypeStruct((1, FF), F32), VMEM_SPEC),
    ]
    extra = []
    if pieces:
        half, piece = weights[0].shape[:2]
        wsems = 2 * Y * X * half
        outs += [
            (jax.ShapeDtypeStruct((max(Y - 1, 1), X, half, piece, width), BF16), ANY),
            (jax.ShapeDtypeStruct((X, half, piece, width), BF16), ANY),
            (jax.ShapeDtypeStruct((max(X - 1, 1), Y, half, piece, width), BF16), ANY),
            (jax.ShapeDtypeStruct((Y, half, piece, width), BF16), ANY),
        ]
        extra = [
            pltpu.VMEM((blocks, Y, X, piece, width), BF16),
            pltpu.VMEM((blocks, Y, X, piece, width), BF16),
            pltpu.SemaphoreType.DMA((blocks * Y * X,)),
            pltpu.SemaphoreType.DMA((blocks * Y * X,)),
        ]
    else:
        wsems = 1
        outs += [(jax.ShapeDtypeStruct((ffw, width), BF16), ANY)]
    return pl.pallas_call(
        functools.partial(middle_kernel, Y, X, R, blocks, pieces),
        out_shape=tuple(o for o, _ in outs),
        in_specs=[ANY, ANY, VMEM_SPEC, VMEM_SPEC, VMEM_SPEC, VMEM_SPEC] + [ANY] * len(weights),
        out_specs=tuple(spec for _, spec in outs),
        scratch_shapes=scatter_scratch(Y, X, items, (GROUP * HD, tok), BF16, None)
        + scatter_scratch(Y, X, items, (2 * GROUP, tok), F32, None)
        + [
            pltpu.SemaphoreType.DMA((merge_sems,)),
            pltpu.SemaphoreType.DMA((merge_sems,)),
            pltpu.SemaphoreType.DMA((items * 2,)),
            pltpu.SemaphoreType.DMA((merge_sems,)),
            pltpu.SemaphoreType.DMA((merge_sems,)),
            pltpu.SemaphoreType.DMA((items * 2,)),
            pltpu.SemaphoreType.DMA((wsems,)),
            pltpu.SemaphoreType.DMA((wsems,)),
            pltpu.SemaphoreType.DMA((wsems,)),
            pltpu.SemaphoreType.DMA((2 * X * Y,)),
            pltpu.VMEM((ffw, width), BF16),
            pltpu.VMEM((micro, width, tok), BF16),
            pltpu.VMEM((micro, tok, width), BF16),
            pltpu.VMEM((micro, tok, width), BF16),
            pltpu.VMEM((micro, tok, FF), BF16),
            pltpu.VMEM((micro, tok, FF), BF16),
            pltpu.VMEM((tok, FF), F32),
            pltpu.VMEM((micro, tok, width), BF16),
            pltpu.VMEM((micro, tok, width), BF16),
            pltpu.VMEM((tok, width), F32),
            pltpu.VMEM((tok, width), F32),
            pltpu.VMEM((micro, width, tok), BF16),
            pltpu.VMEM((micro, groups, strows, tok), F32),
            pltpu.VMEM((2, BLOCK_COLUMNS, width), BF16),
        ]
        + extra,
        compiler_params=pltpu.CompilerParams(
            collective_id=2, has_side_effects=True, vmem_limit_bytes=VMEM_LIMIT
        ),
        name="middle",
    )(o_part, st_part, x_own, cot, vec, bias_up, *weights)


def tail_kernel(
    Y, X, R, inverse,
    dq_ref, dk_ref, dv_ref, x_ref, dz_ref, w_ref, fin_ref, vec_ref, bu_ref,
    tok_ref, late_ref, early_ref, sum_ref,
    qa, q1, q2, q3, send, recv, loc,
    part, a, r1, r2, r3, bsend, brecv, bloc,
    stage, rz, zsend, zrecv, qf, qz, rq, qsend, qrecv,
    small, sbuf, ssend, srecv, w, wsem, dq,
):
    p = Place(Y, X, R)
    micro, tok, width = x_ref.shape
    slots_here = late_ref.shape[0]
    groups = qa.shape[0] // micro
    rows = GROUP * HD
    n = sems_per_item(Y, X)
    piece = part.shape[4]
    wcopy = pltpu.make_async_copy(w_ref, w, wsem)
    wcopy.start()
    p.barrier(True)
    qitems = []
    for m in range(micro):
        for g in range(groups):
            i = m * groups + g
            item = Scatter(
                p, [dq_ref.at[m, :, :, :, pl.ds(g * rows, rows)]],
                [qa.at[i]], [q1.at[i]], [q2.at[i]], [q3.at[i]],
                send, recv, loc, i * n, i, g % 2 == 0, merge_sum,
            )
            item.start1()
            qitems.append(item)

    def reorder(s, carry):
        stage[s] = fin_ref[jnp.maximum(inverse[s] - EARLY, 0)]
        return carry

    lax.fori_loop(0, stage.shape[0], reorder, 0)
    zcopies = []
    for d in range(1, R):
        there = pl.ds(p.ro(d) * slots_here, slots_here)
        copy = remote(stage.at[there], rz.at[d - 1], zsend.at[d], zrecv.at[d], p.z_peer(d))
        copy.start()
        zcopies.append(copy)

    def product(ref, first, count):
        total = dot_f32(ref[0, first : first + count], x_ref[0], ((1,), (0,)))
        for m in range(1, micro):
            total = total + dot_f32(ref[m, first : first + count], x_ref[m], ((1,), (0,)))
        return total.astype(BF16)

    def put(b, first, value):
        at = 0
        while at < value.shape[0]:
            key, off = divmod(first + at, piece)
            count = min(piece - off, value.shape[0] - at)
            y, x, c = key // (2 * X), key // 2 % X, key % 2
            part[b, y, x, c, off : off + count] = value[at : at + count]
            at += count

    cuts = ((0, piece // 32 * 16, True), (piece // 32 * 16, piece - piece // 32 * 16, False))

    def block_items(b):
        out = []
        for t, (first, count, y_first) in enumerate(cuts):
            ds = pl.ds(first, count)
            i = b * len(cuts) + t
            out.append(
                Scatter(
                    p, [part.at[b, :, :, :, ds]], [a.at[b, :, :, ds]], [r1.at[b, :, :, ds]],
                    [r2.at[b, :, :, ds]], [r3.at[b, :, ds]],
                    bsend, brecv, bloc, i * n, i, y_first, merge_sum,
                )
            )
        return out

    class Block:
        def __init__(self, b):
            self.b, self.items = b, block_items(b)
            self.one = [
                remote(qz.at[b, p.ro(d)], rq.at[b, d - 1], qsend.at[b, 0, d], qrecv.at[b, 0, d], p.z_peer(d))
                for d in range(1, R)
            ]
            mine = early_ref.at[b, p.r]
            self.two = [
                remote(mine, mine, qsend.at[b, 1, d], qrecv.at[b, 1, d], p.z_peer(d)) for d in range(1, R)
            ]

        def step(self, name):
            for item in self.items:
                getattr(item, name)()

        def z_one(self):
            for item, (first, count, _) in zip(self.items, cuts):
                (val,) = item.finish()
                qf[first : first + count] = val[...].astype(F32)
            share = qz.shape[2]
            for i in range(R):
                qz[self.b, i] = qf[i * share : (i + 1) * share].astype(BF16)
            for copy in self.one:
                copy.start()

        def z_two(self):
            for copy in self.one:
                copy.wait_recv()
            total = qz[self.b, p.r].astype(F32)
            for d in range(1, R):
                total = total + rq[self.b, d - 1].astype(F32)
            early_ref[self.b, p.r] = total.astype(BF16)
            for copy in self.two:
                copy.start()

        def finish(self):
            for copy in self.two:
                copy.wait_recv()
            for item in self.items:
                item.drain()
            for copy in self.one + self.two:
                copy.wait_send()

    block0, block1 = Block(0), Block(1)
    half = width // 2
    put(1, 0, product(dk_ref, half, half))
    put(1, half, product(dv_ref, 0, width))
    block1.step("start1")
    for item in qitems:
        item.start2()
    block1.step("start2")
    for item in qitems:
        item.start3()
    put(0, width, product(dk_ref, 0, half))
    block1.step("start3")
    for m in range(micro):
        for g in range(groups):
            (val,) = qitems[m * groups + g].finish()
            dq[m, g * rows : (g + 1) * rows, :] = val[...]
    put(0, 0, product(dq, 0, width))
    block0.step("start1")
    block1.z_one()

    ones = jnp.ones((8, tok), BF16)
    sums = []
    for ref in (dq, dv_ref):
        total = dot_f32(ones, ref[0], ((1,), (1,)))
        for m in range(1, micro):
            total = total + dot_f32(ones, ref[m], ((1,), (1,)))
        sums.append(total[:1])
    sums += [vec_ref[:3]]
    sums += [bu_ref[:, i * width : (i + 1) * width] for i in range(FF // width)]
    sums += [vec_ref[3:6], jnp.zeros((4, width), F32)]
    small[...] = jnp.concatenate(sums, axis=0).astype(BF16)
    stages = [[p.core_peer()]]
    stages.append([p.x_peer(d) for d in range(1, X)])
    stages.append([p.y_peer(d) for d in range(1, Y)])
    stages.append([p.z_peer(d) for d in range(1, R)])
    scopies = []
    at = 0
    for peers in stages:
        row = []
        for peer in peers:
            row.append(remote(small, sbuf.at[at], ssend.at[at], srecv.at[at], peer))
            at += 1
        scopies.append(row)

    def small_start(t):
        for copy in scopies[t]:
            copy.start()

    def small_wait(t):
        at = sum(len(row) for row in scopies[:t])
        for copy in scopies[t]:
            copy.wait_recv()
        for copy in scopies[t]:
            copy.wait_send()
        total = small[...].astype(F32)
        for i in range(len(scopies[t])):
            total = total + sbuf[at + i].astype(F32)
        return total

    def token_grad(m):
        total = dz_ref[m] + dot_f32(dq[m], w[:width], ((0,), (0,)))
        total = total + dot_f32(dk_ref[m], w[width : 2 * width], ((0,), (0,)))
        total = total + dot_f32(dv_ref[m], w[2 * width :], ((0,), (0,)))
        tok_ref[m] = total.astype(BF16)

    small_start(0)
    block0.step("start2")
    small[...] = small_wait(0).astype(BF16)
    small_start(1)
    wcopy.wait()
    for m in range(micro // 2):
        token_grad(m)
    block0.step("start3")
    small[...] = small_wait(1).astype(BF16)
    small_start(2)
    block1.z_two()
    for m in range(micro // 2, micro):
        token_grad(m)
    block0.z_one()
    small[...] = small_wait(2).astype(BF16)
    small_start(3)
    for copy in zcopies:
        copy.wait_recv()
    for s in range(slots_here):
        total = stage[p.r * slots_here + s].astype(F32)
        for d in range(1, R):
            total = total + rz[d - 1, s].astype(F32)
        late_ref[s] = total
    block0.z_two()
    sum_ref[...] = small_wait(3)
    block1.finish()
    block0.finish()
    for item in qitems:
        item.drain()
    for copy in zcopies:
        copy.wait_send()


def tail(mesh_dims, inverse, dq_part, dk, dv, x_own, grad_one, w_early, fin, dvec, d_bias_up):
    Y, X, R = mesh_dims
    micro, tok, width = x_own.shape
    late, n = fin.shape[:2]
    blocks = EARLY + late
    slots_here = blocks // R
    groups = width // (GROUP * HD)
    items = micro * groups
    per = sems_per_item(Y, X)
    share = n // R
    cuts = 2
    small = (16, width)
    hops = 1 + (X - 1) + (Y - 1) + (R - 1)
    return pl.pallas_call(
        functools.partial(tail_kernel, Y, X, R),
        out_shape=(
            jax.ShapeDtypeStruct((micro, tok, width), BF16),
            jax.ShapeDtypeStruct((slots_here, n, width), F32),
            jax.ShapeDtypeStruct((EARLY, R, share, width), BF16),
            jax.ShapeDtypeStruct(small, F32),
        ),
        in_specs=[pl.BlockSpec(memory_space=pltpu.SMEM), ANY]
        + [VMEM_SPEC] * 4
        + [ANY, VMEM_SPEC, VMEM_SPEC, VMEM_SPEC],
        out_specs=(VMEM_SPEC,) * 4,
        scratch_shapes=scatter_scratch(Y, X, items, (GROUP * HD, tok), BF16, None)
        + [
            pltpu.SemaphoreType.DMA((per * items,)),
            pltpu.SemaphoreType.DMA((per * items,)),
            pltpu.SemaphoreType.DMA((items,)),
            pltpu.VMEM((EARLY, Y, X, 2, n, width), BF16),
        ]
        + scatter_scratch(Y, X, EARLY, (n, width), BF16, None)
        + [
            pltpu.SemaphoreType.DMA((per * EARLY * cuts,)),
            pltpu.SemaphoreType.DMA((per * EARLY * cuts,)),
            pltpu.SemaphoreType.DMA((EARLY * cuts,)),
            pltpu.VMEM((blocks, n, width), BF16),
            pltpu.VMEM((R - 1, slots_here, n, width), BF16),
            pltpu.SemaphoreType.DMA((R,)),
            pltpu.SemaphoreType.DMA((R,)),
            pltpu.VMEM((n, width), F32),
            pltpu.VMEM((EARLY, R, share, width), BF16),
            pltpu.VMEM((EARLY, R - 1, share, width), BF16),
            pltpu.SemaphoreType.DMA((EARLY, 2, R)),
            pltpu.SemaphoreType.DMA((EARLY, 2, R)),
            pltpu.VMEM(small, BF16),
            pltpu.VMEM((hops,) + small, BF16),
            pltpu.SemaphoreType.DMA((hops,)),
            pltpu.SemaphoreType.DMA((hops,)),
            pltpu.VMEM((3 * width, width), BF16),
            pltpu.SemaphoreType.DMA,
            pltpu.VMEM((micro, width, tok), BF16),
        ],
        compiler_params=pltpu.CompilerParams(
            collective_id=5, has_side_effects=True, vmem_limit_bytes=VMEM_LIMIT
        ),
        name="tail",
    )(inverse, dq_part, dk, dv, x_own, grad_one, w_early.reshape(3 * width, width), fin, dvec, d_bias_up)


def attention_forward_kernel(q_ref, k_ref, v_ref, prev_ref, segk_ref, segq_ref, *refs):
    logit_ref, e_ref, o_ref, st_ref, top_ref, mask_ref = refs[-6:]
    h = pl.program_id(0)
    chunks, wide = o_ref.shape[1], o_ref.shape[3]

    @pl.when(h == 0)
    def _():
        mask_ref[...] = jnp.where(segk_ref[0] == segq_ref[0], 0.0, NEG_BIG)

    hg = lax.rem(h, GROUP)
    score = dot_f32(k_ref[...], q_ref[...], ((0,), (0,)))
    raw = score + prev_ref[0, 0, 0].astype(F32)
    logit_ref[0, 0, 0] = raw.astype(BF16)
    masked = raw + mask_ref[...]
    top = jnp.maximum(jnp.max(masked, axis=0, keepdims=True), NEG_FLOOR)
    expo = jnp.exp(masked - top)
    total = jnp.sum(expo, axis=0, keepdims=True)
    low = expo.astype(BF16)
    e_ref[0, 0] = low
    out = dot_f32(v_ref[...], low, ((1,), (0,))).astype(BF16)
    for t in range(chunks):
        cols = slice(t * wide, (t + 1) * wide)
        o_ref[0, t] = out[:, cols]
        st_ref[0, 0, t, pl.ds(hg, 1), :] = top[:, cols]
        st_ref[0, 0, t, pl.ds(GROUP + hg, 1), :] = total[:, cols]
        top_ref[0, 0, t, pl.ds(hg, 1), :] = top[:, cols]


def attention_forward(m, so_far, q, k, v, prev, segk, segq, chunks, wide):
    micro, _, heads, own, slots = prev.shape
    groups = heads // GROUP
    score = pl.BlockSpec((1, 1, 1, own, slots), lambda h: (m, 0, h, 0, 0))
    stat = pl.BlockSpec((1, 1, chunks, 2 * GROUP, wide), lambda h: (m, h // GROUP, 0, 0, 0))
    return pl.pallas_call(
        attention_forward_kernel,
        grid=(heads,),
        out_shape=(
            jax.ShapeDtypeStruct(prev.shape, BF16),
            jax.ShapeDtypeStruct((micro, heads, own, slots), BF16),
            jax.ShapeDtypeStruct((micro, chunks, heads * HD, wide), BF16),
            jax.ShapeDtypeStruct((micro, groups, chunks, 2 * GROUP, wide), F32),
            jax.ShapeDtypeStruct((micro, groups, chunks, 2 * GROUP, wide), F32),
        ),
        in_specs=[
            pl.BlockSpec((HD, slots), lambda h: (h, 0)),
            pl.BlockSpec((HD, own), lambda h: (h, 0)),
            pl.BlockSpec((HD, own), lambda h: (h, 0)),
            score,
            pl.BlockSpec((1, own, 1), lambda h: (m, 0, 0)),
            pl.BlockSpec((1, 1, slots), lambda h: (m, 0, 0)),
        ]
        + [ANY] * len(so_far),
        out_specs=(
            score,
            pl.BlockSpec((1, 1, own, slots), lambda h: (m, h, 0, 0)),
            pl.BlockSpec((1, chunks, HD, wide), lambda h: (m, 0, h, 0)),
            stat,
            stat,
        ),
        input_output_aliases={6 + i: i for i in range(len(so_far))},
        scratch_shapes=[pltpu.VMEM((own, slots), F32)],
        compiler_params=pltpu.CompilerParams(vmem_limit_bytes=VMEM_LIMIT),
        cost_estimate=pl.CostEstimate(
            flops=heads * 2 * 2 * own * slots * HD,
            bytes_accessed=heads * own * slots * 6,
            transcendentals=heads * own * slots,
        ),
        name="attention_forward",
    )(q, k, v, prev, segk, segq, *so_far)


def attention_backward_kernel(
    scale, e_ref, d_ref, st_ref, top_ref, q_ref, k_ref, v_ref, *refs
):
    g_ref, dq_ref, dk_ref, dv_ref = refs[-4:]
    h = pl.program_id(0)
    chunks, wide = d_ref.shape[1], d_ref.shape[3]
    hg = lax.rem(h, GROUP)

    def row(ref, first):
        return jnp.concatenate([ref[0, 0, t, pl.ds(first + hg, 1), :] for t in range(chunks)], axis=1)

    weight = jnp.exp(row(top_ref, 0) - row(st_ref, 0)) * row(st_ref, GROUP)
    dots = row(st_ref, 2 * GROUP) * weight
    low = e_ref[0, 0]
    datt = jnp.concatenate([d_ref[0, t] for t in range(chunks)], axis=1)
    grad_in = (datt.astype(F32) * weight).astype(BF16)
    soft = dot_f32(v_ref[...], grad_in, ((0,), (0,))) - dots
    grad = (low.astype(F32) * soft).astype(BF16)
    g_ref[0, 0, 0] = grad
    dq = (dot_f32(k_ref[...], grad, ((1,), (0,))) * scale).astype(BF16)
    for t in range(chunks):
        dq_ref[0, t] = dq[:, t * wide : (t + 1) * wide]
    dv_ref[0] = dot_f32(grad_in, low, ((1,), (1,))).astype(BF16)
    dk_ref[0] = dot_f32(q_ref[...], grad, ((1,), (1,))).astype(BF16)


def attention_backward(m, so_far, expo, datt, st, tops, q, k, v, scale):
    micro, heads, own, slots = expo.shape
    chunks, wide = datt.shape[1], datt.shape[3]
    flops = heads * 2 * 4 * own * slots * HD
    sts = st.shape[3]
    return pl.pallas_call(
        functools.partial(attention_backward_kernel, scale),
        grid=(heads,),
        out_shape=(
            jax.ShapeDtypeStruct((micro, 1, heads, own, slots), BF16),
            jax.ShapeDtypeStruct((micro, chunks, heads * HD, wide), BF16),
            jax.ShapeDtypeStruct((micro, heads * HD, own), BF16),
            jax.ShapeDtypeStruct((micro, heads * HD, own), BF16),
        ),
        in_specs=[
            pl.BlockSpec((1, 1, own, slots), lambda h: (m, h, 0, 0)),
            pl.BlockSpec((1, chunks, HD, wide), lambda h: (m, 0, h, 0)),
            pl.BlockSpec((1, 1, chunks, sts, wide), lambda h: (m, h // GROUP, 0, 0, 0)),
            pl.BlockSpec((1, 1, chunks, 2 * GROUP, wide), lambda h: (m, h // GROUP, 0, 0, 0)),
            pl.BlockSpec((HD, slots), lambda h: (h, 0)),
            pl.BlockSpec((HD, own), lambda h: (h, 0)),
            pl.BlockSpec((HD, own), lambda h: (h, 0)),
        ]
        + [ANY] * len(so_far),
        out_specs=(
            pl.BlockSpec((1, 1, 1, own, slots), lambda h: (m, 0, h, 0, 0)),
            pl.BlockSpec((1, chunks, HD, wide), lambda h: (m, 0, h, 0)),
            pl.BlockSpec((1, HD, own), lambda h: (m, h, 0)),
            pl.BlockSpec((1, HD, own), lambda h: (m, h, 0)),
        ),
        input_output_aliases={7 + i: i for i in range(len(so_far))},
        compiler_params=pltpu.CompilerParams(vmem_limit_bytes=VMEM_LIMIT),
        cost_estimate=pl.CostEstimate(
            flops=flops, bytes_accessed=heads * own * slots * 4, transcendentals=0
        ),
        name="attention_backward",
    )(expo, datt, st, tops, q, k, v, *so_far)


def shifted(arr, mesh_dims, dy, dx):
    if dy == 0 and dx == 0:
        return arr
    Y, X, _ = mesh_dims
    key = lambda y, x, c: (y * X + x) * 2 + c
    perm = [
        (key(y, x, c), key((y + dy) % Y, (x + dx) % X, c)) for y in range(Y) for x in range(X) for c in range(2)
    ]
    return lax.ppermute(arr, "keys", perm)


def late_weights_start(mesh_dims, own):
    Y, X, _ = mesh_dims
    half = own.shape[0] // 2
    first = [shifted(own[:half], mesh_dims, 0, dx) for dx in range(X)]
    last = [shifted(own[half:], mesh_dims, dy, 0) for dy in range(Y)]
    return first, last


def late_weights_finish(mesh_dims, first, last):
    Y, X, _ = mesh_dims
    return [shifted(first[dx], mesh_dims, dy, 0) for dy in range(Y) for dx in range(X)] + [
        shifted(last[dy], mesh_dims, 0, dx) for dy in range(Y) for dx in range(X)
    ]


def late_grads_start(mesh_dims, send_a, keep_a, send_b, keep_b):
    Y, X, _ = mesh_dims
    first = [shifted(send_a[d - 1], mesh_dims, d, 0) for d in range(1, Y)]
    last = [shifted(send_b[d - 1], mesh_dims, 0, d) for d in range(1, X)]
    return (keep_a, first), (keep_b, last)


def late_grads_finish(mesh_dims, first, last):
    Y, X, _ = mesh_dims
    key = lax.axis_index("keys")
    x, y = (key // 2) % X, key // (2 * X)
    low = lambda total: total.astype(BF16)

    def line(keep, got, place, move):
        total = keep.astype(F32)
        for piece in got:
            total = total + piece.astype(F32)
        total = low(total)
        count = total.shape[0]
        pick = lambda d: lax.dynamic_index_in_dim(total, (place + d) % count, 0, keepdims=False)
        out = pick(0).astype(F32)
        for d in range(1, count):
            out = out + move(pick(d), d).astype(F32)
        return low(out)

    return jnp.concatenate(
        [
            line(*first, x, lambda a, d: shifted(a, mesh_dims, 0, d)),
            line(*last, y, lambda a, d: shifted(a, mesh_dims, d, 0)),
        ],
        axis=0,
    )


def update_weights_kernel(
    block_ids, first_column, fixes, late_ref, early_ref, basis_ref, master_ref, one_ref, two_ref,
    grad_out, one_out, two_out, master_out, copy_out,
):
    s = pl.program_id(0)
    block = block_ids[s]
    early = early_ref[jnp.minimum(block, EARLY - 1)].astype(F32)
    grad = jnp.where(block < EARLY, early, late_ref[0])
    grad_out[0] = grad
    basis = basis_ref[0]
    exact = functools.partial(
        lax.dot_general, precision=HIGHEST_PREC, preferred_element_type=F32
    )
    rotated = exact(grad, basis, (((1,), (0,)), ((), ())))
    new_one = BETA_ONE * one_ref[0] + (1.0 - BETA_ONE) * rotated
    new_two = BETA_TWO * two_ref[0] + (1.0 - BETA_TWO) * rotated * rotated
    one_out[0] = new_one
    two_out[0] = new_two
    direction = new_one / fixes[0] / (jnp.sqrt(new_two / fixes[1]) + EPS_ADAM)
    back = exact(direction, basis, (((1,), (1,)), ((), ())))
    columns = first_column[s] + lax.broadcasted_iota(jnp.int32, (grad.shape[0], 1), 0)
    master = master_ref[0]
    new_master = master - column_rates(columns) * (back + DECAY * master)
    master_out[0] = new_master
    copy_out[0] = new_master.astype(BF16)


def update_weights(block_ids, first_column, fixes, late, early, basis, master, one, two):
    slots_here, n, width = master.shape
    mat = pl.BlockSpec((1, n, width), lambda s: (s, 0, 0))
    smem = pl.BlockSpec(memory_space=pltpu.SMEM)
    return pl.pallas_call(
        update_weights_kernel,
        grid=(slots_here,),
        out_shape=tuple(jax.ShapeDtypeStruct(master.shape, F32) for _ in range(4))
        + (jax.ShapeDtypeStruct(master.shape, BF16),),
        in_specs=[smem, smem, smem, mat, pl.BlockSpec((EARLY, n, width), lambda s: (0, 0, 0)),
                  pl.BlockSpec((1, width, width), lambda s: (s, 0, 0)), mat, mat, mat],
        out_specs=(mat,) * 5,
        compiler_params=pltpu.CompilerParams(vmem_limit_bytes=VMEM_LIMIT),
        name="update_weights",
    )(block_ids, first_column, fixes, late, early, basis, master, one, two)


def to_chunks(arr, chunks):
    pieces, rows, own = arr.shape[-3:]
    lead = arr.shape[:-3]
    if pieces == chunks:
        return arr
    per = pieces // chunks
    arr = arr.reshape(lead + (chunks, per, rows, own))
    return jnp.moveaxis(arr, -3, -2).reshape(lead + (chunks, rows, per * own))


def from_chunks(arr, pieces):
    chunks, rows, wide = arr.shape[-3:]
    lead = arr.shape[:-3]
    if pieces == chunks:
        return arr
    per = pieces // chunks
    arr = arr.reshape(lead + (chunks, rows, per, wide // per))
    return jnp.moveaxis(arr, -2, -3).reshape(lead + (pieces, rows, wide // per))


def per_device(
    mesh_dims,
    tokens,
    prev_logits,
    segments,
    out_cot,
    master_mat,
    mom1_mat,
    mom2_mat,
    eigen_bases,
    master_small,
    mom1_small,
    mom2_small,
    owners,
    step_count,
):
    Y, X, R = mesh_dims
    keys = Y * X * 2
    micro, row_count, key_len, width = tokens.shape
    slot_count = prev_logits.shape[4]
    slots_here, _, cols_here = master_mat.shape
    blocks = slots_here * R
    token_count = micro * key_len
    scale = HD ** (-0.5)
    key_index = lax.axis_index("keys")
    row_index = lax.axis_index("rows")
    wide = max(key_len, min(256, slot_count))
    chunks = slot_count // wide
    groups = H // GROUP

    x_own = tokens.reshape(micro, key_len, width)
    w_own = jnp.swapaxes(master_mat, 1, 2).astype(BF16)
    small_low = master_small.astype(BF16).reshape(1, slots_here * cols_here)
    ext = lax.dynamic_update_slice(
        jnp.zeros((EXT, width), BF16), small_low, (row_index, jnp.int32(0))
    )
    fast = cols_here % 16 == 0
    wt, w_late, ext_all, xg = gather_weights(mesh_dims, owners, w_own, ext, x_own)
    if fast:
        first, last = late_weights_start(mesh_dims, w_late)
    else:
        late = [lax.all_gather(w_late, "keys", axis=1).reshape(2 * FF + width, width)]
    w_t = wt.reshape(EARLY * BLOCK_COLUMNS, width)
    small_all = ext_all.reshape(keys, EXT, width)[:, :R, : slots_here * cols_here]
    params = (
        jnp.transpose(small_all.reshape(keys, R, slots_here, cols_here), (1, 2, 0, 3))
        .reshape(blocks * GAIN_ROW_WIDTH)
        .astype(F32)
    )
    wq_t = w_t[:width]
    wkv_t = w_t[width : 3 * width]
    bias_q = params[:width]
    bias_v = params[width : 2 * width]
    bias_o = params[2 * width : 3 * width]
    gain_one = params[3 * width : 4 * width]
    shift_one = params[4 * width : 5 * width]
    bias_up = params[5 * width : 5 * width + FF]
    bias_down = params[5 * width + FF : 6 * width + FF]
    gain_two = params[6 * width + FF : 7 * width + FF]
    shift_two = params[7 * width + FF :]

    xg = xg.reshape(micro, slot_count, width)
    q_all, k_all, v_all = [], [], []
    for m in range(micro):
        q_all.append(
            (dot_f32(wq_t, xg[m], ((1,), (1,))) + bias_q[:, None]).astype(BF16) * jnp.asarray(scale, BF16)
        )
        k_all.append(dot_f32(wkv_t[:width], x_own[m], ((1,), (1,))).astype(BF16))
        v_all.append((dot_f32(wkv_t[width:], x_own[m], ((1,), (1,))) + bias_v[:, None]).astype(BF16))
    x_rows = x_own.reshape(token_count, width)

    seg_rows = segments.reshape(micro, slot_count)
    seg_keys = lax.dynamic_slice_in_dim(seg_rows, key_index * key_len, key_len, 1)
    forward = ()
    for m in range(micro):
        forward = attention_forward(
            m, forward, q_all[m], k_all[m], v_all[m], prev_logits,
            seg_keys[:, :, None], seg_rows[:, None, :], chunks, wide,
        )
        if m == 0 and fast:
            forward, first, last = lax.optimization_barrier((tuple(forward), first, last))
            late = late_weights_finish(mesh_dims, first, last)
    logits, expo, o_part, st_part, tops = forward
    o_part = from_chunks(o_part, keys).reshape(micro, Y, X, 2, width, key_len)
    st_part = from_chunks(st_part, keys).reshape(micro, groups, Y, X, 2, 2 * GROUP, key_len)
    zero = jnp.zeros_like(bias_o)
    vec = jnp.stack([bias_o, gain_one, shift_one, bias_down, gain_two, shift_two, zero, zero])
    out_hidden, datt_all, st_all, grad_one, dvec, d_bias_up, *dw_late = middle(
        mesh_dims, o_part, st_part, x_own, out_cot.reshape(x_own.shape), late, vec, bias_up[None]
    )
    out_hidden = out_hidden.reshape(tokens.shape)
    datt_all = to_chunks(datt_all.reshape(micro, keys, width, key_len), chunks)
    st_all = to_chunks(st_all.reshape(micro, groups, keys, 16, key_len), chunks)
    so_far = ()
    if fast:
        first, last = late_grads_start(mesh_dims, *dw_late)
    for m in range(micro):
        so_far = attention_backward(
            m, so_far, expo, datt_all, st_all, tops, q_all[m], k_all[m], v_all[m], scale
        )
        if m == 0 and fast:
            so_far, first, last = lax.optimization_barrier((tuple(so_far), first, last))
            fin = late_grads_finish(mesh_dims, first, last)
    grad_prev, dq_part, dk, dv = so_far
    dq_part = from_chunks(dq_part, keys).reshape(micro, Y, X, 2, width, key_len)
    inverse = inverse_order(owners)
    slot_index_list = row_index * slots_here + jnp.arange(slots_here, dtype=jnp.int32)
    block_ids = jnp.take(inverse, slot_index_list)
    if fast:
        grad_tokens, mine_late, mine_early, small_sum = tail(
            mesh_dims, inverse, dq_part, dk, dv, x_own, grad_one, wt, fin, dvec, d_bias_up
        )
        mine_early = mine_early.reshape(EARLY, cols_here, width)
    else:
        dq = lax.psum_scatter(
            dq_part.reshape(micro, keys, width, key_len), "keys", scatter_dimension=1, tiled=True
        ).reshape(micro, width, key_len)
        grad_proj = jnp.swapaxes(jnp.concatenate([dq, dk, dv], axis=1), 0, 1).reshape(
            3 * width, token_count
        )
        d_qkv = dot_f32(grad_proj, x_rows, ((1,), (0,))).astype(BF16)
        grad_tokens = (
            grad_one.reshape(token_count, width) + dot_f32(grad_proj, w_t, ((0,), (0,)))
        ).astype(BF16)
        sums = jnp.sum(grad_proj.astype(F32).reshape(3, width, token_count), axis=2)
        small_sum = lax.psum(
            jnp.concatenate(
                [sums[0][None], sums[2][None], dvec[:3], d_bias_up.reshape(FF // width, width), dvec[3:6]]
            ),
            ("rows", "keys"),
        )
        grads = jnp.concatenate([d_qkv, dw_late[0]], axis=0).reshape(blocks, keys, cols_here, width)
        grads = lax.psum_scatter(grads, "keys", scatter_dimension=1, tiled=True)
        grads = jnp.take(grads.reshape(blocks, cols_here, width), inverse, axis=0)
        mine_t = lax.psum_scatter(grads, "rows", scatter_dimension=0, tiled=True).astype(F32)
    grad_tokens = grad_tokens.reshape(tokens.shape)
    flat = small_sum.reshape(-1)[: blocks * GAIN_ROW_WIDTH].reshape(blocks, GAIN_ROW_WIDTH)
    mine_small = lax.dynamic_slice(
        flat, (row_index * slots_here, key_index * cols_here), (slots_here, cols_here)
    )

    steps_done = step_count[0].astype(F32)
    fix_one = 1.0 - jnp.power(jnp.asarray(BETA_ONE, F32), steps_done)
    fix_two = 1.0 - jnp.power(jnp.asarray(BETA_TWO, F32), steps_done)
    if fast:
        first_column = block_ids * BLOCK_COLUMNS + key_index * cols_here
        mats = [jnp.swapaxes(a, 1, 2) for a in (master_mat, mom1_mat, mom2_mat)]
        updated = update_weights(
            block_ids, first_column, jnp.stack([fix_one, fix_two]), mine_late, mine_early, eigen_bases, *mats
        )
        mine_mat, new_one, new_two, new_master, copy_mat = (jnp.swapaxes(a, 1, 2) for a in updated)
    else:
        mine_mat = jnp.swapaxes(mine_t, 1, 2)
        rotated = jnp.einsum("sed,sec->sdc", eigen_bases, mine_mat, precision=HIGHEST_PREC)
        new_one = BETA_ONE * mom1_mat + (1.0 - BETA_ONE) * rotated
        new_two = BETA_TWO * mom2_mat + (1.0 - BETA_TWO) * rotated * rotated
        direction = new_one / fix_one / (jnp.sqrt(new_two / fix_two) + EPS_ADAM)
        back_rot = jnp.einsum("sdk,skc->sdc", eigen_bases, direction, precision=HIGHEST_PREC)
        columns = (
            block_ids[:, None] * (cols_here * keys)
            + key_index * cols_here
            + jnp.arange(cols_here, dtype=jnp.int32)[None, :]
        )
        rates = column_rates(columns)[:, None, :]
        new_master = master_mat - rates * (back_rot + DECAY * master_mat)
        copy_mat = new_master.astype(BF16)
    small_one = BETA_ONE * mom1_small + (1.0 - BETA_ONE) * mine_small
    small_two = BETA_TWO * mom2_small + (1.0 - BETA_TWO) * mine_small * mine_small
    new_small = master_small - RATE_SMALL * (small_one / fix_one) / (
        jnp.sqrt(small_two / fix_two) + EPS_ADAM
    )
    return (
        out_hidden,
        logits,
        grad_tokens,
        grad_prev,
        mine_mat,
        new_one,
        new_two,
        new_master,
        copy_mat,
        mine_small,
        small_one,
        small_two,
        new_small,
        new_small.astype(BF16),
    )


def solution(mesh):
    chips = mesh.shape["keys"] // 2
    side = math.isqrt(chips)
    dims = (side, side, mesh.shape["rows"]) if side * side == chips else (1, chips, mesh.shape["rows"])
    acts = P(None, "rows", "keys", None)
    scores = P(None, "rows", None, "keys", None)
    mats = P("rows", None, "keys")
    smalls = P("rows", "keys")
    return jax.shard_map(
        functools.partial(per_device, dims),
        mesh=mesh,
        in_specs=(
            acts, scores, P(None, "rows", None), acts, mats, mats, mats,
            P("rows", None, None), smalls, smalls, smalls, P(), P(),
        ),
        out_specs=(acts, scores, acts, scores) + (mats,) * 5 + (smalls,) * 5,
        check_vma=False,
    )
```

```python
import functools
import math

import jax
import jax.numpy as jnp
from jax import lax
from jax.experimental import pallas as pl
from jax.experimental.pallas import tpu as pltpu
from jax.sharding import PartitionSpec as P

MODEL_WIDTH = 768
H = 12
HD = 64
FF = 3072
BLOCK_COLUMNS = 1152
GAIN_ROW_WIDTH = 1152

EPS_NORM = 1e-06
BETA_ONE = 0.95
BETA_TWO = 0.95
EPS_ADAM = 1e-08
DECAY = 0.01
RATE_SMALL = 0.3
NEG_BIG = -1e30
NEG_FLOOR = -1e29
HIGHEST_PREC = lax.Precision.HIGHEST
MESH = pl.DeviceIdType.MESH
F32 = jnp.float32
BF16 = jnp.bfloat16
ANY = pl.BlockSpec(memory_space=pl.ANY)
VMEM_SPEC = pl.BlockSpec(memory_space=pltpu.VMEM)
EXT = 16
EARLY = 2
PER = 3
VMEM_LIMIT = 60 << 20


def layer_norm(value):
    mean_val = jnp.mean(value, axis=-1, keepdims=True)
    centered = value - mean_val
    inv_dev = lax.rsqrt(jnp.mean(centered * centered, axis=-1, keepdims=True) + EPS_NORM)
    return (centered * inv_dev, inv_dev)


def norm_back(grad_in, normed, inv_dev, gain):
    scaled = grad_in * gain
    return inv_dev * (
        scaled
        - jnp.mean(scaled, axis=-1, keepdims=True)
        - normed * jnp.mean(scaled * normed, axis=-1, keepdims=True)
    )


def inverse_order(owners):
    slot_index_list = jnp.arange(owners.shape[0], dtype=jnp.int32)
    matches = (owners[None, :] == slot_index_list[:, None]).astype(jnp.int32)
    return jnp.sum(matches * slot_index_list[None, :], axis=1)


def column_rates(columns):
    inner = MODEL_WIDTH ** (-0.5)
    return jnp.where(
        columns < 3 * MODEL_WIDTH,
        inner,
        jnp.where(
            columns < 4 * MODEL_WIDTH,
            4.0 * inner,
            jnp.where(columns < 4 * MODEL_WIDTH + FF, inner, FF ** (-0.5)),
        ),
    )


def dot_f32(left, right, contract):
    return lax.dot_general(left, right, (contract, ((), ())), preferred_element_type=F32)


class Place:
    def __init__(self, side_y, side_x, rows):
        self.Y, self.X, self.R = side_y, side_x, rows
        key = lax.axis_index("keys")
        self.key = key
        self.r = lax.axis_index("rows")
        self.c = lax.rem(key, 2)
        self.x = lax.rem(key // 2, side_x)
        self.y = key // (2 * side_x)

    def keyof(self, y, x, c):
        return (y * self.X + x) * 2 + c

    def xo(self, d):
        return lax.rem(self.x + d, self.X)

    def yo(self, d):
        return lax.rem(self.y + d, self.Y)

    def ro(self, d):
        return lax.rem(self.r + d, self.R)

    def x_peer(self, d):
        return {"keys": self.keyof(self.y, self.xo(d), self.c)}

    def y_peer(self, d):
        return {"keys": self.keyof(self.yo(d), self.x, self.c)}

    def core_peer(self):
        return {"keys": self.keyof(self.y, self.x, 1 - self.c)}

    def z_peer(self, d):
        return {"rows": self.ro(d)}

    def barrier(self, with_z):
        sem = pltpu.get_barrier_semaphore()
        peers = [self.core_peer()]
        peers += [self.x_peer(d) for d in range(1, self.X)]
        peers += [self.y_peer(d) for d in range(1, self.Y)]
        if with_z:
            peers += [self.z_peer(d) for d in range(1, self.R)]
        for peer in peers:
            pl.semaphore_signal(sem, inc=1, device_id=peer, device_id_type=MESH)
        pl.semaphore_wait(sem, len(peers))


def remote(src, dst, send_sem, recv_sem, peer):
    return pltpu.make_async_remote_copy(
        src_ref=src,
        dst_ref=dst,
        send_sem=send_sem,
        recv_sem=recv_sem,
        device_id=peer,
        device_id_type=MESH,
    )


def sems_per_item(Y, X):
    return (X - 1) + (Y - 1) + 1


class Gather:
    def __init__(self, place, own, buf, send, recv, base, x_first):
        p = place
        self.sent = []
        n = sems_per_item(p.Y, p.X)
        idx = iter(range(base, base + n))
        first = [(p.x_peer(d)) for d in range(1, p.X)] if x_first else [p.y_peer(d) for d in range(1, p.Y)]
        second = [p.y_peer(d) for d in range(1, p.Y)] if x_first else [p.x_peer(d) for d in range(1, p.X)]
        line = buf.at[p.y, :, p.c] if x_first else buf.at[:, p.x, p.c]
        plane = buf.at[:, :, p.c]
        mine = buf.at[p.y, p.x, p.c]
        self.one = []
        for peer in first:
            i = next(idx)
            self.one.append(remote(own, mine, send.at[i], recv.at[i], peer))
        self.two = []
        for peer in second:
            i = next(idx)
            self.two.append(remote(line, line, send.at[i], recv.at[i], peer))
        i = next(idx)
        self.three = [remote(plane, plane, send.at[i], recv.at[i], p.core_peer())]

    def start1(self):
        for copy in self.one:
            copy.start()

    def start2(self):
        for copy in self.one:
            copy.wait_recv()
        for copy in self.two:
            copy.start()

    def start3(self):
        for copy in self.two:
            copy.wait_recv()
        for copy in self.three:
            copy.start()

    def finish(self):
        for copy in self.three:
            copy.wait_recv()
        for copy in self.one + self.two + self.three:
            copy.wait_send()


def gather_weights_kernel(
    Y, X, R, owners, w_ref, ext_ref, x_ref, wt_out, own_out, ext_out, xg_out,
    zbuf, zext, stage, sext, zsend, zrecv, send, recv, loc,
):
    p = Place(Y, X, R)
    slots_here = w_ref.shape[0]
    blocks = zbuf.shape[0]
    early = wt_out.shape[0]
    micro = x_ref.shape[0]
    n = sems_per_item(Y, X)
    p.barrier(True)
    here = pl.ds(p.r * slots_here, slots_here)

    def hop(src, step, own):
        there = pl.ds(src * slots_here, slots_here)
        way = (step + 1) // 2
        peer = {"rows": p.r + step}
        return [
            remote(w_ref if own else zbuf.at[there], zbuf.at[there], zsend.at[way, src, 0], zrecv.at[src, 0], peer),
            remote(ext_ref if own else zext.at[src], zext.at[src], zsend.at[way, src, 1], zrecv.at[src, 1], peer),
        ]

    def can(step):
        return p.r < R - 1 if step > 0 else p.r > 0

    def pass_on(dist, act):
        for step in (1, -1):
            src = p.r - step * dist

            @pl.when((src >= 0) & (src < R) & can(step))
            def _():
                for copy in hop(src, step, dist == 0):
                    act(copy)

    def arrived(dist):
        for step in (1, -1):
            src = p.r - step * dist

            @pl.when((src >= 0) & (src < R))
            def _():
                for copy in hop(src, step, False):
                    copy.wait_recv()

    pass_on(0, lambda copy: copy.start())
    xitems = []
    xlocal = []
    for m in range(micro):
        item = Gather(p, x_ref.at[m], xg_out.at[m], send, recv, m * n, m % 2 == 0)
        item.start1()
        xitems.append(item)
        copy = pltpu.make_async_copy(x_ref.at[m], xg_out.at[m, p.y, p.x, p.c], loc.at[m])
        copy.start()
        xlocal.append(copy)
    wl = pltpu.make_async_copy(w_ref, zbuf.at[here], loc.at[micro])
    wl.start()
    el = pltpu.make_async_copy(ext_ref, zext.at[p.r], loc.at[micro + 1])
    el.start()
    for m in range(micro):
        xlocal[m].wait()
        xitems[m].start2()
    for dist in range(1, R):
        arrived(dist)
        pass_on(dist, lambda copy: copy.start())
    wl.wait()
    el.wait()
    sext[...] = jnp.sum(zext[...].astype(F32), axis=0).astype(BF16)

    def reorder(b, carry):
        stage[b] = zbuf[owners[b]]
        return carry

    lax.fori_loop(0, blocks, reorder, 0)
    base = micro * n
    eitem = Gather(p, sext, ext_out, send, recv, base, True)
    base += n
    lcopies = []
    items = []
    for b in range(early):
        item = Gather(p, stage.at[b], wt_out.at[b], send, recv, base, b % 2 == 0)
        base += n
        item.start1()
        items.append(item)
        copy = pltpu.make_async_copy(stage.at[b], wt_out.at[b, p.y, p.x, p.c], loc.at[micro + 3 + b])
        copy.start()
        lcopies.append(copy)
    eitem.start1()
    ecopy = pltpu.make_async_copy(sext, ext_out.at[p.y, p.x, p.c], loc.at[micro + 2])
    ecopy.start()
    rest = pltpu.make_async_copy(stage.at[pl.ds(early, blocks - early)], own_out, loc.at[micro + 3 + early])
    rest.start()
    for m in range(micro):
        xitems[m].start3()
    for b in range(early):
        lcopies[b].wait()
        items[b].start2()
    ecopy.wait()
    eitem.start2()
    for b in range(early):
        items[b].start3()
    eitem.start3()
    for item in xitems + [eitem] + items:
        item.finish()
    for dist in range(R):
        pass_on(dist, lambda copy: copy.wait_send())
    rest.wait()


def gather_weights(mesh_dims, owners, w_own, ext, x_own):
    Y, X, R = mesh_dims
    slots_here, n, width = w_own.shape
    micro, tok = x_own.shape[:2]
    blocks = slots_here * R
    total = sems_per_item(Y, X) * (micro + 1 + EARLY)
    return pl.pallas_call(
        functools.partial(gather_weights_kernel, Y, X, R),
        out_shape=(
            jax.ShapeDtypeStruct((EARLY, Y, X, 2, n, width), BF16),
            jax.ShapeDtypeStruct((blocks - EARLY, n, width), BF16),
            jax.ShapeDtypeStruct((Y, X, 2, EXT, width), BF16),
            jax.ShapeDtypeStruct((micro, Y, X, 2, tok, width), BF16),
        ),
        in_specs=[pl.BlockSpec(memory_space=pltpu.SMEM), VMEM_SPEC, VMEM_SPEC, VMEM_SPEC],
        out_specs=(ANY, ANY, ANY, ANY),
        scratch_shapes=[
            pltpu.VMEM((blocks, n, width), BF16),
            pltpu.VMEM((R, EXT, width), BF16),
            pltpu.VMEM((blocks, n, width), BF16),
            pltpu.VMEM((EXT, width), BF16),
            pltpu.SemaphoreType.DMA((2, R, 2)),
            pltpu.SemaphoreType.DMA((R, 2)),
            pltpu.SemaphoreType.DMA((total,)),
            pltpu.SemaphoreType.DMA((total,)),
            pltpu.SemaphoreType.DMA((micro + 4 + EARLY,)),
        ],
        compiler_params=pltpu.CompilerParams(
            collective_id=1, has_side_effects=True, vmem_limit_bytes=VMEM_LIMIT
        ),
        name="gather_weights",
    )(owners, w_own, ext, x_own)


class Scatter:
    def __init__(self, place, parts, accs, r1s, r2s, r3s, send, recv, loc, base, lbase, y_first, merge):
        p = place
        self.p, self.y_first, self.merge = p, y_first, merge
        self.accs, self.r1s, self.r2s, self.r3s = accs, r1s, r2s, r3s
        self.count = len(parts)
        n = sems_per_item(p.Y, p.X) * len(parts)
        idx = iter(range(base, base + n))
        self.zero, self.one, self.two, self.three = [], [], [], []
        for t, part in enumerate(parts):
            i = next(idx)
            self.zero.append(pltpu.make_async_copy(part.at[:, :, p.c], accs[t], loc.at[lbase + t]))
            self.one.append(remote(part.at[:, :, 1 - p.c], r1s[t], send.at[i], recv.at[i], p.core_peer()))
            if y_first:
                for d in range(1, p.Y):
                    i = next(idx)
                    self.two.append(
                        remote(accs[t].at[p.yo(d)], r2s[t].at[d - 1], send.at[i], recv.at[i], p.y_peer(d))
                    )
                for d in range(1, p.X):
                    i = next(idx)
                    self.three.append(
                        remote(accs[t].at[p.y, p.xo(d)], r3s[t].at[d - 1], send.at[i], recv.at[i], p.x_peer(d))
                    )
            else:
                for d in range(1, p.X):
                    i = next(idx)
                    self.two.append(
                        remote(accs[t].at[:, p.xo(d)], r2s[t].at[d - 1], send.at[i], recv.at[i], p.x_peer(d))
                    )
                for d in range(1, p.Y):
                    i = next(idx)
                    self.three.append(
                        remote(accs[t].at[p.yo(d), p.x], r3s[t].at[d - 1], send.at[i], recv.at[i], p.y_peer(d))
                    )

    def start1(self):
        for copy in self.zero + self.one:
            copy.start()

    def start2(self):
        p = self.p
        for copy in self.zero:
            copy.wait()
        for copy in self.one:
            copy.wait_recv()

        def body(i, carry):
            y, x = i // p.X, lax.rem(i, p.X)
            self.merge([a.at[y, x] for a in self.accs], [r.at[y, x] for r in self.r1s])
            return carry

        lax.fori_loop(0, p.Y * p.X, body, 0)
        for copy in self.two:
            copy.start()

    def start3(self):
        p = self.p
        for copy in self.two:
            copy.wait_recv()
        if self.y_first:
            for d in range(1, p.Y):
                for x in range(p.X):
                    self.merge([a.at[p.y, x] for a in self.accs], [r.at[d - 1, x] for r in self.r2s])
        else:
            for d in range(1, p.X):
                for y in range(p.Y):
                    self.merge([a.at[y, p.x] for a in self.accs], [r.at[d - 1, y] for r in self.r2s])
        for copy in self.three:
            copy.start()

    def finish(self):
        p = self.p
        for copy in self.three:
            copy.wait_recv()
        mine = [a.at[p.y, p.x] for a in self.accs]
        for d in range(1, p.X if self.y_first else p.Y):
            self.merge(mine, [r.at[d - 1] for r in self.r3s])
        return mine

    def drain(self):
        for copy in self.one + self.two + self.three:
            copy.wait_send()


def merge_sum(into, other):
    a, b = into[0], other[0]
    a[...] = (a[...].astype(F32) + b[...].astype(F32)).astype(BF16)


def merge_soft(into, other):
    (va, sa), (vb, sb) = into, other
    ta, tb = sa[...], sb[...]
    heads = ta.shape[0] // 2
    top_a, top_b = ta[:heads], tb[:heads]
    top = jnp.maximum(top_a, top_b)
    wa, wb = jnp.exp(top_a - top), jnp.exp(top_b - top)
    sa[...] = jnp.concatenate([top, wa * ta[heads:] + wb * tb[heads:]], axis=0)
    for h in range(heads):
        rows = slice(h * HD, (h + 1) * HD)
        va[rows, :] = (
            va[rows, :].astype(F32) * wa[h : h + 1] + vb[rows, :].astype(F32) * wb[h : h + 1]
        ).astype(BF16)


def scatter_scratch(Y, X, items, shape, dtype, y_first_of):
    most = max((Y - 1) * X, (X - 1) * Y)
    return [
        pltpu.VMEM((items, Y, X) + shape, dtype),
        pltpu.VMEM((items, Y, X) + shape, dtype),
        pltpu.VMEM((items, max(Y, X) - 1, max(Y, X)) + shape, dtype),
        pltpu.VMEM((items, max(Y, X) - 1) + shape, dtype),
    ]


GROUP = 3


def middle_kernel(Y, X, R, blocks, pieces, *refs):
    o_ref, st_ref, x_ref, cot_ref, vec_ref, bu_ref = refs[:6]
    refs = refs[6:]
    count = 2 * Y * X if pieces else 1
    w_refs, refs = refs[:count], refs[count:]
    out_ref, datt_out, stat_out, dz_ref, dvec_ref, dbu_ref = refs[:6]
    refs = refs[6:]
    if pieces:
        send_a, keep_a, send_b, keep_b = refs[:4]
        refs = refs[4:]
    else:
        (dw_out,) = refs[:1]
        refs = refs[1:]
    (
        oa, o1, o2, o3, sa, s1, s2, s3, send, recv, loc, gsend, grecv, gloc, wsem, wsend, wrecv, dwsem,
        w, att, attk, low, hid, dpre, slope, df, da, n1, n2, datt, stat, dw,
    ) = refs[:32]
    if pieces:
        core_acc, core_in, csend, crecv = refs[32:]
    p = Place(Y, X, R)
    micro, tok, width = x_ref.shape
    groups = st_ref.shape[1]
    rows = GROUP * HD
    bo, g1, e1, bd, g2, e2 = (vec_ref[i : i + 1] for i in range(6))
    stat[...] = jnp.zeros_like(stat)
    parts = FF // width
    wcopies, wremote = [], []
    if pieces:
        half, piece = w_refs[0].shape[:2]
        for t in range(2):
            for dy in range(Y):
                for dx in range(X):
                    src = w_refs[(t * Y + dy) * X + dx]
                    key = p.keyof(p.yo(Y - dy), p.xo(X - dx), p.c)
                    for b in range(half):
                        at = (t * half + b) * BLOCK_COLUMNS + key * piece
                        dst = w.at[pl.ds(pl.multiple_of(at, 16), piece)]
                        i = ((t * Y + dy) * X + dx) * half + b
                        wcopies.append(pltpu.make_async_copy(src.at[b], dst, wsem.at[i]))
                        wremote.append(remote(src.at[b], dst, wsend.at[i], wrecv.at[i], p.core_peer()))
    else:
        wcopies.append(pltpu.make_async_copy(w_refs[0], w, wsem.at[0]))
    for copy in wcopies:
        copy.start()
    p.barrier(False)

    n = sems_per_item(Y, X) * 2
    merges = []
    for m in range(micro):
        for g in range(groups):
            i = m * groups + g
            item = Scatter(
                p,
                [o_ref.at[m, :, :, :, pl.ds(g * rows, rows)], st_ref.at[m, g]],
                [oa.at[i], sa.at[i]], [o1.at[i], s1.at[i]], [o2.at[i], s2.at[i]], [o3.at[i], s3.at[i]],
                send, recv, loc, i * n, i * 2, g % 2 == 0, merge_soft,
            )
            item.start1()
            merges.append(item)

    def merge_two(m):
        for g in range(groups):
            merges[m * groups + g].start2()

    def merge_three(m):
        for g in range(groups):
            merges[m * groups + g].start3()

    def merge_finish(m):
        for g in range(groups):
            val, st = merges[m * groups + g].finish()
            tile = st[...]
            inv = 1.0 / tile[GROUP:]
            stat[m, g, : 2 * GROUP] = jnp.concatenate([tile[:GROUP], inv], axis=0)
            for h in range(GROUP):
                att[m, g * rows + h * HD : g * rows + (h + 1) * HD, :] = (
                    val[h * HD : (h + 1) * HD, :].astype(F32) * inv[h : h + 1]
                ).astype(BF16)

    n = sems_per_item(Y, X)
    gathers = [[], []]

    def gather_one(m):
        local = []
        for g in range(groups):
            ds = pl.ds(g * rows, rows)
            for t, (own, out) in enumerate(
                ((datt.at[m, ds], datt_out.at[m, :, :, :, ds]), (stat.at[m, g], stat_out.at[m, g]))
            ):
                i = (m * groups + g) * 2 + t
                item = Gather(p, own, out, gsend, grecv, i * n, g % 2 == 0)
                item.start1()
                copy = pltpu.make_async_copy(own, out.at[p.y, p.x, p.c], gloc.at[i])
                copy.start()
                gathers[m].append((item, copy))

    def gather_two(m):
        for item, copy in gathers[m]:
            copy.wait()
            item.start2()

    def gather_three(m):
        for item, copy in gathers[m]:
            item.start3()

    def forward(m):
        at = att[m].T
        attk[m] = at
        wo = w[:width]
        z1 = x_ref[m].astype(F32) + (dot_f32(at, wo, ((1,), (1,))) + bo)
        norm, inv = layer_norm(z1)
        n1[...] = norm
        mid = norm * g1 + e1
        low[m] = mid.astype(BF16)
        inner = low[m]

        def body(i, acc):
            r = pl.multiple_of(i * width, width)
            pre = dot_f32(inner, w[pl.ds(width + r, width)], ((1,), (1,))) + bu_ref[:, pl.ds(r, width)]
            half = 0.5 + 0.5 * lax.erf(pre * math.sqrt(0.5))
            low_h = (pre * half).astype(BF16)
            hid[m, :, pl.ds(r, width)] = low_h
            slope[:, pl.ds(r, width)] = half + pre * (
                jnp.exp(-0.5 * pre * pre) * (1.0 / math.sqrt(2.0 * math.pi))
            )
            return acc + dot_f32(low_h, w[pl.ds(width + FF + r, width)], ((1,), (0,)))

        f = lax.fori_loop(0, parts, body, jnp.zeros((tok, width), F32)) + bd
        norm2, inv2 = layer_norm(mid + f)
        n2[...] = norm2
        out_ref[m] = (norm2 * g2 + e2).astype(BF16)
        return inv, inv2

    def backward(m, invs):
        inv, inv2 = invs
        cot = cot_ref[m].astype(F32)
        norm2 = n2[...]
        dz2 = norm_back(cot, norm2, inv2, g2)
        dg2 = jnp.sum(cot * norm2, axis=0, keepdims=True)
        de2 = jnp.sum(cot, axis=0, keepdims=True)
        df_low = dz2.astype(BF16)
        df[m] = df_low
        dbd = jnp.sum(df_low.astype(F32), axis=0, keepdims=True)

        def body(i, acc):
            r = pl.multiple_of(i * width, width)
            dh = dot_f32(df_low, w[pl.ds(width + FF + r, width)], ((1,), (1,)))
            dp = (dh * slope[:, pl.ds(r, width)]).astype(BF16)
            dpre[m, :, pl.ds(r, width)] = dp
            part = jnp.sum(dp.astype(F32), axis=0, keepdims=True)
            if m == 0:
                dbu_ref[:, pl.ds(r, width)] = part
            else:
                dbu_ref[:, pl.ds(r, width)] += part
            return acc + dot_f32(dp, w[pl.ds(width + r, width)], ((1,), (0,)))

        dx1 = lax.fori_loop(0, parts, body, dz2)
        norm = n1[...]
        dg1 = jnp.sum(dx1 * norm, axis=0, keepdims=True)
        de1 = jnp.sum(dx1, axis=0, keepdims=True)
        dz1 = norm_back(dx1, norm, inv, g1)
        dz_ref[m] = dz1
        da_low = dz1.astype(BF16)
        da[m] = da_low
        dbo = jnp.sum(da_low.astype(F32), axis=0, keepdims=True)
        sums = jnp.concatenate([dbo, dg1, de1, dbd, dg2, de2, dg2, dg2], axis=0)
        if m == 0:
            dvec_ref[...] = sums
        else:
            dvec_ref[...] += sums
        dt = dot_f32(da_low, w[:width], ((1,), (0,))).astype(BF16).T
        datt[m] = dt
        for g in range(groups):
            for h in range(GROUP):
                r = g * rows + h * HD
                stat[m, g, 2 * GROUP + h : 2 * GROUP + h + 1] = jnp.sum(
                    dt[r : r + HD].astype(F32) * att[m, r : r + HD, :].astype(F32), axis=0, keepdims=True
                )

    step = width // 2

    def chunk_grad(slot, at, chunk):
        for left, right, lo, count in ((da, attk, 0, width), (dpre, low, width, FF), (hid, df, width + FF, FF)):

            @pl.when((chunk * step >= lo) & (chunk * step < lo + count))
            def _():
                cols = pl.ds(pl.multiple_of(chunk * step - lo, step), step)
                total = dot_f32(left[0, :, cols], right[0], ((0,), (0,)))
                for m in range(1, micro):
                    total = total + dot_f32(left[m, :, cols], right[m], ((0,), (0,)))
                dw[slot, pl.ds(pl.multiple_of(at, step), step)] = total.astype(BF16)

    def block_grad(b, slot):
        per = BLOCK_COLUMNS // step

        def body(t, carry):
            chunk_grad(slot, t * step, b * per + t)
            return carry

        lax.fori_loop(0, per, body, 0)

    merge_two(0)
    for copy in wremote:
        copy.start()
    merge_three(0)
    merge_two(1)
    merge_finish(0)
    for copy in wcopies:
        copy.wait()
    for copy in wremote:
        copy.wait_recv()
    invs = forward(0)
    merge_three(1)
    backward(0, invs)
    gather_one(0)
    merge_finish(1)
    invs = forward(1)
    gather_two(0)
    backward(1, invs)
    gather_one(1)
    gather_three(0)
    if pieces:
        half, piece = w_refs[0].shape[:2]
        keeps = []

        def cores(b):
            slot = lax.rem(b, 2)
            copies = []
            for y in range(Y):
                for x in range(X):
                    i = (b * Y + y) * X + x
                    there = pl.multiple_of(p.keyof(y, x, 1 - p.c) * piece, 16)
                    copies.append(
                        remote(
                            dw.at[slot, pl.ds(there, piece)], core_in.at[b, y, x],
                            csend.at[i], crecv.at[i], p.core_peer(),
                        )
                    )
            return copies

        def one_block(b, carry):
            slot = lax.rem(b, 2)

            @pl.when(b >= 2)
            def _():
                for copy in cores(b - 2):
                    copy.wait_send()

            block_grad(b, slot)
            for copy in cores(b):
                copy.start()
            for y in range(Y):
                for x in range(X):
                    here = pl.multiple_of(p.keyof(y, x, p.c) * piece, 16)
                    core_acc[b, y, x] = dw[slot, pl.ds(here, piece)]
            return carry

        lax.fori_loop(0, blocks // 2, one_block, 0)
        gather_two(1)
        lax.fori_loop(blocks // 2, blocks, one_block, 0)
        gather_three(1)

        def add(i, carry):
            b, y, x = i // (Y * X), lax.rem(i // X, Y), lax.rem(i, X)
            merge_sum([core_acc.at[b, y, x]], [core_in.at[b, y, x]])
            return carry

        def add_block(b, carry):
            for copy in cores(b):
                copy.wait_recv()
            lax.fori_loop(b * Y * X, (b + 1) * Y * X, add, 0)
            return carry

        lax.fori_loop(0, blocks, add_block, 0)
        first, last = pl.ds(0, half), pl.ds(half, half)
        for x in range(X):
            keeps.append((core_acc.at[first, p.y, x], keep_a.at[x]))
            for d in range(1, Y):
                keeps.append((core_acc.at[first, p.yo(d), x], send_a.at[d - 1, x]))
        for y in range(Y):
            keeps.append((core_acc.at[last, y, p.x], keep_b.at[y]))
            for d in range(1, X):
                keeps.append((core_acc.at[last, y, p.xo(d)], send_b.at[d - 1, y]))
        keeps = [pltpu.make_async_copy(src, dst, dwsem.at[i]) for i, (src, dst) in enumerate(keeps)]
        for copy in keeps:
            copy.start()
        for copy in keeps:
            copy.wait()
        for b in (blocks - 2, blocks - 1):
            for copy in cores(jnp.int32(b)):
                copy.wait_send()
    else:
        copies = []
        for b in range(blocks):
            slot = b % 2
            if b >= 2:
                copies[b - 2].wait()
            block_grad(b, slot)
            copies.append(
                pltpu.make_async_copy(
                    dw.at[slot], dw_out.at[pl.ds(b * BLOCK_COLUMNS, BLOCK_COLUMNS)], dwsem.at[slot]
                )
            )
            copies[-1].start()
            if b == blocks // 2:
                gather_two(1)
        for copy in copies[-2:]:
            copy.wait()
        gather_three(1)
    for item in merges:
        item.drain()
    for copy in wremote:
        copy.wait_send()
    for m in range(micro):
        for item, copy in gathers[m]:
            item.finish()


def middle(mesh_dims, o_part, st_part, x_own, cot, weights, vec, bias_up):
    Y, X, R = mesh_dims
    micro, tok, width = x_own.shape
    groups = st_part.shape[1]
    items = micro * groups
    merge_sems = sems_per_item(Y, X) * 2 * items
    strows = 16
    ffw = 2 * FF + width
    blocks = ffw // BLOCK_COLUMNS
    pieces = len(weights) > 1
    outs = [
        (jax.ShapeDtypeStruct((micro, tok, width), BF16), VMEM_SPEC),
        (jax.ShapeDtypeStruct((micro, Y, X, 2, width, tok), BF16), ANY),
        (jax.ShapeDtypeStruct((micro, groups, Y, X, 2, strows, tok), F32), ANY),
        (jax.ShapeDtypeStruct((micro, tok, width), F32), VMEM_SPEC),
        (jax.ShapeDtypeStruct((8, width), F32), VMEM_SPEC),
        (jax.ShapeDtypeStruct((1, FF), F32), VMEM_SPEC),
    ]
    extra = []
    if pieces:
        half, piece = weights[0].shape[:2]
        wsems = 2 * Y * X * half
        outs += [
            (jax.ShapeDtypeStruct((max(Y - 1, 1), X, half, piece, width), BF16), ANY),
            (jax.ShapeDtypeStruct((X, half, piece, width), BF16), ANY),
            (jax.ShapeDtypeStruct((max(X - 1, 1), Y, half, piece, width), BF16), ANY),
            (jax.ShapeDtypeStruct((Y, half, piece, width), BF16), ANY),
        ]
        extra = [
            pltpu.VMEM((blocks, Y, X, piece, width), BF16),
            pltpu.VMEM((blocks, Y, X, piece, width), BF16),
            pltpu.SemaphoreType.DMA((blocks * Y * X,)),
            pltpu.SemaphoreType.DMA((blocks * Y * X,)),
        ]
    else:
        wsems = 1
        outs += [(jax.ShapeDtypeStruct((ffw, width), BF16), ANY)]
    return pl.pallas_call(
        functools.partial(middle_kernel, Y, X, R, blocks, pieces),
        out_shape=tuple(o for o, _ in outs),
        in_specs=[ANY, ANY, VMEM_SPEC, VMEM_SPEC, VMEM_SPEC, VMEM_SPEC] + [ANY] * len(weights),
        out_specs=tuple(spec for _, spec in outs),
        scratch_shapes=scatter_scratch(Y, X, items, (GROUP * HD, tok), BF16, None)
        + scatter_scratch(Y, X, items, (2 * GROUP, tok), F32, None)
        + [
            pltpu.SemaphoreType.DMA((merge_sems,)),
            pltpu.SemaphoreType.DMA((merge_sems,)),
            pltpu.SemaphoreType.DMA((items * 2,)),
            pltpu.SemaphoreType.DMA((merge_sems,)),
            pltpu.SemaphoreType.DMA((merge_sems,)),
            pltpu.SemaphoreType.DMA((items * 2,)),
            pltpu.SemaphoreType.DMA((wsems,)),
            pltpu.SemaphoreType.DMA((wsems,)),
            pltpu.SemaphoreType.DMA((wsems,)),
            pltpu.SemaphoreType.DMA((2 * X * Y,)),
            pltpu.VMEM((ffw, width), BF16),
            pltpu.VMEM((micro, width, tok), BF16),
            pltpu.VMEM((micro, tok, width), BF16),
            pltpu.VMEM((micro, tok, width), BF16),
            pltpu.VMEM((micro, tok, FF), BF16),
            pltpu.VMEM((micro, tok, FF), BF16),
            pltpu.VMEM((tok, FF), F32),
            pltpu.VMEM((micro, tok, width), BF16),
            pltpu.VMEM((micro, tok, width), BF16),
            pltpu.VMEM((tok, width), F32),
            pltpu.VMEM((tok, width), F32),
            pltpu.VMEM((micro, width, tok), BF16),
            pltpu.VMEM((micro, groups, strows, tok), F32),
            pltpu.VMEM((2, BLOCK_COLUMNS, width), BF16),
        ]
        + extra,
        compiler_params=pltpu.CompilerParams(
            collective_id=2, has_side_effects=True, vmem_limit_bytes=VMEM_LIMIT
        ),
        name="middle",
    )(o_part, st_part, x_own, cot, vec, bias_up, *weights)


def tail_kernel(
    Y, X, R, inverse,
    dq_ref, dk_ref, dv_ref, x_ref, dz_ref, w_ref, fin_ref, vec_ref, bu_ref, xg_ref, dqs_ref,
    tok_ref, late_ref, early_ref, sum_ref,
    qa, q1, q2, q3, send, recv, loc,
    part, a, r1, r2, r3, bsend, brecv, bloc,
    stage, rz, zsend, zrecv, qf, qz, rq, qsend, qrecv,
    small, sbuf, ssend, srecv, w, wsem, dq, dqv, xv, acc, vsem,
):
    p = Place(Y, X, R)
    micro, tok, width = x_ref.shape
    slots_here = late_ref.shape[0]
    groups = qa.shape[0] // micro
    rows = GROUP * HD
    n = sems_per_item(Y, X)
    piece = part.shape[4]
    loads = [
        pltpu.make_async_copy(dq_ref, dqv, vsem.at[0]),
        pltpu.make_async_copy(xg_ref, xv, vsem.at[1]),
    ]
    wcopy = pltpu.make_async_copy(w_ref, w, wsem)
    for copy in loads + [wcopy]:
        copy.start()
    ones = jnp.ones((8, tok), BF16)
    bias_v = dot_f32(ones, dv_ref[0], ((1,), (1,)))
    sum_q = dqs_ref[0]
    for m in range(1, micro):
        bias_v = bias_v + dot_f32(ones, dv_ref[m], ((1,), (1,)))
        sum_q = sum_q + dqs_ref[m]
    sums = [sum_q.T[:1], bias_v[:1], vec_ref[:3]]
    sums += [bu_ref[:, i * width : (i + 1) * width] for i in range(FF // width)]
    sums += [vec_ref[3:6], jnp.zeros((4, width), F32)]
    small[...] = jnp.concatenate(sums, axis=0).astype(BF16)
    stages = [[p.core_peer()]]
    stages.append([p.x_peer(d) for d in range(1, X)])
    stages.append([p.y_peer(d) for d in range(1, Y)])
    stages.append([p.z_peer(d) for d in range(1, R)])
    scopies = []
    at = 0
    for peers in stages:
        row = []
        for peer in peers:
            row.append(remote(small, sbuf.at[at], ssend.at[at], srecv.at[at], peer))
            at += 1
        scopies.append(row)

    def small_start(t):
        for copy in scopies[t]:
            copy.start()

    def small_wait(t):
        at = sum(len(row) for row in scopies[:t])
        for copy in scopies[t]:
            copy.wait_recv()
        for copy in scopies[t]:
            copy.wait_send()
        total = small[...].astype(F32)
        for i in range(len(scopies[t])):
            total = total + sbuf[at + i].astype(F32)
        return total

    def token_grad(m):
        total = dz_ref[m] + dot_f32(dq[m], w[:width], ((0,), (0,)))
        total = total + dot_f32(dk_ref[m], w[width : 2 * width], ((0,), (0,)))
        total = total + dot_f32(dv_ref[m], w[2 * width :], ((0,), (0,)))
        tok_ref[m] = total.astype(BF16)

    p.barrier(True)
    small_start(0)
    qitems = []
    for m in range(micro):
        for g in range(groups):
            i = m * groups + g
            item = Scatter(
                p, [dq_ref.at[m, :, :, :, pl.ds(g * rows, rows)]],
                [qa.at[i]], [q1.at[i]], [q2.at[i]], [q3.at[i]],
                send, recv, loc, i * n, i, g % 2 == 0, merge_sum,
            )
            item.start1()
            qitems.append(item)

    def reorder(s, carry):
        stage[s] = fin_ref[jnp.maximum(inverse[s] - EARLY, 0)]
        return carry

    lax.fori_loop(0, stage.shape[0], reorder, 0)
    zcopies = []
    for d in range(1, R):
        there = pl.ds(p.ro(d) * slots_here, slots_here)
        copy = remote(stage.at[there], rz.at[d - 1], zsend.at[d], zrecv.at[d], p.z_peer(d))
        copy.start()
        zcopies.append(copy)

    def product(ref, first, count):
        total = dot_f32(ref[0, first : first + count], x_ref[0], ((1,), (0,)))
        for m in range(1, micro):
            total = total + dot_f32(ref[m, first : first + count], x_ref[m], ((1,), (0,)))
        return total.astype(BF16)

    def put(b, first, value):
        at = 0
        while at < value.shape[0]:
            key, off = divmod(first + at, piece)
            count = min(piece - off, value.shape[0] - at)
            y, x, c = key // (2 * X), key // 2 % X, key % 2
            part[b, y, x, c, off : off + count] = value[at : at + count]
            at += count

    cuts = ((0, piece // 32 * 16, True), (piece // 32 * 16, piece - piece // 32 * 16, False))

    def block_items(b):
        out = []
        for t, (first, count, y_first) in enumerate(cuts):
            ds = pl.ds(first, count)
            i = b * len(cuts) + t
            out.append(
                Scatter(
                    p, [part.at[b, :, :, :, ds]], [a.at[b, :, :, ds]], [r1.at[b, :, :, ds]],
                    [r2.at[b, :, :, ds]], [r3.at[b, :, ds]],
                    bsend, brecv, bloc, i * n, i, y_first, merge_sum,
                )
            )
        return out

    class Block:
        def __init__(self, b):
            self.b, self.items = b, block_items(b)
            self.one = [
                remote(qz.at[b, p.ro(d)], rq.at[b, d - 1], qsend.at[b, 0, d], qrecv.at[b, 0, d], p.z_peer(d))
                for d in range(1, R)
            ]
            mine = early_ref.at[b, p.r]
            self.two = [
                remote(mine, mine, qsend.at[b, 1, d], qrecv.at[b, 1, d], p.z_peer(d)) for d in range(1, R)
            ]

        def step(self, name):
            for item in self.items:
                getattr(item, name)()

        def z_one(self):
            for item, (first, count, _) in zip(self.items, cuts):
                (val,) = item.finish()
                qf[first : first + count] = val[...].astype(F32)
            share = qz.shape[2]
            for i in range(R):
                qz[self.b, i] = qf[i * share : (i + 1) * share].astype(BF16)
            for copy in self.one:
                copy.start()

        def z_two(self):
            for copy in self.one:
                copy.wait_recv()
            total = qz[self.b, p.r].astype(F32)
            for d in range(1, R):
                total = total + rq[self.b, d - 1].astype(F32)
            early_ref[self.b, p.r] = total.astype(BF16)
            for copy in self.two:
                copy.start()

        def finish(self):
            for copy in self.two:
                copy.wait_recv()
            for item in self.items:
                item.drain()
            for copy in self.one + self.two:
                copy.wait_send()

    block0, block1 = Block(0), Block(1)
    half = width // 2
    put(1, 0, product(dk_ref, half, half))
    small[...] = small_wait(0).astype(BF16)
    small_start(1)
    put(1, half, product(dv_ref, 0, width))
    block1.step("start1")
    small[...] = small_wait(1).astype(BF16)
    small_start(2)
    put(0, width, product(dk_ref, 0, half))
    small[...] = small_wait(2).astype(BF16)
    small_start(3)
    first, last = qitems[: len(qitems) - groups], qitems[len(qitems) - groups :]
    for item in first:
        item.start2()
    for copy in loads:
        copy.wait()
    acc[...] = jnp.zeros_like(acc)
    line = 2 * X * tok

    def query_grad(i, carry):
        m, y = i // Y, lax.rem(i, Y)
        left = jnp.concatenate([dqv[m, y, x, c] for x in range(X) for c in range(2)], axis=1)
        right = xv[m, pl.ds(pl.multiple_of(y * line, line), line)]
        acc[...] += dot_f32(left, right, ((1,), (0,)))
        return carry

    lax.fori_loop(0, micro * Y, query_grad, 0)
    put(0, 0, acc[...].astype(BF16))
    block0.step("start1")
    block1.step("start2")
    block0.step("start2")
    block1.step("start3")
    block0.step("start3")
    for item in last:
        item.start2()
    for item in first:
        item.start3()
    block1.z_one()
    block0.z_one()
    for item in last:
        item.start3()
    block1.z_two()
    block0.z_two()
    for copy in zcopies:
        copy.wait_recv()
    for s in range(slots_here):
        total = stage[p.r * slots_here + s].astype(F32)
        for d in range(1, R):
            total = total + rz[d - 1, s].astype(F32)
        late_ref[s] = total
    wcopy.wait()
    for m in range(micro):
        for g in range(groups):
            (val,) = qitems[m * groups + g].finish()
            dq[m, g * rows : (g + 1) * rows, :] = val[...]
        total = dz_ref[m] + dot_f32(dq[m], w[:width], ((0,), (0,)))
        total = total + dot_f32(dk_ref[m], w[width : 2 * width], ((0,), (0,)))
        total = total + dot_f32(dv_ref[m], w[2 * width :], ((0,), (0,)))
        tok_ref[m] = total.astype(BF16)
    sum_ref[...] = small_wait(3)
    block1.finish()
    block0.finish()
    for item in qitems:
        item.drain()
    for copy in zcopies:
        copy.wait_send()


def tail(mesh_dims, inverse, dq_part, dk, dv, x_own, grad_one, w_early, fin, dvec, d_bias_up, x_all, dq_sum):
    Y, X, R = mesh_dims
    micro, tok, width = x_own.shape
    late, n = fin.shape[:2]
    blocks = EARLY + late
    slots_here = blocks // R
    groups = width // (GROUP * HD)
    items = micro * groups
    per = sems_per_item(Y, X)
    share = n // R
    cuts = 2
    small = (16, width)
    hops = 1 + (X - 1) + (Y - 1) + (R - 1)
    return pl.pallas_call(
        functools.partial(tail_kernel, Y, X, R),
        out_shape=(
            jax.ShapeDtypeStruct((micro, tok, width), BF16),
            jax.ShapeDtypeStruct((slots_here, n, width), F32),
            jax.ShapeDtypeStruct((EARLY, R, share, width), BF16),
            jax.ShapeDtypeStruct(small, F32),
        ),
        in_specs=[pl.BlockSpec(memory_space=pltpu.SMEM), ANY]
        + [VMEM_SPEC] * 4
        + [ANY, VMEM_SPEC, VMEM_SPEC, VMEM_SPEC, ANY, VMEM_SPEC],
        out_specs=(VMEM_SPEC,) * 4,
        scratch_shapes=scatter_scratch(Y, X, items, (GROUP * HD, tok), BF16, None)
        + [
            pltpu.SemaphoreType.DMA((per * items,)),
            pltpu.SemaphoreType.DMA((per * items,)),
            pltpu.SemaphoreType.DMA((items,)),
            pltpu.VMEM((EARLY, Y, X, 2, n, width), BF16),
        ]
        + scatter_scratch(Y, X, EARLY, (n, width), BF16, None)
        + [
            pltpu.SemaphoreType.DMA((per * EARLY * cuts,)),
            pltpu.SemaphoreType.DMA((per * EARLY * cuts,)),
            pltpu.SemaphoreType.DMA((EARLY * cuts,)),
            pltpu.VMEM((blocks, n, width), BF16),
            pltpu.VMEM((R - 1, slots_here, n, width), BF16),
            pltpu.SemaphoreType.DMA((R,)),
            pltpu.SemaphoreType.DMA((R,)),
            pltpu.VMEM((n, width), F32),
            pltpu.VMEM((EARLY, R, share, width), BF16),
            pltpu.VMEM((EARLY, R - 1, share, width), BF16),
            pltpu.SemaphoreType.DMA((EARLY, 2, R)),
            pltpu.SemaphoreType.DMA((EARLY, 2, R)),
            pltpu.VMEM(small, BF16),
            pltpu.VMEM((hops,) + small, BF16),
            pltpu.SemaphoreType.DMA((hops,)),
            pltpu.SemaphoreType.DMA((hops,)),
            pltpu.VMEM((3 * width, width), BF16),
            pltpu.SemaphoreType.DMA,
            pltpu.VMEM((micro, width, tok), BF16),
            pltpu.VMEM(dq_part.shape, BF16),
            pltpu.VMEM(x_all.shape, BF16),
            pltpu.VMEM((width, width), F32),
            pltpu.SemaphoreType.DMA((2,)),
        ],
        compiler_params=pltpu.CompilerParams(
            collective_id=5, has_side_effects=True, vmem_limit_bytes=VMEM_LIMIT
        ),
        name="tail",
    )(inverse, dq_part, dk, dv, x_own, grad_one, w_early.reshape(3 * width, width), fin, dvec, d_bias_up, x_all, dq_sum)


def project_kernel(scale, x_ref, own_ref, w_ref, vec_ref, q_ref, k_ref, v_ref, bias):
    width = x_ref.shape[2]

    @pl.when((pl.program_id(0) == 0) & (pl.program_id(1) == 0))
    def _():
        bias[...] = vec_ref[...].T

    q = dot_f32(w_ref[:width], x_ref[0], ((1,), (1,))) + bias[:, 6:7]
    q_ref[0] = q.astype(BF16) * jnp.asarray(scale, BF16)

    @pl.when(pl.program_id(1) == 0)
    def _():
        own = own_ref[0]
        k_ref[0] = dot_f32(w_ref[width : 2 * width], own, ((1,), (1,))).astype(BF16)
        v_ref[0] = (dot_f32(w_ref[2 * width :], own, ((1,), (1,))) + bias[:, 7:8]).astype(BF16)


def project(x_all, x_own, w_t, vec, scale):
    micro, slots, width = x_all.shape
    own = x_own.shape[1]
    wide = min(1024, slots)
    return pl.pallas_call(
        functools.partial(project_kernel, scale),
        grid=(micro, slots // wide),
        out_shape=(
            jax.ShapeDtypeStruct((micro, width, slots), BF16),
            jax.ShapeDtypeStruct((micro, width, own), BF16),
            jax.ShapeDtypeStruct((micro, width, own), BF16),
        ),
        in_specs=[
            pl.BlockSpec((1, wide, width), lambda m, t: (m, t, 0)),
            pl.BlockSpec((1, own, width), lambda m, t: (m, 0, 0)),
            pl.BlockSpec((3 * width, width), lambda m, t: (0, 0)),
            pl.BlockSpec((8, width), lambda m, t: (0, 0)),
        ],
        out_specs=(
            pl.BlockSpec((1, width, wide), lambda m, t: (m, 0, t)),
            pl.BlockSpec((1, width, own), lambda m, t: (m, 0, 0)),
            pl.BlockSpec((1, width, own), lambda m, t: (m, 0, 0)),
        ),
        scratch_shapes=[pltpu.VMEM((width, 8), F32)],
        compiler_params=pltpu.CompilerParams(vmem_limit_bytes=VMEM_LIMIT),
        cost_estimate=pl.CostEstimate(
            flops=2 * micro * width * width * (slots + 2 * own),
            bytes_accessed=4 * micro * width * slots,
            transcendentals=0,
        ),
        name="project",
    )(x_all, x_own, w_t, vec)


def attention_forward_kernel(q_ref, k_ref, v_ref, prev_ref, segk_ref, segq_ref, *refs):
    logit_ref, e_ref, o_ref, st_ref, top_ref, mask_ref = refs[-6:]
    h = pl.program_id(0)
    chunks, wide = o_ref.shape[1], o_ref.shape[3]

    @pl.when(h == 0)
    def _():
        mask_ref[...] = jnp.where(segk_ref[0] == segq_ref[0], 0.0, NEG_BIG)

    for i in range(PER):
        rows = slice(i * HD, (i + 1) * HD)
        hg = lax.rem(h * PER + i, GROUP)
        score = dot_f32(k_ref[rows], q_ref[rows], ((0,), (0,)))
        raw = score + prev_ref[0, 0, i].astype(F32)
        logit_ref[0, 0, i] = raw.astype(BF16)
        masked = raw + mask_ref[...]
        top = jnp.maximum(jnp.max(masked, axis=0, keepdims=True), NEG_FLOOR)
        expo = jnp.exp(masked - top)
        total = jnp.sum(expo, axis=0, keepdims=True)
        low = expo.astype(BF16)
        e_ref[0, i] = low
        out = dot_f32(v_ref[rows], low, ((1,), (0,))).astype(BF16)
        for t in range(chunks):
            cols = slice(t * wide, (t + 1) * wide)
            o_ref[0, t, rows] = out[:, cols]
            st_ref[0, 0, t, pl.ds(hg, 1), :] = top[:, cols]
            st_ref[0, 0, t, pl.ds(GROUP + hg, 1), :] = total[:, cols]
            top_ref[0, 0, t, pl.ds(hg, 1), :] = top[:, cols]


def attention_forward(m, so_far, q, k, v, prev, segk, segq, chunks, wide):
    micro, _, heads, own, slots = prev.shape
    groups = heads // GROUP
    score = pl.BlockSpec((1, 1, PER, own, slots), lambda h: (m, 0, h, 0, 0))
    stat = pl.BlockSpec((1, 1, chunks, 2 * GROUP, wide), lambda h: (m, h * PER // GROUP, 0, 0, 0))
    return pl.pallas_call(
        attention_forward_kernel,
        grid=(heads // PER,),
        out_shape=(
            jax.ShapeDtypeStruct(prev.shape, BF16),
            jax.ShapeDtypeStruct((micro, heads, own, slots), BF16),
            jax.ShapeDtypeStruct((micro, chunks, heads * HD, wide), BF16),
            jax.ShapeDtypeStruct((micro, groups, chunks, 2 * GROUP, wide), F32),
            jax.ShapeDtypeStruct((micro, groups, chunks, 2 * GROUP, wide), F32),
        ),
        in_specs=[
            pl.BlockSpec((None, PER * HD, slots), lambda h: (m, h, 0)),
            pl.BlockSpec((None, PER * HD, own), lambda h: (m, h, 0)),
            pl.BlockSpec((None, PER * HD, own), lambda h: (m, h, 0)),
            score,
            pl.BlockSpec((1, own, 1), lambda h: (m, 0, 0)),
            pl.BlockSpec((1, 1, slots), lambda h: (m, 0, 0)),
        ]
        + [ANY] * len(so_far),
        out_specs=(
            score,
            pl.BlockSpec((1, PER, own, slots), lambda h: (m, h, 0, 0)),
            pl.BlockSpec((1, chunks, PER * HD, wide), lambda h: (m, 0, h, 0)),
            stat,
            stat,
        ),
        input_output_aliases={6 + i: i for i in range(len(so_far))},
        scratch_shapes=[pltpu.VMEM((own, slots), F32)],
        compiler_params=pltpu.CompilerParams(vmem_limit_bytes=VMEM_LIMIT),
        cost_estimate=pl.CostEstimate(
            flops=heads * 2 * 2 * own * slots * HD,
            bytes_accessed=heads * own * slots * 6,
            transcendentals=heads * own * slots,
        ),
        name="attention_forward",
    )(q, k, v, prev, segk, segq, *so_far)


def attention_backward_kernel(
    scale, e_ref, d_ref, st_ref, top_ref, q_ref, k_ref, v_ref, *refs
):
    g_ref, dq_ref, dk_ref, dv_ref, sum_ref = refs[-5:]
    h = pl.program_id(0)
    chunks, wide = d_ref.shape[1], d_ref.shape[3]
    for i in range(PER):
        rows = slice(i * HD, (i + 1) * HD)
        hg = lax.rem(h * PER + i, GROUP)

        def row(ref, first):
            return jnp.concatenate([ref[0, 0, t, pl.ds(first + hg, 1), :] for t in range(chunks)], axis=1)

        weight = jnp.exp(row(top_ref, 0) - row(st_ref, 0)) * row(st_ref, GROUP)
        dots = row(st_ref, 2 * GROUP) * weight
        low = e_ref[0, i]
        datt = jnp.concatenate([d_ref[0, t, rows] for t in range(chunks)], axis=1)
        grad_in = (datt.astype(F32) * weight).astype(BF16)
        soft = dot_f32(v_ref[rows], grad_in, ((0,), (0,))) - dots
        grad = (low.astype(F32) * soft).astype(BF16)
        g_ref[0, 0, i] = grad
        dq = dot_f32(k_ref[rows], grad, ((1,), (0,))) * scale
        sum_ref[0, rows] = jnp.broadcast_to(jnp.sum(dq, axis=1, keepdims=True), (HD, 128))
        dq = dq.astype(BF16)
        for t in range(chunks):
            dq_ref[0, t, rows] = dq[:, t * wide : (t + 1) * wide]
        dv_ref[0, rows] = dot_f32(grad_in, low, ((1,), (1,))).astype(BF16)
        dk_ref[0, rows] = dot_f32(q_ref[rows], grad, ((1,), (1,))).astype(BF16)


def attention_backward(m, so_far, expo, datt, st, tops, q, k, v, scale):
    micro, heads, own, slots = expo.shape
    chunks, wide = datt.shape[1], datt.shape[3]
    flops = heads * 2 * 4 * own * slots * HD
    sts = st.shape[3]
    return pl.pallas_call(
        functools.partial(attention_backward_kernel, scale),
        grid=(heads // PER,),
        out_shape=(
            jax.ShapeDtypeStruct((micro, 1, heads, own, slots), BF16),
            jax.ShapeDtypeStruct((micro, chunks, heads * HD, wide), BF16),
            jax.ShapeDtypeStruct((micro, heads * HD, own), BF16),
            jax.ShapeDtypeStruct((micro, heads * HD, own), BF16),
            jax.ShapeDtypeStruct((micro, heads * HD, 128), F32),
        ),
        in_specs=[
            pl.BlockSpec((1, PER, own, slots), lambda h: (m, h, 0, 0)),
            pl.BlockSpec((1, chunks, PER * HD, wide), lambda h: (m, 0, h, 0)),
            pl.BlockSpec((1, 1, chunks, sts, wide), lambda h: (m, h * PER // GROUP, 0, 0, 0)),
            pl.BlockSpec((1, 1, chunks, 2 * GROUP, wide), lambda h: (m, h * PER // GROUP, 0, 0, 0)),
            pl.BlockSpec((None, PER * HD, slots), lambda h: (m, h, 0)),
            pl.BlockSpec((None, PER * HD, own), lambda h: (m, h, 0)),
            pl.BlockSpec((None, PER * HD, own), lambda h: (m, h, 0)),
        ]
        + [ANY] * len(so_far),
        out_specs=(
            pl.BlockSpec((1, 1, PER, own, slots), lambda h: (m, 0, h, 0, 0)),
            pl.BlockSpec((1, chunks, PER * HD, wide), lambda h: (m, 0, h, 0)),
            pl.BlockSpec((1, PER * HD, own), lambda h: (m, h, 0)),
            pl.BlockSpec((1, PER * HD, own), lambda h: (m, h, 0)),
            pl.BlockSpec((1, PER * HD, 128), lambda h: (m, h, 0)),
        ),
        input_output_aliases={7 + i: i for i in range(len(so_far))},
        compiler_params=pltpu.CompilerParams(vmem_limit_bytes=VMEM_LIMIT),
        cost_estimate=pl.CostEstimate(
            flops=flops, bytes_accessed=heads * own * slots * 4, transcendentals=0
        ),
        name="attention_backward",
    )(expo, datt, st, tops, q, k, v, *so_far)


def shifted(arr, mesh_dims, dy, dx):
    if dy == 0 and dx == 0:
        return arr
    Y, X, _ = mesh_dims
    key = lambda y, x, c: (y * X + x) * 2 + c
    perm = [
        (key(y, x, c), key((y + dy) % Y, (x + dx) % X, c)) for y in range(Y) for x in range(X) for c in range(2)
    ]
    return lax.ppermute(arr, "keys", perm)


def late_weights_start(mesh_dims, own):
    Y, X, _ = mesh_dims
    half = own.shape[0] // 2
    first = [shifted(own[:half], mesh_dims, 0, dx) for dx in range(X)]
    last = [shifted(own[half:], mesh_dims, dy, 0) for dy in range(Y)]
    first_own = [shifted(own[:half], mesh_dims, dy, 0) for dy in range(1, Y)]
    last_own = [shifted(own[half:], mesh_dims, 0, dx) for dx in range(1, X)]
    return first, last, first_own, last_own


def late_weights_finish(mesh_dims, first, last, first_own, last_own):
    Y, X, _ = mesh_dims
    out = []
    for dy in range(Y):
        for dx in range(X):
            out.append(first_own[dy - 1] if dx == 0 and dy > 0 else shifted(first[dx], mesh_dims, dy, 0))
    for dy in range(Y):
        for dx in range(X):
            out.append(last_own[dx - 1] if dy == 0 and dx > 0 else shifted(last[dy], mesh_dims, 0, dx))
    return out


def late_grads_start(mesh_dims, send_a, keep_a, send_b, keep_b):
    Y, X, _ = mesh_dims
    first = [shifted(send_a[d - 1], mesh_dims, d, 0) for d in range(1, Y)]
    last = [shifted(send_b[d - 1], mesh_dims, 0, d) for d in range(1, X)]
    return (keep_a, first), (keep_b, last)


def late_grads_finish(mesh_dims, first, last):
    Y, X, _ = mesh_dims
    key = lax.axis_index("keys")
    x, y = (key // 2) % X, key // (2 * X)
    low = lambda total: total.astype(BF16)

    def line(keep, got, place, move):
        total = keep.astype(F32)
        for piece in got:
            total = total + piece.astype(F32)
        total = low(total)
        count = total.shape[0]
        pick = lambda d: lax.dynamic_index_in_dim(total, (place + d) % count, 0, keepdims=False)
        out = pick(0).astype(F32)
        for d in range(1, count):
            out = out + move(pick(d), d).astype(F32)
        return low(out)

    return jnp.concatenate(
        [
            line(*first, x, lambda a, d: shifted(a, mesh_dims, 0, d)),
            line(*last, y, lambda a, d: shifted(a, mesh_dims, d, 0)),
        ],
        axis=0,
    )


def halves(value):
    high = value.astype(BF16)
    return high, (value - high.astype(F32)).astype(BF16)


def update_weights_kernel(
    block_ids, first_column, fixes, late_ref, early_ref, basis_ref, master_ref, one_ref, two_ref,
    grad_out, one_out, two_out, master_out, copy_out,
):
    s = pl.program_id(0)
    block = block_ids[s]
    early = early_ref[jnp.minimum(block, EARLY - 1)].astype(F32)
    grad = jnp.where(block < EARLY, early, late_ref[0])
    grad_out[0] = grad
    basis = basis_ref[0]
    basis_high, basis_low = halves(basis)

    def product(value, contract):
        n = value.shape[0]
        high, rest = halves(value)
        both = dot_f32(jnp.concatenate([high, rest], axis=0), basis_high, contract)
        return both[:n] + (both[n:] + dot_f32(high, basis_low, contract))

    rotated = product(grad, ((1,), (0,)))
    new_one = BETA_ONE * one_ref[0] + (1.0 - BETA_ONE) * rotated
    new_two = BETA_TWO * two_ref[0] + (1.0 - BETA_TWO) * rotated * rotated
    one_out[0] = new_one
    two_out[0] = new_two
    direction = new_one / fixes[0] / (jnp.sqrt(new_two / fixes[1]) + EPS_ADAM)
    back = product(direction, ((1,), (1,)))
    columns = first_column[s] + lax.broadcasted_iota(jnp.int32, (grad.shape[0], 1), 0)
    master = master_ref[0]
    new_master = master - column_rates(columns) * (back + DECAY * master)
    master_out[0] = new_master
    copy_out[0] = new_master.astype(BF16)


def update_weights(block_ids, first_column, fixes, late, early, basis, master, one, two):
    slots_here, n, width = master.shape
    mat = pl.BlockSpec((1, n, width), lambda s: (s, 0, 0))
    smem = pl.BlockSpec(memory_space=pltpu.SMEM)
    return pl.pallas_call(
        update_weights_kernel,
        grid=(slots_here,),
        out_shape=tuple(jax.ShapeDtypeStruct(master.shape, F32) for _ in range(4))
        + (jax.ShapeDtypeStruct(master.shape, BF16),),
        in_specs=[smem, smem, smem, mat, pl.BlockSpec((EARLY, n, width), lambda s: (0, 0, 0)),
                  pl.BlockSpec((1, width, width), lambda s: (s, 0, 0)), mat, mat, mat],
        out_specs=(mat,) * 5,
        compiler_params=pltpu.CompilerParams(vmem_limit_bytes=VMEM_LIMIT),
        name="update_weights",
    )(block_ids, first_column, fixes, late, early, basis, master, one, two)


def to_chunks(arr, chunks):
    pieces, rows, own = arr.shape[-3:]
    lead = arr.shape[:-3]
    if pieces == chunks:
        return arr
    per = pieces // chunks
    arr = arr.reshape(lead + (chunks, per, rows, own))
    return jnp.moveaxis(arr, -3, -2).reshape(lead + (chunks, rows, per * own))


def from_chunks(arr, pieces):
    chunks, rows, wide = arr.shape[-3:]
    lead = arr.shape[:-3]
    if pieces == chunks:
        return arr
    per = pieces // chunks
    arr = arr.reshape(lead + (chunks, rows, per, wide // per))
    return jnp.moveaxis(arr, -2, -3).reshape(lead + (pieces, rows, wide // per))


def per_device(
    mesh_dims,
    tokens,
    prev_logits,
    segments,
    out_cot,
    master_mat,
    mom1_mat,
    mom2_mat,
    eigen_bases,
    master_small,
    mom1_small,
    mom2_small,
    owners,
    step_count,
):
    Y, X, R = mesh_dims
    keys = Y * X * 2
    micro, row_count, key_len, width = tokens.shape
    slot_count = prev_logits.shape[4]
    slots_here, _, cols_here = master_mat.shape
    blocks = slots_here * R
    token_count = micro * key_len
    scale = HD ** (-0.5)
    key_index = lax.axis_index("keys")
    row_index = lax.axis_index("rows")
    wide = max(key_len, min(256, slot_count))
    chunks = slot_count // wide
    groups = H // GROUP

    x_own = tokens.reshape(micro, key_len, width)
    w_own = jnp.swapaxes(master_mat, 1, 2).astype(BF16)
    small_low = master_small.astype(BF16).reshape(1, slots_here * cols_here)
    ext = lax.dynamic_update_slice(
        jnp.zeros((EXT, width), BF16), small_low, (row_index, jnp.int32(0))
    )
    fast = cols_here % 16 == 0
    wt, w_late, ext_all, xg = gather_weights(mesh_dims, owners, w_own, ext, x_own)
    if fast:
        pieces = late_weights_start(mesh_dims, w_late)
    else:
        late = [lax.all_gather(w_late, "keys", axis=1).reshape(2 * FF + width, width)]
    w_t = wt.reshape(EARLY * BLOCK_COLUMNS, width)
    small_all = ext_all.reshape(keys, EXT, width)[:, :R, : slots_here * cols_here]
    params = (
        jnp.transpose(small_all.reshape(keys, R, slots_here, cols_here), (1, 2, 0, 3))
        .reshape(blocks * GAIN_ROW_WIDTH)
        .astype(F32)
    )
    bias_q = params[:width]
    bias_v = params[width : 2 * width]
    bias_o = params[2 * width : 3 * width]
    gain_one = params[3 * width : 4 * width]
    shift_one = params[4 * width : 5 * width]
    bias_up = params[5 * width : 5 * width + FF]
    bias_down = params[5 * width + FF : 6 * width + FF]
    gain_two = params[6 * width + FF : 7 * width + FF]
    shift_two = params[7 * width + FF :]

    vec = jnp.stack([bias_o, gain_one, shift_one, bias_down, gain_two, shift_two, bias_q, bias_v])
    q_all, k_all, v_all = project(xg.reshape(micro, slot_count, width), x_own, w_t, vec, scale)
    x_rows = x_own.reshape(token_count, width)

    seg_rows = segments.reshape(micro, slot_count)
    seg_keys = lax.dynamic_slice_in_dim(seg_rows, key_index * key_len, key_len, 1)
    forward = ()
    for m in range(micro):
        forward = attention_forward(
            m, forward, q_all, k_all, v_all, prev_logits,
            seg_keys[:, :, None], seg_rows[:, None, :], chunks, wide,
        )
        if m == 0 and fast:
            forward, first, last = lax.optimization_barrier((tuple(forward), *pieces[:2]))
            late = late_weights_finish(mesh_dims, first, last, *pieces[2:])
    logits, expo, o_part, st_part, tops = forward
    o_part = from_chunks(o_part, keys).reshape(micro, Y, X, 2, width, key_len)
    st_part = from_chunks(st_part, keys).reshape(micro, groups, Y, X, 2, 2 * GROUP, key_len)
    out_hidden, datt_all, st_all, grad_one, dvec, d_bias_up, *dw_late = middle(
        mesh_dims, o_part, st_part, x_own, out_cot.reshape(x_own.shape), late, vec, bias_up[None]
    )
    out_hidden = out_hidden.reshape(tokens.shape)
    datt_all = to_chunks(datt_all.reshape(micro, keys, width, key_len), chunks)
    st_all = to_chunks(st_all.reshape(micro, groups, keys, 16, key_len), chunks)
    so_far = ()
    if fast:
        first, last = late_grads_start(mesh_dims, *dw_late)
    for m in range(micro):
        so_far = attention_backward(
            m, so_far, expo, datt_all, st_all, tops, q_all, k_all, v_all, scale
        )
        if m == 0 and fast:
            so_far, first, last = lax.optimization_barrier((tuple(so_far), first, last))
            fin = late_grads_finish(mesh_dims, first, last)
    grad_prev, dq_part, dk, dv, dq_sum = so_far
    dq_part = from_chunks(dq_part, keys).reshape(micro, Y, X, 2, width, key_len)
    inverse = inverse_order(owners)
    slot_index_list = row_index * slots_here + jnp.arange(slots_here, dtype=jnp.int32)
    block_ids = jnp.take(inverse, slot_index_list)
    if fast:
        grad_tokens, mine_late, mine_early, small_sum = tail(
            mesh_dims, inverse, dq_part, dk, dv, x_own, grad_one, wt, fin, dvec, d_bias_up,
            xg.reshape(micro, slot_count, width), dq_sum,
        )
        mine_early = mine_early.reshape(EARLY, cols_here, width)
    else:
        dq = lax.psum_scatter(
            dq_part.reshape(micro, keys, width, key_len), "keys", scatter_dimension=1, tiled=True
        ).reshape(micro, width, key_len)
        grad_proj = jnp.swapaxes(jnp.concatenate([dq, dk, dv], axis=1), 0, 1).reshape(
            3 * width, token_count
        )
        d_qkv = dot_f32(grad_proj, x_rows, ((1,), (0,))).astype(BF16)
        grad_tokens = (
            grad_one.reshape(token_count, width) + dot_f32(grad_proj, w_t, ((0,), (0,)))
        ).astype(BF16)
        sums = jnp.sum(grad_proj.astype(F32).reshape(3, width, token_count), axis=2)
        small_sum = lax.psum(
            jnp.concatenate(
                [sums[0][None], sums[2][None], dvec[:3], d_bias_up.reshape(FF // width, width), dvec[3:6]]
            ),
            ("rows", "keys"),
        )
        grads = jnp.concatenate([d_qkv, dw_late[0]], axis=0).reshape(blocks, keys, cols_here, width)
        grads = lax.psum_scatter(grads, "keys", scatter_dimension=1, tiled=True)
        grads = jnp.take(grads.reshape(blocks, cols_here, width), inverse, axis=0)
        mine_t = lax.psum_scatter(grads, "rows", scatter_dimension=0, tiled=True).astype(F32)
    grad_tokens = grad_tokens.reshape(tokens.shape)
    flat = small_sum.reshape(-1)[: blocks * GAIN_ROW_WIDTH].reshape(blocks, GAIN_ROW_WIDTH)
    mine_small = lax.dynamic_slice(
        flat, (row_index * slots_here, key_index * cols_here), (slots_here, cols_here)
    )

    steps_done = step_count[0].astype(F32)
    fix_one = 1.0 - jnp.power(jnp.asarray(BETA_ONE, F32), steps_done)
    fix_two = 1.0 - jnp.power(jnp.asarray(BETA_TWO, F32), steps_done)
    if fast:
        first_column = block_ids * BLOCK_COLUMNS + key_index * cols_here
        mats = [jnp.swapaxes(a, 1, 2) for a in (master_mat, mom1_mat, mom2_mat)]
        updated = update_weights(
            block_ids, first_column, jnp.stack([fix_one, fix_two]), mine_late, mine_early, eigen_bases, *mats
        )
        mine_mat, new_one, new_two, new_master, copy_mat = (jnp.swapaxes(a, 1, 2) for a in updated)
    else:
        mine_mat = jnp.swapaxes(mine_t, 1, 2)
        rotated = jnp.einsum("sed,sec->sdc", eigen_bases, mine_mat, precision=HIGHEST_PREC)
        new_one = BETA_ONE * mom1_mat + (1.0 - BETA_ONE) * rotated
        new_two = BETA_TWO * mom2_mat + (1.0 - BETA_TWO) * rotated * rotated
        direction = new_one / fix_one / (jnp.sqrt(new_two / fix_two) + EPS_ADAM)
        back_rot = jnp.einsum("sdk,skc->sdc", eigen_bases, direction, precision=HIGHEST_PREC)
        columns = (
            block_ids[:, None] * (cols_here * keys)
            + key_index * cols_here
            + jnp.arange(cols_here, dtype=jnp.int32)[None, :]
        )
        rates = column_rates(columns)[:, None, :]
        new_master = master_mat - rates * (back_rot + DECAY * master_mat)
        copy_mat = new_master.astype(BF16)
    small_one = BETA_ONE * mom1_small + (1.0 - BETA_ONE) * mine_small
    small_two = BETA_TWO * mom2_small + (1.0 - BETA_TWO) * mine_small * mine_small
    new_small = master_small - RATE_SMALL * (small_one / fix_one) / (
        jnp.sqrt(small_two / fix_two) + EPS_ADAM
    )
    return (
        out_hidden,
        logits,
        grad_tokens,
        grad_prev,
        mine_mat,
        new_one,
        new_two,
        new_master,
        copy_mat,
        mine_small,
        small_one,
        small_two,
        new_small,
        new_small.astype(BF16),
    )


def solution(mesh):
    chips = mesh.shape["keys"] // 2
    side = math.isqrt(chips)
    dims = (side, side, mesh.shape["rows"]) if side * side == chips else (1, chips, mesh.shape["rows"])
    acts = P(None, "rows", "keys", None)
    scores = P(None, "rows", None, "keys", None)
    mats = P("rows", None, "keys")
    smalls = P("rows", "keys")
    return jax.shard_map(
        functools.partial(per_device, dims),
        mesh=mesh,
        in_specs=(
            acts, scores, P(None, "rows", None), acts, mats, mats, mats,
            P("rows", None, None), smalls, smalls, smalls, P(), P(),
        ),
        out_specs=(acts, scores, acts, scores) + (mats,) * 5 + (smalls,) * 5,
        check_vma=False,
    )
```

```python
import functools
import math

import jax
import jax.numpy as jnp
from jax import lax
from jax.experimental import pallas as pl
from jax.experimental.pallas import tpu as pltpu
from jax.sharding import PartitionSpec as P

MODEL_WIDTH = 768
H = 12
HD = 64
FF = 3072
BLOCK_COLUMNS = 1152
GAIN_ROW_WIDTH = 1152

EPS_NORM = 1e-06
BETA_ONE = 0.95
BETA_TWO = 0.95
EPS_ADAM = 1e-08
DECAY = 0.01
RATE_SMALL = 0.3
NEG_BIG = -1e30
NEG_FLOOR = -1e29
HIGHEST_PREC = lax.Precision.HIGHEST
MESH = pl.DeviceIdType.MESH
F32 = jnp.float32
BF16 = jnp.bfloat16
ANY = pl.BlockSpec(memory_space=pl.ANY)
VMEM_SPEC = pl.BlockSpec(memory_space=pltpu.VMEM)
EXT = 16
EARLY = 2
PER = 3
VMEM_LIMIT = 60 << 20


def layer_norm(value):
    mean_val = jnp.mean(value, axis=-1, keepdims=True)
    centered = value - mean_val
    inv_dev = lax.rsqrt(jnp.mean(centered * centered, axis=-1, keepdims=True) + EPS_NORM)
    return (centered * inv_dev, inv_dev)


def norm_back(grad_in, normed, inv_dev, gain):
    scaled = grad_in * gain
    return inv_dev * (
        scaled
        - jnp.mean(scaled, axis=-1, keepdims=True)
        - normed * jnp.mean(scaled * normed, axis=-1, keepdims=True)
    )


def inverse_order(owners):
    slot_index_list = jnp.arange(owners.shape[0], dtype=jnp.int32)
    matches = (owners[None, :] == slot_index_list[:, None]).astype(jnp.int32)
    return jnp.sum(matches * slot_index_list[None, :], axis=1)


def column_rates(columns):
    inner = MODEL_WIDTH ** (-0.5)
    return jnp.where(
        columns < 3 * MODEL_WIDTH,
        inner,
        jnp.where(
            columns < 4 * MODEL_WIDTH,
            4.0 * inner,
            jnp.where(columns < 4 * MODEL_WIDTH + FF, inner, FF ** (-0.5)),
        ),
    )


def dot_f32(left, right, contract):
    return lax.dot_general(left, right, (contract, ((), ())), preferred_element_type=F32)


class Place:
    def __init__(self, side_y, side_x, rows):
        self.Y, self.X, self.R = side_y, side_x, rows
        key = lax.axis_index("keys")
        self.key = key
        self.r = lax.axis_index("rows")
        self.c = lax.rem(key, 2)
        self.x = lax.rem(key // 2, side_x)
        self.y = key // (2 * side_x)

    def keyof(self, y, x, c):
        return (y * self.X + x) * 2 + c

    def xo(self, d):
        return lax.rem(self.x + d, self.X)

    def yo(self, d):
        return lax.rem(self.y + d, self.Y)

    def ro(self, d):
        return lax.rem(self.r + d, self.R)

    def x_peer(self, d):
        return {"keys": self.keyof(self.y, self.xo(d), self.c)}

    def y_peer(self, d):
        return {"keys": self.keyof(self.yo(d), self.x, self.c)}

    def core_peer(self):
        return {"keys": self.keyof(self.y, self.x, 1 - self.c)}

    def z_peer(self, d):
        return {"rows": self.ro(d)}

    def announce(self, with_z):
        peers = [self.core_peer()]
        peers += [self.x_peer(d) for d in range(1, self.X)]
        peers += [self.y_peer(d) for d in range(1, self.Y)]
        if with_z:
            peers += [self.z_peer(d) for d in range(1, self.R)]
        sem = pltpu.get_barrier_semaphore()
        for peer in peers:
            pl.semaphore_signal(sem, inc=1, device_id=peer, device_id_type=MESH)
        self.greeted = len(peers)

    def meet(self):
        pl.semaphore_wait(pltpu.get_barrier_semaphore(), self.greeted)

    def barrier(self, with_z):
        self.announce(with_z)
        self.meet()


def remote(src, dst, send_sem, recv_sem, peer):
    return pltpu.make_async_remote_copy(
        src_ref=src,
        dst_ref=dst,
        send_sem=send_sem,
        recv_sem=recv_sem,
        device_id=peer,
        device_id_type=MESH,
    )


def sems_per_item(Y, X):
    return (X - 1) + (Y - 1) + 1


class Gather:
    def __init__(self, place, own, buf, send, recv, base, x_first):
        p = place
        self.sent = []
        n = sems_per_item(p.Y, p.X)
        idx = iter(range(base, base + n))
        first = [(p.x_peer(d)) for d in range(1, p.X)] if x_first else [p.y_peer(d) for d in range(1, p.Y)]
        second = [p.y_peer(d) for d in range(1, p.Y)] if x_first else [p.x_peer(d) for d in range(1, p.X)]
        line = buf.at[p.y, :, p.c] if x_first else buf.at[:, p.x, p.c]
        plane = buf.at[:, :, p.c]
        mine = buf.at[p.y, p.x, p.c]
        self.one = []
        for peer in first:
            i = next(idx)
            self.one.append(remote(own, mine, send.at[i], recv.at[i], peer))
        self.two = []
        for peer in second:
            i = next(idx)
            self.two.append(remote(line, line, send.at[i], recv.at[i], peer))
        i = next(idx)
        self.three = [remote(plane, plane, send.at[i], recv.at[i], p.core_peer())]

    def start1(self):
        for copy in self.one:
            copy.start()

    def start2(self):
        for copy in self.one:
            copy.wait_recv()
        for copy in self.two:
            copy.start()

    def start3(self):
        for copy in self.two:
            copy.wait_recv()
        for copy in self.three:
            copy.start()

    def finish(self):
        for copy in self.three:
            copy.wait_recv()
        for copy in self.one + self.two + self.three:
            copy.wait_send()


def gather_weights_kernel(
    Y, X, R, owners, w_ref, ext_ref, x_ref, wt_out, first_out, last_out, ext_out, xg_out,
    zbuf, zext, stage, sext, zsend, zrecv, send, recv, loc,
):
    p = Place(Y, X, R)
    slots_here = w_ref.shape[0]
    blocks = zbuf.shape[0]
    early = wt_out.shape[0]
    micro = x_ref.shape[0]
    n = sems_per_item(Y, X)
    p.barrier(True)
    here = pl.ds(p.r * slots_here, slots_here)

    def hop(src, step, own):
        there = pl.ds(src * slots_here, slots_here)
        way = (step + 1) // 2
        peer = {"rows": p.r + step}
        return [
            remote(w_ref if own else zbuf.at[there], zbuf.at[there], zsend.at[way, src, 0], zrecv.at[src, 0], peer),
            remote(ext_ref if own else zext.at[src], zext.at[src], zsend.at[way, src, 1], zrecv.at[src, 1], peer),
        ]

    def can(step):
        return p.r < R - 1 if step > 0 else p.r > 0

    def pass_on(dist, act):
        for step in (1, -1):
            src = p.r - step * dist

            @pl.when((src >= 0) & (src < R) & can(step))
            def _():
                for copy in hop(src, step, dist == 0):
                    act(copy)

    def arrived(dist):
        for step in (1, -1):
            src = p.r - step * dist

            @pl.when((src >= 0) & (src < R))
            def _():
                for copy in hop(src, step, False):
                    copy.wait_recv()

    pass_on(0, lambda copy: copy.start())
    xitems = []
    xlocal = []
    for m in range(micro):
        item = Gather(p, x_ref.at[m], xg_out.at[m], send, recv, m * n, m % 2 == 0)
        item.start1()
        xitems.append(item)
        copy = pltpu.make_async_copy(x_ref.at[m], xg_out.at[m, p.y, p.x, p.c], loc.at[m])
        copy.start()
        xlocal.append(copy)
    wl = pltpu.make_async_copy(w_ref, zbuf.at[here], loc.at[micro])
    wl.start()
    el = pltpu.make_async_copy(ext_ref, zext.at[p.r], loc.at[micro + 1])
    el.start()
    for m in range(micro):
        xlocal[m].wait()
        xitems[m].start2()
    for dist in range(1, R):
        arrived(dist)
        pass_on(dist, lambda copy: copy.start())
    wl.wait()
    el.wait()
    sext[...] = jnp.sum(zext[...].astype(F32), axis=0).astype(BF16)

    def reorder(b, carry):
        stage[b] = zbuf[owners[b]]
        return carry

    lax.fori_loop(0, blocks, reorder, 0)
    base = micro * n
    eitem = Gather(p, sext, ext_out, send, recv, base, True)
    base += n
    lcopies = []
    items = []
    for b in range(early):
        item = Gather(p, stage.at[b], wt_out.at[b], send, recv, base, b % 2 == 0)
        base += n
        item.start1()
        items.append(item)
        copy = pltpu.make_async_copy(stage.at[b], wt_out.at[b, p.y, p.x, p.c], loc.at[micro + 3 + b])
        copy.start()
        lcopies.append(copy)
    eitem.start1()
    ecopy = pltpu.make_async_copy(sext, ext_out.at[p.y, p.x, p.c], loc.at[micro + 2])
    ecopy.start()
    late = (blocks - early) // 2
    rest = [
        pltpu.make_async_copy(stage.at[pl.ds(early + i * late, late)], out, loc.at[micro + 3 + early + i])
        for i, out in enumerate((first_out, last_out))
    ]
    for copy in rest:
        copy.start()
    for m in range(micro):
        xitems[m].start3()
    for b in range(early):
        lcopies[b].wait()
        items[b].start2()
    ecopy.wait()
    eitem.start2()
    for b in range(early):
        items[b].start3()
    eitem.start3()
    for item in xitems + [eitem] + items:
        item.finish()
    for dist in range(R):
        pass_on(dist, lambda copy: copy.wait_send())
    for copy in rest:
        copy.wait()


def gather_weights(mesh_dims, owners, w_own, ext, x_own):
    Y, X, R = mesh_dims
    slots_here, n, width = w_own.shape
    micro, tok = x_own.shape[:2]
    blocks = slots_here * R
    total = sems_per_item(Y, X) * (micro + 1 + EARLY)
    return pl.pallas_call(
        functools.partial(gather_weights_kernel, Y, X, R),
        out_shape=(
            jax.ShapeDtypeStruct((EARLY, Y, X, 2, n, width), BF16),
            jax.ShapeDtypeStruct(((blocks - EARLY) // 2, n, width), BF16),
            jax.ShapeDtypeStruct(((blocks - EARLY) // 2, n, width), BF16),
            jax.ShapeDtypeStruct((Y, X, 2, EXT, width), BF16),
            jax.ShapeDtypeStruct((micro, Y, X, 2, tok, width), BF16),
        ),
        in_specs=[pl.BlockSpec(memory_space=pltpu.SMEM), VMEM_SPEC, VMEM_SPEC, VMEM_SPEC],
        out_specs=(ANY,) * 5,
        scratch_shapes=[
            pltpu.VMEM((blocks, n, width), BF16),
            pltpu.VMEM((R, EXT, width), BF16),
            pltpu.VMEM((blocks, n, width), BF16),
            pltpu.VMEM((EXT, width), BF16),
            pltpu.SemaphoreType.DMA((2, R, 2)),
            pltpu.SemaphoreType.DMA((R, 2)),
            pltpu.SemaphoreType.DMA((total,)),
            pltpu.SemaphoreType.DMA((total,)),
            pltpu.SemaphoreType.DMA((micro + 5 + EARLY,)),
        ],
        compiler_params=pltpu.CompilerParams(
            collective_id=1, has_side_effects=True, vmem_limit_bytes=VMEM_LIMIT
        ),
        name="gather_weights",
    )(owners, w_own, ext, x_own)


class Scatter:
    def __init__(self, place, parts, accs, r1s, r2s, r3s, send, recv, loc, base, lbase, y_first, merge):
        p = place
        self.p, self.y_first, self.merge = p, y_first, merge
        self.accs, self.r1s, self.r2s, self.r3s = accs, r1s, r2s, r3s
        self.count = len(parts)
        n = sems_per_item(p.Y, p.X) * len(parts)
        idx = iter(range(base, base + n))
        self.zero, self.one, self.two, self.three = [], [], [], []
        for t, part in enumerate(parts):
            i = next(idx)
            self.zero.append(pltpu.make_async_copy(part.at[:, :, p.c], accs[t], loc.at[lbase + t]))
            self.one.append(remote(part.at[:, :, 1 - p.c], r1s[t], send.at[i], recv.at[i], p.core_peer()))
            if y_first:
                for d in range(1, p.Y):
                    i = next(idx)
                    self.two.append(
                        remote(accs[t].at[p.yo(d)], r2s[t].at[d - 1], send.at[i], recv.at[i], p.y_peer(d))
                    )
                for d in range(1, p.X):
                    i = next(idx)
                    self.three.append(
                        remote(accs[t].at[p.y, p.xo(d)], r3s[t].at[d - 1], send.at[i], recv.at[i], p.x_peer(d))
                    )
            else:
                for d in range(1, p.X):
                    i = next(idx)
                    self.two.append(
                        remote(accs[t].at[:, p.xo(d)], r2s[t].at[d - 1], send.at[i], recv.at[i], p.x_peer(d))
                    )
                for d in range(1, p.Y):
                    i = next(idx)
                    self.three.append(
                        remote(accs[t].at[p.yo(d), p.x], r3s[t].at[d - 1], send.at[i], recv.at[i], p.y_peer(d))
                    )

    def start1(self):
        for copy in self.zero + self.one:
            copy.start()

    def start2(self):
        p = self.p
        for copy in self.zero:
            copy.wait()
        for copy in self.one:
            copy.wait_recv()

        def body(i, carry):
            y, x = i // p.X, lax.rem(i, p.X)
            self.merge([a.at[y, x] for a in self.accs], [r.at[y, x] for r in self.r1s])
            return carry

        lax.fori_loop(0, p.Y * p.X, body, 0)
        for copy in self.two:
            copy.start()

    def start3(self):
        p = self.p
        for copy in self.two:
            copy.wait_recv()
        if self.y_first:
            for d in range(1, p.Y):
                for x in range(p.X):
                    self.merge([a.at[p.y, x] for a in self.accs], [r.at[d - 1, x] for r in self.r2s])
        else:
            for d in range(1, p.X):
                for y in range(p.Y):
                    self.merge([a.at[y, p.x] for a in self.accs], [r.at[d - 1, y] for r in self.r2s])
        for copy in self.three:
            copy.start()

    def finish(self):
        p = self.p
        for copy in self.three:
            copy.wait_recv()
        mine = [a.at[p.y, p.x] for a in self.accs]
        for d in range(1, p.X if self.y_first else p.Y):
            self.merge(mine, [r.at[d - 1] for r in self.r3s])
        return mine

    def drain(self):
        for copy in self.one + self.two + self.three:
            copy.wait_send()


def merge_sum(into, other):
    a, b = into[0], other[0]
    a[...] = (a[...].astype(F32) + b[...].astype(F32)).astype(BF16)


def merge_soft(into, other):
    (va, sa), (vb, sb) = into, other
    ta, tb = sa[...], sb[...]
    heads = ta.shape[0] // 2
    top_a, top_b = ta[:heads], tb[:heads]
    top = jnp.maximum(top_a, top_b)
    wa, wb = jnp.exp(top_a - top), jnp.exp(top_b - top)
    sa[...] = jnp.concatenate([top, wa * ta[heads:] + wb * tb[heads:]], axis=0)
    for h in range(heads):
        rows = slice(h * HD, (h + 1) * HD)
        va[rows, :] = (
            va[rows, :].astype(F32) * wa[h : h + 1] + vb[rows, :].astype(F32) * wb[h : h + 1]
        ).astype(BF16)


def scatter_scratch(Y, X, items, shape, dtype, y_first_of):
    most = max((Y - 1) * X, (X - 1) * Y)
    return [
        pltpu.VMEM((items, Y, X) + shape, dtype),
        pltpu.VMEM((items, Y, X) + shape, dtype),
        pltpu.VMEM((items, max(Y, X) - 1, max(Y, X)) + shape, dtype),
        pltpu.VMEM((items, max(Y, X) - 1) + shape, dtype),
    ]


GROUP = 3


def middle_kernel(Y, X, R, blocks, pieces, *refs):
    o_ref, st_ref, x_ref, cot_ref, vec_ref, bu_ref = refs[:6]
    refs = refs[6:]
    count = 2 * Y * X if pieces else 1
    w_refs, refs = refs[:count], refs[count:]
    out_ref, datt_out, stat_out, dz_ref, dvec_ref, dbu_ref = refs[:6]
    refs = refs[6:]
    if pieces:
        send_a, keep_a, send_b, keep_b = refs[:4]
        refs = refs[4:]
    else:
        (dw_out,) = refs[:1]
        refs = refs[1:]
    (
        oa, o1, o2, o3, sa, s1, s2, s3, send, recv, loc, gsend, grecv, gloc, wsem, wsend, wrecv, dwsem,
        w, att, attk, low, hid, dpre, slope, df, da, n1, n2, datt, stat, dw,
    ) = refs[:32]
    if pieces:
        core_acc, core_in, csend, crecv = refs[32:]
    p = Place(Y, X, R)
    micro, tok, width = x_ref.shape
    groups = st_ref.shape[1]
    rows = GROUP * HD
    bo, g1, e1, bd, g2, e2 = (vec_ref[i : i + 1] for i in range(6))
    p.announce(False)
    stat[...] = jnp.zeros_like(stat)
    parts = FF // width
    wcopies, wremote = [], []
    if pieces:
        half, piece = w_refs[0].shape[:2]
        for t in range(2):
            for dy in range(Y):
                for dx in range(X):
                    src = w_refs[(t * Y + dy) * X + dx]
                    key = p.keyof(p.yo(Y - dy), p.xo(X - dx), p.c)
                    for b in range(half):
                        at = (t * half + b) * BLOCK_COLUMNS + key * piece
                        dst = w.at[pl.ds(pl.multiple_of(at, 16), piece)]
                        i = ((t * Y + dy) * X + dx) * half + b
                        wcopies.append(pltpu.make_async_copy(src.at[b], dst, wsem.at[i]))
                        wremote.append(remote(src.at[b], dst, wsend.at[i], wrecv.at[i], p.core_peer()))
    else:
        wcopies.append(pltpu.make_async_copy(w_refs[0], w, wsem.at[0]))
    for copy in wcopies:
        copy.start()
    p.meet()

    n = sems_per_item(Y, X) * 2
    merges = []
    for m in range(micro):
        for g in range(groups):
            i = m * groups + g
            item = Scatter(
                p,
                [o_ref.at[m, :, :, :, pl.ds(g * rows, rows)], st_ref.at[m, g]],
                [oa.at[i], sa.at[i]], [o1.at[i], s1.at[i]], [o2.at[i], s2.at[i]], [o3.at[i], s3.at[i]],
                send, recv, loc, i * n, i * 2, g % 2 == 0, merge_soft,
            )
            merges.append(item)

    def merge_one(m):
        for g in range(groups):
            merges[m * groups + g].start1()

    def merge_two(m):
        for g in range(groups):
            merges[m * groups + g].start2()

    def merge_three(m):
        for g in range(groups):
            merges[m * groups + g].start3()

    def merge_finish(m):
        for g in range(groups):
            val, st = merges[m * groups + g].finish()
            tile = st[...]
            inv = 1.0 / tile[GROUP:]
            stat[m, g, : 2 * GROUP] = jnp.concatenate([tile[:GROUP], inv], axis=0)
            for h in range(GROUP):
                att[m, g * rows + h * HD : g * rows + (h + 1) * HD, :] = (
                    val[h * HD : (h + 1) * HD, :].astype(F32) * inv[h : h + 1]
                ).astype(BF16)

    n = sems_per_item(Y, X)
    gathers = [[], []]

    def gather_one(m):
        local = []
        for g in range(groups):
            ds = pl.ds(g * rows, rows)
            for t, (own, out) in enumerate(
                ((datt.at[m, ds], datt_out.at[m, :, :, :, ds]), (stat.at[m, g], stat_out.at[m, g]))
            ):
                i = (m * groups + g) * 2 + t
                item = Gather(p, own, out, gsend, grecv, i * n, g % 2 == 0)
                item.start1()
                copy = pltpu.make_async_copy(own, out.at[p.y, p.x, p.c], gloc.at[i])
                copy.start()
                gathers[m].append((item, copy))

    def gather_two(m):
        for item, copy in gathers[m]:
            copy.wait()
            item.start2()

    def gather_three(m):
        for item, copy in gathers[m]:
            item.start3()

    def forward(m):
        at = att[m].T
        attk[m] = at
        wo = w[:width]
        z1 = x_ref[m].astype(F32) + (dot_f32(at, wo, ((1,), (1,))) + bo)
        norm, inv = layer_norm(z1)
        n1[...] = norm
        mid = norm * g1 + e1
        low[m] = mid.astype(BF16)
        inner = low[m]

        def body(i, acc):
            r = pl.multiple_of(i * width, width)
            pre = dot_f32(inner, w[pl.ds(width + r, width)], ((1,), (1,))) + bu_ref[:, pl.ds(r, width)]
            half = 0.5 + 0.5 * lax.erf(pre * math.sqrt(0.5))
            low_h = (pre * half).astype(BF16)
            hid[m, :, pl.ds(r, width)] = low_h
            slope[:, pl.ds(r, width)] = half + pre * (
                jnp.exp(-0.5 * pre * pre) * (1.0 / math.sqrt(2.0 * math.pi))
            )
            return acc + dot_f32(low_h, w[pl.ds(width + FF + r, width)], ((1,), (0,)))

        f = lax.fori_loop(0, parts, body, jnp.zeros((tok, width), F32)) + bd
        norm2, inv2 = layer_norm(mid + f)
        n2[...] = norm2
        out_ref[m] = (norm2 * g2 + e2).astype(BF16)
        return inv, inv2

    def backward(m, invs, between=lambda: None):
        inv, inv2 = invs
        cot = cot_ref[m].astype(F32)
        norm2 = n2[...]
        dz2 = norm_back(cot, norm2, inv2, g2)
        dg2 = jnp.sum(cot * norm2, axis=0, keepdims=True)
        de2 = jnp.sum(cot, axis=0, keepdims=True)
        df_low = dz2.astype(BF16)
        df[m] = df_low
        dbd = jnp.sum(df_low.astype(F32), axis=0, keepdims=True)

        def body(i, acc):
            r = pl.multiple_of(i * width, width)
            dh = dot_f32(df_low, w[pl.ds(width + FF + r, width)], ((1,), (1,)))
            dp = (dh * slope[:, pl.ds(r, width)]).astype(BF16)
            dpre[m, :, pl.ds(r, width)] = dp
            part = jnp.sum(dp.astype(F32), axis=0, keepdims=True)
            if m == 0:
                dbu_ref[:, pl.ds(r, width)] = part
            else:
                dbu_ref[:, pl.ds(r, width)] += part
            return acc + dot_f32(dp, w[pl.ds(width + r, width)], ((1,), (0,)))

        dx1 = lax.fori_loop(0, parts // 2, body, dz2)
        between()
        dx1 = lax.fori_loop(parts // 2, parts, body, dx1)
        norm = n1[...]
        dg1 = jnp.sum(dx1 * norm, axis=0, keepdims=True)
        de1 = jnp.sum(dx1, axis=0, keepdims=True)
        dz1 = norm_back(dx1, norm, inv, g1)
        dz_ref[m] = dz1
        da_low = dz1.astype(BF16)
        da[m] = da_low
        dbo = jnp.sum(da_low.astype(F32), axis=0, keepdims=True)
        sums = jnp.concatenate([dbo, dg1, de1, dbd, dg2, de2, dg2, dg2], axis=0)
        if m == 0:
            dvec_ref[...] = sums
        else:
            dvec_ref[...] += sums
        dt = dot_f32(da_low, w[:width], ((1,), (0,))).astype(BF16).T
        datt[m] = dt
        for g in range(groups):
            for h in range(GROUP):
                r = g * rows + h * HD
                stat[m, g, 2 * GROUP + h : 2 * GROUP + h + 1] = jnp.sum(
                    dt[r : r + HD].astype(F32) * att[m, r : r + HD, :].astype(F32), axis=0, keepdims=True
                )

    step = width // 2

    def chunk_grad(slot, at, chunk):
        for left, right, lo, count in ((da, attk, 0, width), (dpre, low, width, FF), (hid, df, width + FF, FF)):

            @pl.when((chunk * step >= lo) & (chunk * step < lo + count))
            def _():
                cols = pl.ds(pl.multiple_of(chunk * step - lo, step), step)
                total = dot_f32(left[0, :, cols], right[0], ((0,), (0,)))
                for m in range(1, micro):
                    total = total + dot_f32(left[m, :, cols], right[m], ((0,), (0,)))
                dw[slot, pl.ds(pl.multiple_of(at, step), step)] = total.astype(BF16)

    def block_grad(b, slot):
        per = BLOCK_COLUMNS // step

        def body(t, carry):
            chunk_grad(slot, t * step, b * per + t)
            return carry

        lax.fori_loop(0, per, body, 0)

    merge_one(0)
    merge_two(0)
    for copy in wremote:
        copy.start()
    merge_one(1)
    merge_three(0)
    merge_two(1)
    merge_finish(0)
    for copy in wcopies:
        copy.wait()
    for copy in wremote:
        copy.wait_recv()
    invs = forward(0)
    backward(0, invs, lambda: merge_three(1))
    gather_one(0)
    merge_finish(1)
    invs = forward(1)
    gather_two(0)
    backward(1, invs)
    gather_one(1)
    gather_three(0)
    if pieces:
        half, piece = w_refs[0].shape[:2]
        keeps = []

        def cores(b):
            slot = lax.rem(b, 2)
            copies = []
            for y in range(Y):
                for x in range(X):
                    i = (b * Y + y) * X + x
                    there = pl.multiple_of(p.keyof(y, x, 1 - p.c) * piece, 16)
                    copies.append(
                        remote(
                            dw.at[slot, pl.ds(there, piece)], core_in.at[b, y, x],
                            csend.at[i], crecv.at[i], p.core_peer(),
                        )
                    )
            return copies

        def one_block(b, carry):
            slot = lax.rem(b, 2)

            @pl.when(b >= 2)
            def _():
                for copy in cores(b - 2):
                    copy.wait_send()

            block_grad(b, slot)
            for copy in cores(b):
                copy.start()
            for y in range(Y):
                for x in range(X):
                    here = pl.multiple_of(p.keyof(y, x, p.c) * piece, 16)
                    core_acc[b, y, x] = dw[slot, pl.ds(here, piece)]
            return carry

        lax.fori_loop(0, blocks // 2, one_block, 0)
        gather_two(1)
        lax.fori_loop(blocks // 2, blocks, one_block, 0)
        gather_three(1)

        def add(i, carry):
            b, y, x = i // (Y * X), lax.rem(i // X, Y), lax.rem(i, X)
            merge_sum([core_acc.at[b, y, x]], [core_in.at[b, y, x]])
            return carry

        def add_block(b, carry):
            for copy in cores(b):
                copy.wait_recv()
            lax.fori_loop(b * Y * X, (b + 1) * Y * X, add, 0)
            return carry

        lax.fori_loop(0, blocks, add_block, 0)
        first, last = pl.ds(0, half), pl.ds(half, half)
        for x in range(X):
            keeps.append((core_acc.at[first, p.y, x], keep_a.at[x]))
            for d in range(1, Y):
                keeps.append((core_acc.at[first, p.yo(d), x], send_a.at[d - 1, x]))
        for y in range(Y):
            keeps.append((core_acc.at[last, y, p.x], keep_b.at[y]))
            for d in range(1, X):
                keeps.append((core_acc.at[last, y, p.xo(d)], send_b.at[d - 1, y]))
        keeps = [pltpu.make_async_copy(src, dst, dwsem.at[i]) for i, (src, dst) in enumerate(keeps)]
        for copy in keeps:
            copy.start()
        for copy in keeps:
            copy.wait()
        for b in (blocks - 2, blocks - 1):
            for copy in cores(jnp.int32(b)):
                copy.wait_send()
    else:
        copies = []
        for b in range(blocks):
            slot = b % 2
            if b >= 2:
                copies[b - 2].wait()
            block_grad(b, slot)
            copies.append(
                pltpu.make_async_copy(
                    dw.at[slot], dw_out.at[pl.ds(b * BLOCK_COLUMNS, BLOCK_COLUMNS)], dwsem.at[slot]
                )
            )
            copies[-1].start()
            if b == blocks // 2:
                gather_two(1)
        for copy in copies[-2:]:
            copy.wait()
        gather_three(1)
    for item in merges:
        item.drain()
    for copy in wremote:
        copy.wait_send()
    for m in range(micro):
        for item, copy in gathers[m]:
            item.finish()


def middle(mesh_dims, o_part, st_part, x_own, cot, weights, vec, bias_up):
    Y, X, R = mesh_dims
    micro, tok, width = x_own.shape
    groups = st_part.shape[1]
    items = micro * groups
    merge_sems = sems_per_item(Y, X) * 2 * items
    strows = 16
    ffw = 2 * FF + width
    blocks = ffw // BLOCK_COLUMNS
    pieces = len(weights) > 1
    outs = [
        (jax.ShapeDtypeStruct((micro, tok, width), BF16), VMEM_SPEC),
        (jax.ShapeDtypeStruct((micro, Y, X, 2, width, tok), BF16), ANY),
        (jax.ShapeDtypeStruct((micro, groups, Y, X, 2, strows, tok), F32), ANY),
        (jax.ShapeDtypeStruct((micro, tok, width), F32), VMEM_SPEC),
        (jax.ShapeDtypeStruct((8, width), F32), VMEM_SPEC),
        (jax.ShapeDtypeStruct((1, FF), F32), VMEM_SPEC),
    ]
    extra = []
    if pieces:
        half, piece = weights[0].shape[:2]
        wsems = 2 * Y * X * half
        outs += [
            (jax.ShapeDtypeStruct((max(Y - 1, 1), X, half, piece, width), BF16), ANY),
            (jax.ShapeDtypeStruct((X, half, piece, width), BF16), ANY),
            (jax.ShapeDtypeStruct((max(X - 1, 1), Y, half, piece, width), BF16), ANY),
            (jax.ShapeDtypeStruct((Y, half, piece, width), BF16), ANY),
        ]
        extra = [
            pltpu.VMEM((blocks, Y, X, piece, width), BF16),
            pltpu.VMEM((blocks, Y, X, piece, width), BF16),
            pltpu.SemaphoreType.DMA((blocks * Y * X,)),
            pltpu.SemaphoreType.DMA((blocks * Y * X,)),
        ]
    else:
        wsems = 1
        outs += [(jax.ShapeDtypeStruct((ffw, width), BF16), ANY)]
    return pl.pallas_call(
        functools.partial(middle_kernel, Y, X, R, blocks, pieces),
        out_shape=tuple(o for o, _ in outs),
        in_specs=[ANY, ANY, VMEM_SPEC, VMEM_SPEC, VMEM_SPEC, VMEM_SPEC] + [ANY] * len(weights),
        out_specs=tuple(spec for _, spec in outs),
        scratch_shapes=scatter_scratch(Y, X, items, (GROUP * HD, tok), BF16, None)
        + scatter_scratch(Y, X, items, (2 * GROUP, tok), F32, None)
        + [
            pltpu.SemaphoreType.DMA((merge_sems,)),
            pltpu.SemaphoreType.DMA((merge_sems,)),
            pltpu.SemaphoreType.DMA((items * 2,)),
            pltpu.SemaphoreType.DMA((merge_sems,)),
            pltpu.SemaphoreType.DMA((merge_sems,)),
            pltpu.SemaphoreType.DMA((items * 2,)),
            pltpu.SemaphoreType.DMA((wsems,)),
            pltpu.SemaphoreType.DMA((wsems,)),
            pltpu.SemaphoreType.DMA((wsems,)),
            pltpu.SemaphoreType.DMA((2 * X * Y,)),
            pltpu.VMEM((ffw, width), BF16),
            pltpu.VMEM((micro, width, tok), BF16),
            pltpu.VMEM((micro, tok, width), BF16),
            pltpu.VMEM((micro, tok, width), BF16),
            pltpu.VMEM((micro, tok, FF), BF16),
            pltpu.VMEM((micro, tok, FF), BF16),
            pltpu.VMEM((tok, FF), F32),
            pltpu.VMEM((micro, tok, width), BF16),
            pltpu.VMEM((micro, tok, width), BF16),
            pltpu.VMEM((tok, width), F32),
            pltpu.VMEM((tok, width), F32),
            pltpu.VMEM((micro, width, tok), BF16),
            pltpu.VMEM((micro, groups, strows, tok), F32),
            pltpu.VMEM((2, BLOCK_COLUMNS, width), BF16),
        ]
        + extra,
        compiler_params=pltpu.CompilerParams(
            collective_id=2, has_side_effects=True, vmem_limit_bytes=VMEM_LIMIT
        ),
        name="middle",
    )(o_part, st_part, x_own, cot, vec, bias_up, *weights)


def tail_kernel(
    Y, X, R, inverse,
    dq_ref, dk_hbm, dv_hbm, x_hbm, dz_hbm, w_ref, vec_ref, bu_ref, xg_ref, dqs_hbm, *refs,
):
    suma_hbm, got_a, sumb_hbm, got_b = refs[0], refs[1:X], refs[X], refs[X + 1 : X + Y]
    tok_ref, late_ref, early_ref, sum_ref = refs[X + Y : X + Y + 4]
    (
        qa, q1, q2, q3, send, recv, loc,
        part, a, r1, r2, r3, bsend, brecv, bloc,
        fin, stage, rz, zsend, zrecv, qf, qz, rq, qsend, qrecv,
        small, sbuf, ssend, srecv, w, wsem, dq, dqv, xv, acc, vsem,
        dk_ref, dv_ref, x_ref, dqs_ref, sum_a, sum_b, dz_ref, fsem,
    ) = refs[X + Y + 4 :]
    p = Place(Y, X, R)
    micro, tok, width = x_ref.shape
    slots_here = late_ref.shape[0]
    groups = qa.shape[0] // micro
    rows = GROUP * HD
    n = sems_per_item(Y, X)
    piece = part.shape[4]
    p.announce(True)
    outer = (dk_hbm, dv_hbm, x_hbm, dqs_hbm, suma_hbm, sumb_hbm, dz_hbm)
    inner = (dk_ref, dv_ref, x_ref, dqs_ref, sum_a, sum_b, dz_ref)
    fetch = [pltpu.make_async_copy(a, b, fsem.at[i]) for i, (a, b) in enumerate(zip(outer, inner))]
    loads = [
        pltpu.make_async_copy(dq_ref, dqv, vsem.at[0]),
        pltpu.make_async_copy(xg_ref, xv, vsem.at[1]),
    ]
    wcopy = pltpu.make_async_copy(w_ref, w, wsem)
    for copy in fetch + loads + [wcopy]:
        copy.start()
    p.meet()
    qitems = []
    for m in range(micro):
        for g in range(groups):
            i = m * groups + g
            item = Scatter(
                p, [dq_ref.at[m, :, :, :, pl.ds(g * rows, rows)]],
                [qa.at[i]], [q1.at[i]], [q2.at[i]], [q3.at[i]],
                send, recv, loc, i * n, i, g % 2 == 0, merge_sum,
            )
            item.start1()
            qitems.append(item)

    for copy in fetch[:6]:
        copy.wait()
    for at, total, got in ((p.x, sum_a, got_a), (p.y, sum_b, got_b)):
        count = total.shape[1]
        base = 0 if total is sum_a else count

        def add(b, carry, at=at, total=total, got=got, base=base):
            value = total[at, b].astype(F32)
            for ref in got:
                value = value + ref[b].astype(F32)
            fin[base + b] = value.astype(BF16)
            return carry

        lax.fori_loop(0, count, add, 0)

    def reorder(s, carry):
        stage[s] = fin[jnp.maximum(inverse[s] - EARLY, 0)]
        return carry

    lax.fori_loop(0, stage.shape[0], reorder, 0)
    zcopies = []
    if R == 4:
        near = p.r + 1 - 2 * lax.rem(p.r, 2)
        far = p.ro(2)
        classes = (p.r, far)
        one = [
            [
                remote(
                    stage.at[q * slots_here + s], rz.at[k, s], zsend.at[k, s], zrecv.at[k, s], {"rows": near}
                )
                for k, q in enumerate((near, lax.rem(near + 2, R)))
            ]
            for s in range(slots_here)
        ]
        two = [
            remote(stage.at[far * slots_here + s], rz.at[2, s], zsend.at[2, s], zrecv.at[2, s], {"rows": far})
            for s in range(slots_here)
        ]
        for copies in one:
            for copy in copies:
                copy.start()

        def z_pass(s):
            for copy in one[s]:
                copy.wait_recv()
            for k, q in enumerate(classes):
                merge_sum([stage.at[q * slots_here + s]], [rz.at[k, s]])
            two[s].start()

        def z_total(s):
            two[s].wait_recv()
            return stage[p.r * slots_here + s].astype(F32) + rz[2, s].astype(F32)

        zcopies = [copy for copies in one for copy in copies] + two
    else:
        for d in range(1, R):
            there = pl.ds(p.ro(d) * slots_here, slots_here)
            copy = remote(stage.at[there], rz.at[d - 1], zsend.at[d - 1, 0], zrecv.at[d - 1, 0], p.z_peer(d))
            copy.start()
            zcopies.append(copy)

        def z_pass(s):
            pass

        def z_total(s):
            if s == 0:
                for copy in zcopies:
                    copy.wait_recv()
            total = stage[p.r * slots_here + s].astype(F32)
            for d in range(1, R):
                total = total + rz[d - 1, s].astype(F32)
            return total

    def product(ref, first, count):
        total = dot_f32(ref[0, first : first + count], x_ref[0], ((1,), (0,)))
        for m in range(1, micro):
            total = total + dot_f32(ref[m, first : first + count], x_ref[m], ((1,), (0,)))
        return total.astype(BF16)

    def put(b, first, value):
        at = 0
        while at < value.shape[0]:
            key, off = divmod(first + at, piece)
            count = min(piece - off, value.shape[0] - at)
            y, x, c = key // (2 * X), key // 2 % X, key % 2
            part[b, y, x, c, off : off + count] = value[at : at + count]
            at += count

    cuts = ((0, piece // 32 * 16, True), (piece // 32 * 16, piece - piece // 32 * 16, False))

    def block_items(b):
        out = []
        for t, (first, count, y_first) in enumerate(cuts):
            ds = pl.ds(first, count)
            i = b * len(cuts) + t
            out.append(
                Scatter(
                    p, [part.at[b, :, :, :, ds]], [a.at[b, :, :, ds]], [r1.at[b, :, :, ds]],
                    [r2.at[b, :, :, ds]], [r3.at[b, :, ds]],
                    bsend, brecv, bloc, i * n, i, y_first, merge_sum,
                )
            )
        return out

    class Block:
        def __init__(self, b):
            self.b, self.items = b, block_items(b)
            self.one = [
                remote(qz.at[b, p.ro(d)], rq.at[b, d - 1], qsend.at[b, 0, d], qrecv.at[b, 0, d], p.z_peer(d))
                for d in range(1, R)
            ]
            mine = early_ref.at[b, p.r]
            self.two = [
                remote(mine, mine, qsend.at[b, 1, d], qrecv.at[b, 1, d], p.z_peer(d)) for d in range(1, R)
            ]

        def step(self, name):
            for item in self.items:
                getattr(item, name)()

        def z_one(self):
            for item, (first, count, _) in zip(self.items, cuts):
                (val,) = item.finish()
                qf[first : first + count] = val[...].astype(F32)
            share = qz.shape[2]
            for i in range(R):
                qz[self.b, i] = qf[i * share : (i + 1) * share].astype(BF16)
            for copy in self.one:
                copy.start()

        def z_two(self):
            for copy in self.one:
                copy.wait_recv()
            total = qz[self.b, p.r].astype(F32)
            for d in range(1, R):
                total = total + rq[self.b, d - 1].astype(F32)
            early_ref[self.b, p.r] = total.astype(BF16)
            for copy in self.two:
                copy.start()

        def finish(self):
            for copy in self.two:
                copy.wait_recv()
            for item in self.items:
                item.drain()
            for copy in self.one + self.two:
                copy.wait_send()

    ones = jnp.ones((8, tok), BF16)
    bias_v = dot_f32(ones, dv_ref[0], ((1,), (1,)))
    sum_q = dqs_ref[0]
    for m in range(1, micro):
        bias_v = bias_v + dot_f32(ones, dv_ref[m], ((1,), (1,)))
        sum_q = sum_q + dqs_ref[m]
    sums = [sum_q.T[:1], bias_v[:1], vec_ref[:3]]
    sums += [bu_ref[:, i * width : (i + 1) * width] for i in range(FF // width)]
    sums += [vec_ref[3:6], jnp.zeros((4, width), F32)]
    small[...] = jnp.concatenate(sums, axis=0).astype(BF16)
    stages = [[p.core_peer()]]
    stages.append([p.x_peer(d) for d in range(1, X)])
    stages.append([p.y_peer(d) for d in range(1, Y)])
    stages.append([p.z_peer(d) for d in range(1, R)])
    scopies = []
    at = 0
    for peers in stages:
        row = []
        for peer in peers:
            row.append(remote(small, sbuf.at[at], ssend.at[at], srecv.at[at], peer))
            at += 1
        scopies.append(row)

    def small_start(t):
        for copy in scopies[t]:
            copy.start()

    def small_wait(t):
        at = sum(len(row) for row in scopies[:t])
        for copy in scopies[t]:
            copy.wait_recv()
        for copy in scopies[t]:
            copy.wait_send()
        total = small[...].astype(F32)
        for i in range(len(scopies[t])):
            total = total + sbuf[at + i].astype(F32)
        return total

    def token_grad(m):
        total = dz_ref[m] + dot_f32(dq[m], w[:width], ((0,), (0,)))
        total = total + dot_f32(dk_ref[m], w[width : 2 * width], ((0,), (0,)))
        total = total + dot_f32(dv_ref[m], w[2 * width :], ((0,), (0,)))
        tok_ref[m] = total.astype(BF16)

    small_start(0)
    block0, block1 = Block(0), Block(1)
    half = width // 2
    put(1, 0, product(dk_ref, half, half))
    small[...] = small_wait(0).astype(BF16)
    small_start(1)
    put(1, half, product(dv_ref, 0, width))
    block1.step("start1")
    small[...] = small_wait(1).astype(BF16)
    small_start(2)
    put(0, width, product(dk_ref, 0, half))
    small[...] = small_wait(2).astype(BF16)
    small_start(3)
    first, last = qitems[: len(qitems) - groups], qitems[len(qitems) - groups :]
    for item in first:
        item.start2()
    for copy in loads:
        copy.wait()
    acc[...] = jnp.zeros_like(acc)
    line = 2 * X * tok

    def query_grad(i, carry):
        m, y = i // Y, lax.rem(i, Y)
        left = jnp.concatenate([dqv[m, y, x, c] for x in range(X) for c in range(2)], axis=1)
        right = xv[m, pl.ds(pl.multiple_of(y * line, line), line)]
        acc[...] += dot_f32(left, right, ((1,), (0,)))
        return carry

    lax.fori_loop(0, micro * Y, query_grad, 0)
    put(0, 0, acc[...].astype(BF16))
    block0.step("start1")
    block1.step("start2")
    z_pass(0)
    block0.step("start2")
    for s in range(1, slots_here):
        z_pass(s)
    block1.step("start3")
    block0.step("start3")
    for item in last:
        item.start2()
    for item in first:
        item.start3()
    block1.z_one()
    block0.z_one()
    for item in last:
        item.start3()
    block1.z_two()
    block0.z_two()
    for s in range(slots_here):
        late_ref[s] = z_total(s)
    wcopy.wait()
    fetch[6].wait()
    for m in range(micro):
        for g in range(groups):
            (val,) = qitems[m * groups + g].finish()
            dq[m, g * rows : (g + 1) * rows, :] = val[...]
        total = dz_ref[m] + dot_f32(dq[m], w[:width], ((0,), (0,)))
        total = total + dot_f32(dk_ref[m], w[width : 2 * width], ((0,), (0,)))
        total = total + dot_f32(dv_ref[m], w[2 * width :], ((0,), (0,)))
        tok_ref[m] = total.astype(BF16)
    sum_ref[...] = small_wait(3)
    block1.finish()
    block0.finish()
    for item in qitems:
        item.drain()
    for copy in zcopies:
        copy.wait_send()


def tail(mesh_dims, inverse, dq_part, dk, dv, x_own, grad_one, w_early, fin_a, fin_b, dvec, d_bias_up, x_all, dq_sum):
    Y, X, R = mesh_dims
    micro, tok, width = x_own.shape
    half, n = fin_a[0].shape[1:3]
    late = 2 * half
    blocks = EARLY + late
    slots_here = blocks // R
    groups = width // (GROUP * HD)
    items = micro * groups
    per = sems_per_item(Y, X)
    share = n // R
    cuts = 2
    small = (16, width)
    hops = 1 + (X - 1) + (Y - 1) + (R - 1)
    return pl.pallas_call(
        functools.partial(tail_kernel, Y, X, R),
        out_shape=(
            jax.ShapeDtypeStruct((micro, tok, width), BF16),
            jax.ShapeDtypeStruct((slots_here, n, width), F32),
            jax.ShapeDtypeStruct((EARLY, R, share, width), BF16),
            jax.ShapeDtypeStruct(small, F32),
        ),
        in_specs=[pl.BlockSpec(memory_space=pltpu.SMEM), ANY]
        + [ANY] * 4
        + [ANY, VMEM_SPEC, VMEM_SPEC, ANY, ANY]
        + ([ANY] + [VMEM_SPEC] * (X - 1) + [ANY] + [VMEM_SPEC] * (Y - 1)),
        out_specs=(VMEM_SPEC,) * 4,
        scratch_shapes=scatter_scratch(Y, X, items, (GROUP * HD, tok), BF16, None)
        + [
            pltpu.SemaphoreType.DMA((per * items,)),
            pltpu.SemaphoreType.DMA((per * items,)),
            pltpu.SemaphoreType.DMA((items,)),
            pltpu.VMEM((EARLY, Y, X, 2, n, width), BF16),
        ]
        + scatter_scratch(Y, X, EARLY, (n, width), BF16, None)
        + [
            pltpu.SemaphoreType.DMA((per * EARLY * cuts,)),
            pltpu.SemaphoreType.DMA((per * EARLY * cuts,)),
            pltpu.SemaphoreType.DMA((EARLY * cuts,)),
            pltpu.VMEM((late, n, width), BF16),
            pltpu.VMEM((blocks, n, width), BF16),
            pltpu.VMEM((R - 1, slots_here, n, width), BF16),
            pltpu.SemaphoreType.DMA((R - 1, slots_here)),
            pltpu.SemaphoreType.DMA((R - 1, slots_here)),
            pltpu.VMEM((n, width), F32),
            pltpu.VMEM((EARLY, R, share, width), BF16),
            pltpu.VMEM((EARLY, R - 1, share, width), BF16),
            pltpu.SemaphoreType.DMA((EARLY, 2, R)),
            pltpu.SemaphoreType.DMA((EARLY, 2, R)),
            pltpu.VMEM(small, BF16),
            pltpu.VMEM((hops,) + small, BF16),
            pltpu.SemaphoreType.DMA((hops,)),
            pltpu.SemaphoreType.DMA((hops,)),
            pltpu.VMEM((3 * width, width), BF16),
            pltpu.SemaphoreType.DMA,
            pltpu.VMEM((micro, width, tok), BF16),
            pltpu.VMEM(dq_part.shape, BF16),
            pltpu.VMEM(x_all.shape, BF16),
            pltpu.VMEM((width, width), F32),
            pltpu.SemaphoreType.DMA((2,)),
            pltpu.VMEM(dk.shape, BF16),
            pltpu.VMEM(dv.shape, BF16),
            pltpu.VMEM(x_own.shape, BF16),
            pltpu.VMEM(dq_sum.shape, F32),
            pltpu.VMEM(fin_a[0].shape, BF16),
            pltpu.VMEM(fin_b[0].shape, BF16),
            pltpu.VMEM(grad_one.shape, F32),
            pltpu.SemaphoreType.DMA((7,)),
        ],
        compiler_params=pltpu.CompilerParams(
            collective_id=5, has_side_effects=True, vmem_limit_bytes=VMEM_LIMIT
        ),
        name="tail",
    )(inverse, dq_part, dk, dv, x_own, grad_one, w_early.reshape(3 * width, width), dvec, d_bias_up, x_all, dq_sum, *fin_a, *fin_b)


def project_kernel(scale, x_ref, own_ref, w_ref, vec_ref, q_ref, k_ref, v_ref, bias):
    width = x_ref.shape[2]

    @pl.when((pl.program_id(0) == 0) & (pl.program_id(1) == 0))
    def _():
        bias[...] = vec_ref[...].T

    q = dot_f32(w_ref[:width], x_ref[0], ((1,), (1,))) + bias[:, 6:7]
    q_ref[0] = q.astype(BF16) * jnp.asarray(scale, BF16)

    @pl.when(pl.program_id(1) == 0)
    def _():
        own = own_ref[0]
        k_ref[0] = dot_f32(w_ref[width : 2 * width], own, ((1,), (1,))).astype(BF16)
        v_ref[0] = (dot_f32(w_ref[2 * width :], own, ((1,), (1,))) + bias[:, 7:8]).astype(BF16)


def project(x_all, x_own, w_t, vec, scale):
    micro, slots, width = x_all.shape
    own = x_own.shape[1]
    wide = min(1024, slots)
    return pl.pallas_call(
        functools.partial(project_kernel, scale),
        grid=(micro, slots // wide),
        out_shape=(
            jax.ShapeDtypeStruct((micro, width, slots), BF16),
            jax.ShapeDtypeStruct((micro, width, own), BF16),
            jax.ShapeDtypeStruct((micro, width, own), BF16),
        ),
        in_specs=[
            pl.BlockSpec((1, wide, width), lambda m, t: (m, t, 0)),
            pl.BlockSpec((1, own, width), lambda m, t: (m, 0, 0)),
            pl.BlockSpec((3 * width, width), lambda m, t: (0, 0)),
            pl.BlockSpec((8, width), lambda m, t: (0, 0)),
        ],
        out_specs=(
            pl.BlockSpec((1, width, wide), lambda m, t: (m, 0, t)),
            pl.BlockSpec((1, width, own), lambda m, t: (m, 0, 0)),
            pl.BlockSpec((1, width, own), lambda m, t: (m, 0, 0)),
        ),
        scratch_shapes=[pltpu.VMEM((width, 8), F32)],
        compiler_params=pltpu.CompilerParams(vmem_limit_bytes=VMEM_LIMIT),
        cost_estimate=pl.CostEstimate(
            flops=2 * micro * width * width * (slots + 2 * own),
            bytes_accessed=4 * micro * width * slots,
            transcendentals=0,
        ),
        name="project",
    )(x_all, x_own, w_t, vec)


def attention_forward_kernel(q_ref, k_ref, v_ref, prev_ref, segk_ref, segq_ref, *refs):
    logit_ref, e_ref, o_ref, st_ref, top_ref, mask_ref = refs[-6:]
    h = pl.program_id(0)
    chunks, wide = o_ref.shape[1], o_ref.shape[3]

    @pl.when(h == 0)
    def _():
        mask_ref[...] = jnp.where(segk_ref[0] == segq_ref[0], 0.0, NEG_BIG)

    for i in range(PER):
        rows = slice(i * HD, (i + 1) * HD)
        hg = lax.rem(h * PER + i, GROUP)
        score = dot_f32(k_ref[rows], q_ref[rows], ((0,), (0,)))
        raw = score + prev_ref[0, 0, i].astype(F32)
        logit_ref[0, 0, i] = raw.astype(BF16)
        masked = raw + mask_ref[...]
        top = jnp.maximum(jnp.max(masked, axis=0, keepdims=True), NEG_FLOOR)
        expo = jnp.exp(masked - top)
        total = jnp.sum(expo, axis=0, keepdims=True)
        low = expo.astype(BF16)
        e_ref[0, i] = low
        out = dot_f32(v_ref[rows], low, ((1,), (0,))).astype(BF16)
        for t in range(chunks):
            cols = slice(t * wide, (t + 1) * wide)
            o_ref[0, t, rows] = out[:, cols]
            st_ref[0, 0, t, pl.ds(hg, 1), :] = top[:, cols]
            st_ref[0, 0, t, pl.ds(GROUP + hg, 1), :] = total[:, cols]
            top_ref[0, 0, t, pl.ds(hg, 1), :] = top[:, cols]


def attention_forward(m, so_far, q, k, v, prev, segk, segq, chunks, wide):
    micro, _, heads, own, slots = prev.shape
    groups = heads // GROUP
    score = pl.BlockSpec((1, 1, PER, own, slots), lambda h: (m, 0, h, 0, 0))
    stat = pl.BlockSpec((1, 1, chunks, 2 * GROUP, wide), lambda h: (m, h * PER // GROUP, 0, 0, 0))
    return pl.pallas_call(
        attention_forward_kernel,
        grid=(heads // PER,),
        out_shape=(
            jax.ShapeDtypeStruct(prev.shape, BF16),
            jax.ShapeDtypeStruct((micro, heads, own, slots), BF16),
            jax.ShapeDtypeStruct((micro, chunks, heads * HD, wide), BF16),
            jax.ShapeDtypeStruct((micro, groups, chunks, 2 * GROUP, wide), F32),
            jax.ShapeDtypeStruct((micro, groups, chunks, 2 * GROUP, wide), F32),
        ),
        in_specs=[
            pl.BlockSpec((None, PER * HD, slots), lambda h: (m, h, 0)),
            pl.BlockSpec((None, PER * HD, own), lambda h: (m, h, 0)),
            pl.BlockSpec((None, PER * HD, own), lambda h: (m, h, 0)),
            score,
            pl.BlockSpec((1, own, 1), lambda h: (m, 0, 0)),
            pl.BlockSpec((1, 1, slots), lambda h: (m, 0, 0)),
        ]
        + [ANY] * len(so_far),
        out_specs=(
            score,
            pl.BlockSpec((1, PER, own, slots), lambda h: (m, h, 0, 0)),
            pl.BlockSpec((1, chunks, PER * HD, wide), lambda h: (m, 0, h, 0)),
            stat,
            stat,
        ),
        input_output_aliases={6 + i: i for i in range(len(so_far))},
        scratch_shapes=[pltpu.VMEM((own, slots), F32)],
        compiler_params=pltpu.CompilerParams(vmem_limit_bytes=VMEM_LIMIT),
        cost_estimate=pl.CostEstimate(
            flops=heads * 2 * 2 * own * slots * HD,
            bytes_accessed=heads * own * slots * 6,
            transcendentals=heads * own * slots,
        ),
        name="attention_forward",
    )(q, k, v, prev, segk, segq, *so_far)


def attention_backward_kernel(
    scale, first, e_ref, d_ref, st_ref, top_ref, q_ref, k_ref, v_ref, *refs
):
    g_ref, dq_ref, dk_ref, dv_ref, sum_ref = refs[-5:]
    h = pl.program_id(0) + first
    chunks, wide = d_ref.shape[1], d_ref.shape[3]
    for i in range(PER):
        rows = slice(i * HD, (i + 1) * HD)
        hg = lax.rem(h * PER + i, GROUP)

        def row(ref, first):
            return jnp.concatenate([ref[0, 0, t, pl.ds(first + hg, 1), :] for t in range(chunks)], axis=1)

        weight = jnp.exp(row(top_ref, 0) - row(st_ref, 0)) * row(st_ref, GROUP)
        dots = row(st_ref, 2 * GROUP) * weight
        low = e_ref[0, i]
        datt = jnp.concatenate([d_ref[0, t, rows] for t in range(chunks)], axis=1)
        grad_in = (datt.astype(F32) * weight).astype(BF16)
        soft = dot_f32(v_ref[rows], grad_in, ((0,), (0,))) - dots
        grad = (low.astype(F32) * soft).astype(BF16)
        g_ref[0, 0, i] = grad
        dq = dot_f32(k_ref[rows], grad, ((1,), (0,))) * scale
        sum_ref[0, rows] = jnp.broadcast_to(jnp.sum(dq, axis=1, keepdims=True), (HD, 128))
        dq = dq.astype(BF16)
        for t in range(chunks):
            dq_ref[0, t, rows] = dq[:, t * wide : (t + 1) * wide]
        dv_ref[0, rows] = dot_f32(grad_in, low, ((1,), (1,))).astype(BF16)
        dk_ref[0, rows] = dot_f32(q_ref[rows], grad, ((1,), (1,))).astype(BF16)


def attention_backward(first, last, so_far, expo, datt, st, tops, q, k, v, scale):
    micro, heads, own, slots = expo.shape
    chunks, wide = datt.shape[1], datt.shape[3]
    steps = heads // PER
    at = lambda i: ((i + first) // steps, (i + first) % steps)
    flops = heads * 2 * 4 * own * slots * HD
    sts = st.shape[3]
    return pl.pallas_call(
        functools.partial(attention_backward_kernel, scale, first),
        grid=(last - first,),
        out_shape=(
            jax.ShapeDtypeStruct((micro, 1, heads, own, slots), BF16),
            jax.ShapeDtypeStruct((micro, chunks, heads * HD, wide), BF16),
            jax.ShapeDtypeStruct((micro, heads * HD, own), BF16),
            jax.ShapeDtypeStruct((micro, heads * HD, own), BF16),
            jax.ShapeDtypeStruct((micro, heads * HD, 128), F32),
        ),
        in_specs=[
            pl.BlockSpec((1, PER, own, slots), lambda i: (*at(i), 0, 0)),
            pl.BlockSpec((1, chunks, PER * HD, wide), lambda i: (at(i)[0], 0, at(i)[1], 0)),
            pl.BlockSpec((1, 1, chunks, sts, wide), lambda i: (at(i)[0], at(i)[1] * PER // GROUP, 0, 0, 0)),
            pl.BlockSpec((1, 1, chunks, 2 * GROUP, wide), lambda i: (at(i)[0], at(i)[1] * PER // GROUP, 0, 0, 0)),
            pl.BlockSpec((None, PER * HD, slots), lambda i: (*at(i), 0)),
            pl.BlockSpec((None, PER * HD, own), lambda i: (*at(i), 0)),
            pl.BlockSpec((None, PER * HD, own), lambda i: (*at(i), 0)),
        ]
        + [ANY] * len(so_far),
        out_specs=(
            pl.BlockSpec((1, 1, PER, own, slots), lambda i: (at(i)[0], 0, at(i)[1], 0, 0)),
            pl.BlockSpec((1, chunks, PER * HD, wide), lambda i: (at(i)[0], 0, at(i)[1], 0)),
            pl.BlockSpec((1, PER * HD, own), lambda i: (*at(i), 0)),
            pl.BlockSpec((1, PER * HD, own), lambda i: (*at(i), 0)),
            pl.BlockSpec((1, PER * HD, 128), lambda i: (*at(i), 0)),
        ),
        input_output_aliases={7 + i: i for i in range(len(so_far))},
        compiler_params=pltpu.CompilerParams(vmem_limit_bytes=VMEM_LIMIT),
        cost_estimate=pl.CostEstimate(
            flops=flops, bytes_accessed=heads * own * slots * 4, transcendentals=0
        ),
        name="attention_backward",
    )(expo, datt, st, tops, q, k, v, *so_far)


def shifted(arr, mesh_dims, dy, dx):
    if dy == 0 and dx == 0:
        return arr
    Y, X, _ = mesh_dims
    key = lambda y, x, c: (y * X + x) * 2 + c
    perm = [
        (key(y, x, c), key((y + dy) % Y, (x + dx) % X, c)) for y in range(Y) for x in range(X) for c in range(2)
    ]
    return lax.ppermute(arr, "keys", perm)


def late_weights_start(mesh_dims, own_first, own_last):
    Y, X, _ = mesh_dims
    first = [shifted(own_first, mesh_dims, 0, dx) for dx in range(X)]
    last = [shifted(own_last, mesh_dims, dy, 0) for dy in range(Y)]
    first_own = [shifted(own_first, mesh_dims, dy, 0) for dy in range(1, Y)]
    last_own = [shifted(own_last, mesh_dims, 0, dx) for dx in range(1, X)]
    return first, last, first_own, last_own


def late_weights_finish(mesh_dims, first, last, first_own, last_own):
    Y, X, _ = mesh_dims
    out = []
    for dy in range(Y):
        for dx in range(X):
            out.append(first_own[dy - 1] if dx == 0 and dy > 0 else shifted(first[dx], mesh_dims, dy, 0))
    for dy in range(Y):
        for dx in range(X):
            out.append(last_own[dx - 1] if dy == 0 and dx > 0 else shifted(last[dy], mesh_dims, 0, dx))
    return out


def late_grads_start(mesh_dims, send_a, keep_a, send_b, keep_b):
    Y, X, _ = mesh_dims
    first = [shifted(send_a[d - 1], mesh_dims, d, 0) for d in range(1, Y)]
    last = [shifted(send_b[d - 1], mesh_dims, 0, d) for d in range(1, X)]
    return (keep_a, first), (keep_b, last)


def late_grads_finish(mesh_dims, first, last):
    Y, X, _ = mesh_dims
    key = lax.axis_index("keys")
    x, y = (key // 2) % X, key // (2 * X)

    def line(keep, got, place, move):
        total = keep.astype(F32)
        for piece in got:
            total = total + piece.astype(F32)
        total = total.astype(BF16)
        count = total.shape[0]
        pick = lambda d: lax.dynamic_index_in_dim(total, (place + d) % count, 0, keepdims=False)
        return [total] + [move(pick(d), d) for d in range(1, count)]

    return (
        line(*first, x, lambda a, d: shifted(a, mesh_dims, 0, d)),
        line(*last, y, lambda a, d: shifted(a, mesh_dims, d, 0)),
    )


def halves(value):
    high = value.astype(BF16)
    return high, (value - high.astype(F32)).astype(BF16)


def update_weights_kernel(
    block_ids, first_column, fixes, late_ref, early_ref, basis_ref, master_ref, one_ref, two_ref,
    grad_out, one_out, two_out, master_out, copy_out, joined,
):
    s = pl.program_id(0)
    block = block_ids[s]
    early = early_ref[jnp.minimum(block, EARLY - 1)].astype(F32)
    share = early.shape[1]
    for i in range(early.shape[0]):
        joined[i * share : (i + 1) * share] = early[i]
    grad = jnp.where(block < EARLY, joined[...], late_ref[0])
    grad_out[0] = grad
    basis = basis_ref[0]
    basis_high, basis_low = halves(basis)

    def product(value, contract):
        n = value.shape[0]
        high, rest = halves(value)
        both = dot_f32(jnp.concatenate([high, rest], axis=0), basis_high, contract)
        return both[:n] + (both[n:] + dot_f32(high, basis_low, contract))

    rotated = product(grad, ((1,), (0,)))
    new_one = BETA_ONE * one_ref[0] + (1.0 - BETA_ONE) * rotated
    new_two = BETA_TWO * two_ref[0] + (1.0 - BETA_TWO) * rotated * rotated
    one_out[0] = new_one
    two_out[0] = new_two
    direction = new_one / fixes[0] / (jnp.sqrt(new_two / fixes[1]) + EPS_ADAM)
    back = product(direction, ((1,), (1,)))
    columns = first_column[s] + lax.broadcasted_iota(jnp.int32, (grad.shape[0], 1), 0)
    master = master_ref[0]
    new_master = master - column_rates(columns) * (back + DECAY * master)
    master_out[0] = new_master
    copy_out[0] = new_master.astype(BF16)


def update_weights(block_ids, first_column, fixes, late, early, basis, master, one, two):
    slots_here, n, width = master.shape
    mat = pl.BlockSpec((1, n, width), lambda s: (s, 0, 0))
    smem = pl.BlockSpec(memory_space=pltpu.SMEM)
    return pl.pallas_call(
        update_weights_kernel,
        grid=(slots_here,),
        out_shape=tuple(jax.ShapeDtypeStruct(master.shape, F32) for _ in range(4))
        + (jax.ShapeDtypeStruct(master.shape, BF16),),
        in_specs=[smem, smem, smem, mat, pl.BlockSpec(early.shape, lambda s: (0, 0, 0, 0)),
                  pl.BlockSpec((1, width, width), lambda s: (s, 0, 0)), mat, mat, mat],
        out_specs=(mat,) * 5,
        scratch_shapes=[pltpu.VMEM((n, width), F32)],
        compiler_params=pltpu.CompilerParams(vmem_limit_bytes=VMEM_LIMIT),
        name="update_weights",
    )(block_ids, first_column, fixes, late, early, basis, master, one, two)


def to_chunks(arr, chunks):
    pieces, rows, own = arr.shape[-3:]
    lead = arr.shape[:-3]
    if pieces == chunks:
        return arr
    per = pieces // chunks
    arr = arr.reshape(lead + (chunks, per, rows, own))
    return jnp.moveaxis(arr, -3, -2).reshape(lead + (chunks, rows, per * own))


def from_chunks(arr, pieces):
    chunks, rows, wide = arr.shape[-3:]
    lead = arr.shape[:-3]
    if pieces == chunks:
        return arr
    per = pieces // chunks
    arr = arr.reshape(lead + (chunks, rows, per, wide // per))
    return jnp.moveaxis(arr, -2, -3).reshape(lead + (pieces, rows, wide // per))


def per_device(
    mesh_dims,
    tokens,
    prev_logits,
    segments,
    out_cot,
    master_mat,
    mom1_mat,
    mom2_mat,
    eigen_bases,
    master_small,
    mom1_small,
    mom2_small,
    owners,
    step_count,
):
    Y, X, R = mesh_dims
    keys = Y * X * 2
    micro, row_count, key_len, width = tokens.shape
    slot_count = prev_logits.shape[4]
    slots_here, _, cols_here = master_mat.shape
    blocks = slots_here * R
    token_count = micro * key_len
    scale = HD ** (-0.5)
    key_index = lax.axis_index("keys")
    row_index = lax.axis_index("rows")
    wide = max(key_len, min(256, slot_count))
    chunks = slot_count // wide
    groups = H // GROUP

    x_own = tokens.reshape(micro, key_len, width)
    w_own = jnp.swapaxes(master_mat, 1, 2).astype(BF16)
    small_low = master_small.astype(BF16).reshape(1, slots_here * cols_here)
    ext = lax.dynamic_update_slice(
        jnp.zeros((EXT, width), BF16), small_low, (row_index, jnp.int32(0))
    )
    fast = cols_here % 16 == 0
    wt, *w_late, ext_all, xg = gather_weights(mesh_dims, owners, w_own, ext, x_own)
    if fast:
        pieces = late_weights_start(mesh_dims, *w_late)
    else:
        late = [lax.all_gather(jnp.concatenate(w_late), "keys", axis=1).reshape(2 * FF + width, width)]
    w_t = wt.reshape(EARLY * BLOCK_COLUMNS, width)
    small_all = ext_all.reshape(keys, EXT, width)[:, :R, : slots_here * cols_here]
    params = (
        jnp.transpose(small_all.reshape(keys, R, slots_here, cols_here), (1, 2, 0, 3))
        .reshape(blocks * GAIN_ROW_WIDTH)
        .astype(F32)
    )
    bias_q = params[:width]
    bias_v = params[width : 2 * width]
    bias_o = params[2 * width : 3 * width]
    gain_one = params[3 * width : 4 * width]
    shift_one = params[4 * width : 5 * width]
    bias_up = params[5 * width : 5 * width + FF]
    bias_down = params[5 * width + FF : 6 * width + FF]
    gain_two = params[6 * width + FF : 7 * width + FF]
    shift_two = params[7 * width + FF :]

    vec = jnp.stack([bias_o, gain_one, shift_one, bias_down, gain_two, shift_two, bias_q, bias_v])
    q_all, k_all, v_all = project(xg.reshape(micro, slot_count, width), x_own, w_t, vec, scale)
    x_rows = x_own.reshape(token_count, width)

    seg_rows = segments.reshape(micro, slot_count)
    seg_keys = lax.dynamic_slice_in_dim(seg_rows, key_index * key_len, key_len, 1)
    forward = ()
    for m in range(micro):
        forward = attention_forward(
            m, forward, q_all, k_all, v_all, prev_logits,
            seg_keys[:, :, None], seg_rows[:, None, :], chunks, wide,
        )
        if m == 0 and fast:
            forward, first, last = lax.optimization_barrier((tuple(forward), *pieces[:2]))
            late = late_weights_finish(mesh_dims, first, last, *pieces[2:])
    logits, expo, o_part, st_part, tops = forward
    o_part = from_chunks(o_part, keys).reshape(micro, Y, X, 2, width, key_len)
    st_part = from_chunks(st_part, keys).reshape(micro, groups, Y, X, 2, 2 * GROUP, key_len)
    out_hidden, datt_all, st_all, grad_one, dvec, d_bias_up, *dw_late = middle(
        mesh_dims, o_part, st_part, x_own, out_cot.reshape(x_own.shape), late, vec, bias_up[None]
    )
    out_hidden = out_hidden.reshape(tokens.shape)
    datt_all = to_chunks(datt_all.reshape(micro, keys, width, key_len), chunks)
    st_all = to_chunks(st_all.reshape(micro, groups, keys, 16, key_len), chunks)
    so_far = ()
    if fast:
        first, last = late_grads_start(mesh_dims, *dw_late)
    steps = micro * (H // PER)
    turns = (0, steps * 5 // 8, steps)
    for turn in range(2):
        so_far = attention_backward(
            turns[turn], turns[turn + 1], so_far, expo, datt_all, st_all, tops, q_all, k_all, v_all, scale
        )
        if turn == 0 and fast:
            so_far, first, last = lax.optimization_barrier((tuple(so_far), first, last))
            fin = late_grads_finish(mesh_dims, first, last)
    grad_prev, dq_part, dk, dv, dq_sum = so_far
    dq_part = from_chunks(dq_part, keys).reshape(micro, Y, X, 2, width, key_len)
    inverse = inverse_order(owners)
    slot_index_list = row_index * slots_here + jnp.arange(slots_here, dtype=jnp.int32)
    block_ids = jnp.take(inverse, slot_index_list)
    if fast:
        grad_tokens, mine_late, mine_early, small_sum = tail(
            mesh_dims, inverse, dq_part, dk, dv, x_own, grad_one, wt, *fin, dvec, d_bias_up,
            xg.reshape(micro, slot_count, width), dq_sum,
        )
    else:
        dq = lax.psum_scatter(
            dq_part.reshape(micro, keys, width, key_len), "keys", scatter_dimension=1, tiled=True
        ).reshape(micro, width, key_len)
        grad_proj = jnp.swapaxes(jnp.concatenate([dq, dk, dv], axis=1), 0, 1).reshape(
            3 * width, token_count
        )
        d_qkv = dot_f32(grad_proj, x_rows, ((1,), (0,))).astype(BF16)
        grad_tokens = (
            grad_one.reshape(token_count, width) + dot_f32(grad_proj, w_t, ((0,), (0,)))
        ).astype(BF16)
        sums = jnp.sum(grad_proj.astype(F32).reshape(3, width, token_count), axis=2)
        small_sum = lax.psum(
            jnp.concatenate(
                [sums[0][None], sums[2][None], dvec[:3], d_bias_up.reshape(FF // width, width), dvec[3:6]]
            ),
            ("rows", "keys"),
        )
        grads = jnp.concatenate([d_qkv, dw_late[0]], axis=0).reshape(blocks, keys, cols_here, width)
        grads = lax.psum_scatter(grads, "keys", scatter_dimension=1, tiled=True)
        grads = jnp.take(grads.reshape(blocks, cols_here, width), inverse, axis=0)
        mine_t = lax.psum_scatter(grads, "rows", scatter_dimension=0, tiled=True).astype(F32)
    grad_tokens = grad_tokens.reshape(tokens.shape)
    flat = small_sum.reshape(-1)[: blocks * GAIN_ROW_WIDTH].reshape(blocks, GAIN_ROW_WIDTH)
    mine_small = lax.dynamic_slice(
        flat, (row_index * slots_here, key_index * cols_here), (slots_here, cols_here)
    )

    steps_done = step_count[0].astype(F32)
    fix_one = 1.0 - jnp.power(jnp.asarray(BETA_ONE, F32), steps_done)
    fix_two = 1.0 - jnp.power(jnp.asarray(BETA_TWO, F32), steps_done)
    if fast:
        first_column = block_ids * BLOCK_COLUMNS + key_index * cols_here
        mats = [jnp.swapaxes(a, 1, 2) for a in (master_mat, mom1_mat, mom2_mat)]
        updated = update_weights(
            block_ids, first_column, jnp.stack([fix_one, fix_two]), mine_late, mine_early, eigen_bases, *mats
        )
        mine_mat, new_one, new_two, new_master, copy_mat = (jnp.swapaxes(a, 1, 2) for a in updated)
    else:
        mine_mat = jnp.swapaxes(mine_t, 1, 2)
        rotated = jnp.einsum("sed,sec->sdc", eigen_bases, mine_mat, precision=HIGHEST_PREC)
        new_one = BETA_ONE * mom1_mat + (1.0 - BETA_ONE) * rotated
        new_two = BETA_TWO * mom2_mat + (1.0 - BETA_TWO) * rotated * rotated
        direction = new_one / fix_one / (jnp.sqrt(new_two / fix_two) + EPS_ADAM)
        back_rot = jnp.einsum("sdk,skc->sdc", eigen_bases, direction, precision=HIGHEST_PREC)
        columns = (
            block_ids[:, None] * (cols_here * keys)
            + key_index * cols_here
            + jnp.arange(cols_here, dtype=jnp.int32)[None, :]
        )
        rates = column_rates(columns)[:, None, :]
        new_master = master_mat - rates * (back_rot + DECAY * master_mat)
        copy_mat = new_master.astype(BF16)
    small_one = BETA_ONE * mom1_small + (1.0 - BETA_ONE) * mine_small
    small_two = BETA_TWO * mom2_small + (1.0 - BETA_TWO) * mine_small * mine_small
    new_small = master_small - RATE_SMALL * (small_one / fix_one) / (
        jnp.sqrt(small_two / fix_two) + EPS_ADAM
    )
    return (
        out_hidden,
        logits,
        grad_tokens,
        grad_prev,
        mine_mat,
        new_one,
        new_two,
        new_master,
        copy_mat,
        mine_small,
        small_one,
        small_two,
        new_small,
        new_small.astype(BF16),
    )


def solution(mesh):
    chips = mesh.shape["keys"] // 2
    side = math.isqrt(chips)
    dims = (side, side, mesh.shape["rows"]) if side * side == chips else (1, chips, mesh.shape["rows"])
    acts = P(None, "rows", "keys", None)
    scores = P(None, "rows", None, "keys", None)
    mats = P("rows", None, "keys")
    smalls = P("rows", "keys")
    return jax.shard_map(
        functools.partial(per_device, dims),
        mesh=mesh,
        in_specs=(
            acts, scores, P(None, "rows", None), acts, mats, mats, mats,
            P("rows", None, None), smalls, smalls, smalls, P(), P(),
        ),
        out_specs=(acts, scores, acts, scores) + (mats,) * 5 + (smalls,) * 5,
        check_vma=False,
    )
```

```python
import functools
import math

import jax
import jax.numpy as jnp
from jax import lax
from jax.experimental import pallas as pl
from jax.experimental.pallas import tpu as pltpu
from jax.sharding import PartitionSpec as P

MODEL_WIDTH = 768
H = 12
HD = 64
FF = 3072
BLOCK_COLUMNS = 1152
GAIN_ROW_WIDTH = 1152

EPS_NORM = 1e-06
BETA_ONE = 0.95
BETA_TWO = 0.95
EPS_ADAM = 1e-08
DECAY = 0.01
RATE_SMALL = 0.3
NEG_BIG = -1e30
NEG_FLOOR = -1e29
HIGHEST_PREC = lax.Precision.HIGHEST
MESH = pl.DeviceIdType.MESH
F32 = jnp.float32
BF16 = jnp.bfloat16
ANY = pl.BlockSpec(memory_space=pl.ANY)
VMEM_SPEC = pl.BlockSpec(memory_space=pltpu.VMEM)
EXT = 16
EARLY = 2
PER = 3
VMEM_LIMIT = 60 << 20


def layer_norm(value):
    mean_val = jnp.mean(value, axis=-1, keepdims=True)
    centered = value - mean_val
    inv_dev = lax.rsqrt(jnp.mean(centered * centered, axis=-1, keepdims=True) + EPS_NORM)
    return (centered * inv_dev, inv_dev)


def norm_back(grad_in, normed, inv_dev, gain):
    scaled = grad_in * gain
    return inv_dev * (
        scaled
        - jnp.mean(scaled, axis=-1, keepdims=True)
        - normed * jnp.mean(scaled * normed, axis=-1, keepdims=True)
    )


def inverse_order(owners):
    slot_index_list = jnp.arange(owners.shape[0], dtype=jnp.int32)
    matches = (owners[None, :] == slot_index_list[:, None]).astype(jnp.int32)
    return jnp.sum(matches * slot_index_list[None, :], axis=1)


def column_rates(columns):
    inner = MODEL_WIDTH ** (-0.5)
    return jnp.where(
        columns < 3 * MODEL_WIDTH,
        inner,
        jnp.where(
            columns < 4 * MODEL_WIDTH,
            4.0 * inner,
            jnp.where(columns < 4 * MODEL_WIDTH + FF, inner, FF ** (-0.5)),
        ),
    )


def dot_f32(left, right, contract):
    return lax.dot_general(left, right, (contract, ((), ())), preferred_element_type=F32)


class Place:
    def __init__(self, side_y, side_x, rows):
        self.Y, self.X, self.R = side_y, side_x, rows
        key = lax.axis_index("keys")
        self.key = key
        self.r = lax.axis_index("rows")
        self.c = lax.rem(key, 2)
        self.x = lax.rem(key // 2, side_x)
        self.y = key // (2 * side_x)

    def keyof(self, y, x, c):
        return (y * self.X + x) * 2 + c

    def xo(self, d):
        return lax.rem(self.x + d, self.X)

    def yo(self, d):
        return lax.rem(self.y + d, self.Y)

    def ro(self, d):
        return lax.rem(self.r + d, self.R)

    def x_peer(self, d):
        return {"keys": self.keyof(self.y, self.xo(d), self.c)}

    def y_peer(self, d):
        return {"keys": self.keyof(self.yo(d), self.x, self.c)}

    def core_peer(self):
        return {"keys": self.keyof(self.y, self.x, 1 - self.c)}

    def z_peer(self, d):
        return {"rows": self.ro(d)}

    def announce(self, with_z):
        peers = [self.core_peer()]
        peers += [self.x_peer(d) for d in range(1, self.X)]
        peers += [self.y_peer(d) for d in range(1, self.Y)]
        if with_z:
            peers += [self.z_peer(d) for d in range(1, self.R)]
        sem = pltpu.get_barrier_semaphore()
        for peer in peers:
            pl.semaphore_signal(sem, inc=1, device_id=peer, device_id_type=MESH)
        self.greeted = len(peers)

    def meet(self):
        pl.semaphore_wait(pltpu.get_barrier_semaphore(), self.greeted)

    def barrier(self, with_z):
        self.announce(with_z)
        self.meet()


def remote(src, dst, send_sem, recv_sem, peer):
    return pltpu.make_async_remote_copy(
        src_ref=src,
        dst_ref=dst,
        send_sem=send_sem,
        recv_sem=recv_sem,
        device_id=peer,
        device_id_type=MESH,
    )


def sems_per_item(Y, X):
    return (X - 1) + (Y - 1) + 1


class Gather:
    def __init__(self, place, own, buf, send, recv, base, x_first):
        p = place
        self.sent = []
        n = sems_per_item(p.Y, p.X)
        idx = iter(range(base, base + n))
        first = [(p.x_peer(d)) for d in range(1, p.X)] if x_first else [p.y_peer(d) for d in range(1, p.Y)]
        second = [p.y_peer(d) for d in range(1, p.Y)] if x_first else [p.x_peer(d) for d in range(1, p.X)]
        line = buf.at[p.y, :, p.c] if x_first else buf.at[:, p.x, p.c]
        plane = buf.at[:, :, p.c]
        mine = buf.at[p.y, p.x, p.c]
        self.one = []
        for peer in first:
            i = next(idx)
            self.one.append(remote(own, mine, send.at[i], recv.at[i], peer))
        self.two = []
        for peer in second:
            i = next(idx)
            self.two.append(remote(line, line, send.at[i], recv.at[i], peer))
        i = next(idx)
        self.three = [remote(plane, plane, send.at[i], recv.at[i], p.core_peer())]

    def start1(self):
        for copy in self.one:
            copy.start()

    def start2(self):
        for copy in self.one:
            copy.wait_recv()
        for copy in self.two:
            copy.start()

    def start3(self):
        for copy in self.two:
            copy.wait_recv()
        for copy in self.three:
            copy.start()

    def finish(self):
        for copy in self.three:
            copy.wait_recv()
        for copy in self.one + self.two + self.three:
            copy.wait_send()


def gather_weights_kernel(
    Y, X, R, owners, w_ref, ext_ref, x_ref, wt_out, first_out, last_out, ext_out, xg_out,
    zbuf, zext, stage, sext, wlow, zsend, zrecv, send, recv, loc,
):
    p = Place(Y, X, R)
    slots_here = w_ref.shape[0]
    blocks = zbuf.shape[0]
    early = wt_out.shape[0]
    micro = x_ref.shape[0]
    n = sems_per_item(Y, X)
    p.announce(True)
    wlow[...] = w_ref[...].astype(BF16)
    p.meet()
    here = pl.ds(p.r * slots_here, slots_here)

    def hop(src, step, own):
        there = pl.ds(src * slots_here, slots_here)
        way = (step + 1) // 2
        peer = {"rows": p.r + step}
        return [
            remote(wlow if own else zbuf.at[there], zbuf.at[there], zsend.at[way, src, 0], zrecv.at[src, 0], peer),
            remote(ext_ref if own else zext.at[src], zext.at[src], zsend.at[way, src, 1], zrecv.at[src, 1], peer),
        ]

    def can(step):
        return p.r < R - 1 if step > 0 else p.r > 0

    def pass_on(dist, act):
        for step in (1, -1):
            src = p.r - step * dist

            @pl.when((src >= 0) & (src < R) & can(step))
            def _():
                for copy in hop(src, step, dist == 0):
                    act(copy)

    def arrived(dist):
        for step in (1, -1):
            src = p.r - step * dist

            @pl.when((src >= 0) & (src < R))
            def _():
                for copy in hop(src, step, False):
                    copy.wait_recv()

    pass_on(0, lambda copy: copy.start())
    xitems = []
    xlocal = []
    for m in range(micro):
        item = Gather(p, x_ref.at[m], xg_out.at[m], send, recv, m * n, m % 2 == 0)
        item.start1()
        xitems.append(item)
        copy = pltpu.make_async_copy(x_ref.at[m], xg_out.at[m, p.y, p.x, p.c], loc.at[m])
        copy.start()
        xlocal.append(copy)
    wl = pltpu.make_async_copy(wlow, zbuf.at[here], loc.at[micro])
    wl.start()
    el = pltpu.make_async_copy(ext_ref, zext.at[p.r], loc.at[micro + 1])
    el.start()
    for m in range(micro):
        xlocal[m].wait()
        xitems[m].start2()
    for dist in range(1, R):
        arrived(dist)
        pass_on(dist, lambda copy: copy.start())
    wl.wait()
    el.wait()
    sext[...] = jnp.sum(zext[...].astype(F32), axis=0).astype(BF16)

    def reorder(b, carry):
        stage[b] = zbuf[owners[b]]
        return carry

    lax.fori_loop(0, blocks, reorder, 0)
    base = micro * n
    eitem = Gather(p, sext, ext_out, send, recv, base, True)
    base += n
    lcopies = []
    items = []
    for b in range(early):
        item = Gather(p, stage.at[b], wt_out.at[b], send, recv, base, b % 2 == 0)
        base += n
        item.start1()
        items.append(item)
        copy = pltpu.make_async_copy(stage.at[b], wt_out.at[b, p.y, p.x, p.c], loc.at[micro + 3 + b])
        copy.start()
        lcopies.append(copy)
    eitem.start1()
    ecopy = pltpu.make_async_copy(sext, ext_out.at[p.y, p.x, p.c], loc.at[micro + 2])
    ecopy.start()
    late = (blocks - early) // 2
    rest = [
        pltpu.make_async_copy(stage.at[pl.ds(early + i * late, late)], out, loc.at[micro + 3 + early + i])
        for i, out in enumerate((first_out, last_out))
    ]
    for copy in rest:
        copy.start()
    for m in range(micro):
        xitems[m].start3()
    for b in range(early):
        lcopies[b].wait()
        items[b].start2()
    ecopy.wait()
    eitem.start2()
    for b in range(early):
        items[b].start3()
    eitem.start3()
    for item in xitems + [eitem] + items:
        item.finish()
    for dist in range(R):
        pass_on(dist, lambda copy: copy.wait_send())
    for copy in rest:
        copy.wait()


def gather_weights(mesh_dims, owners, w_own, ext, x_own):
    Y, X, R = mesh_dims
    slots_here, n, width = w_own.shape
    micro, tok = x_own.shape[:2]
    blocks = slots_here * R
    total = sems_per_item(Y, X) * (micro + 1 + EARLY)
    return pl.pallas_call(
        functools.partial(gather_weights_kernel, Y, X, R),
        out_shape=(
            jax.ShapeDtypeStruct((EARLY, Y, X, 2, n, width), BF16),
            jax.ShapeDtypeStruct(((blocks - EARLY) // 2, n, width), BF16),
            jax.ShapeDtypeStruct(((blocks - EARLY) // 2, n, width), BF16),
            jax.ShapeDtypeStruct((Y, X, 2, EXT, width), BF16),
            jax.ShapeDtypeStruct((micro, Y, X, 2, tok, width), BF16),
        ),
        in_specs=[pl.BlockSpec(memory_space=pltpu.SMEM), VMEM_SPEC, VMEM_SPEC, VMEM_SPEC],
        out_specs=(ANY,) * 5,
        scratch_shapes=[
            pltpu.VMEM((blocks, n, width), BF16),
            pltpu.VMEM((R, EXT, width), BF16),
            pltpu.VMEM((blocks, n, width), BF16),
            pltpu.VMEM((EXT, width), BF16),
            pltpu.VMEM(w_own.shape, BF16),
            pltpu.SemaphoreType.DMA((2, R, 2)),
            pltpu.SemaphoreType.DMA((R, 2)),
            pltpu.SemaphoreType.DMA((total,)),
            pltpu.SemaphoreType.DMA((total,)),
            pltpu.SemaphoreType.DMA((micro + 5 + EARLY,)),
        ],
        compiler_params=pltpu.CompilerParams(
            collective_id=1, has_side_effects=True, vmem_limit_bytes=VMEM_LIMIT
        ),
        name="gather_weights",
    )(owners, w_own, ext, x_own)


class Scatter:
    def __init__(self, place, parts, accs, r1s, r2s, r3s, send, recv, loc, base, lbase, y_first, merge):
        p = place
        self.p, self.y_first, self.merge = p, y_first, merge
        self.accs, self.r1s, self.r2s, self.r3s = accs, r1s, r2s, r3s
        self.count = len(parts)
        n = sems_per_item(p.Y, p.X) * len(parts)
        idx = iter(range(base, base + n))
        self.zero, self.one, self.two, self.three = [], [], [], []
        for t, part in enumerate(parts):
            i = next(idx)
            self.zero.append(pltpu.make_async_copy(part.at[:, :, p.c], accs[t], loc.at[lbase + t]))
            self.one.append(remote(part.at[:, :, 1 - p.c], r1s[t], send.at[i], recv.at[i], p.core_peer()))
            if y_first:
                for d in range(1, p.Y):
                    i = next(idx)
                    self.two.append(
                        remote(accs[t].at[p.yo(d)], r2s[t].at[d - 1], send.at[i], recv.at[i], p.y_peer(d))
                    )
                for d in range(1, p.X):
                    i = next(idx)
                    self.three.append(
                        remote(accs[t].at[p.y, p.xo(d)], r3s[t].at[d - 1], send.at[i], recv.at[i], p.x_peer(d))
                    )
            else:
                for d in range(1, p.X):
                    i = next(idx)
                    self.two.append(
                        remote(accs[t].at[:, p.xo(d)], r2s[t].at[d - 1], send.at[i], recv.at[i], p.x_peer(d))
                    )
                for d in range(1, p.Y):
                    i = next(idx)
                    self.three.append(
                        remote(accs[t].at[p.yo(d), p.x], r3s[t].at[d - 1], send.at[i], recv.at[i], p.y_peer(d))
                    )

    def start1(self):
        for copy in self.zero + self.one:
            copy.start()

    def start2(self):
        p = self.p
        for copy in self.zero:
            copy.wait()
        for copy in self.one:
            copy.wait_recv()

        def body(i, carry):
            y, x = i // p.X, lax.rem(i, p.X)
            self.merge([a.at[y, x] for a in self.accs], [r.at[y, x] for r in self.r1s])
            return carry

        lax.fori_loop(0, p.Y * p.X, body, 0)
        for copy in self.two:
            copy.start()

    def start3(self):
        p = self.p
        for copy in self.two:
            copy.wait_recv()
        if self.y_first:
            for d in range(1, p.Y):

                def body(x, carry, d=d):
                    self.merge([a.at[p.y, x] for a in self.accs], [r.at[d - 1, x] for r in self.r2s])
                    return carry

                lax.fori_loop(0, p.X, body, 0)
        else:
            for d in range(1, p.X):

                def body(y, carry, d=d):
                    self.merge([a.at[y, p.x] for a in self.accs], [r.at[d - 1, y] for r in self.r2s])
                    return carry

                lax.fori_loop(0, p.Y, body, 0)
        for copy in self.three:
            copy.start()

    def finish(self):
        p = self.p
        for copy in self.three:
            copy.wait_recv()
        mine = [a.at[p.y, p.x] for a in self.accs]
        for d in range(1, p.X if self.y_first else p.Y):
            self.merge(mine, [r.at[d - 1] for r in self.r3s])
        return mine

    def drain(self):
        for copy in self.one + self.two + self.three:
            copy.wait_send()


def merge_sum(into, other):
    a, b = into[0], other[0]
    a[...] = (a[...].astype(F32) + b[...].astype(F32)).astype(BF16)


def merge_soft(into, other):
    (va, sa), (vb, sb) = into, other
    ta, tb = sa[...], sb[...]
    heads = ta.shape[0] // 2
    top_a, top_b = ta[:heads], tb[:heads]
    top = jnp.maximum(top_a, top_b)
    wa, wb = jnp.exp(top_a - top), jnp.exp(top_b - top)
    sa[...] = jnp.concatenate([top, wa * ta[heads:] + wb * tb[heads:]], axis=0)
    for h in range(heads):
        rows = slice(h * HD, (h + 1) * HD)
        va[rows, :] = (
            va[rows, :].astype(F32) * wa[h : h + 1] + vb[rows, :].astype(F32) * wb[h : h + 1]
        ).astype(BF16)


def scatter_scratch(Y, X, items, shape, dtype, y_first_of):
    most = max((Y - 1) * X, (X - 1) * Y)
    return [
        pltpu.VMEM((items, Y, X) + shape, dtype),
        pltpu.VMEM((items, Y, X) + shape, dtype),
        pltpu.VMEM((items, max(Y, X) - 1, max(Y, X)) + shape, dtype),
        pltpu.VMEM((items, max(Y, X) - 1) + shape, dtype),
    ]


GROUP = 3
STAT_ROWS = 8


def middle_kernel(Y, X, R, blocks, pieces, *refs):
    o_ref, st_ref, x_ref, cot_ref, vec_ref, bu_ref = refs[:6]
    refs = refs[6:]
    count = 2 * Y * X if pieces else 1
    w_refs, refs = refs[:count], refs[count:]
    out_ref, datt_out, stat_out, dz_ref, dvec_ref, dbu_ref = refs[:6]
    refs = refs[6:]
    if pieces:
        send_a, keep_a, send_b, keep_b = refs[:4]
        refs = refs[4:]
    else:
        (dw_out,) = refs[:1]
        refs = refs[1:]
    (
        oa, o1, o2, o3, sa, s1, s2, s3, send, recv, loc, gsend, grecv, gloc, wsem, wsend, wrecv, dwsem,
        w, att, attk, low, hid, dpre, slope, df, da, n1, n2, datt, stat, invs_ref, dw,
    ) = refs[:33]
    if pieces:
        core_acc, core_in, csend, crecv = refs[33:]
    p = Place(Y, X, R)
    micro, tok, width = x_ref.shape
    groups = st_ref.shape[1]
    rows = GROUP * HD
    bo, g1, e1, bd, g2, e2 = (vec_ref[i : i + 1] for i in range(6))
    p.announce(False)
    stat[...] = jnp.zeros_like(stat)
    wide = width
    parts = FF // wide
    wcopies, wremote = [], []
    if pieces:
        half, piece = w_refs[0].shape[:2]
        for t in range(2):
            for dy in range(Y):
                for dx in range(X):
                    src = w_refs[(t * Y + dy) * X + dx]
                    key = p.keyof(p.yo(Y - dy), p.xo(X - dx), p.c)
                    for b in range(half):
                        at = (t * half + b) * BLOCK_COLUMNS + key * piece
                        dst = w.at[pl.ds(pl.multiple_of(at, 16), piece)]
                        i = ((t * Y + dy) * X + dx) * half + b
                        wcopies.append(pltpu.make_async_copy(src.at[b], dst, wsem.at[i]))
                        wremote.append(remote(src.at[b], dst, wsend.at[i], wrecv.at[i], p.core_peer()))
    else:
        wcopies.append(pltpu.make_async_copy(w_refs[0], w, wsem.at[0]))
    for copy in wcopies:
        copy.start()
    p.meet()

    n = sems_per_item(Y, X) * 2
    merges = []
    for m in range(micro):
        for g in range(groups):
            i = m * groups + g
            item = Scatter(
                p,
                [o_ref.at[m, :, :, :, pl.ds(g * rows, rows)], st_ref.at[m, g]],
                [oa.at[i], sa.at[i]], [o1.at[i], s1.at[i]], [o2.at[i], s2.at[i]], [o3.at[i], s3.at[i]],
                send, recv, loc, i * n, i * 2, g % 2 == 0, merge_soft,
            )
            merges.append(item)

    def merge_one(m):
        for g in range(groups):
            merges[m * groups + g].start1()

    def merge_two(m):
        for g in range(groups):
            merges[m * groups + g].start2()

    def merge_three(m):
        for g in range(groups):
            merges[m * groups + g].start3()

    def merge_finish(m):
        for g in range(groups):
            val, st = merges[m * groups + g].finish()
            tile = st[...]
            inv = 1.0 / tile[GROUP:]
            stat[m, g, :GROUP] = tile[:GROUP]
            invs_ref[m, g] = inv
            for h in range(GROUP):
                att[m, g * rows + h * HD : g * rows + (h + 1) * HD, :] = (
                    val[h * HD : (h + 1) * HD, :].astype(F32) * inv[h : h + 1]
                ).astype(BF16)

    n = sems_per_item(Y, X)
    gathers = [[], []]
    for m in range(micro):
        for g in range(groups):
            ds = pl.ds(g * rows, rows)
            for t, (own, out) in enumerate(
                ((datt.at[m, ds], datt_out.at[m, :, :, :, ds]), (stat.at[m, g], stat_out.at[m, g]))
            ):
                i = (m * groups + g) * 2 + t
                gathers[m].append(
                    (
                        Gather(p, own, out, gsend, grecv, i * n, g % 2 == 0),
                        pltpu.make_async_copy(own, out.at[p.y, p.x, p.c], gloc.at[i]),
                    )
                )

    def gather_one(m):
        for item, copy in gathers[m]:
            item.start1()
            copy.start()

    def gather_two(m):
        for item, copy in gathers[m]:
            copy.wait()
            item.start2()

    def gather_three(m):
        for item, copy in gathers[m]:
            item.start3()

    def forward(m):
        at = att[m].T
        attk[m] = at
        wo = w[:width]
        z1 = x_ref[m].astype(F32) + (dot_f32(at, wo, ((1,), (1,))) + bo)
        norm, inv = layer_norm(z1)
        n1[...] = norm
        mid = norm * g1 + e1
        low[m] = mid.astype(BF16)
        inner = low[m]

        def body(i, acc):
            r = pl.multiple_of(i * wide, wide)
            pre = dot_f32(inner, w[pl.ds(width + r, wide)], ((1,), (1,))) + bu_ref[:, pl.ds(r, wide)]
            half = 0.5 + 0.5 * lax.erf(pre * math.sqrt(0.5))
            low_h = (pre * half).astype(BF16)
            hid[m, :, pl.ds(r, wide)] = low_h
            slope[:, pl.ds(r, wide)] = half + pre * (
                jnp.exp(-0.5 * pre * pre) * (1.0 / math.sqrt(2.0 * math.pi))
            )
            return acc + dot_f32(low_h, w[pl.ds(width + FF + r, wide)], ((1,), (0,)))

        f = lax.fori_loop(0, parts, body, jnp.zeros((tok, width), F32)) + bd
        norm2, inv2 = layer_norm(mid + f)
        n2[...] = norm2
        out_ref[m] = (norm2 * g2 + e2).astype(BF16)
        return inv, inv2

    def backward(m, invs, between=lambda: None):
        inv, inv2 = invs
        cot = cot_ref[m].astype(F32)
        norm2 = n2[...]
        dz2 = norm_back(cot, norm2, inv2, g2)
        dg2 = jnp.sum(cot * norm2, axis=0, keepdims=True)
        de2 = jnp.sum(cot, axis=0, keepdims=True)
        df_low = dz2.astype(BF16)
        df[m] = df_low
        dbd = jnp.sum(df_low.astype(F32), axis=0, keepdims=True)

        def body(i, acc):
            r = pl.multiple_of(i * wide, wide)
            dh = dot_f32(df_low, w[pl.ds(width + FF + r, wide)], ((1,), (1,)))
            dp = (dh * slope[:, pl.ds(r, wide)]).astype(BF16)
            dpre[m, :, pl.ds(r, wide)] = dp
            part = jnp.sum(dp.astype(F32), axis=0, keepdims=True)
            dbu_ref[:, pl.ds(r, wide)] += part
            return acc + dot_f32(dp, w[pl.ds(width + r, wide)], ((1,), (0,)))

        dx1 = lax.fori_loop(0, parts // 2, body, dz2)
        between()
        dx1 = lax.fori_loop(parts // 2, parts, body, dx1)
        norm = n1[...]
        dg1 = jnp.sum(dx1 * norm, axis=0, keepdims=True)
        de1 = jnp.sum(dx1, axis=0, keepdims=True)
        dz1 = norm_back(dx1, norm, inv, g1)
        dz_ref[m] = dz1
        da_low = dz1.astype(BF16)
        da[m] = da_low
        dbo = jnp.sum(da_low.astype(F32), axis=0, keepdims=True)
        sums = jnp.concatenate([dbo, dg1, de1, dbd, dg2, de2, dg2, dg2], axis=0)
        dvec_ref[...] += sums
        dt = dot_f32(da_low, w[:width], ((1,), (0,))).T
        for g in range(groups):
            for h in range(GROUP):
                r = g * rows + h * HD
                part = dt[r : r + HD] * invs_ref[m, g, h : h + 1]
                datt[m, r : r + HD, :] = part.astype(BF16)
                stat[m, g, GROUP + h : GROUP + h + 1] = jnp.sum(
                    part * att[m, r : r + HD, :].astype(F32), axis=0, keepdims=True
                )

    step = width // 2

    def chunk_grad(slot, at, chunk):
        for left, right, lo, count in ((da, attk, 0, width), (dpre, low, width, FF), (hid, df, width + FF, FF)):

            @pl.when((chunk * step >= lo) & (chunk * step < lo + count))
            def _():
                cols = pl.ds(pl.multiple_of(chunk * step - lo, step), step)
                total = dot_f32(left[0, :, cols], right[0], ((0,), (0,)))
                for m in range(1, micro):
                    total = total + dot_f32(left[m, :, cols], right[m], ((0,), (0,)))
                dw[slot, pl.ds(pl.multiple_of(at, step), step)] = total.astype(BF16)

    def block_grad(b, slot):
        per = BLOCK_COLUMNS // step

        def body(t, carry):
            chunk_grad(slot, t * step, b * per + t)
            return carry

        lax.fori_loop(0, per, body, 0)

    merge_one(0)
    merge_two(0)
    for copy in wremote:
        copy.start()
    merge_one(1)
    merge_three(0)
    merge_two(1)
    merge_finish(0)
    for copy in wcopies:
        copy.wait()
    for copy in wremote:
        copy.wait_recv()
    dvec_ref[...] = jnp.zeros_like(dvec_ref)
    dbu_ref[...] = jnp.zeros_like(dbu_ref)

    def turn(m, carry):
        invs = forward(m)
        pl.when(m == 1)(lambda: gather_two(0))
        backward(m, invs, lambda: pl.when(m == 0)(lambda: merge_three(1)))

        @pl.when(m == 0)
        def _():
            gather_one(0)
            merge_finish(1)

        @pl.when(m == 1)
        def _():
            gather_one(1)
            gather_three(0)

        return carry

    lax.fori_loop(0, micro, turn, 0)
    if pieces:
        half, piece = w_refs[0].shape[:2]
        keeps = []

        def cores(b):
            slot = lax.rem(b, 2)
            copies = []
            for y in range(Y):
                for x in range(X):
                    i = (b * Y + y) * X + x
                    there = pl.multiple_of(p.keyof(y, x, 1 - p.c) * piece, 16)
                    copies.append(
                        remote(
                            dw.at[slot, pl.ds(there, piece)], core_in.at[b, y, x],
                            csend.at[i], crecv.at[i], p.core_peer(),
                        )
                    )
            return copies

        def one_block(b, carry):
            slot = lax.rem(b, 2)

            @pl.when(b >= 2)
            def _():
                for copy in cores(b - 2):
                    copy.wait_send()

            block_grad(b, slot)
            for copy in cores(b):
                copy.start()
            for y in range(Y):
                for x in range(X):
                    here = pl.multiple_of(p.keyof(y, x, p.c) * piece, 16)
                    core_acc[b, y, x] = dw[slot, pl.ds(here, piece)]
            return carry

        lax.fori_loop(0, blocks // 2, one_block, 0)
        gather_two(1)
        lax.fori_loop(blocks // 2, blocks, one_block, 0)
        gather_three(1)

        def add(i, carry):
            b, y, x = i // (Y * X), lax.rem(i // X, Y), lax.rem(i, X)
            merge_sum([core_acc.at[b, y, x]], [core_in.at[b, y, x]])
            return carry

        def add_block(b, carry):
            for copy in cores(b):
                copy.wait_recv()
            lax.fori_loop(b * Y * X, (b + 1) * Y * X, add, 0)
            return carry

        lax.fori_loop(0, blocks, add_block, 0)
        first, last = pl.ds(0, half), pl.ds(half, half)
        for x in range(X):
            keeps.append((core_acc.at[first, p.y, x], keep_a.at[x]))
            for d in range(1, Y):
                keeps.append((core_acc.at[first, p.yo(d), x], send_a.at[d - 1, x]))
        for y in range(Y):
            keeps.append((core_acc.at[last, y, p.x], keep_b.at[y]))
            for d in range(1, X):
                keeps.append((core_acc.at[last, y, p.xo(d)], send_b.at[d - 1, y]))
        keeps = [pltpu.make_async_copy(src, dst, dwsem.at[i]) for i, (src, dst) in enumerate(keeps)]
        for copy in keeps:
            copy.start()
        for copy in keeps:
            copy.wait()
        for b in (blocks - 2, blocks - 1):
            for copy in cores(jnp.int32(b)):
                copy.wait_send()
    else:
        copies = []
        for b in range(blocks):
            slot = b % 2
            if b >= 2:
                copies[b - 2].wait()
            block_grad(b, slot)
            copies.append(
                pltpu.make_async_copy(
                    dw.at[slot], dw_out.at[pl.ds(b * BLOCK_COLUMNS, BLOCK_COLUMNS)], dwsem.at[slot]
                )
            )
            copies[-1].start()
            if b == blocks // 2:
                gather_two(1)
        for copy in copies[-2:]:
            copy.wait()
        gather_three(1)
    for item in merges:
        item.drain()
    for copy in wremote:
        copy.wait_send()
    for m in range(micro):
        for item, copy in gathers[m]:
            item.finish()


def middle(mesh_dims, o_part, st_part, x_own, cot, weights, vec, bias_up):
    Y, X, R = mesh_dims
    micro, tok, width = x_own.shape
    groups = st_part.shape[1]
    items = micro * groups
    merge_sems = sems_per_item(Y, X) * 2 * items
    strows = STAT_ROWS
    ffw = 2 * FF + width
    blocks = ffw // BLOCK_COLUMNS
    pieces = len(weights) > 1
    outs = [
        (jax.ShapeDtypeStruct((micro, tok, width), BF16), VMEM_SPEC),
        (jax.ShapeDtypeStruct((micro, Y, X, 2, width, tok), BF16), ANY),
        (jax.ShapeDtypeStruct((micro, groups, Y, X, 2, strows, tok), F32), ANY),
        (jax.ShapeDtypeStruct((micro, tok, width), F32), VMEM_SPEC),
        (jax.ShapeDtypeStruct((8, width), F32), VMEM_SPEC),
        (jax.ShapeDtypeStruct((1, FF), F32), VMEM_SPEC),
    ]
    extra = []
    if pieces:
        half, piece = weights[0].shape[:2]
        wsems = 2 * Y * X * half
        outs += [
            (jax.ShapeDtypeStruct((max(Y - 1, 1), X, half, piece, width), BF16), ANY),
            (jax.ShapeDtypeStruct((X, half, piece, width), BF16), ANY),
            (jax.ShapeDtypeStruct((max(X - 1, 1), Y, half, piece, width), BF16), ANY),
            (jax.ShapeDtypeStruct((Y, half, piece, width), BF16), ANY),
        ]
        extra = [
            pltpu.VMEM((blocks, Y, X, piece, width), BF16),
            pltpu.VMEM((blocks, Y, X, piece, width), BF16),
            pltpu.SemaphoreType.DMA((blocks * Y * X,)),
            pltpu.SemaphoreType.DMA((blocks * Y * X,)),
        ]
    else:
        wsems = 1
        outs += [(jax.ShapeDtypeStruct((ffw, width), BF16), ANY)]
    return pl.pallas_call(
        functools.partial(middle_kernel, Y, X, R, blocks, pieces),
        out_shape=tuple(o for o, _ in outs),
        in_specs=[ANY, ANY, VMEM_SPEC, VMEM_SPEC, VMEM_SPEC, VMEM_SPEC] + [ANY] * len(weights),
        out_specs=tuple(spec for _, spec in outs),
        scratch_shapes=scatter_scratch(Y, X, items, (GROUP * HD, tok), BF16, None)
        + scatter_scratch(Y, X, items, (2 * GROUP, tok), F32, None)
        + [
            pltpu.SemaphoreType.DMA((merge_sems,)),
            pltpu.SemaphoreType.DMA((merge_sems,)),
            pltpu.SemaphoreType.DMA((items * 2,)),
            pltpu.SemaphoreType.DMA((merge_sems,)),
            pltpu.SemaphoreType.DMA((merge_sems,)),
            pltpu.SemaphoreType.DMA((items * 2,)),
            pltpu.SemaphoreType.DMA((wsems,)),
            pltpu.SemaphoreType.DMA((wsems,)),
            pltpu.SemaphoreType.DMA((wsems,)),
            pltpu.SemaphoreType.DMA((2 * X * Y,)),
            pltpu.VMEM((ffw, width), BF16),
            pltpu.VMEM((micro, width, tok), BF16),
            pltpu.VMEM((micro, tok, width), BF16),
            pltpu.VMEM((micro, tok, width), BF16),
            pltpu.VMEM((micro, tok, FF), BF16),
            pltpu.VMEM((micro, tok, FF), BF16),
            pltpu.VMEM((tok, FF), F32),
            pltpu.VMEM((micro, tok, width), BF16),
            pltpu.VMEM((micro, tok, width), BF16),
            pltpu.VMEM((tok, width), F32),
            pltpu.VMEM((tok, width), F32),
            pltpu.VMEM((micro, width, tok), BF16),
            pltpu.VMEM((micro, groups, strows, tok), F32),
            pltpu.VMEM((micro, groups, GROUP, tok), F32),
            pltpu.VMEM((2, BLOCK_COLUMNS, width), BF16),
        ]
        + extra,
        compiler_params=pltpu.CompilerParams(
            collective_id=2, has_side_effects=True, vmem_limit_bytes=VMEM_LIMIT
        ),
        name="middle",
    )(o_part, st_part, x_own, cot, vec, bias_up, *weights)


def tail_kernel(
    Y, X, R, inverse,
    dq_ref, dk_hbm, dv_hbm, x_hbm, dz_hbm, w_ref, vec_ref, bu_ref, xg_ref, dqs_hbm, *refs,
):
    suma_hbm, got_a, sumb_hbm, got_b = refs[0], refs[1:X], refs[X], refs[X + 1 : X + Y]
    tok_ref, late_ref, early_ref, sum_ref = refs[X + Y : X + Y + 4]
    (
        qa, q1, q2, q3, send, recv, loc,
        part, a, r1, r2, r3, bsend, brecv, bloc,
        fin, stage, rz, zsend, zrecv, qf, qz, rq, qsend, qrecv,
        small, sbuf, ssend, srecv, w, wsem, dq, dqv, xv, acc, vsem,
        dk_ref, dv_ref, x_ref, dqs_ref, sum_a, sum_b, dz_ref, fsem,
    ) = refs[X + Y + 4 :]
    p = Place(Y, X, R)
    micro, tok, width = x_ref.shape
    slots_here = late_ref.shape[0]
    groups = qa.shape[0] // micro
    rows = GROUP * HD
    n = sems_per_item(Y, X)
    piece = part.shape[4]
    p.announce(True)
    outer = (dk_hbm, dv_hbm, x_hbm, dqs_hbm, suma_hbm, sumb_hbm, dz_hbm)
    inner = (dk_ref, dv_ref, x_ref, dqs_ref, sum_a, sum_b, dz_ref)
    fetch = [pltpu.make_async_copy(a, b, fsem.at[i]) for i, (a, b) in enumerate(zip(outer, inner))]
    loads = [
        pltpu.make_async_copy(dq_ref, dqv, vsem.at[0]),
        pltpu.make_async_copy(xg_ref, xv, vsem.at[1]),
    ]
    wcopy = pltpu.make_async_copy(w_ref, w, wsem)
    for copy in fetch + loads + [wcopy]:
        copy.start()
    for copy in fetch[:6]:
        copy.wait()
    for at, total, got in ((p.x, sum_a, got_a), (p.y, sum_b, got_b)):
        count = total.shape[1]
        base = 0 if total is sum_a else count

        def add(b, carry, at=at, total=total, got=got, base=base):
            value = total[at, b].astype(F32)
            for ref in got:
                value = value + ref[b].astype(F32)
            fin[base + b] = value.astype(BF16)
            return carry

        lax.fori_loop(0, count, add, 0)

    def reorder(s, carry):
        stage[s] = fin[jnp.maximum(inverse[s] - EARLY, 0)]
        return carry

    lax.fori_loop(0, stage.shape[0], reorder, 0)
    ones = jnp.ones((8, tok), BF16)
    bias_v = dot_f32(ones, dv_ref[0], ((1,), (1,)))
    sum_q = dqs_ref[0]
    for m in range(1, micro):
        bias_v = bias_v + dot_f32(ones, dv_ref[m], ((1,), (1,)))
        sum_q = sum_q + dqs_ref[m]
    sums = [sum_q.T[:1], bias_v[:1], vec_ref[:3]]
    sums += [bu_ref[:, i * width : (i + 1) * width] for i in range(FF // width)]
    sums += [vec_ref[3:6], jnp.zeros((4, width), F32)]
    small[...] = jnp.concatenate(sums, axis=0).astype(BF16)
    stages = [[p.core_peer()]]
    stages.append([p.x_peer(d) for d in range(1, X)])
    stages.append([p.y_peer(d) for d in range(1, Y)])
    stages.append([p.z_peer(d) for d in range(1, R)])
    scopies = []
    at = 0
    for peers in stages:
        row = []
        for peer in peers:
            row.append(remote(small, sbuf.at[at], ssend.at[at], srecv.at[at], peer))
            at += 1
        scopies.append(row)

    def small_start(t):
        for copy in scopies[t]:
            copy.start()

    def small_wait(t):
        at = sum(len(row) for row in scopies[:t])
        for copy in scopies[t]:
            copy.wait_recv()
        for copy in scopies[t]:
            copy.wait_send()
        total = small[...].astype(F32)
        for i in range(len(scopies[t])):
            total = total + sbuf[at + i].astype(F32)
        return total

    def token_grad(m):
        total = dz_ref[m] + dot_f32(dq[m], w[:width], ((0,), (0,)))
        total = total + dot_f32(dk_ref[m], w[width : 2 * width], ((0,), (0,)))
        total = total + dot_f32(dv_ref[m], w[2 * width :], ((0,), (0,)))
        tok_ref[m] = total.astype(BF16)

    p.meet()
    small_start(0)
    zcopies = []
    if R == 4:
        near = p.r + 1 - 2 * lax.rem(p.r, 2)
        far = p.ro(2)
        classes = (p.r, far)
        one = [
            [
                remote(
                    stage.at[q * slots_here + s], rz.at[k, s], zsend.at[k, s], zrecv.at[k, s], {"rows": near}
                )
                for k, q in enumerate((near, lax.rem(near + 2, R)))
            ]
            for s in range(slots_here)
        ]
        two = [
            remote(stage.at[far * slots_here + s], rz.at[2, s], zsend.at[2, s], zrecv.at[2, s], {"rows": far})
            for s in range(slots_here)
        ]
        for copies in one:
            for copy in copies:
                copy.start()

        def z_pass(s):
            for copy in one[s]:
                copy.wait_recv()
            for k, q in enumerate(classes):
                merge_sum([stage.at[q * slots_here + s]], [rz.at[k, s]])
            two[s].start()

        def z_total(s):
            two[s].wait_recv()
            return stage[p.r * slots_here + s].astype(F32) + rz[2, s].astype(F32)

        zcopies = [copy for copies in one for copy in copies] + two
    else:
        for d in range(1, R):
            there = pl.ds(p.ro(d) * slots_here, slots_here)
            copy = remote(stage.at[there], rz.at[d - 1], zsend.at[d - 1, 0], zrecv.at[d - 1, 0], p.z_peer(d))
            copy.start()
            zcopies.append(copy)

        def z_pass(s):
            pass

        def z_total(s):
            if s == 0:
                for copy in zcopies:
                    copy.wait_recv()
            total = stage[p.r * slots_here + s].astype(F32)
            for d in range(1, R):
                total = total + rz[d - 1, s].astype(F32)
            return total

    qitems = []
    for m in range(micro):
        for g in range(groups):
            i = m * groups + g
            item = Scatter(
                p, [dq_ref.at[m, :, :, :, pl.ds(g * rows, rows)]],
                [qa.at[i]], [q1.at[i]], [q2.at[i]], [q3.at[i]],
                send, recv, loc, i * n, i, g % 2 == 0, merge_sum,
            )
            qitems.append(item)
    first, last = qitems[: len(qitems) - groups], qitems[len(qitems) - groups :]
    for item in first:
        item.start1()

    def product(ref, first, count):
        total = dot_f32(ref[0, first : first + count], x_ref[0], ((1,), (0,)))
        for m in range(1, micro):
            total = total + dot_f32(ref[m, first : first + count], x_ref[m], ((1,), (0,)))
        return total.astype(BF16)

    def put(b, first, value):
        at = 0
        while at < value.shape[0]:
            key, off = divmod(first + at, piece)
            count = min(piece - off, value.shape[0] - at)
            y, x, c = key // (2 * X), key // 2 % X, key % 2
            part[b, y, x, c, off : off + count] = value[at : at + count]
            at += count

    cuts = ((0, piece // 32 * 16, True), (piece // 32 * 16, piece - piece // 32 * 16, False))

    def block_items(b):
        out = []
        for t, (first, count, y_first) in enumerate(cuts):
            ds = pl.ds(first, count)
            i = b * len(cuts) + t
            out.append(
                Scatter(
                    p, [part.at[b, :, :, :, ds]], [a.at[b, :, :, ds]], [r1.at[b, :, :, ds]],
                    [r2.at[b, :, :, ds]], [r3.at[b, :, ds]],
                    bsend, brecv, bloc, i * n, i, y_first, merge_sum,
                )
            )
        return out

    class Block:
        def __init__(self, b):
            self.b, self.items = b, block_items(b)
            self.one = [
                remote(qz.at[b, p.ro(d)], rq.at[b, d - 1], qsend.at[b, 0, d], qrecv.at[b, 0, d], p.z_peer(d))
                for d in range(1, R)
            ]
            mine = early_ref.at[b, p.r]
            self.two = [
                remote(mine, mine, qsend.at[b, 1, d], qrecv.at[b, 1, d], p.z_peer(d)) for d in range(1, R)
            ]

        def step(self, name):
            for item in self.items:
                getattr(item, name)()

        def z_one(self):
            for item, (first, count, _) in zip(self.items, cuts):
                (val,) = item.finish()
                qf[first : first + count] = val[...].astype(F32)
            share = qz.shape[2]
            for i in range(R):
                qz[self.b, i] = qf[i * share : (i + 1) * share].astype(BF16)
            for copy in self.one:
                copy.start()

        def z_two(self):
            for copy in self.one:
                copy.wait_recv()
            total = qz[self.b, p.r].astype(F32)
            for d in range(1, R):
                total = total + rq[self.b, d - 1].astype(F32)
            early_ref[self.b, p.r] = total.astype(BF16)
            for copy in self.two:
                copy.start()

        def finish(self):
            for copy in self.two:
                copy.wait_recv()
            for item in self.items:
                item.drain()
            for copy in self.one + self.two:
                copy.wait_send()

    block0, block1 = Block(0), Block(1)
    half = width // 2
    put(1, 0, product(dk_ref, half, half))
    small[...] = small_wait(0).astype(BF16)
    small_start(1)
    put(1, half, product(dv_ref, 0, width))
    block1.step("start1")
    small[...] = small_wait(1).astype(BF16)
    small_start(2)
    put(0, width, product(dk_ref, 0, half))
    small[...] = small_wait(2).astype(BF16)
    small_start(3)
    for item in first:
        item.start2()
    for item in last:
        item.start1()
    for copy in loads:
        copy.wait()
    acc[...] = jnp.zeros_like(acc)
    line = 2 * tok
    turns = micro * Y * X

    def query_grad(i, carry):
        m, y, x = i // (Y * X), lax.rem(i // X, Y), lax.rem(i, X)
        left = jnp.concatenate([dqv[m, y, x, c] for c in range(2)], axis=1)
        right = xv[m, pl.ds(pl.multiple_of(lax.rem(i, Y * X) * line, line), line)]
        acc[...] += dot_f32(left, right, ((1,), (0,)))
        return carry

    lax.fori_loop(0, turns // 2, query_grad, 0)
    z_pass(0)
    lax.fori_loop(turns // 2, turns, query_grad, 0)
    put(0, 0, acc[...].astype(BF16))
    block0.step("start1")
    block1.step("start2")
    block0.step("start2")
    for s in range(1, slots_here):
        z_pass(s)
    block1.step("start3")
    block0.step("start3")
    for item in last:
        item.start2()
    for item in first:
        item.start3()
    block1.z_one()
    block0.z_one()
    for item in last:
        item.start3()
    block1.z_two()
    block0.z_two()
    for s in range(slots_here):
        late_ref[s] = z_total(s)
    wcopy.wait()
    fetch[6].wait()
    def token_grad(m, carry):
        for k in range(micro):

            @pl.when(m == k)
            def _():
                for g in range(groups):
                    (val,) = qitems[k * groups + g].finish()
                    dq[k, g * rows : (g + 1) * rows, :] = val[...]

        total = dz_ref[m] + dot_f32(dq[m], w[:width], ((0,), (0,)))
        total = total + dot_f32(dk_ref[m], w[width : 2 * width], ((0,), (0,)))
        total = total + dot_f32(dv_ref[m], w[2 * width :], ((0,), (0,)))
        tok_ref[m] = total.astype(BF16)
        return carry

    lax.fori_loop(0, micro, token_grad, 0)
    sum_ref[...] = small_wait(3)
    block1.finish()
    block0.finish()
    for item in qitems:
        item.drain()
    for copy in zcopies:
        copy.wait_send()


def tail(mesh_dims, inverse, dq_part, dk, dv, x_own, grad_one, w_early, fin_a, fin_b, dvec, d_bias_up, x_all, dq_sum):
    Y, X, R = mesh_dims
    micro, tok, width = x_own.shape
    half, n = fin_a[0].shape[1:3]
    late = 2 * half
    blocks = EARLY + late
    slots_here = blocks // R
    groups = width // (GROUP * HD)
    items = micro * groups
    per = sems_per_item(Y, X)
    share = n // R
    cuts = 2
    small = (16, width)
    hops = 1 + (X - 1) + (Y - 1) + (R - 1)
    return pl.pallas_call(
        functools.partial(tail_kernel, Y, X, R),
        out_shape=(
            jax.ShapeDtypeStruct((micro, tok, width), BF16),
            jax.ShapeDtypeStruct((slots_here, n, width), F32),
            jax.ShapeDtypeStruct((EARLY, R, share, width), BF16),
            jax.ShapeDtypeStruct(small, F32),
        ),
        in_specs=[pl.BlockSpec(memory_space=pltpu.SMEM), ANY]
        + [ANY] * 4
        + [ANY, VMEM_SPEC, VMEM_SPEC, ANY, ANY]
        + ([ANY] + [VMEM_SPEC] * (X - 1) + [ANY] + [VMEM_SPEC] * (Y - 1)),
        out_specs=(VMEM_SPEC,) * 4,
        scratch_shapes=scatter_scratch(Y, X, items, (GROUP * HD, tok), BF16, None)
        + [
            pltpu.SemaphoreType.DMA((per * items,)),
            pltpu.SemaphoreType.DMA((per * items,)),
            pltpu.SemaphoreType.DMA((items,)),
            pltpu.VMEM((EARLY, Y, X, 2, n, width), BF16),
        ]
        + scatter_scratch(Y, X, EARLY, (n, width), BF16, None)
        + [
            pltpu.SemaphoreType.DMA((per * EARLY * cuts,)),
            pltpu.SemaphoreType.DMA((per * EARLY * cuts,)),
            pltpu.SemaphoreType.DMA((EARLY * cuts,)),
            pltpu.VMEM((late, n, width), BF16),
            pltpu.VMEM((blocks, n, width), BF16),
            pltpu.VMEM((R - 1, slots_here, n, width), BF16),
            pltpu.SemaphoreType.DMA((R - 1, slots_here)),
            pltpu.SemaphoreType.DMA((R - 1, slots_here)),
            pltpu.VMEM((n, width), F32),
            pltpu.VMEM((EARLY, R, share, width), BF16),
            pltpu.VMEM((EARLY, R - 1, share, width), BF16),
            pltpu.SemaphoreType.DMA((EARLY, 2, R)),
            pltpu.SemaphoreType.DMA((EARLY, 2, R)),
            pltpu.VMEM(small, BF16),
            pltpu.VMEM((hops,) + small, BF16),
            pltpu.SemaphoreType.DMA((hops,)),
            pltpu.SemaphoreType.DMA((hops,)),
            pltpu.VMEM((3 * width, width), BF16),
            pltpu.SemaphoreType.DMA,
            pltpu.VMEM((micro, width, tok), BF16),
            pltpu.VMEM(dq_part.shape, BF16),
            pltpu.VMEM(x_all.shape, BF16),
            pltpu.VMEM((width, width), F32),
            pltpu.SemaphoreType.DMA((2,)),
            pltpu.VMEM(dk.shape, BF16),
            pltpu.VMEM(dv.shape, BF16),
            pltpu.VMEM(x_own.shape, BF16),
            pltpu.VMEM(dq_sum.shape, F32),
            pltpu.VMEM(fin_a[0].shape, BF16),
            pltpu.VMEM(fin_b[0].shape, BF16),
            pltpu.VMEM(grad_one.shape, F32),
            pltpu.SemaphoreType.DMA((7,)),
        ],
        compiler_params=pltpu.CompilerParams(
            collective_id=5, has_side_effects=True, vmem_limit_bytes=VMEM_LIMIT
        ),
        name="tail",
    )(inverse, dq_part, dk, dv, x_own, grad_one, w_early.reshape(3 * width, width), dvec, d_bias_up, x_all, dq_sum, *fin_a, *fin_b)


def project_kernel(scale, x_ref, own_ref, w_ref, vec_ref, q_ref, k_ref, v_ref, bias):
    width = x_ref.shape[2]

    @pl.when((pl.program_id(0) == 0) & (pl.program_id(1) == 0))
    def _():
        bias[...] = vec_ref[...].T

    q = dot_f32(w_ref[:width], x_ref[0], ((1,), (1,))) + bias[:, 6:7]
    q_ref[0] = q.astype(BF16) * jnp.asarray(scale, BF16)

    @pl.when(pl.program_id(1) == 0)
    def _():
        own = own_ref[0]
        k_ref[0] = dot_f32(w_ref[width : 2 * width], own, ((1,), (1,))).astype(BF16)
        v_ref[0] = (dot_f32(w_ref[2 * width :], own, ((1,), (1,))) + bias[:, 7:8]).astype(BF16)


def project(x_all, x_own, w_t, vec, scale):
    micro, slots, width = x_all.shape
    own = x_own.shape[1]
    wide = min(1024, slots)
    return pl.pallas_call(
        functools.partial(project_kernel, scale),
        grid=(micro, slots // wide),
        out_shape=(
            jax.ShapeDtypeStruct((micro, width, slots), BF16),
            jax.ShapeDtypeStruct((micro, width, own), BF16),
            jax.ShapeDtypeStruct((micro, width, own), BF16),
        ),
        in_specs=[
            pl.BlockSpec((1, wide, width), lambda m, t: (m, t, 0)),
            pl.BlockSpec((1, own, width), lambda m, t: (m, 0, 0)),
            pl.BlockSpec((3 * width, width), lambda m, t: (0, 0)),
            pl.BlockSpec((8, width), lambda m, t: (0, 0)),
        ],
        out_specs=(
            pl.BlockSpec((1, width, wide), lambda m, t: (m, 0, t)),
            pl.BlockSpec((1, width, own), lambda m, t: (m, 0, 0)),
            pl.BlockSpec((1, width, own), lambda m, t: (m, 0, 0)),
        ),
        scratch_shapes=[pltpu.VMEM((width, 8), F32)],
        compiler_params=pltpu.CompilerParams(vmem_limit_bytes=VMEM_LIMIT),
        cost_estimate=pl.CostEstimate(
            flops=2 * micro * width * width * (slots + 2 * own),
            bytes_accessed=4 * micro * width * slots,
            transcendentals=0,
        ),
        name="project",
    )(x_all, x_own, w_t, vec)


def attention_forward_kernel(q_ref, k_ref, v_ref, prev_ref, segk_ref, segq_ref, *refs):
    logit_ref, e_ref, o_ref, st_ref, top_ref, mask_ref = refs[-6:]
    h = pl.program_id(0)
    chunks, wide = o_ref.shape[1], o_ref.shape[3]

    @pl.when(h == 0)
    def _():
        mask_ref[...] = jnp.where(segk_ref[0] == segq_ref[0], 0.0, NEG_BIG)

    for i in range(PER):
        rows = slice(i * HD, (i + 1) * HD)
        hg = lax.rem(h * PER + i, GROUP)
        score = dot_f32(k_ref[rows], q_ref[rows], ((0,), (0,)))
        raw = score + prev_ref[0, 0, i].astype(F32)
        logit_ref[0, 0, i] = raw.astype(BF16)
        masked = raw + mask_ref[...]
        top = jnp.maximum(jnp.max(masked, axis=0, keepdims=True), NEG_FLOOR)
        expo = jnp.exp(masked - top)
        total = jnp.sum(expo, axis=0, keepdims=True)
        low = expo.astype(BF16)
        e_ref[0, i] = low
        out = dot_f32(v_ref[rows], low, ((1,), (0,))).astype(BF16)
        for t in range(chunks):
            cols = slice(t * wide, (t + 1) * wide)
            o_ref[0, t, rows] = out[:, cols]
            st_ref[0, 0, t, pl.ds(hg, 1), :] = top[:, cols]
            st_ref[0, 0, t, pl.ds(GROUP + hg, 1), :] = total[:, cols]
            top_ref[0, 0, t, pl.ds(hg, 1), :] = top[:, cols]


def attention_forward(m, so_far, q, k, v, prev, segk, segq, chunks, wide):
    micro, _, heads, own, slots = prev.shape
    groups = heads // GROUP
    score = pl.BlockSpec((1, 1, PER, own, slots), lambda h: (m, 0, h, 0, 0))
    stat = pl.BlockSpec((1, 1, chunks, 2 * GROUP, wide), lambda h: (m, h * PER // GROUP, 0, 0, 0))
    return pl.pallas_call(
        attention_forward_kernel,
        grid=(heads // PER,),
        out_shape=(
            jax.ShapeDtypeStruct(prev.shape, BF16),
            jax.ShapeDtypeStruct((micro, heads, own, slots), BF16),
            jax.ShapeDtypeStruct((micro, chunks, heads * HD, wide), BF16),
            jax.ShapeDtypeStruct((micro, groups, chunks, 2 * GROUP, wide), F32),
            jax.ShapeDtypeStruct((micro, groups, chunks, 2 * GROUP, wide), F32),
        ),
        in_specs=[
            pl.BlockSpec((None, PER * HD, slots), lambda h: (m, h, 0)),
            pl.BlockSpec((None, PER * HD, own), lambda h: (m, h, 0)),
            pl.BlockSpec((None, PER * HD, own), lambda h: (m, h, 0)),
            score,
            pl.BlockSpec((1, own, 1), lambda h: (m, 0, 0)),
            pl.BlockSpec((1, 1, slots), lambda h: (m, 0, 0)),
        ]
        + [ANY] * len(so_far),
        out_specs=(
            score,
            pl.BlockSpec((1, PER, own, slots), lambda h: (m, h, 0, 0)),
            pl.BlockSpec((1, chunks, PER * HD, wide), lambda h: (m, 0, h, 0)),
            stat,
            stat,
        ),
        input_output_aliases={6 + i: i for i in range(len(so_far))},
        scratch_shapes=[pltpu.VMEM((own, slots), F32)],
        compiler_params=pltpu.CompilerParams(vmem_limit_bytes=VMEM_LIMIT),
        cost_estimate=pl.CostEstimate(
            flops=heads * 2 * 2 * own * slots * HD,
            bytes_accessed=heads * own * slots * 6,
            transcendentals=heads * own * slots,
        ),
        name="attention_forward",
    )(q, k, v, prev, segk, segq, *so_far)


def attention_backward_kernel(
    scale, first, e_ref, d_ref, st_ref, top_ref, q_ref, k_ref, v_ref, *refs
):
    g_ref, dq_ref, dk_ref, dv_ref, sum_ref = refs[-5:]
    h = pl.program_id(0) + first
    chunks, wide = d_ref.shape[1], d_ref.shape[3]
    for i in range(PER):
        rows = slice(i * HD, (i + 1) * HD)
        hg = lax.rem(h * PER + i, GROUP)

        def row(ref, first):
            return jnp.concatenate([ref[0, 0, t, pl.ds(first + hg, 1), :] for t in range(chunks)], axis=1)

        weight = jnp.exp(row(top_ref, 0) - row(st_ref, 0))
        dots = row(st_ref, GROUP) * weight
        low = e_ref[0, i]
        datt = jnp.concatenate([d_ref[0, t, rows] for t in range(chunks)], axis=1)
        grad_in = (datt.astype(F32) * weight).astype(BF16)
        soft = dot_f32(v_ref[rows], grad_in, ((0,), (0,))) - dots
        grad = (low.astype(F32) * soft).astype(BF16)
        g_ref[0, 0, i] = grad
        dq = dot_f32(k_ref[rows], grad, ((1,), (0,))) * scale
        sum_ref[0, rows] = jnp.broadcast_to(jnp.sum(dq, axis=1, keepdims=True), (HD, 128))
        dq = dq.astype(BF16)
        for t in range(chunks):
            dq_ref[0, t, rows] = dq[:, t * wide : (t + 1) * wide]
        dv_ref[0, rows] = dot_f32(grad_in, low, ((1,), (1,))).astype(BF16)
        dk_ref[0, rows] = dot_f32(q_ref[rows], grad, ((1,), (1,))).astype(BF16)


def attention_backward(first, last, so_far, expo, datt, st, tops, q, k, v, scale):
    micro, heads, own, slots = expo.shape
    chunks, wide = datt.shape[1], datt.shape[3]
    steps = heads // PER
    at = lambda i: ((i + first) // steps, (i + first) % steps)
    flops = heads * 2 * 4 * own * slots * HD
    sts = st.shape[3]
    return pl.pallas_call(
        functools.partial(attention_backward_kernel, scale, first),
        grid=(last - first,),
        out_shape=(
            jax.ShapeDtypeStruct((micro, 1, heads, own, slots), BF16),
            jax.ShapeDtypeStruct((micro, chunks, heads * HD, wide), BF16),
            jax.ShapeDtypeStruct((micro, heads * HD, own), BF16),
            jax.ShapeDtypeStruct((micro, heads * HD, own), BF16),
            jax.ShapeDtypeStruct((micro, heads * HD, 128), F32),
        ),
        in_specs=[
            pl.BlockSpec((1, PER, own, slots), lambda i: (*at(i), 0, 0)),
            pl.BlockSpec((1, chunks, PER * HD, wide), lambda i: (at(i)[0], 0, at(i)[1], 0)),
            pl.BlockSpec((1, 1, chunks, sts, wide), lambda i: (at(i)[0], at(i)[1] * PER // GROUP, 0, 0, 0)),
            pl.BlockSpec((1, 1, chunks, 2 * GROUP, wide), lambda i: (at(i)[0], at(i)[1] * PER // GROUP, 0, 0, 0)),
            pl.BlockSpec((None, PER * HD, slots), lambda i: (*at(i), 0)),
            pl.BlockSpec((None, PER * HD, own), lambda i: (*at(i), 0)),
            pl.BlockSpec((None, PER * HD, own), lambda i: (*at(i), 0)),
        ]
        + [ANY] * len(so_far),
        out_specs=(
            pl.BlockSpec((1, 1, PER, own, slots), lambda i: (at(i)[0], 0, at(i)[1], 0, 0)),
            pl.BlockSpec((1, chunks, PER * HD, wide), lambda i: (at(i)[0], 0, at(i)[1], 0)),
            pl.BlockSpec((1, PER * HD, own), lambda i: (*at(i), 0)),
            pl.BlockSpec((1, PER * HD, own), lambda i: (*at(i), 0)),
            pl.BlockSpec((1, PER * HD, 128), lambda i: (*at(i), 0)),
        ),
        input_output_aliases={7 + i: i for i in range(len(so_far))},
        compiler_params=pltpu.CompilerParams(vmem_limit_bytes=VMEM_LIMIT),
        cost_estimate=pl.CostEstimate(
            flops=flops, bytes_accessed=heads * own * slots * 4, transcendentals=0
        ),
        name="attention_backward",
    )(expo, datt, st, tops, q, k, v, *so_far)


def shifted(arr, mesh_dims, dy, dx):
    if dy == 0 and dx == 0:
        return arr
    Y, X, _ = mesh_dims
    key = lambda y, x, c: (y * X + x) * 2 + c
    perm = [
        (key(y, x, c), key((y + dy) % Y, (x + dx) % X, c)) for y in range(Y) for x in range(X) for c in range(2)
    ]
    return lax.ppermute(arr, "keys", perm)


def late_weights_start(mesh_dims, own_first, own_last):
    Y, X, _ = mesh_dims
    first = [shifted(own_first, mesh_dims, 0, dx) for dx in range(X)]
    last = [shifted(own_last, mesh_dims, dy, 0) for dy in range(Y)]
    first_own = [shifted(own_first, mesh_dims, dy, 0) for dy in range(1, Y)]
    last_own = [shifted(own_last, mesh_dims, 0, dx) for dx in range(1, X)]
    return first, last, first_own, last_own


def late_weights_finish(mesh_dims, first, last, first_own, last_own):
    Y, X, _ = mesh_dims
    out = []
    for dy in range(Y):
        for dx in range(X):
            out.append(first_own[dy - 1] if dx == 0 and dy > 0 else shifted(first[dx], mesh_dims, dy, 0))
    for dy in range(Y):
        for dx in range(X):
            out.append(last_own[dx - 1] if dy == 0 and dx > 0 else shifted(last[dy], mesh_dims, 0, dx))
    return out


def late_grads_start(mesh_dims, send_a, keep_a, send_b, keep_b):
    Y, X, _ = mesh_dims
    first = [shifted(send_a[d - 1], mesh_dims, d, 0) for d in range(1, Y)]
    last = [shifted(send_b[d - 1], mesh_dims, 0, d) for d in range(1, X)]
    return (keep_a, first), (keep_b, last)


def late_grads_finish(mesh_dims, first, last):
    Y, X, _ = mesh_dims
    key = lax.axis_index("keys")
    x, y = (key // 2) % X, key // (2 * X)

    def line(keep, got, place, move):
        total = keep.astype(F32)
        for piece in got:
            total = total + piece.astype(F32)
        total = total.astype(BF16)
        count = total.shape[0]
        pick = lambda d: lax.dynamic_index_in_dim(total, (place + d) % count, 0, keepdims=False)
        return [total] + [move(pick(d), d) for d in range(1, count)]

    return (
        line(*first, x, lambda a, d: shifted(a, mesh_dims, 0, d)),
        line(*last, y, lambda a, d: shifted(a, mesh_dims, d, 0)),
    )


def halves(value):
    high = value.astype(BF16)
    return high, (value - high.astype(F32)).astype(BF16)


def update_weights_kernel(
    block_ids, first_column, fixes, late_ref, early_ref, basis_ref, master_ref, one_ref, two_ref,
    grad_out, one_out, two_out, master_out, copy_out, joined,
):
    s = pl.program_id(0)
    block = block_ids[s]
    early = early_ref[jnp.minimum(block, EARLY - 1)].astype(F32)
    share = early.shape[1]
    for i in range(early.shape[0]):
        joined[i * share : (i + 1) * share] = early[i]
    grad = jnp.where(block < EARLY, joined[...], late_ref[0])
    grad_out[0] = grad
    basis = basis_ref[0]
    basis_high, basis_low = halves(basis)

    def product(value, contract):
        n = value.shape[0]
        high, rest = halves(value)
        both = dot_f32(jnp.concatenate([high, rest], axis=0), basis_high, contract)
        return both[:n] + (both[n:] + dot_f32(high, basis_low, contract))

    rotated = product(grad, ((1,), (0,)))
    new_one = BETA_ONE * one_ref[0] + (1.0 - BETA_ONE) * rotated
    new_two = BETA_TWO * two_ref[0] + (1.0 - BETA_TWO) * rotated * rotated
    one_out[0] = new_one
    two_out[0] = new_two
    direction = new_one / fixes[0] / (jnp.sqrt(new_two / fixes[1]) + EPS_ADAM)
    back = product(direction, ((1,), (1,)))
    columns = first_column[s] + lax.broadcasted_iota(jnp.int32, (grad.shape[0], 1), 0)
    master = master_ref[0]
    new_master = master - column_rates(columns) * (back + DECAY * master)
    master_out[0] = new_master
    copy_out[0] = new_master.astype(BF16)


def update_weights(block_ids, first_column, fixes, late, early, basis, master, one, two):
    slots_here, n, width = master.shape
    mat = pl.BlockSpec((1, n, width), lambda s: (s, 0, 0))
    smem = pl.BlockSpec(memory_space=pltpu.SMEM)
    return pl.pallas_call(
        update_weights_kernel,
        grid=(slots_here,),
        out_shape=tuple(jax.ShapeDtypeStruct(master.shape, F32) for _ in range(4))
        + (jax.ShapeDtypeStruct(master.shape, BF16),),
        in_specs=[smem, smem, smem, mat, pl.BlockSpec(early.shape, lambda s: (0, 0, 0, 0)),
                  pl.BlockSpec((1, width, width), lambda s: (s, 0, 0)), mat, mat, mat],
        out_specs=(mat,) * 5,
        scratch_shapes=[pltpu.VMEM((n, width), F32)],
        compiler_params=pltpu.CompilerParams(vmem_limit_bytes=VMEM_LIMIT),
        name="update_weights",
    )(block_ids, first_column, fixes, late, early, basis, master, one, two)


def to_chunks(arr, chunks):
    pieces, rows, own = arr.shape[-3:]
    lead = arr.shape[:-3]
    if pieces == chunks:
        return arr
    per = pieces // chunks
    arr = arr.reshape(lead + (chunks, per, rows, own))
    return jnp.moveaxis(arr, -3, -2).reshape(lead + (chunks, rows, per * own))


def from_chunks(arr, pieces):
    chunks, rows, wide = arr.shape[-3:]
    lead = arr.shape[:-3]
    if pieces == chunks:
        return arr
    per = pieces // chunks
    arr = arr.reshape(lead + (chunks, rows, per, wide // per))
    return jnp.moveaxis(arr, -2, -3).reshape(lead + (pieces, rows, wide // per))


def per_device(
    mesh_dims,
    tokens,
    prev_logits,
    segments,
    out_cot,
    master_mat,
    mom1_mat,
    mom2_mat,
    eigen_bases,
    master_small,
    mom1_small,
    mom2_small,
    owners,
    step_count,
):
    Y, X, R = mesh_dims
    keys = Y * X * 2
    micro, row_count, key_len, width = tokens.shape
    slot_count = prev_logits.shape[4]
    slots_here, _, cols_here = master_mat.shape
    blocks = slots_here * R
    token_count = micro * key_len
    scale = HD ** (-0.5)
    key_index = lax.axis_index("keys")
    row_index = lax.axis_index("rows")
    wide = max(key_len, min(256, slot_count))
    chunks = slot_count // wide
    groups = H // GROUP

    x_own = tokens.reshape(micro, key_len, width)
    w_own = jnp.swapaxes(master_mat, 1, 2)
    small_low = master_small.astype(BF16).reshape(1, slots_here * cols_here)
    ext = lax.dynamic_update_slice(
        jnp.zeros((EXT, width), BF16), small_low, (row_index, jnp.int32(0))
    )
    fast = cols_here % 16 == 0
    wt, *w_late, ext_all, xg = gather_weights(mesh_dims, owners, w_own, ext, x_own)
    if fast:
        pieces = late_weights_start(mesh_dims, *w_late)
    else:
        late = [lax.all_gather(jnp.concatenate(w_late), "keys", axis=1).reshape(2 * FF + width, width)]
    w_t = wt.reshape(EARLY * BLOCK_COLUMNS, width)
    small_all = ext_all.reshape(keys, EXT, width)[:, :R, : slots_here * cols_here]
    params = (
        jnp.transpose(small_all.reshape(keys, R, slots_here, cols_here), (1, 2, 0, 3))
        .reshape(blocks * GAIN_ROW_WIDTH)
        .astype(F32)
    )
    bias_q = params[:width]
    bias_v = params[width : 2 * width]
    bias_o = params[2 * width : 3 * width]
    gain_one = params[3 * width : 4 * width]
    shift_one = params[4 * width : 5 * width]
    bias_up = params[5 * width : 5 * width + FF]
    bias_down = params[5 * width + FF : 6 * width + FF]
    gain_two = params[6 * width + FF : 7 * width + FF]
    shift_two = params[7 * width + FF :]

    vec = jnp.stack([bias_o, gain_one, shift_one, bias_down, gain_two, shift_two, bias_q, bias_v])
    q_all, k_all, v_all = project(xg.reshape(micro, slot_count, width), x_own, w_t, vec, scale)
    x_rows = x_own.reshape(token_count, width)

    seg_rows = segments.reshape(micro, slot_count)
    seg_keys = lax.dynamic_slice_in_dim(seg_rows, key_index * key_len, key_len, 1)
    forward = ()
    for m in range(micro):
        forward = attention_forward(
            m, forward, q_all, k_all, v_all, prev_logits,
            seg_keys[:, :, None], seg_rows[:, None, :], chunks, wide,
        )
        if m == 0 and fast:
            forward, first, last = lax.optimization_barrier((tuple(forward), *pieces[:2]))
            late = late_weights_finish(mesh_dims, first, last, *pieces[2:])
    logits, expo, o_part, st_part, tops = forward
    o_part = from_chunks(o_part, keys).reshape(micro, Y, X, 2, width, key_len)
    st_part = from_chunks(st_part, keys).reshape(micro, groups, Y, X, 2, 2 * GROUP, key_len)
    out_hidden, datt_all, st_all, grad_one, dvec, d_bias_up, *dw_late = middle(
        mesh_dims, o_part, st_part, x_own, out_cot.reshape(x_own.shape), late, vec, bias_up[None]
    )
    out_hidden = out_hidden.reshape(tokens.shape)
    datt_all = to_chunks(datt_all.reshape(micro, keys, width, key_len), chunks)
    st_all = to_chunks(st_all.reshape(micro, groups, keys, STAT_ROWS, key_len), chunks)
    so_far = ()
    if fast:
        first, last = late_grads_start(mesh_dims, *dw_late)
    steps = micro * (H // PER)
    turns = (0, steps * 5 // 8, steps)
    for turn in range(2):
        so_far = attention_backward(
            turns[turn], turns[turn + 1], so_far, expo, datt_all, st_all, tops, q_all, k_all, v_all, scale
        )
        if turn == 0 and fast:
            so_far, first, last = lax.optimization_barrier((tuple(so_far), first, last))
            fin = late_grads_finish(mesh_dims, first, last)
    grad_prev, dq_part, dk, dv, dq_sum = so_far
    dq_part = from_chunks(dq_part, keys).reshape(micro, Y, X, 2, width, key_len)
    inverse = inverse_order(owners)
    slot_index_list = row_index * slots_here + jnp.arange(slots_here, dtype=jnp.int32)
    block_ids = jnp.take(inverse, slot_index_list)
    if fast:
        grad_tokens, mine_late, mine_early, small_sum = tail(
            mesh_dims, inverse, dq_part, dk, dv, x_own, grad_one, wt, *fin, dvec, d_bias_up,
            xg.reshape(micro, slot_count, width), dq_sum,
        )
    else:
        dq = lax.psum_scatter(
            dq_part.reshape(micro, keys, width, key_len), "keys", scatter_dimension=1, tiled=True
        ).reshape(micro, width, key_len)
        grad_proj = jnp.swapaxes(jnp.concatenate([dq, dk, dv], axis=1), 0, 1).reshape(
            3 * width, token_count
        )
        d_qkv = dot_f32(grad_proj, x_rows, ((1,), (0,))).astype(BF16)
        grad_tokens = (
            grad_one.reshape(token_count, width) + dot_f32(grad_proj, w_t, ((0,), (0,)))
        ).astype(BF16)
        sums = jnp.sum(grad_proj.astype(F32).reshape(3, width, token_count), axis=2)
        small_sum = lax.psum(
            jnp.concatenate(
                [sums[0][None], sums[2][None], dvec[:3], d_bias_up.reshape(FF // width, width), dvec[3:6]]
            ),
            ("rows", "keys"),
        )
        grads = jnp.concatenate([d_qkv, dw_late[0]], axis=0).reshape(blocks, keys, cols_here, width)
        grads = lax.psum_scatter(grads, "keys", scatter_dimension=1, tiled=True)
        grads = jnp.take(grads.reshape(blocks, cols_here, width), inverse, axis=0)
        mine_t = lax.psum_scatter(grads, "rows", scatter_dimension=0, tiled=True).astype(F32)
    grad_tokens = grad_tokens.reshape(tokens.shape)
    flat = small_sum.reshape(-1)[: blocks * GAIN_ROW_WIDTH].reshape(blocks, GAIN_ROW_WIDTH)
    mine_small = lax.dynamic_slice(
        flat, (row_index * slots_here, key_index * cols_here), (slots_here, cols_here)
    )

    steps_done = step_count[0].astype(F32)
    fix_one = 1.0 - jnp.power(jnp.asarray(BETA_ONE, F32), steps_done)
    fix_two = 1.0 - jnp.power(jnp.asarray(BETA_TWO, F32), steps_done)
    if fast:
        first_column = block_ids * BLOCK_COLUMNS + key_index * cols_here
        mats = [jnp.swapaxes(a, 1, 2) for a in (master_mat, mom1_mat, mom2_mat)]
        updated = update_weights(
            block_ids, first_column, jnp.stack([fix_one, fix_two]), mine_late, mine_early, eigen_bases, *mats
        )
        mine_mat, new_one, new_two, new_master, copy_mat = (jnp.swapaxes(a, 1, 2) for a in updated)
    else:
        mine_mat = jnp.swapaxes(mine_t, 1, 2)
        rotated = jnp.einsum("sed,sec->sdc", eigen_bases, mine_mat, precision=HIGHEST_PREC)
        new_one = BETA_ONE * mom1_mat + (1.0 - BETA_ONE) * rotated
        new_two = BETA_TWO * mom2_mat + (1.0 - BETA_TWO) * rotated * rotated
        direction = new_one / fix_one / (jnp.sqrt(new_two / fix_two) + EPS_ADAM)
        back_rot = jnp.einsum("sdk,skc->sdc", eigen_bases, direction, precision=HIGHEST_PREC)
        columns = (
            block_ids[:, None] * (cols_here * keys)
            + key_index * cols_here
            + jnp.arange(cols_here, dtype=jnp.int32)[None, :]
        )
        rates = column_rates(columns)[:, None, :]
        new_master = master_mat - rates * (back_rot + DECAY * master_mat)
        copy_mat = new_master.astype(BF16)
    small_one = BETA_ONE * mom1_small + (1.0 - BETA_ONE) * mine_small
    small_two = BETA_TWO * mom2_small + (1.0 - BETA_TWO) * mine_small * mine_small
    new_small = master_small - RATE_SMALL * (small_one / fix_one) / (
        jnp.sqrt(small_two / fix_two) + EPS_ADAM
    )
    return (
        out_hidden,
        logits,
        grad_tokens,
        grad_prev,
        mine_mat,
        new_one,
        new_two,
        new_master,
        copy_mat,
        mine_small,
        small_one,
        small_two,
        new_small,
        new_small.astype(BF16),
    )


def solution(mesh):
    chips = mesh.shape["keys"] // 2
    side = math.isqrt(chips)
    dims = (side, side, mesh.shape["rows"]) if side * side == chips else (1, chips, mesh.shape["rows"])
    acts = P(None, "rows", "keys", None)
    scores = P(None, "rows", None, "keys", None)
    mats = P("rows", None, "keys")
    smalls = P("rows", "keys")
    return jax.shard_map(
        functools.partial(per_device, dims),
        mesh=mesh,
        in_specs=(
            acts, scores, P(None, "rows", None), acts, mats, mats, mats,
            P("rows", None, None), smalls, smalls, smalls, P(), P(),
        ),
        out_specs=(acts, scores, acts, scores) + (mats,) * 5 + (smalls,) * 5,
        check_vma=False,
    )
```

```python
import functools
import math

import jax
import jax.numpy as jnp
from jax import lax
from jax.experimental import pallas as pl
from jax.experimental.pallas import tpu as pltpu
from jax.sharding import PartitionSpec as P

MODEL_WIDTH = 768
H = 12
HD = 64
FF = 3072
BLOCK_COLUMNS = 1152
GAIN_ROW_WIDTH = 1152

EPS_NORM = 1e-06
BETA_ONE = 0.95
BETA_TWO = 0.95
EPS_ADAM = 1e-08
DECAY = 0.01
RATE_SMALL = 0.3
NEG_BIG = -1e30
NEG_FLOOR = -1e29
HIGHEST_PREC = lax.Precision.HIGHEST
MESH = pl.DeviceIdType.MESH
F32 = jnp.float32
BF16 = jnp.bfloat16
ANY = pl.BlockSpec(memory_space=pl.ANY)
VMEM_SPEC = pl.BlockSpec(memory_space=pltpu.VMEM)
EXT = 16
EARLY = 2
PER = 3
VMEM_LIMIT = 60 << 20


def layer_norm(value):
    mean_val = jnp.mean(value, axis=-1, keepdims=True)
    centered = value - mean_val
    inv_dev = lax.rsqrt(jnp.mean(centered * centered, axis=-1, keepdims=True) + EPS_NORM)
    return (centered * inv_dev, inv_dev)


def norm_back(grad_in, normed, inv_dev, gain):
    scaled = grad_in * gain
    return inv_dev * (
        scaled
        - jnp.mean(scaled, axis=-1, keepdims=True)
        - normed * jnp.mean(scaled * normed, axis=-1, keepdims=True)
    )


def inverse_order(owners):
    slot_index_list = jnp.arange(owners.shape[0], dtype=jnp.int32)
    matches = (owners[None, :] == slot_index_list[:, None]).astype(jnp.int32)
    return jnp.sum(matches * slot_index_list[None, :], axis=1)


def column_rates(columns):
    inner = MODEL_WIDTH ** (-0.5)
    return jnp.where(
        columns < 3 * MODEL_WIDTH,
        inner,
        jnp.where(
            columns < 4 * MODEL_WIDTH,
            4.0 * inner,
            jnp.where(columns < 4 * MODEL_WIDTH + FF, inner, FF ** (-0.5)),
        ),
    )


def dot_f32(left, right, contract):
    return lax.dot_general(left, right, (contract, ((), ())), preferred_element_type=F32)


class Place:
    def __init__(self, side_y, side_x, rows):
        self.Y, self.X, self.R = side_y, side_x, rows
        key = lax.axis_index("keys")
        self.key = key
        self.r = lax.axis_index("rows")
        self.c = lax.rem(key, 2)
        self.x = lax.rem(key // 2, side_x)
        self.y = key // (2 * side_x)

    def keyof(self, y, x, c):
        return (y * self.X + x) * 2 + c

    def xo(self, d):
        return lax.rem(self.x + d, self.X)

    def yo(self, d):
        return lax.rem(self.y + d, self.Y)

    def ro(self, d):
        return lax.rem(self.r + d, self.R)

    def x_peer(self, d):
        return {"keys": self.keyof(self.y, self.xo(d), self.c)}

    def y_peer(self, d):
        return {"keys": self.keyof(self.yo(d), self.x, self.c)}

    def core_peer(self):
        return {"keys": self.keyof(self.y, self.x, 1 - self.c)}

    def z_peer(self, d):
        return {"rows": self.ro(d)}

    def announce(self, with_z):
        peers = [self.core_peer()]
        peers += [self.x_peer(d) for d in range(1, self.X)]
        peers += [self.y_peer(d) for d in range(1, self.Y)]
        if with_z:
            peers += [self.z_peer(d) for d in range(1, self.R)]
        sem = pltpu.get_barrier_semaphore()
        for peer in peers:
            pl.semaphore_signal(sem, inc=1, device_id=peer, device_id_type=MESH)
        self.greeted = len(peers)

    def meet(self):
        pl.semaphore_wait(pltpu.get_barrier_semaphore(), self.greeted)

    def barrier(self, with_z):
        self.announce(with_z)
        self.meet()


def remote(src, dst, send_sem, recv_sem, peer):
    return pltpu.make_async_remote_copy(
        src_ref=src,
        dst_ref=dst,
        send_sem=send_sem,
        recv_sem=recv_sem,
        device_id=peer,
        device_id_type=MESH,
    )


def sems_per_item(Y, X):
    return (X - 1) + (Y - 1) + 1


class Gather:
    def __init__(self, place, own, buf, send, recv, base, x_first):
        p = place
        self.sent = []
        n = sems_per_item(p.Y, p.X)
        idx = iter(range(base, base + n))
        first = [(p.x_peer(d)) for d in range(1, p.X)] if x_first else [p.y_peer(d) for d in range(1, p.Y)]
        second = [p.y_peer(d) for d in range(1, p.Y)] if x_first else [p.x_peer(d) for d in range(1, p.X)]
        line = buf.at[p.y, :, p.c] if x_first else buf.at[:, p.x, p.c]
        plane = buf.at[:, :, p.c]
        mine = buf.at[p.y, p.x, p.c]
        self.one = []
        for peer in first:
            i = next(idx)
            self.one.append(remote(own, mine, send.at[i], recv.at[i], peer))
        self.two = []
        for peer in second:
            i = next(idx)
            self.two.append(remote(line, line, send.at[i], recv.at[i], peer))
        i = next(idx)
        self.three = [remote(plane, plane, send.at[i], recv.at[i], p.core_peer())]

    def start1(self):
        for copy in self.one:
            copy.start()

    def start2(self):
        for copy in self.one:
            copy.wait_recv()
        for copy in self.two:
            copy.start()

    def start3(self):
        for copy in self.two:
            copy.wait_recv()
        for copy in self.three:
            copy.start()

    def finish(self):
        for copy in self.three:
            copy.wait_recv()
        for copy in self.one + self.two + self.three:
            copy.wait_send()


def gather_weights_kernel(
    Y, X, R, owners, w_ref, ext_ref, x_ref, wt_out, first_out, last_out, ext_out, xg_out,
    zbuf, zext, stage, sext, wlow, zsend, zrecv, send, recv, loc,
):
    p = Place(Y, X, R)
    slots_here = w_ref.shape[0]
    blocks = zbuf.shape[0]
    early = wt_out.shape[0]
    micro = x_ref.shape[0]
    n = sems_per_item(Y, X)
    p.announce(True)
    wlow[...] = w_ref[...].astype(BF16)
    p.meet()
    here = pl.ds(p.r * slots_here, slots_here)

    def hop(src, step, own):
        there = pl.ds(src * slots_here, slots_here)
        way = (step + 1) // 2
        peer = {"rows": p.r + step}
        return [
            remote(wlow if own else zbuf.at[there], zbuf.at[there], zsend.at[way, src, 0], zrecv.at[src, 0], peer),
            remote(ext_ref if own else zext.at[src], zext.at[src], zsend.at[way, src, 1], zrecv.at[src, 1], peer),
        ]

    def can(step):
        return p.r < R - 1 if step > 0 else p.r > 0

    def pass_on(dist, act):
        for step in (1, -1):
            src = p.r - step * dist

            @pl.when((src >= 0) & (src < R) & can(step))
            def _():
                for copy in hop(src, step, dist == 0):
                    act(copy)

    def arrived(dist):
        for step in (1, -1):
            src = p.r - step * dist

            @pl.when((src >= 0) & (src < R))
            def _():
                for copy in hop(src, step, False):
                    copy.wait_recv()

    pass_on(0, lambda copy: copy.start())
    xitems = []
    xlocal = []
    for m in range(micro):
        item = Gather(p, x_ref.at[m], xg_out.at[m], send, recv, m * n, m % 2 == 0)
        item.start1()
        xitems.append(item)
        copy = pltpu.make_async_copy(x_ref.at[m], xg_out.at[m, p.y, p.x, p.c], loc.at[m])
        copy.start()
        xlocal.append(copy)
    wl = pltpu.make_async_copy(wlow, zbuf.at[here], loc.at[micro])
    wl.start()
    el = pltpu.make_async_copy(ext_ref, zext.at[p.r], loc.at[micro + 1])
    el.start()
    for m in range(micro):
        xlocal[m].wait()
        xitems[m].start2()
    for dist in range(1, R):
        arrived(dist)
        pass_on(dist, lambda copy: copy.start())
    wl.wait()
    el.wait()
    sext[...] = jnp.sum(zext[...].astype(F32), axis=0).astype(BF16)

    def reorder(b, carry):
        stage[b] = zbuf[owners[b]]
        return carry

    lax.fori_loop(0, blocks, reorder, 0)
    base = micro * n
    eitem = Gather(p, sext, ext_out, send, recv, base, True)
    base += n
    lcopies = []
    items = []
    for b in range(early):
        item = Gather(p, stage.at[b], wt_out.at[b], send, recv, base, b % 2 == 0)
        base += n
        item.start1()
        items.append(item)
        copy = pltpu.make_async_copy(stage.at[b], wt_out.at[b, p.y, p.x, p.c], loc.at[micro + 3 + b])
        copy.start()
        lcopies.append(copy)
    eitem.start1()
    ecopy = pltpu.make_async_copy(sext, ext_out.at[p.y, p.x, p.c], loc.at[micro + 2])
    ecopy.start()
    late = (blocks - early) // 2
    rest = [
        pltpu.make_async_copy(stage.at[pl.ds(early + i * late, late)], out, loc.at[micro + 3 + early + i])
        for i, out in enumerate((first_out, last_out))
    ]
    for copy in rest:
        copy.start()
    for m in range(micro):
        xitems[m].start3()
    for b in range(early):
        lcopies[b].wait()
        items[b].start2()
    ecopy.wait()
    eitem.start2()
    for b in range(early):
        items[b].start3()
    eitem.start3()
    for item in xitems + [eitem] + items:
        item.finish()
    for dist in range(R):
        pass_on(dist, lambda copy: copy.wait_send())
    for copy in rest:
        copy.wait()


def gather_weights(mesh_dims, owners, w_own, ext, x_own):
    Y, X, R = mesh_dims
    slots_here, n, width = w_own.shape
    micro, tok = x_own.shape[:2]
    blocks = slots_here * R
    total = sems_per_item(Y, X) * (micro + 1 + EARLY)
    return pl.pallas_call(
        functools.partial(gather_weights_kernel, Y, X, R),
        out_shape=(
            jax.ShapeDtypeStruct((EARLY, Y, X, 2, n, width), BF16),
            jax.ShapeDtypeStruct(((blocks - EARLY) // 2, n, width), BF16),
            jax.ShapeDtypeStruct(((blocks - EARLY) // 2, n, width), BF16),
            jax.ShapeDtypeStruct((Y, X, 2, EXT, width), BF16),
            jax.ShapeDtypeStruct((micro, Y, X, 2, tok, width), BF16),
        ),
        in_specs=[pl.BlockSpec(memory_space=pltpu.SMEM), VMEM_SPEC, VMEM_SPEC, VMEM_SPEC],
        out_specs=(ANY,) * 5,
        scratch_shapes=[
            pltpu.VMEM((blocks, n, width), BF16),
            pltpu.VMEM((R, EXT, width), BF16),
            pltpu.VMEM((blocks, n, width), BF16),
            pltpu.VMEM((EXT, width), BF16),
            pltpu.VMEM(w_own.shape, BF16),
            pltpu.SemaphoreType.DMA((2, R, 2)),
            pltpu.SemaphoreType.DMA((R, 2)),
            pltpu.SemaphoreType.DMA((total,)),
            pltpu.SemaphoreType.DMA((total,)),
            pltpu.SemaphoreType.DMA((micro + 5 + EARLY,)),
        ],
        compiler_params=pltpu.CompilerParams(
            collective_id=1, has_side_effects=True, vmem_limit_bytes=VMEM_LIMIT
        ),
        name="gather_weights",
    )(owners, w_own, ext, x_own)


class Scatter:
    def __init__(self, place, parts, accs, r1s, r2s, r3s, send, recv, loc, base, lbase, y_first, merge):
        p = place
        self.p, self.y_first, self.merge = p, y_first, merge
        self.accs, self.r1s, self.r2s, self.r3s = accs, r1s, r2s, r3s
        self.count = len(parts)
        n = sems_per_item(p.Y, p.X) * len(parts)
        idx = iter(range(base, base + n))
        self.zero, self.one, self.two, self.three = [], [], [], []
        for t, part in enumerate(parts):
            i = next(idx)
            self.zero.append(pltpu.make_async_copy(part.at[:, :, p.c], accs[t], loc.at[lbase + t]))
            self.one.append(remote(part.at[:, :, 1 - p.c], r1s[t], send.at[i], recv.at[i], p.core_peer()))
            if y_first:
                for d in range(1, p.Y):
                    i = next(idx)
                    self.two.append(
                        remote(accs[t].at[p.yo(d)], r2s[t].at[d - 1], send.at[i], recv.at[i], p.y_peer(d))
                    )
                for d in range(1, p.X):
                    i = next(idx)
                    self.three.append(
                        remote(accs[t].at[p.y, p.xo(d)], r3s[t].at[d - 1], send.at[i], recv.at[i], p.x_peer(d))
                    )
            else:
                for d in range(1, p.X):
                    i = next(idx)
                    self.two.append(
                        remote(accs[t].at[:, p.xo(d)], r2s[t].at[d - 1], send.at[i], recv.at[i], p.x_peer(d))
                    )
                for d in range(1, p.Y):
                    i = next(idx)
                    self.three.append(
                        remote(accs[t].at[p.yo(d), p.x], r3s[t].at[d - 1], send.at[i], recv.at[i], p.y_peer(d))
                    )

    def start1(self):
        for copy in self.zero + self.one:
            copy.start()

    def start2(self):
        p = self.p
        for copy in self.zero:
            copy.wait()
        for copy in self.one:
            copy.wait_recv()

        def body(i, carry):
            y, x = i // p.X, lax.rem(i, p.X)
            self.merge([a.at[y, x] for a in self.accs], [r.at[y, x] for r in self.r1s])
            return carry

        lax.fori_loop(0, p.Y * p.X, body, 0)
        for copy in self.two:
            copy.start()

    def start3(self):
        p = self.p
        for copy in self.two:
            copy.wait_recv()
        if self.y_first:
            for d in range(1, p.Y):

                def body(x, carry, d=d):
                    self.merge([a.at[p.y, x] for a in self.accs], [r.at[d - 1, x] for r in self.r2s])
                    return carry

                lax.fori_loop(0, p.X, body, 0)
        else:
            for d in range(1, p.X):

                def body(y, carry, d=d):
                    self.merge([a.at[y, p.x] for a in self.accs], [r.at[d - 1, y] for r in self.r2s])
                    return carry

                lax.fori_loop(0, p.Y, body, 0)
        for copy in self.three:
            copy.start()

    def finish(self):
        p = self.p
        for copy in self.three:
            copy.wait_recv()
        mine = [a.at[p.y, p.x] for a in self.accs]
        for d in range(1, p.X if self.y_first else p.Y):
            self.merge(mine, [r.at[d - 1] for r in self.r3s])
        return mine

    def drain(self):
        for copy in self.one + self.two + self.three:
            copy.wait_send()


def merge_sum(into, other):
    a, b = into[0], other[0]
    a[...] = (a[...].astype(F32) + b[...].astype(F32)).astype(BF16)


def merge_soft(into, other):
    (va, sa), (vb, sb) = into, other
    ta, tb = sa[...], sb[...]
    heads = ta.shape[0] // 2
    top_a, top_b = ta[:heads], tb[:heads]
    top = jnp.maximum(top_a, top_b)
    wa, wb = jnp.exp(top_a - top), jnp.exp(top_b - top)
    sa[...] = jnp.concatenate([top, wa * ta[heads:] + wb * tb[heads:]], axis=0)
    for h in range(heads):
        rows = slice(h * HD, (h + 1) * HD)
        va[rows, :] = (
            va[rows, :].astype(F32) * wa[h : h + 1] + vb[rows, :].astype(F32) * wb[h : h + 1]
        ).astype(BF16)


def scatter_scratch(Y, X, items, shape, dtype, y_first_of):
    most = max((Y - 1) * X, (X - 1) * Y)
    return [
        pltpu.VMEM((items, Y, X) + shape, dtype),
        pltpu.VMEM((items, Y, X) + shape, dtype),
        pltpu.VMEM((items, max(Y, X) - 1, max(Y, X)) + shape, dtype),
        pltpu.VMEM((items, max(Y, X) - 1) + shape, dtype),
    ]


GROUP = 3
STAT_ROWS = 8


def middle_kernel(Y, X, R, blocks, pieces, *refs):
    o_ref, st_ref, x_ref, cot_ref, vec_ref, bu_ref = refs[:6]
    refs = refs[6:]
    count = 2 * Y * X if pieces else 1
    w_refs, refs = refs[:count], refs[count:]
    out_ref, datt_out, stat_out, dz_ref, dvec_ref, dbu_ref = refs[:6]
    refs = refs[6:]
    if pieces:
        send_a, keep_a, send_b, keep_b = refs[:4]
        refs = refs[4:]
    else:
        (dw_out,) = refs[:1]
        refs = refs[1:]
    (
        oa, o1, o2, o3, sa, s1, s2, s3, send, recv, loc, gsend, grecv, gloc, wsem, wsend, wrecv, dwsem,
        w, att, attk, low, hid, dpre, slope, df, da, n1, n2, datt, stat, invs_ref, dw,
    ) = refs[:33]
    if pieces:
        core_acc, core_in, csend, crecv = refs[33:]
    p = Place(Y, X, R)
    micro, tok, width = x_ref.shape
    groups = st_ref.shape[1]
    rows = GROUP * HD
    bo, g1, e1, bd, g2, e2 = (vec_ref[i : i + 1] for i in range(6))
    p.announce(False)
    stat[...] = jnp.zeros_like(stat)
    wide = width
    parts = FF // wide
    wcopies, wremote = [], []
    if pieces:
        half, piece = w_refs[0].shape[:2]
        for t in range(2):
            for dy in range(Y):
                for dx in range(X):
                    src = w_refs[(t * Y + dy) * X + dx]
                    key = p.keyof(p.yo(Y - dy), p.xo(X - dx), p.c)
                    for b in range(half):
                        at = (t * half + b) * BLOCK_COLUMNS + key * piece
                        dst = w.at[pl.ds(pl.multiple_of(at, 16), piece)]
                        i = ((t * Y + dy) * X + dx) * half + b
                        wcopies.append(pltpu.make_async_copy(src.at[b], dst, wsem.at[i]))
                        wremote.append(remote(src.at[b], dst, wsend.at[i], wrecv.at[i], p.core_peer()))
    else:
        wcopies.append(pltpu.make_async_copy(w_refs[0], w, wsem.at[0]))
    for copy in wcopies:
        copy.start()
    p.meet()

    n = sems_per_item(Y, X) * 2
    merges = []
    for m in range(micro):
        for g in range(groups):
            i = m * groups + g
            item = Scatter(
                p,
                [o_ref.at[m, :, :, :, pl.ds(g * rows, rows)], st_ref.at[m, g]],
                [oa.at[i], sa.at[i]], [o1.at[i], s1.at[i]], [o2.at[i], s2.at[i]], [o3.at[i], s3.at[i]],
                send, recv, loc, i * n, i * 2, g % 2 == 0, merge_soft,
            )
            merges.append(item)

    def merge_one(m):
        for g in range(groups):
            merges[m * groups + g].start1()

    def merge_two(m):
        for g in range(groups):
            merges[m * groups + g].start2()

    def merge_three(m):
        for g in range(groups):
            merges[m * groups + g].start3()

    def merge_finish(m):
        for g in range(groups):
            val, st = merges[m * groups + g].finish()
            tile = st[...]
            inv = 1.0 / tile[GROUP:]
            stat[m, g, :GROUP] = tile[:GROUP]
            invs_ref[m, g] = inv
            for h in range(GROUP):
                att[m, g * rows + h * HD : g * rows + (h + 1) * HD, :] = (
                    val[h * HD : (h + 1) * HD, :].astype(F32) * inv[h : h + 1]
                ).astype(BF16)

    n = sems_per_item(Y, X)
    gathers = [[], []]
    for m in range(micro):
        for g in range(groups):
            ds = pl.ds(g * rows, rows)
            for t, (own, out) in enumerate(
                ((datt.at[m, ds], datt_out.at[m, :, :, :, ds]), (stat.at[m, g], stat_out.at[m, g]))
            ):
                i = (m * groups + g) * 2 + t
                gathers[m].append(
                    (
                        Gather(p, own, out, gsend, grecv, i * n, g % 2 == 0),
                        pltpu.make_async_copy(own, out.at[p.y, p.x, p.c], gloc.at[i]),
                    )
                )

    def gather_one(m):
        for item, copy in gathers[m]:
            item.start1()
            copy.start()

    def gather_two(m):
        for item, copy in gathers[m]:
            copy.wait()
            item.start2()

    def gather_three(m):
        for item, copy in gathers[m]:
            item.start3()

    def forward(m):
        at = att[m].T
        attk[m] = at
        wo = w[:width]
        z1 = x_ref[m].astype(F32) + (dot_f32(at, wo, ((1,), (1,))) + bo)
        norm, inv = layer_norm(z1)
        n1[...] = norm
        mid = norm * g1 + e1
        low[m] = mid.astype(BF16)
        inner = low[m]

        def body(i, acc):
            r = pl.multiple_of(i * wide, wide)
            pre = dot_f32(inner, w[pl.ds(width + r, wide)], ((1,), (1,))) + bu_ref[:, pl.ds(r, wide)]
            half = 0.5 + 0.5 * lax.erf(pre * math.sqrt(0.5))
            low_h = (pre * half).astype(BF16)
            hid[m, :, pl.ds(r, wide)] = low_h
            slope[:, pl.ds(r, wide)] = half + pre * (
                jnp.exp(-0.5 * pre * pre) * (1.0 / math.sqrt(2.0 * math.pi))
            )
            return acc + dot_f32(low_h, w[pl.ds(width + FF + r, wide)], ((1,), (0,)))

        f = lax.fori_loop(0, parts, body, jnp.zeros((tok, width), F32)) + bd
        norm2, inv2 = layer_norm(mid + f)
        n2[...] = norm2
        out_ref[m] = (norm2 * g2 + e2).astype(BF16)
        return inv, inv2

    def backward(m, invs, between=lambda: None):
        inv, inv2 = invs
        cot = cot_ref[m].astype(F32)
        norm2 = n2[...]
        dz2 = norm_back(cot, norm2, inv2, g2)
        dg2 = jnp.sum(cot * norm2, axis=0, keepdims=True)
        de2 = jnp.sum(cot, axis=0, keepdims=True)
        df_low = dz2.astype(BF16)
        df[m] = df_low
        dbd = jnp.sum(df_low.astype(F32), axis=0, keepdims=True)

        def body(i, acc):
            r = pl.multiple_of(i * wide, wide)
            dh = dot_f32(df_low, w[pl.ds(width + FF + r, wide)], ((1,), (1,)))
            dp = (dh * slope[:, pl.ds(r, wide)]).astype(BF16)
            dpre[m, :, pl.ds(r, wide)] = dp
            part = jnp.sum(dp.astype(F32), axis=0, keepdims=True)
            dbu_ref[:, pl.ds(r, wide)] += part
            return acc + dot_f32(dp, w[pl.ds(width + r, wide)], ((1,), (0,)))

        dx1 = lax.fori_loop(0, parts // 2, body, dz2)
        between()
        dx1 = lax.fori_loop(parts // 2, parts, body, dx1)
        norm = n1[...]
        dg1 = jnp.sum(dx1 * norm, axis=0, keepdims=True)
        de1 = jnp.sum(dx1, axis=0, keepdims=True)
        dz1 = norm_back(dx1, norm, inv, g1)
        dz_ref[m] = dz1
        da_low = dz1.astype(BF16)
        da[m] = da_low
        dbo = jnp.sum(da_low.astype(F32), axis=0, keepdims=True)
        sums = jnp.concatenate([dbo, dg1, de1, dbd, dg2, de2, dg2, dg2], axis=0)
        dvec_ref[...] += sums
        dt = dot_f32(da_low, w[:width], ((1,), (0,))).T
        for g in range(groups):
            for h in range(GROUP):
                r = g * rows + h * HD
                part = dt[r : r + HD] * invs_ref[m, g, h : h + 1]
                datt[m, r : r + HD, :] = part.astype(BF16)
                stat[m, g, GROUP + h : GROUP + h + 1] = jnp.sum(
                    part * att[m, r : r + HD, :].astype(F32), axis=0, keepdims=True
                )

    step = width // 2

    def chunk_grad(slot, at, chunk):
        for left, right, lo, count in ((da, attk, 0, width), (dpre, low, width, FF), (hid, df, width + FF, FF)):

            @pl.when((chunk * step >= lo) & (chunk * step < lo + count))
            def _():
                cols = pl.ds(pl.multiple_of(chunk * step - lo, step), step)
                total = dot_f32(left[0, :, cols], right[0], ((0,), (0,)))
                for m in range(1, micro):
                    total = total + dot_f32(left[m, :, cols], right[m], ((0,), (0,)))
                dw[slot, pl.ds(pl.multiple_of(at, step), step)] = total.astype(BF16)

    def block_grad(b, slot):
        per = BLOCK_COLUMNS // step

        def body(t, carry):
            chunk_grad(slot, t * step, b * per + t)
            return carry

        lax.fori_loop(0, per, body, 0)

    merge_one(0)
    merge_two(0)
    for copy in wremote:
        copy.start()
    merge_one(1)
    merge_three(0)
    merge_two(1)
    merge_finish(0)
    for copy in wcopies:
        copy.wait()
    for copy in wremote:
        copy.wait_recv()
    dvec_ref[...] = jnp.zeros_like(dvec_ref)
    dbu_ref[...] = jnp.zeros_like(dbu_ref)

    def turn(m, carry):
        invs = forward(m)
        pl.when(m == 1)(lambda: gather_two(0))
        backward(m, invs, lambda: pl.when(m == 0)(lambda: merge_three(1)))

        @pl.when(m == 0)
        def _():
            gather_one(0)
            merge_finish(1)

        @pl.when(m == 1)
        def _():
            gather_one(1)
            gather_three(0)

        return carry

    lax.fori_loop(0, micro, turn, 0)
    if pieces:
        half, piece = w_refs[0].shape[:2]
        keeps = []

        def cores(b):
            slot = lax.rem(b, 2)
            copies = []
            for y in range(Y):
                for x in range(X):
                    i = (b * Y + y) * X + x
                    there = pl.multiple_of(p.keyof(y, x, 1 - p.c) * piece, 16)
                    copies.append(
                        remote(
                            dw.at[slot, pl.ds(there, piece)], core_in.at[b, y, x],
                            csend.at[i], crecv.at[i], p.core_peer(),
                        )
                    )
            return copies

        def one_block(b, carry):
            slot = lax.rem(b, 2)

            @pl.when(b >= 2)
            def _():
                for copy in cores(b - 2):
                    copy.wait_send()

            block_grad(b, slot)
            for copy in cores(b):
                copy.start()
            for y in range(Y):
                for x in range(X):
                    here = pl.multiple_of(p.keyof(y, x, p.c) * piece, 16)
                    core_acc[b, y, x] = dw[slot, pl.ds(here, piece)]
            return carry

        lax.fori_loop(0, blocks // 2, one_block, 0)
        gather_two(1)
        lax.fori_loop(blocks // 2, blocks, one_block, 0)
        gather_three(1)

        def add(i, carry):
            b, y, x = i // (Y * X), lax.rem(i // X, Y), lax.rem(i, X)
            merge_sum([core_acc.at[b, y, x]], [core_in.at[b, y, x]])
            return carry

        def add_block(b, carry):
            for copy in cores(b):
                copy.wait_recv()
            lax.fori_loop(b * Y * X, (b + 1) * Y * X, add, 0)
            return carry

        lax.fori_loop(0, blocks, add_block, 0)
        first, last = pl.ds(0, half), pl.ds(half, half)
        for x in range(X):
            keeps.append((core_acc.at[first, p.y, x], keep_a.at[x]))
            for d in range(1, Y):
                keeps.append((core_acc.at[first, p.yo(d), x], send_a.at[d - 1, x]))
        for y in range(Y):
            keeps.append((core_acc.at[last, y, p.x], keep_b.at[y]))
            for d in range(1, X):
                keeps.append((core_acc.at[last, y, p.xo(d)], send_b.at[d - 1, y]))
        keeps = [pltpu.make_async_copy(src, dst, dwsem.at[i]) for i, (src, dst) in enumerate(keeps)]
        for copy in keeps:
            copy.start()
        for copy in keeps:
            copy.wait()
        for b in (blocks - 2, blocks - 1):
            for copy in cores(jnp.int32(b)):
                copy.wait_send()
    else:
        copies = []
        for b in range(blocks):
            slot = b % 2
            if b >= 2:
                copies[b - 2].wait()
            block_grad(b, slot)
            copies.append(
                pltpu.make_async_copy(
                    dw.at[slot], dw_out.at[pl.ds(b * BLOCK_COLUMNS, BLOCK_COLUMNS)], dwsem.at[slot]
                )
            )
            copies[-1].start()
            if b == blocks // 2:
                gather_two(1)
        for copy in copies[-2:]:
            copy.wait()
        gather_three(1)
    for item in merges:
        item.drain()
    for copy in wremote:
        copy.wait_send()
    for m in range(micro):
        for item, copy in gathers[m]:
            item.finish()


def middle(mesh_dims, o_part, st_part, x_own, cot, weights, vec, bias_up):
    Y, X, R = mesh_dims
    micro, tok, width = x_own.shape
    groups = st_part.shape[1]
    items = micro * groups
    merge_sems = sems_per_item(Y, X) * 2 * items
    strows = STAT_ROWS
    ffw = 2 * FF + width
    blocks = ffw // BLOCK_COLUMNS
    pieces = len(weights) > 1
    outs = [
        (jax.ShapeDtypeStruct((micro, tok, width), BF16), VMEM_SPEC),
        (jax.ShapeDtypeStruct((micro, Y, X, 2, width, tok), BF16), ANY),
        (jax.ShapeDtypeStruct((micro, groups, Y, X, 2, strows, tok), F32), ANY),
        (jax.ShapeDtypeStruct((micro, tok, width), F32), VMEM_SPEC),
        (jax.ShapeDtypeStruct((8, width), F32), VMEM_SPEC),
        (jax.ShapeDtypeStruct((1, FF), F32), VMEM_SPEC),
    ]
    extra = []
    if pieces:
        half, piece = weights[0].shape[:2]
        wsems = 2 * Y * X * half
        outs += [
            (jax.ShapeDtypeStruct((max(Y - 1, 1), X, half, piece, width), BF16), ANY),
            (jax.ShapeDtypeStruct((X, half, piece, width), BF16), ANY),
            (jax.ShapeDtypeStruct((max(X - 1, 1), Y, half, piece, width), BF16), ANY),
            (jax.ShapeDtypeStruct((Y, half, piece, width), BF16), ANY),
        ]
        extra = [
            pltpu.VMEM((blocks, Y, X, piece, width), BF16),
            pltpu.VMEM((blocks, Y, X, piece, width), BF16),
            pltpu.SemaphoreType.DMA((blocks * Y * X,)),
            pltpu.SemaphoreType.DMA((blocks * Y * X,)),
        ]
    else:
        wsems = 1
        outs += [(jax.ShapeDtypeStruct((ffw, width), BF16), ANY)]
    return pl.pallas_call(
        functools.partial(middle_kernel, Y, X, R, blocks, pieces),
        out_shape=tuple(o for o, _ in outs),
        in_specs=[ANY, ANY, VMEM_SPEC, VMEM_SPEC, VMEM_SPEC, VMEM_SPEC] + [ANY] * len(weights),
        out_specs=tuple(spec for _, spec in outs),
        scratch_shapes=scatter_scratch(Y, X, items, (GROUP * HD, tok), BF16, None)
        + scatter_scratch(Y, X, items, (2 * GROUP, tok), F32, None)
        + [
            pltpu.SemaphoreType.DMA((merge_sems,)),
            pltpu.SemaphoreType.DMA((merge_sems,)),
            pltpu.SemaphoreType.DMA((items * 2,)),
            pltpu.SemaphoreType.DMA((merge_sems,)),
            pltpu.SemaphoreType.DMA((merge_sems,)),
            pltpu.SemaphoreType.DMA((items * 2,)),
            pltpu.SemaphoreType.DMA((wsems,)),
            pltpu.SemaphoreType.DMA((wsems,)),
            pltpu.SemaphoreType.DMA((wsems,)),
            pltpu.SemaphoreType.DMA((2 * X * Y,)),
            pltpu.VMEM((ffw, width), BF16),
            pltpu.VMEM((micro, width, tok), BF16),
            pltpu.VMEM((micro, tok, width), BF16),
            pltpu.VMEM((micro, tok, width), BF16),
            pltpu.VMEM((micro, tok, FF), BF16),
            pltpu.VMEM((micro, tok, FF), BF16),
            pltpu.VMEM((tok, FF), F32),
            pltpu.VMEM((micro, tok, width), BF16),
            pltpu.VMEM((micro, tok, width), BF16),
            pltpu.VMEM((tok, width), F32),
            pltpu.VMEM((tok, width), F32),
            pltpu.VMEM((micro, width, tok), BF16),
            pltpu.VMEM((micro, groups, strows, tok), F32),
            pltpu.VMEM((micro, groups, GROUP, tok), F32),
            pltpu.VMEM((2, BLOCK_COLUMNS, width), BF16),
        ]
        + extra,
        compiler_params=pltpu.CompilerParams(
            collective_id=2, has_side_effects=True, vmem_limit_bytes=VMEM_LIMIT
        ),
        name="middle",
    )(o_part, st_part, x_own, cot, vec, bias_up, *weights)


def tail_kernel(
    Y, X, R, inverse,
    dq_ref, dk_hbm, dv_hbm, x_hbm, dz_hbm, w_ref, vec_ref, bu_ref, xg_ref, dqs_hbm, *refs,
):
    suma_hbm, got_a, sumb_hbm, got_b = refs[0], refs[1:X], refs[X], refs[X + 1 : X + Y]
    tok_ref, late_ref, early_ref, sum_ref = refs[X + Y : X + Y + 4]
    (
        qa, q1, q2, q3, send, recv, loc,
        part, a, r1, r2, r3, bsend, brecv, bloc,
        fin, stage, rz, zsend, zrecv, qf, qz, rq, qsend, qrecv,
        small, sbuf, ssend, srecv, w, wsem, dq, dqv, xv, acc, vsem,
        dk_ref, dv_ref, x_ref, dqs_ref, sum_a, sum_b, dz_ref, fsem,
    ) = refs[X + Y + 4 :]
    p = Place(Y, X, R)
    micro, tok, width = x_ref.shape
    slots_here = late_ref.shape[0]
    groups = qa.shape[0] // micro
    rows = GROUP * HD
    n = sems_per_item(Y, X)
    piece = part.shape[4]
    p.announce(True)
    outer = (dk_hbm, dv_hbm, x_hbm, dqs_hbm, suma_hbm, sumb_hbm, dz_hbm)
    inner = (dk_ref, dv_ref, x_ref, dqs_ref, sum_a, sum_b, dz_ref)
    fetch = [pltpu.make_async_copy(a, b, fsem.at[i]) for i, (a, b) in enumerate(zip(outer, inner))]
    loads = [
        pltpu.make_async_copy(dq_ref, dqv, vsem.at[0]),
        pltpu.make_async_copy(xg_ref, xv, vsem.at[1]),
    ]
    wcopy = pltpu.make_async_copy(w_ref, w, wsem)
    for copy in fetch + loads + [wcopy]:
        copy.start()
    for copy in fetch[:6]:
        copy.wait()
    for at, total, got in ((p.x, sum_a, got_a), (p.y, sum_b, got_b)):
        count = total.shape[1]
        base = 0 if total is sum_a else count

        def add(b, carry, at=at, total=total, got=got, base=base):
            value = total[at, b].astype(F32)
            for ref in got:
                value = value + ref[b].astype(F32)
            fin[base + b] = value.astype(BF16)
            return carry

        lax.fori_loop(0, count, add, 0)

    def reorder(s, carry):
        stage[s] = fin[jnp.maximum(inverse[s] - EARLY, 0)]
        return carry

    lax.fori_loop(0, stage.shape[0], reorder, 0)
    ones = jnp.ones((8, tok), BF16)
    bias_v = dot_f32(ones, dv_ref[0], ((1,), (1,)))
    sum_q = dqs_ref[0]
    for m in range(1, micro):
        bias_v = bias_v + dot_f32(ones, dv_ref[m], ((1,), (1,)))
        sum_q = sum_q + dqs_ref[m]
    sums = [sum_q.T[:1], bias_v[:1], vec_ref[:3]]
    sums += [bu_ref[:, i * width : (i + 1) * width] for i in range(FF // width)]
    sums += [vec_ref[3:6], jnp.zeros((4, width), F32)]
    small[...] = jnp.concatenate(sums, axis=0).astype(BF16)
    stages = [[p.core_peer()]]
    stages.append([p.x_peer(d) for d in range(1, X)])
    stages.append([p.y_peer(d) for d in range(1, Y)])
    stages.append([p.z_peer(d) for d in range(1, R)])
    scopies = []
    at = 0
    for peers in stages:
        row = []
        for peer in peers:
            row.append(remote(small, sbuf.at[at], ssend.at[at], srecv.at[at], peer))
            at += 1
        scopies.append(row)

    def small_start(t):
        for copy in scopies[t]:
            copy.start()

    def small_wait(t):
        at = sum(len(row) for row in scopies[:t])
        for copy in scopies[t]:
            copy.wait_recv()
        for copy in scopies[t]:
            copy.wait_send()
        total = small[...].astype(F32)
        for i in range(len(scopies[t])):
            total = total + sbuf[at + i].astype(F32)
        return total

    def token_grad(m):
        total = dz_ref[m] + dot_f32(dq[m], w[:width], ((0,), (0,)))
        total = total + dot_f32(dk_ref[m], w[width : 2 * width], ((0,), (0,)))
        total = total + dot_f32(dv_ref[m], w[2 * width :], ((0,), (0,)))
        tok_ref[m] = total.astype(BF16)

    p.meet()
    small_start(0)
    zcopies = []
    if R == 4:
        near = p.r + 1 - 2 * lax.rem(p.r, 2)
        far = p.ro(2)
        classes = (p.r, far)
        one = [
            [
                remote(
                    stage.at[q * slots_here + s], rz.at[k, s], zsend.at[k, s], zrecv.at[k, s], {"rows": near}
                )
                for k, q in enumerate((near, lax.rem(near + 2, R)))
            ]
            for s in range(slots_here)
        ]
        two = [
            remote(stage.at[far * slots_here + s], rz.at[2, s], zsend.at[2, s], zrecv.at[2, s], {"rows": far})
            for s in range(slots_here)
        ]
        for copies in one:
            for copy in copies:
                copy.start()

        def z_pass(s):
            for copy in one[s]:
                copy.wait_recv()
            for k, q in enumerate(classes):
                merge_sum([stage.at[q * slots_here + s]], [rz.at[k, s]])
            two[s].start()

        def z_total(s):
            two[s].wait_recv()
            return stage[p.r * slots_here + s].astype(F32) + rz[2, s].astype(F32)

        zcopies = [copy for copies in one for copy in copies] + two
    else:
        for d in range(1, R):
            there = pl.ds(p.ro(d) * slots_here, slots_here)
            copy = remote(stage.at[there], rz.at[d - 1], zsend.at[d - 1, 0], zrecv.at[d - 1, 0], p.z_peer(d))
            copy.start()
            zcopies.append(copy)

        def z_pass(s):
            pass

        def z_total(s):
            if s == 0:
                for copy in zcopies:
                    copy.wait_recv()
            total = stage[p.r * slots_here + s].astype(F32)
            for d in range(1, R):
                total = total + rz[d - 1, s].astype(F32)
            return total

    qitems = []
    for m in range(micro):
        for g in range(groups):
            i = m * groups + g
            item = Scatter(
                p, [dq_ref.at[m, :, :, :, pl.ds(g * rows, rows)]],
                [qa.at[i]], [q1.at[i]], [q2.at[i]], [q3.at[i]],
                send, recv, loc, i * n, i, g % 2 == 0, merge_sum,
            )
            qitems.append(item)
    first, last = qitems[: len(qitems) - groups], qitems[len(qitems) - groups :]
    for item in first:
        item.start1()

    def product(ref, first, count):
        total = dot_f32(ref[0, first : first + count], x_ref[0], ((1,), (0,)))
        for m in range(1, micro):
            total = total + dot_f32(ref[m, first : first + count], x_ref[m], ((1,), (0,)))
        return total.astype(BF16)

    def put(b, first, value):
        at = 0
        while at < value.shape[0]:
            key, off = divmod(first + at, piece)
            count = min(piece - off, value.shape[0] - at)
            y, x, c = key // (2 * X), key // 2 % X, key % 2
            part[b, y, x, c, off : off + count] = value[at : at + count]
            at += count

    cuts = ((0, piece // 32 * 16, True), (piece // 32 * 16, piece - piece // 32 * 16, False))

    def block_items(b):
        out = []
        for t, (first, count, y_first) in enumerate(cuts):
            ds = pl.ds(first, count)
            i = b * len(cuts) + t
            out.append(
                Scatter(
                    p, [part.at[b, :, :, :, ds]], [a.at[b, :, :, ds]], [r1.at[b, :, :, ds]],
                    [r2.at[b, :, :, ds]], [r3.at[b, :, ds]],
                    bsend, brecv, bloc, i * n, i, y_first, merge_sum,
                )
            )
        return out

    class Block:
        def __init__(self, b):
            self.b, self.items = b, block_items(b)
            self.one = [
                remote(qz.at[b, p.ro(d)], rq.at[b, d - 1], qsend.at[b, 0, d], qrecv.at[b, 0, d], p.z_peer(d))
                for d in range(1, R)
            ]
            mine = early_ref.at[b, p.r]
            self.two = [
                remote(mine, mine, qsend.at[b, 1, d], qrecv.at[b, 1, d], p.z_peer(d)) for d in range(1, R)
            ]

        def step(self, name):
            for item in self.items:
                getattr(item, name)()

        def z_one(self):
            for item, (first, count, _) in zip(self.items, cuts):
                (val,) = item.finish()
                qf[first : first + count] = val[...].astype(F32)
            share = qz.shape[2]
            for i in range(R):
                qz[self.b, i] = qf[i * share : (i + 1) * share].astype(BF16)
            for copy in self.one:
                copy.start()

        def z_two(self):
            for copy in self.one:
                copy.wait_recv()
            total = qz[self.b, p.r].astype(F32)
            for d in range(1, R):
                total = total + rq[self.b, d - 1].astype(F32)
            early_ref[self.b, p.r] = total.astype(BF16)
            for copy in self.two:
                copy.start()

        def finish(self):
            for copy in self.two:
                copy.wait_recv()
            for item in self.items:
                item.drain()
            for copy in self.one + self.two:
                copy.wait_send()

    block0, block1 = Block(0), Block(1)
    half = width // 2
    put(1, 0, product(dk_ref, half, half))
    small[...] = small_wait(0).astype(BF16)
    small_start(1)
    put(1, half, product(dv_ref, 0, width))
    block1.step("start1")
    small[...] = small_wait(1).astype(BF16)
    small_start(2)
    put(0, width, product(dk_ref, 0, half))
    small[...] = small_wait(2).astype(BF16)
    small_start(3)
    for item in first:
        item.start2()
    for item in last:
        item.start1()
    for copy in loads:
        copy.wait()
    acc[...] = jnp.zeros_like(acc)
    line = 2 * tok
    turns = micro * Y * X

    def query_grad(i, carry):
        m, y, x = i // (Y * X), lax.rem(i // X, Y), lax.rem(i, X)
        left = jnp.concatenate([dqv[m, y, x, c] for c in range(2)], axis=1)
        right = xv[m, pl.ds(pl.multiple_of(lax.rem(i, Y * X) * line, line), line)]
        acc[...] += dot_f32(left, right, ((1,), (0,)))
        return carry

    lax.fori_loop(0, turns // 2, query_grad, 0)
    z_pass(0)
    lax.fori_loop(turns // 2, turns, query_grad, 0)
    put(0, 0, acc[...].astype(BF16))
    block0.step("start1")
    block1.step("start2")
    block0.step("start2")
    for s in range(1, slots_here):
        z_pass(s)
    block1.step("start3")
    block0.step("start3")
    for item in last:
        item.start2()
    for item in first:
        item.start3()
    block1.z_one()
    block0.z_one()
    for item in last:
        item.start3()
    block1.z_two()
    block0.z_two()
    for s in range(slots_here):
        late_ref[s] = z_total(s)
    wcopy.wait()
    fetch[6].wait()
    def token_grad(m, carry):
        for k in range(micro):

            @pl.when(m == k)
            def _():
                for g in range(groups):
                    (val,) = qitems[k * groups + g].finish()
                    dq[k, g * rows : (g + 1) * rows, :] = val[...]

        total = dz_ref[m] + dot_f32(dq[m], w[:width], ((0,), (0,)))
        total = total + dot_f32(dk_ref[m], w[width : 2 * width], ((0,), (0,)))
        total = total + dot_f32(dv_ref[m], w[2 * width :], ((0,), (0,)))
        tok_ref[m] = total.astype(BF16)
        return carry

    lax.fori_loop(0, micro, token_grad, 0)
    sum_ref[...] = small_wait(3)
    block1.finish()
    block0.finish()
    for item in qitems:
        item.drain()
    for copy in zcopies:
        copy.wait_send()


def tail(mesh_dims, inverse, dq_part, dk, dv, x_own, grad_one, w_early, fin_a, fin_b, dvec, d_bias_up, x_all, dq_sum):
    Y, X, R = mesh_dims
    micro, tok, width = x_own.shape
    half, n = fin_a[0].shape[1:3]
    late = 2 * half
    blocks = EARLY + late
    slots_here = blocks // R
    groups = width // (GROUP * HD)
    items = micro * groups
    per = sems_per_item(Y, X)
    share = n // R
    cuts = 2
    small = (16, width)
    hops = 1 + (X - 1) + (Y - 1) + (R - 1)
    return pl.pallas_call(
        functools.partial(tail_kernel, Y, X, R),
        out_shape=(
            jax.ShapeDtypeStruct((micro, tok, width), BF16),
            jax.ShapeDtypeStruct((slots_here, n, width), F32),
            jax.ShapeDtypeStruct((EARLY, R, share, width), BF16),
            jax.ShapeDtypeStruct(small, F32),
        ),
        in_specs=[pl.BlockSpec(memory_space=pltpu.SMEM), ANY]
        + [ANY] * 4
        + [ANY, VMEM_SPEC, VMEM_SPEC, ANY, ANY]
        + ([ANY] + [VMEM_SPEC] * (X - 1) + [ANY] + [VMEM_SPEC] * (Y - 1)),
        out_specs=(VMEM_SPEC,) * 4,
        scratch_shapes=scatter_scratch(Y, X, items, (GROUP * HD, tok), BF16, None)
        + [
            pltpu.SemaphoreType.DMA((per * items,)),
            pltpu.SemaphoreType.DMA((per * items,)),
            pltpu.SemaphoreType.DMA((items,)),
            pltpu.VMEM((EARLY, Y, X, 2, n, width), BF16),
        ]
        + scatter_scratch(Y, X, EARLY, (n, width), BF16, None)
        + [
            pltpu.SemaphoreType.DMA((per * EARLY * cuts,)),
            pltpu.SemaphoreType.DMA((per * EARLY * cuts,)),
            pltpu.SemaphoreType.DMA((EARLY * cuts,)),
            pltpu.VMEM((late, n, width), BF16),
            pltpu.VMEM((blocks, n, width), BF16),
            pltpu.VMEM((R - 1, slots_here, n, width), BF16),
            pltpu.SemaphoreType.DMA((R - 1, slots_here)),
            pltpu.SemaphoreType.DMA((R - 1, slots_here)),
            pltpu.VMEM((n, width), F32),
            pltpu.VMEM((EARLY, R, share, width), BF16),
            pltpu.VMEM((EARLY, R - 1, share, width), BF16),
            pltpu.SemaphoreType.DMA((EARLY, 2, R)),
            pltpu.SemaphoreType.DMA((EARLY, 2, R)),
            pltpu.VMEM(small, BF16),
            pltpu.VMEM((hops,) + small, BF16),
            pltpu.SemaphoreType.DMA((hops,)),
            pltpu.SemaphoreType.DMA((hops,)),
            pltpu.VMEM((3 * width, width), BF16),
            pltpu.SemaphoreType.DMA,
            pltpu.VMEM((micro, width, tok), BF16),
            pltpu.VMEM(dq_part.shape, BF16),
            pltpu.VMEM(x_all.shape, BF16),
            pltpu.VMEM((width, width), F32),
            pltpu.SemaphoreType.DMA((2,)),
            pltpu.VMEM(dk.shape, BF16),
            pltpu.VMEM(dv.shape, BF16),
            pltpu.VMEM(x_own.shape, BF16),
            pltpu.VMEM(dq_sum.shape, F32),
            pltpu.VMEM(fin_a[0].shape, BF16),
            pltpu.VMEM(fin_b[0].shape, BF16),
            pltpu.VMEM(grad_one.shape, F32),
            pltpu.SemaphoreType.DMA((7,)),
        ],
        compiler_params=pltpu.CompilerParams(
            collective_id=5, has_side_effects=True, vmem_limit_bytes=VMEM_LIMIT
        ),
        name="tail",
    )(inverse, dq_part, dk, dv, x_own, grad_one, w_early.reshape(3 * width, width), dvec, d_bias_up, x_all, dq_sum, *fin_a, *fin_b)


def project_kernel(scale, x_ref, own_ref, w_ref, vec_ref, q_ref, k_ref, v_ref, bias):
    width = x_ref.shape[2]

    @pl.when((pl.program_id(0) == 0) & (pl.program_id(1) == 0))
    def _():
        bias[...] = vec_ref[...].T

    q = dot_f32(w_ref[:width], x_ref[0], ((1,), (1,))) + bias[:, 6:7]
    q_ref[0] = q.astype(BF16) * jnp.asarray(scale, BF16)

    @pl.when(pl.program_id(1) == 0)
    def _():
        own = own_ref[0]
        k_ref[0] = dot_f32(w_ref[width : 2 * width], own, ((1,), (1,))).astype(BF16)
        v_ref[0] = (dot_f32(w_ref[2 * width :], own, ((1,), (1,))) + bias[:, 7:8]).astype(BF16)


def project(x_all, x_own, w_t, vec, scale):
    micro, slots, width = x_all.shape
    own = x_own.shape[1]
    wide = min(1024, slots)
    return pl.pallas_call(
        functools.partial(project_kernel, scale),
        grid=(micro, slots // wide),
        out_shape=(
            jax.ShapeDtypeStruct((micro, width, slots), BF16),
            jax.ShapeDtypeStruct((micro, width, own), BF16),
            jax.ShapeDtypeStruct((micro, width, own), BF16),
        ),
        in_specs=[
            pl.BlockSpec((1, wide, width), lambda m, t: (m, t, 0)),
            pl.BlockSpec((1, own, width), lambda m, t: (m, 0, 0)),
            pl.BlockSpec((3 * width, width), lambda m, t: (0, 0)),
            pl.BlockSpec((8, width), lambda m, t: (0, 0)),
        ],
        out_specs=(
            pl.BlockSpec((1, width, wide), lambda m, t: (m, 0, t)),
            pl.BlockSpec((1, width, own), lambda m, t: (m, 0, 0)),
            pl.BlockSpec((1, width, own), lambda m, t: (m, 0, 0)),
        ),
        scratch_shapes=[pltpu.VMEM((width, 8), F32)],
        compiler_params=pltpu.CompilerParams(vmem_limit_bytes=VMEM_LIMIT),
        cost_estimate=pl.CostEstimate(
            flops=2 * micro * width * width * (slots + 2 * own),
            bytes_accessed=4 * micro * width * slots,
            transcendentals=0,
        ),
        name="project",
    )(x_all, x_own, w_t, vec)


def attention_forward_kernel(q_ref, k_ref, v_ref, prev_ref, segk_ref, segq_ref, *refs):
    logit_ref, e_ref, o_ref, st_ref, top_ref, mask_ref = refs[-6:]
    h = pl.program_id(0)
    chunks, wide = o_ref.shape[1], o_ref.shape[3]

    @pl.when(h == 0)
    def _():
        mask_ref[...] = jnp.where(segk_ref[0] == segq_ref[0], 0.0, NEG_BIG)

    for i in range(PER):
        rows = slice(i * HD, (i + 1) * HD)
        hg = lax.rem(h * PER + i, GROUP)
        score = dot_f32(k_ref[rows], q_ref[rows], ((0,), (0,)))
        raw = score + prev_ref[0, 0, i].astype(F32)
        logit_ref[0, 0, i] = raw.astype(BF16)
        masked = raw + mask_ref[...]
        top = jnp.maximum(jnp.max(masked, axis=0, keepdims=True), NEG_FLOOR)
        expo = jnp.exp(masked - top)
        total = jnp.sum(expo, axis=0, keepdims=True)
        low = expo.astype(BF16)
        e_ref[0, i] = low
        out = dot_f32(v_ref[rows], low, ((1,), (0,))).astype(BF16)
        for t in range(chunks):
            cols = slice(t * wide, (t + 1) * wide)
            o_ref[0, t, rows] = out[:, cols]
            st_ref[0, 0, t, pl.ds(hg, 1), :] = top[:, cols]
            st_ref[0, 0, t, pl.ds(GROUP + hg, 1), :] = total[:, cols]
            top_ref[0, 0, t, pl.ds(hg, 1), :] = top[:, cols]


def attention_forward(m, so_far, q, k, v, prev, segk, segq, chunks, wide):
    micro, _, heads, own, slots = prev.shape
    groups = heads // GROUP
    score = pl.BlockSpec((1, 1, PER, own, slots), lambda h: (m, 0, h, 0, 0))
    stat = pl.BlockSpec((1, 1, chunks, 2 * GROUP, wide), lambda h: (m, h * PER // GROUP, 0, 0, 0))
    return pl.pallas_call(
        attention_forward_kernel,
        grid=(heads // PER,),
        out_shape=(
            jax.ShapeDtypeStruct(prev.shape, BF16),
            jax.ShapeDtypeStruct((micro, heads, own, slots), BF16),
            jax.ShapeDtypeStruct((micro, chunks, heads * HD, wide), BF16),
            jax.ShapeDtypeStruct((micro, groups, chunks, 2 * GROUP, wide), F32),
            jax.ShapeDtypeStruct((micro, groups, chunks, 2 * GROUP, wide), F32),
        ),
        in_specs=[
            pl.BlockSpec((None, PER * HD, slots), lambda h: (m, h, 0)),
            pl.BlockSpec((None, PER * HD, own), lambda h: (m, h, 0)),
            pl.BlockSpec((None, PER * HD, own), lambda h: (m, h, 0)),
            score,
            pl.BlockSpec((1, own, 1), lambda h: (m, 0, 0)),
            pl.BlockSpec((1, 1, slots), lambda h: (m, 0, 0)),
        ]
        + [ANY] * len(so_far),
        out_specs=(
            score,
            pl.BlockSpec((1, PER, own, slots), lambda h: (m, h, 0, 0)),
            pl.BlockSpec((1, chunks, PER * HD, wide), lambda h: (m, 0, h, 0)),
            stat,
            stat,
        ),
        input_output_aliases={6 + i: i for i in range(len(so_far))},
        scratch_shapes=[pltpu.VMEM((own, slots), F32)],
        compiler_params=pltpu.CompilerParams(vmem_limit_bytes=VMEM_LIMIT),
        cost_estimate=pl.CostEstimate(
            flops=heads * 2 * 2 * own * slots * HD,
            bytes_accessed=heads * own * slots * 6,
            transcendentals=heads * own * slots,
        ),
        name="attention_forward",
    )(q, k, v, prev, segk, segq, *so_far)


def attention_backward_kernel(
    scale, first, e_ref, d_ref, st_ref, top_ref, q_ref, k_ref, v_ref, *refs
):
    g_ref, dq_ref, dk_ref, dv_ref, sum_ref = refs[-5:]
    h = pl.program_id(0) + first
    chunks, wide = d_ref.shape[1], d_ref.shape[3]
    for i in range(PER):
        rows = slice(i * HD, (i + 1) * HD)
        hg = lax.rem(h * PER + i, GROUP)

        def row(ref, first):
            return jnp.concatenate([ref[0, 0, t, pl.ds(first + hg, 1), :] for t in range(chunks)], axis=1)

        weight = jnp.exp(row(top_ref, 0) - row(st_ref, 0))
        dots = row(st_ref, GROUP) * weight
        low = e_ref[0, i]
        datt = jnp.concatenate([d_ref[0, t, rows] for t in range(chunks)], axis=1)
        grad_in = (datt.astype(F32) * weight).astype(BF16)
        soft = dot_f32(v_ref[rows], grad_in, ((0,), (0,))) - dots
        grad = (low.astype(F32) * soft).astype(BF16)
        g_ref[0, 0, i] = grad
        dq = dot_f32(k_ref[rows], grad, ((1,), (0,))) * scale
        sum_ref[0, rows] = jnp.broadcast_to(jnp.sum(dq, axis=1, keepdims=True), (HD, 128))
        dq = dq.astype(BF16)
        for t in range(chunks):
            dq_ref[0, t, rows] = dq[:, t * wide : (t + 1) * wide]
        dv_ref[0, rows] = dot_f32(grad_in, low, ((1,), (1,))).astype(BF16)
        dk_ref[0, rows] = dot_f32(q_ref[rows], grad, ((1,), (1,))).astype(BF16)


def attention_backward(first, last, so_far, expo, datt, st, tops, q, k, v, scale):
    micro, heads, own, slots = expo.shape
    chunks, wide = datt.shape[1], datt.shape[3]
    steps = heads // PER
    at = lambda i: ((i + first) // steps, (i + first) % steps)
    flops = heads * 2 * 4 * own * slots * HD
    sts = st.shape[3]
    return pl.pallas_call(
        functools.partial(attention_backward_kernel, scale, first),
        grid=(last - first,),
        out_shape=(
            jax.ShapeDtypeStruct((micro, 1, heads, own, slots), BF16),
            jax.ShapeDtypeStruct((micro, chunks, heads * HD, wide), BF16),
            jax.ShapeDtypeStruct((micro, heads * HD, own), BF16),
            jax.ShapeDtypeStruct((micro, heads * HD, own), BF16),
            jax.ShapeDtypeStruct((micro, heads * HD, 128), F32),
        ),
        in_specs=[
            pl.BlockSpec((1, PER, own, slots), lambda i: (*at(i), 0, 0)),
            pl.BlockSpec((1, chunks, PER * HD, wide), lambda i: (at(i)[0], 0, at(i)[1], 0)),
            pl.BlockSpec((1, 1, chunks, sts, wide), lambda i: (at(i)[0], at(i)[1] * PER // GROUP, 0, 0, 0)),
            pl.BlockSpec((1, 1, chunks, 2 * GROUP, wide), lambda i: (at(i)[0], at(i)[1] * PER // GROUP, 0, 0, 0)),
            pl.BlockSpec((None, PER * HD, slots), lambda i: (*at(i), 0)),
            pl.BlockSpec((None, PER * HD, own), lambda i: (*at(i), 0)),
            pl.BlockSpec((None, PER * HD, own), lambda i: (*at(i), 0)),
        ]
        + [ANY] * len(so_far),
        out_specs=(
            pl.BlockSpec((1, 1, PER, own, slots), lambda i: (at(i)[0], 0, at(i)[1], 0, 0)),
            pl.BlockSpec((1, chunks, PER * HD, wide), lambda i: (at(i)[0], 0, at(i)[1], 0)),
            pl.BlockSpec((1, PER * HD, own), lambda i: (*at(i), 0)),
            pl.BlockSpec((1, PER * HD, own), lambda i: (*at(i), 0)),
            pl.BlockSpec((1, PER * HD, 128), lambda i: (*at(i), 0)),
        ),
        input_output_aliases={7 + i: i for i in range(len(so_far))},
        compiler_params=pltpu.CompilerParams(vmem_limit_bytes=VMEM_LIMIT),
        cost_estimate=pl.CostEstimate(
            flops=flops, bytes_accessed=heads * own * slots * 4, transcendentals=0
        ),
        name="attention_backward",
    )(expo, datt, st, tops, q, k, v, *so_far)


def shifted(arr, mesh_dims, dy, dx):
    if dy == 0 and dx == 0:
        return arr
    Y, X, _ = mesh_dims
    key = lambda y, x, c: (y * X + x) * 2 + c
    perm = [
        (key(y, x, c), key((y + dy) % Y, (x + dx) % X, c)) for y in range(Y) for x in range(X) for c in range(2)
    ]
    return lax.ppermute(arr, "keys", perm)


def late_weights_start(mesh_dims, own_first, own_last):
    Y, X, _ = mesh_dims
    first = [shifted(own_first, mesh_dims, 0, dx) for dx in range(X)]
    last = [shifted(own_last, mesh_dims, dy, 0) for dy in range(Y)]
    first_own = [shifted(own_first, mesh_dims, dy, 0) for dy in range(1, Y)]
    last_own = [shifted(own_last, mesh_dims, 0, dx) for dx in range(1, X)]
    return first, last, first_own, last_own


def late_weights_finish(mesh_dims, first, last, first_own, last_own):
    Y, X, _ = mesh_dims
    out = []
    for dy in range(Y):
        for dx in range(X):
            out.append(first_own[dy - 1] if dx == 0 and dy > 0 else shifted(first[dx], mesh_dims, dy, 0))
    for dy in range(Y):
        for dx in range(X):
            out.append(last_own[dx - 1] if dy == 0 and dx > 0 else shifted(last[dy], mesh_dims, 0, dx))
    return out


def late_grads_start(mesh_dims, send_a, keep_a, send_b, keep_b):
    Y, X, _ = mesh_dims
    first = [shifted(send_a[d - 1], mesh_dims, d, 0) for d in range(1, Y)]
    last = [shifted(send_b[d - 1], mesh_dims, 0, d) for d in range(1, X)]
    return (keep_a, first), (keep_b, last)


def late_grads_finish(mesh_dims, first, last):
    Y, X, _ = mesh_dims
    key = lax.axis_index("keys")
    x, y = (key // 2) % X, key // (2 * X)

    def line(keep, got, place, move):
        total = keep.astype(F32)
        for piece in got:
            total = total + piece.astype(F32)
        total = total.astype(BF16)
        count = total.shape[0]
        pick = lambda d: lax.dynamic_index_in_dim(total, (place + d) % count, 0, keepdims=False)
        return [total] + [move(pick(d), d) for d in range(1, count)]

    return (
        line(*first, x, lambda a, d: shifted(a, mesh_dims, 0, d)),
        line(*last, y, lambda a, d: shifted(a, mesh_dims, d, 0)),
    )


def halves(value):
    high = value.astype(BF16)
    return high, (value - high.astype(F32)).astype(BF16)


def update_weights_kernel(
    block_ids, first_column, fixes, late_ref, early_ref, basis_ref, master_ref, one_ref, two_ref,
    grad_out, one_out, two_out, master_out, copy_out, joined,
):
    s = pl.program_id(0)
    block = block_ids[s]
    early = early_ref[jnp.minimum(block, EARLY - 1)].astype(F32)
    share = early.shape[1]
    for i in range(early.shape[0]):
        joined[i * share : (i + 1) * share] = early[i]
    grad = jnp.where(block < EARLY, joined[...], late_ref[0])
    grad_out[0] = grad
    basis = basis_ref[0]
    basis_high, basis_low = halves(basis)

    def product(value, contract):
        n = value.shape[0]
        high, rest = halves(value)
        both = dot_f32(jnp.concatenate([high, rest], axis=0), basis_high, contract)
        return both[:n] + (both[n:] + dot_f32(high, basis_low, contract))

    rotated = product(grad, ((1,), (0,)))
    new_one = BETA_ONE * one_ref[0] + (1.0 - BETA_ONE) * rotated
    new_two = BETA_TWO * two_ref[0] + (1.0 - BETA_TWO) * rotated * rotated
    one_out[0] = new_one
    two_out[0] = new_two
    direction = new_one / fixes[0] / (jnp.sqrt(new_two / fixes[1]) + EPS_ADAM)
    back = product(direction, ((1,), (1,)))
    columns = first_column[s] + lax.broadcasted_iota(jnp.int32, (grad.shape[0], 1), 0)
    master = master_ref[0]
    new_master = master - column_rates(columns) * (back + DECAY * master)
    master_out[0] = new_master
    copy_out[0] = new_master.astype(BF16)


def update_weights(block_ids, first_column, fixes, late, early, basis, master, one, two):
    slots_here, n, width = master.shape
    mat = pl.BlockSpec((1, n, width), lambda s: (s, 0, 0))
    smem = pl.BlockSpec(memory_space=pltpu.SMEM)
    return pl.pallas_call(
        update_weights_kernel,
        grid=(slots_here,),
        out_shape=tuple(jax.ShapeDtypeStruct(master.shape, F32) for _ in range(4))
        + (jax.ShapeDtypeStruct(master.shape, BF16),),
        in_specs=[smem, smem, smem, mat, pl.BlockSpec(early.shape, lambda s: (0, 0, 0, 0)),
                  pl.BlockSpec((1, width, width), lambda s: (s, 0, 0)), mat, mat, mat],
        out_specs=(mat,) * 5,
        scratch_shapes=[pltpu.VMEM((n, width), F32)],
        compiler_params=pltpu.CompilerParams(vmem_limit_bytes=VMEM_LIMIT),
        name="update_weights",
    )(block_ids, first_column, fixes, late, early, basis, master, one, two)


def to_chunks(arr, chunks):
    pieces, rows, own = arr.shape[-3:]
    lead = arr.shape[:-3]
    if pieces == chunks:
        return arr
    per = pieces // chunks
    arr = arr.reshape(lead + (chunks, per, rows, own))
    return jnp.moveaxis(arr, -3, -2).reshape(lead + (chunks, rows, per * own))


def from_chunks(arr, pieces):
    chunks, rows, wide = arr.shape[-3:]
    lead = arr.shape[:-3]
    if pieces == chunks:
        return arr
    per = pieces // chunks
    arr = arr.reshape(lead + (chunks, rows, per, wide // per))
    return jnp.moveaxis(arr, -2, -3).reshape(lead + (pieces, rows, wide // per))


def per_device(
    mesh_dims,
    tokens,
    prev_logits,
    segments,
    out_cot,
    master_mat,
    mom1_mat,
    mom2_mat,
    eigen_bases,
    master_small,
    mom1_small,
    mom2_small,
    owners,
    step_count,
):
    Y, X, R = mesh_dims
    keys = Y * X * 2
    micro, row_count, key_len, width = tokens.shape
    slot_count = prev_logits.shape[4]
    slots_here, _, cols_here = master_mat.shape
    blocks = slots_here * R
    token_count = micro * key_len
    scale = HD ** (-0.5)
    key_index = lax.axis_index("keys")
    row_index = lax.axis_index("rows")
    wide = max(key_len, min(256, slot_count))
    chunks = slot_count // wide
    groups = H // GROUP

    x_own = tokens.reshape(micro, key_len, width)
    w_own = jnp.swapaxes(master_mat, 1, 2)
    small_low = master_small.astype(BF16).reshape(1, slots_here * cols_here)
    ext = lax.dynamic_update_slice(
        jnp.zeros((EXT, width), BF16), small_low, (row_index, jnp.int32(0))
    )
    fast = cols_here % 16 == 0
    wt, *w_late, ext_all, xg = gather_weights(mesh_dims, owners, w_own, ext, x_own)
    if fast:
        pieces = late_weights_start(mesh_dims, *w_late)
    else:
        late = [lax.all_gather(jnp.concatenate(w_late), "keys", axis=1).reshape(2 * FF + width, width)]
    w_t = wt.reshape(EARLY * BLOCK_COLUMNS, width)
    small_all = ext_all.reshape(keys, EXT, width)[:, :R, : slots_here * cols_here]
    params = (
        jnp.transpose(small_all.reshape(keys, R, slots_here, cols_here), (1, 2, 0, 3))
        .reshape(blocks * GAIN_ROW_WIDTH)
        .astype(F32)
    )
    bias_q = params[:width]
    bias_v = params[width : 2 * width]
    bias_o = params[2 * width : 3 * width]
    gain_one = params[3 * width : 4 * width]
    shift_one = params[4 * width : 5 * width]
    bias_up = params[5 * width : 5 * width + FF]
    bias_down = params[5 * width + FF : 6 * width + FF]
    gain_two = params[6 * width + FF : 7 * width + FF]
    shift_two = params[7 * width + FF :]

    vec = jnp.stack([bias_o, gain_one, shift_one, bias_down, gain_two, shift_two, bias_q, bias_v])
    q_all, k_all, v_all = project(xg.reshape(micro, slot_count, width), x_own, w_t, vec, scale)
    x_rows = x_own.reshape(token_count, width)

    seg_rows = segments.reshape(micro, slot_count)
    seg_keys = lax.dynamic_slice_in_dim(seg_rows, key_index * key_len, key_len, 1)
    forward = ()
    for m in range(micro):
        forward = attention_forward(
            m, forward, q_all, k_all, v_all, prev_logits,
            seg_keys[:, :, None], seg_rows[:, None, :], chunks, wide,
        )
        if m == 0 and fast:
            forward, first, last = lax.optimization_barrier((tuple(forward), *pieces[:2]))
            late = late_weights_finish(mesh_dims, first, last, *pieces[2:])
    logits, expo, o_part, st_part, tops = forward
    o_part = from_chunks(o_part, keys).reshape(micro, Y, X, 2, width, key_len)
    st_part = from_chunks(st_part, keys).reshape(micro, groups, Y, X, 2, 2 * GROUP, key_len)
    out_hidden, datt_all, st_all, grad_one, dvec, d_bias_up, *dw_late = middle(
        mesh_dims, o_part, st_part, x_own, out_cot.reshape(x_own.shape), late, vec, bias_up[None]
    )
    out_hidden = out_hidden.reshape(tokens.shape)
    datt_all = to_chunks(datt_all.reshape(micro, keys, width, key_len), chunks)
    st_all = to_chunks(st_all.reshape(micro, groups, keys, STAT_ROWS, key_len), chunks)
    so_far = ()
    if fast:
        first, last = late_grads_start(mesh_dims, *dw_late)
    steps = micro * (H // PER)
    turns = (0, steps * 6 // 8, steps)
    for turn in range(2):
        so_far = attention_backward(
            turns[turn], turns[turn + 1], so_far, expo, datt_all, st_all, tops, q_all, k_all, v_all, scale
        )
        if turn == 0 and fast:
            so_far, first, last = lax.optimization_barrier((tuple(so_far), first, last))
            fin = late_grads_finish(mesh_dims, first, last)
    grad_prev, dq_part, dk, dv, dq_sum = so_far
    dq_part = from_chunks(dq_part, keys).reshape(micro, Y, X, 2, width, key_len)
    inverse = inverse_order(owners)
    slot_index_list = row_index * slots_here + jnp.arange(slots_here, dtype=jnp.int32)
    block_ids = jnp.take(inverse, slot_index_list)
    if fast:
        grad_tokens, mine_late, mine_early, small_sum = tail(
            mesh_dims, inverse, dq_part, dk, dv, x_own, grad_one, wt, *fin, dvec, d_bias_up,
            xg.reshape(micro, slot_count, width), dq_sum,
        )
    else:
        dq = lax.psum_scatter(
            dq_part.reshape(micro, keys, width, key_len), "keys", scatter_dimension=1, tiled=True
        ).reshape(micro, width, key_len)
        grad_proj = jnp.swapaxes(jnp.concatenate([dq, dk, dv], axis=1), 0, 1).reshape(
            3 * width, token_count
        )
        d_qkv = dot_f32(grad_proj, x_rows, ((1,), (0,))).astype(BF16)
        grad_tokens = (
            grad_one.reshape(token_count, width) + dot_f32(grad_proj, w_t, ((0,), (0,)))
        ).astype(BF16)
        sums = jnp.sum(grad_proj.astype(F32).reshape(3, width, token_count), axis=2)
        small_sum = lax.psum(
            jnp.concatenate(
                [sums[0][None], sums[2][None], dvec[:3], d_bias_up.reshape(FF // width, width), dvec[3:6]]
            ),
            ("rows", "keys"),
        )
        grads = jnp.concatenate([d_qkv, dw_late[0]], axis=0).reshape(blocks, keys, cols_here, width)
        grads = lax.psum_scatter(grads, "keys", scatter_dimension=1, tiled=True)
        grads = jnp.take(grads.reshape(blocks, cols_here, width), inverse, axis=0)
        mine_t = lax.psum_scatter(grads, "rows", scatter_dimension=0, tiled=True).astype(F32)
    grad_tokens = grad_tokens.reshape(tokens.shape)
    flat = small_sum.reshape(-1)[: blocks * GAIN_ROW_WIDTH].reshape(blocks, GAIN_ROW_WIDTH)
    mine_small = lax.dynamic_slice(
        flat, (row_index * slots_here, key_index * cols_here), (slots_here, cols_here)
    )

    steps_done = step_count[0].astype(F32)
    fix_one = 1.0 - jnp.power(jnp.asarray(BETA_ONE, F32), steps_done)
    fix_two = 1.0 - jnp.power(jnp.asarray(BETA_TWO, F32), steps_done)
    if fast:
        first_column = block_ids * BLOCK_COLUMNS + key_index * cols_here
        mats = [jnp.swapaxes(a, 1, 2) for a in (master_mat, mom1_mat, mom2_mat)]
        updated = update_weights(
            block_ids, first_column, jnp.stack([fix_one, fix_two]), mine_late, mine_early, eigen_bases, *mats
        )
        mine_mat, new_one, new_two, new_master, copy_mat = (jnp.swapaxes(a, 1, 2) for a in updated)
    else:
        mine_mat = jnp.swapaxes(mine_t, 1, 2)
        rotated = jnp.einsum("sed,sec->sdc", eigen_bases, mine_mat, precision=HIGHEST_PREC)
        new_one = BETA_ONE * mom1_mat + (1.0 - BETA_ONE) * rotated
        new_two = BETA_TWO * mom2_mat + (1.0 - BETA_TWO) * rotated * rotated
        direction = new_one / fix_one / (jnp.sqrt(new_two / fix_two) + EPS_ADAM)
        back_rot = jnp.einsum("sdk,skc->sdc", eigen_bases, direction, precision=HIGHEST_PREC)
        columns = (
            block_ids[:, None] * (cols_here * keys)
            + key_index * cols_here
            + jnp.arange(cols_here, dtype=jnp.int32)[None, :]
        )
        rates = column_rates(columns)[:, None, :]
        new_master = master_mat - rates * (back_rot + DECAY * master_mat)
        copy_mat = new_master.astype(BF16)
    small_one = BETA_ONE * mom1_small + (1.0 - BETA_ONE) * mine_small
    small_two = BETA_TWO * mom2_small + (1.0 - BETA_TWO) * mine_small * mine_small
    new_small = master_small - RATE_SMALL * (small_one / fix_one) / (
        jnp.sqrt(small_two / fix_two) + EPS_ADAM
    )
    return (
        out_hidden,
        logits,
        grad_tokens,
        grad_prev,
        mine_mat,
        new_one,
        new_two,
        new_master,
        copy_mat,
        mine_small,
        small_one,
        small_two,
        new_small,
        new_small.astype(BF16),
    )


def solution(mesh):
    chips = mesh.shape["keys"] // 2
    side = math.isqrt(chips)
    dims = (side, side, mesh.shape["rows"]) if side * side == chips else (1, chips, mesh.shape["rows"])
    acts = P(None, "rows", "keys", None)
    scores = P(None, "rows", None, "keys", None)
    mats = P("rows", None, "keys")
    smalls = P("rows", "keys")
    return jax.shard_map(
        functools.partial(per_device, dims),
        mesh=mesh,
        in_specs=(
            acts, scores, P(None, "rows", None), acts, mats, mats, mats,
            P("rows", None, None), smalls, smalls, smalls, P(), P(),
        ),
        out_specs=(acts, scores, acts, scores) + (mats,) * 5 + (smalls,) * 5,
        check_vma=False,
    )
```
